32 devices in a mesh: rows: 2 (over core), seq: 16 (over z, y, x).
Axes of the slice: x: 2, y: 2, z: 4, core: 2. Of those that a mesh axis runs over, the one named last changes fastest.
Arguments:
- tokens: bfloat16 [2, 2048, 1024], P('rows', 'seq'), may hold values from -6 to 6
- doc_lengths: int32 [2, 8], P('rows'), may hold values from 1 to 1024, 2048 in all within a row
- cotangent: bfloat16 [2, 2048, 1024], P('rows', 'seq'), may hold values from -6 to 6
- gain_conv: bfloat16 [1024], P(('rows', 'seq')), may hold values from 0.5 to 1.5
- w_in: bfloat16 [1024, 3072], P(('rows', 'seq')), may hold values from -0.1875 to 0.1875
- kernel: bfloat16 [3, 1024], P(None, ('rows', 'seq')), may hold values from -3.5 to 3.5
- w_mix: bfloat16 [1024, 1024], P(('rows', 'seq')), may hold values from -0.1875 to 0.1875
- gain_ffa: bfloat16 [1024], P(('rows', 'seq')), may hold values from 0.5 to 1.5
- gate_a: bfloat16 [1024, 4608], P(('rows', 'seq')), may hold values from -0.1875 to 0.1875
- up_a: bfloat16 [1024, 4608], P(('rows', 'seq')), may hold values from -0.1875 to 0.1875
- down_a: bfloat16 [4608, 1024], P(None, ('rows', 'seq')), may hold values from -0.09375 to 0.09375
- gain_att: bfloat16 [1024], P(('rows', 'seq')), may hold values from 0.5 to 1.5
- w_query: bfloat16 [1024, 1024], P(('rows', 'seq')), may hold values from -0.1875 to 0.1875
- w_key: bfloat16 [1024, 512], P(('rows', 'seq')), may hold values from -0.1875 to 0.1875
- w_value: bfloat16 [1024, 512], P(('rows', 'seq')), may hold values from -0.1875 to 0.1875
- head_gains: bfloat16 [2, 64], replicated, may hold values from 0.5 to 1.5
- w_attout: bfloat16 [1024, 1024], P(None, ('rows', 'seq')), may hold values from -1 to 1
- gain_ffb: bfloat16 [1024], P(('rows', 'seq')), may hold values from 0.5 to 1.5
- gate_b: bfloat16 [1024, 4608], P(('rows', 'seq')), may hold values from -0.1875 to 0.1875
- up_b: bfloat16 [1024, 4608], P(('rows', 'seq')), may hold values from -0.1875 to 0.1875
- down_b: bfloat16 [4608, 1024], P(None, ('rows', 'seq')), may hold values from -0.09375 to 0.09375
Outputs:
- mixed: bfloat16 [2, 2048, 1024], P('rows', 'seq')
- d_tokens: bfloat16 [2, 2048, 1024], P('rows', 'seq')
- d_gain_conv: float32 [1024], P(('rows', 'seq'))
- d_w_in: float32 [1024, 3072], P(('rows', 'seq'))
- d_kernel: float32 [3, 1024], P(None, ('rows', 'seq'))
- d_w_mix: float32 [1024, 1024], P(('rows', 'seq'))
- d_gain_ffa: float32 [1024], P(('rows', 'seq'))
- d_gate_a: float32 [1024, 4608], P(('rows', 'seq'))
- d_up_a: float32 [1024, 4608], P(('rows', 'seq'))
- d_down_a: float32 [4608, 1024], P(None, ('rows', 'seq'))
- d_gain_att: float32 [1024], P(('rows', 'seq'))
- d_w_query: float32 [1024, 1024], P(('rows', 'seq'))
- d_w_key: float32 [1024, 512], P(('rows', 'seq'))
- d_w_value: float32 [1024, 512], P(('rows', 'seq'))
- d_head_gains: float32 [2, 64], replicated
- d_w_attout: float32 [1024, 1024], P(None, ('rows', 'seq'))
- d_gain_ffb: float32 [1024], P(('rows', 'seq'))
- d_gate_b: float32 [1024, 4608], P(('rows', 'seq'))
- d_up_b: float32 [1024, 4608], P(('rows', 'seq'))
- d_down_b: float32 [4608, 1024], P(None, ('rows', 'seq'))
The draws below stay inside these ranges and needn't reach their ends.
Inputs may be any that keep to these rules, and one draw needn't show every extreme that they name: `doc_lengths`: the 8 lengths of a row sum to 2048, the documents lying end to end from the row's first token; in every row the longest is exactly 1024.
All inputs are finite; a program needn't handle non-finite values.
Results may differ from the reference program's by a relative error of at most 0.019.
Values may be sent and summed in bfloat16 or wider, within the bound.
A program may use at most 384 MiB of HBM per device.

```python
import math
import jax
import jax.numpy as jnp
import numpy as np
from jax import lax

D = 1024
FF = 4608
H = 16
KVH = 8
HD = 64
KW = 3
DOCS = 8
ROWS = 2
SEQ_LEN = 2048


def spiked(drawn, own_key, source, target, shards_of, factor):
    def block_of(dim):
        return (jnp.arange(drawn.shape[dim]) // (drawn.shape[dim] // shards_of)).reshape((-1,) + (1,) * (drawn.ndim - 1 - dim))

    one_side = jax.random.permutation(own_key, shards_of)[block_of(target)]
    second = (block_of(target) + shards_of // 2) % shards_of
    return jnp.where((block_of(source) == one_side) | (block_of(source) == second), factor * drawn, drawn)


def steps_of(own_key, shape, split, least, largest):
    loudness, own = 1.0, jax.random.fold_in(own_key, 6)
    for dim, shards_of in split:
        heights = jnp.exp(jax.random.uniform(jax.random.fold_in(own, dim), (shards_of,), jnp.float32, least / len(split), largest / len(split)))
        loudness = loudness * jnp.repeat(heights, shape[dim] // shards_of).reshape([-1 if axis == dim else 1 for axis in range(len(shape))])
    return loudness


def profile(number_of, total, reach, skew):
    loads = [(1 << 20) // math.isqrt(rank ** skew) + 1 for rank in range(2, number_of + 1)]
    spare, holding = total - reach - (number_of - 1), [1] * (number_of - 1)
    while spare > 0:
        free = [i for i in range(number_of - 1) if holding[i] < reach]
        pool, left = sum([loads[i] for i in free]), spare
        for i in free:
            extra = min(reach - holding[i], max(1, left * loads[i] // pool), spare)
            holding[i] = holding[i] + extra
            spare = spare - extra
    return np.array([reach] + holding)


def uneven_parts(own_key, number_of, total, bound, skew):
    if number_of == 2:
        one = jax.random.randint(own_key, (), max(1, total - bound), min(bound, total - 1) + 1)
        return jnp.stack([one, total - one])
    tallies = jnp.asarray(profile(number_of, total, bound, skew), jnp.int32)
    pairs = (number_of - 1) // 2
    source_of, sink = tallies[1:1 + 2 * pairs:2], tallies[2:2 + 2 * pairs:2]
    room = jnp.minimum(source_of - 1, bound - sink)
    moved = jax.random.randint(jax.random.fold_in(own_key, 1), (pairs,), 0, 1 << 20) % (room + 1)
    tallies = tallies.at[1:1 + 2 * pairs:2].set(source_of - moved).at[2:2 + 2 * pairs:2].set(sink + moved)
    return tallies[jax.random.permutation(jax.random.fold_in(own_key, 2), number_of)]


def centred(key, dims, scale, most, split=(), kind=jnp.bfloat16):
    drawn = jax.random.normal(key, dims, jnp.float32) * scale
    if len(split) > 0:
        drawn = steps_of(key, dims, split, -0.22, 0.18) * drawn
    return jnp.clip(drawn, min=-most, max=most).astype(kind)


def heavy_noise(own_key, extent, deviation, limit, shards, heavy, kind=jnp.bfloat16):
    values = deviation * jax.random.normal(own_key, extent, jnp.float32)
    if shards:
        values = values * steps_of(own_key, extent, shards, -0.22, 0.18)
    return jnp.clip(spiked(values, jax.random.fold_in(own_key, 3), *heavy), -limit, limit).astype(kind)


def setup_inputs(seed: int = 0) -> dict:
    seeds = jax.random.split(jax.random.key(seed), 22)
    return {
        "tokens": heavy_noise(seeds[0], (ROWS, SEQ_LEN, D), 1.0, 6.0, ((0, 2), (1, 16)), (1, 2, 16, 2.0)),
        "doc_lengths": jax.vmap(lambda own: uneven_parts(own, DOCS, SEQ_LEN, SEQ_LEN // 2, 2))(jax.random.split(seeds[1], ROWS)).reshape((ROWS, DOCS)).astype(jnp.int32),
        "cotangent": heavy_noise(seeds[2], (ROWS, SEQ_LEN, D), 1.0, 6.0, ((0, 2), (1, 16)), (1, 2, 16, 2.0)),
        "gain_conv": jnp.clip(1.0 + 0.1 * jax.random.normal(seeds[3], (D,), jnp.float32), 0.5, 1.5).astype(jnp.bfloat16),
        "w_in": centred(seeds[4], (D, 3 * D), D ** -0.5, 0.1875, ((0, 32),)),
        "kernel": centred(seeds[5], (KW, D), KW ** -0.5, 3.5, ((1, 32),)),
        "w_mix": centred(seeds[6], (D, D), D ** -0.5, 0.1875, ((0, 32),)),
        "gain_ffa": jnp.clip(1.0 + 0.1 * jax.random.normal(seeds[7], (D,), jnp.float32), 0.5, 1.5).astype(jnp.bfloat16),
        "gate_a": centred(seeds[8], (D, FF), D ** -0.5, 0.1875, ((0, 32),)),
        "up_a": centred(seeds[9], (D, FF), D ** -0.5, 0.1875, ((0, 32),)),
        "down_a": centred(seeds[10], (FF, D), FF ** -0.5, 0.09375, ((1, 32),)),
        "gain_att": jnp.clip(1.0 + 0.1 * jax.random.normal(seeds[11], (D,), jnp.float32), 0.5, 1.5).astype(jnp.bfloat16),
        "w_query": centred(seeds[12], (D, H * HD), D ** -0.5, 0.1875, ((0, 32),)),
        "w_key": centred(seeds[13], (D, KVH * HD), D ** -0.5, 0.1875, ((0, 32),)),
        "w_value": centred(seeds[14], (D, KVH * HD), D ** -0.5, 0.1875, ((0, 32),)),
        "head_gains": jnp.clip(1.0 + 0.1 * jax.random.normal(seeds[15], (2, HD), jnp.float32), 0.5, 1.5).astype(jnp.bfloat16),
        "w_attout": centred(seeds[16], (H * HD, D), (H * HD // 32) ** -0.5, 1.0, ((1, 32),)),
        "gain_ffb": jnp.clip(1.0 + 0.1 * jax.random.normal(seeds[17], (D,), jnp.float32), 0.5, 1.5).astype(jnp.bfloat16),
        "gate_b": centred(seeds[18], (D, FF), D ** -0.5, 0.1875, ((0, 32),)),
        "up_b": centred(seeds[19], (D, FF), D ** -0.5, 0.1875, ((0, 32),)),
        "down_b": centred(seeds[20], (FF, D), FF ** -0.5, 0.09375, ((1, 32),)),
    }


EPSILON = 1e-05
THETA = 1000000.0
MASKED = -1e+30
HIGHEST = lax.Precision.HIGHEST

@jax.custom_vjp
def low(v):
    return lax.optimization_barrier(v.astype(jnp.bfloat16)).astype(jnp.float32)

@jax.custom_vjp
def low_back(v):
    return v

def low_keep(v):
    return (low(v), None)

def low_pass(kept, grad):
    return (grad,)

def back_keep(v):
    return (v, None)

def back_low(kept, grad):
    return (low(grad),)
low.defvjp(low_keep, low_pass)
low_back.defvjp(back_keep, back_low)

def matmul_hi(left, right):
    return jnp.dot(left, right, precision=HIGHEST, preferred_element_type=jnp.float32)

def doc_info(positions, lengths):
    doc_ends = jnp.cumsum(lengths, dtype=jnp.int32)
    passed = positions[:, None] >= doc_ends[None, :]
    segment = lax.optimization_barrier(jnp.sum(passed.astype(jnp.int32), axis=1, dtype=jnp.int32))
    opening = lax.optimization_barrier(jnp.sum(jnp.where(passed, lengths[None, :], 0), axis=1, dtype=jnp.int32))
    return (segment, positions - opening)

def rms_norm(values, norm_gain):
    return values * lax.rsqrt(lax.optimization_barrier(jnp.mean(values * values, axis=-1, keepdims=True)) + EPSILON) * norm_gain

def rope_tables(relative, head_size):
    half_size = head_size // 2
    frequency = jnp.exp(jnp.arange(half_size, dtype=jnp.float32) * (-2.0 * math.log(THETA) / head_size))
    angles = relative.astype(jnp.float32)[:, None] * frequency[None, :]
    return (jnp.cos(angles)[:, None, :], jnp.sin(angles)[:, None, :])

def rope_apply(values, cosine, sine_table):
    half_size = values.shape[-1] // 2
    front_half = values[..., :half_size]
    back_half = values[..., half_size:]
    return jnp.concatenate([front_half * cosine - back_half * sine_table, back_half * cosine + front_half * sine_table], axis=-1)

def feed_forward(hidden, norm_gain, gate_w, up_w, down_w):
    normed = low(rms_norm(hidden, norm_gain))
    gate_pre = low_back(matmul_hi(normed, gate_w))
    up_pre = low_back(matmul_hi(normed, up_w))
    activated = low(jax.nn.silu(gate_pre) * up_pre)
    return hidden + low_back(matmul_hi(activated, down_w))

def forward(hidden, lengths, weights):
    gain_conv, w_in, kernel, w_mix, gain_ffa, gate_a, up_a, down_a, gain_att, w_query, w_key, w_value, head_gains, w_attout, gain_ffb, gate_b, up_b, down_b = weights
    total_rows = hidden.shape[0]
    features = hidden.shape[1]
    halo_rows = kernel.shape[0] - 1
    positions = jnp.arange(total_rows, dtype=jnp.int32)
    segment, relative = doc_info(positions, lengths)
    ext_seg, unused = doc_info(jnp.arange(total_rows + halo_rows, dtype=jnp.int32) - halo_rows, lengths)
    normed = low(rms_norm(hidden, gain_conv))
    projected = low_back(matmul_hi(normed, w_in))
    gate_front = projected[:, :features]
    gate_back = projected[:, features:2 * features]
    signal = projected[:, 2 * features:]
    product = low(gate_front * signal)
    extended = jnp.concatenate([jnp.zeros((halo_rows, features), jnp.float32), product], axis=0)
    convolved = kernel[0] * extended[0:total_rows] * (ext_seg[0:total_rows] == segment).astype(jnp.float32)[:, None]
    for offset in range(1, halo_rows + 1):
        allowed = (ext_seg[offset:offset + total_rows] == segment).astype(jnp.float32)[:, None]
        convolved = convolved + kernel[offset] * extended[offset:offset + total_rows] * allowed
    convolved = low_back(convolved)
    hidden_one = hidden + low_back(matmul_hi(low(gate_back * convolved), w_mix))
    hidden_two = feed_forward(hidden_one, gain_ffa, gate_a, up_a, down_a)
    normed = low(rms_norm(hidden_two, gain_att))
    query_pre = low_back(matmul_hi(normed, w_query)).reshape(total_rows, H, HD)
    key_pre = low_back(matmul_hi(normed, w_key)).reshape(total_rows, KVH, HD)
    values_all = low(low_back(matmul_hi(normed, w_value))).reshape(total_rows, KVH, HD)
    cosine, sine_table = rope_tables(relative, HD)
    groups = H // KVH
    queries = low(rope_apply(rms_norm(query_pre, head_gains[0]), cosine, sine_table)).reshape(total_rows, KVH, groups, HD)
    keys_all = low(rope_apply(rms_norm(key_pre, head_gains[1]), cosine, sine_table))
    factor = 1.0 / math.sqrt(HD)
    query_block = math.gcd(total_rows, 512)
    blocks = total_rows // query_block

    @jax.checkpoint
    def attend(piece):
        block_queries, block_seg, block_pos = piece
        allowed = (block_seg[:, None] == segment[None, :]) & (positions[None, :] <= block_pos[:, None])
        raw_scores = jnp.einsum('qkgd,tkd->kgqt', block_queries, keys_all, precision=HIGHEST)
        scores = jnp.where(allowed[None, None], low_back(raw_scores * factor), MASKED)
        shares = jax.nn.softmax(scores, axis=-1)
        return low_back(jnp.einsum('kgqt,tkd->qkgd', low(shares), values_all, precision=HIGHEST))
    attended = lax.map(attend, (queries.reshape(blocks, query_block, KVH, groups, HD), segment.reshape(blocks, query_block), positions.reshape(blocks, query_block)))
    attended = low(attended.reshape(total_rows, H * HD))
    hidden_three = hidden_two + low_back(matmul_hi(attended, w_attout))
    return feed_forward(hidden_three, gain_ffb, gate_b, up_b, down_b)

def reference(tokens, doc_lengths, cotangent, gain_conv, w_in, kernel, w_mix, gain_ffa, gate_a, up_a, down_a, gain_att, w_query, w_key, w_value, head_gains, w_attout, gain_ffb, gate_b, up_b, down_b):
    weights = tuple((weight.astype(jnp.float32) for weight in (gain_conv, w_in, kernel, w_mix, gain_ffa, gate_a, up_a, down_a, gain_att, w_query, w_key, w_value, head_gains, w_attout, gain_ffb, gate_b, up_b, down_b)))

    def one_row(totals, row):
        row_tokens, row_lengths, row_cot = row
        result, pull = jax.vjp(lambda hidden, params: forward(hidden, row_lengths, params), row_tokens.astype(jnp.float32), weights)
        d_hidden, d_params = pull(row_cot.astype(jnp.float32))
        totals = jax.tree.map(jnp.add, totals, d_params)
        return (totals, (result.astype(jnp.bfloat16), d_hidden.astype(jnp.bfloat16)))
    zeros = tuple((jnp.zeros_like(weight) for weight in weights))
    sums, (mixed, d_tokens) = lax.scan(one_row, zeros, (tokens, doc_lengths, cotangent))
    return (mixed, d_tokens, sums[0], sums[1], sums[2], sums[3], sums[4], sums[5], sums[6], sums[7], sums[8], sums[9], sums[10], sums[11], sums[12], sums[13], sums[14], sums[15], sums[16], sums[17])
```

```python
import functools
import math

import jax
import jax.numpy as jnp
from jax import lax
from jax.experimental import pallas as pl
from jax.experimental.pallas import tpu as pltpu
from jax.sharding import PartitionSpec as P

H = 16
KVH = 8
HD = 64
TP = 4
HALO = 16

EPSILON = 1e-05
THETA = 1000000.0
MASKED = -1e30
MESH_ID = pl.DeviceIdType.MESH
BF = jnp.bfloat16
F32 = jnp.float32


def dot(left, right):
    return jnp.dot(left, right, preferred_element_type=F32)


def dot_tn(left, right):
    return lax.dot_general(left, right, (((0,), (0,)), ((), ())), preferred_element_type=F32)


def dot_nt(left, right):
    return lax.dot_general(left, right, (((1,), (1,)), ((), ())), preferred_element_type=F32)


class Place:
    def __init__(self, rows, seq):
        self.R, self.S = rows, seq
        self.Q = seq // TP

    def here(self):
        here = Place(self.R, self.S)
        here.r = lax.axis_index("rows")
        here.s = lax.axis_index("seq")
        here.q = here.s // TP
        here.p = lax.rem(here.s, TP)
        return here


class Copies:
    def __init__(self, send, recv):
        self.send, self.recv, self.count, self.sent = send, recv, 0, []

    def slot(self):
        self.count += 1
        return self.count - 1

    def remote(self, src, dst, slot, where, recv_slot=None):
        return pltpu.make_async_remote_copy(
            src_ref=src,
            dst_ref=dst,
            send_sem=self.send.at[slot],
            recv_sem=self.recv.at[slot if recv_slot is None else recv_slot],
            device_id=where,
            device_id_type=MESH_ID,
        )

    def push(self, src, dst, slot, where, cond=None, recv_slot=None):
        copy = self.remote(src, dst, slot, where, recv_slot)
        when(cond, copy.start)
        self.sent.append((copy.wait_send, cond))

    def arrived(self, dst, slot, where, cond=None):
        copy = self.remote(dst, dst, slot, where)
        when(cond, copy.wait_recv)

    def local(self, src, dst):
        slot = self.slot()
        copy = pltpu.make_async_copy(src, dst, self.recv.at[slot])
        copy.start()
        self.sent.append((copy.wait, None))

    def drain(self):
        for wait, cond in self.sent:
            when(cond, wait)


def when(cond, action):
    if cond is None:
        action()
    else:
        pl.when(cond)(lambda: action())


class Job:
    def __init__(self, ins, outs, run, kinds, aliases=(), vmem=(), relay=False, late=False):
        self.ins, self.outs, self.run, self.kinds = ins, outs, run, kinds
        self.aliases, self.vmem, self.relay, self.late = aliases, vmem, relay, late


def together(runs):
    while runs:
        runs = [steps for steps in runs if next(steps, "done") != "done"]
        yield "go"


def partners(at, kinds):
    found = []
    if "plane" in kinds:
        for j in range(1, TP):
            found.append((None, at.r, at.q * TP + lax.rem(at.p + j, TP)))
    if "core" in kinds:
        for j in range(1, at.R):
            found.append((None, lax.rem(at.r + j, at.R), at.s))
    if "zall" in kinds:
        for j in range(1, at.Q):
            found.append((None, at.r, lax.rem(at.q + j, at.Q) * TP + at.p))
    elif "chain" in kinds:
        found.append((at.q > 0, at.r, at.s - TP))
        found.append((at.q < at.Q - 1, at.r, at.s + TP))
    if "halo" in kinds:
        found.append((at.q > 0, at.r, (at.q - 1) * TP + TP - 1))
        found.append((at.q < at.Q - 1, at.r, (at.q + 1) * TP))
        for j in range(TP):
            found.append(((at.p == TP - 1) & (at.q < at.Q - 1), at.r, (at.q + 1) * TP + j))
            found.append(((at.p == 0) & (at.q > 0), at.r, (at.q - 1) * TP + j))
    return found


def meet(at, kinds):
    barrier = pltpu.get_barrier_semaphore()
    peers = partners(at, kinds)
    for cond, r, s in peers:
        when(
            cond,
            functools.partial(
                pl.semaphore_signal, barrier, inc=1, device_id=(r, s), device_id_type=MESH_ID
            ),
        )
    awaited = sum(1 for cond, r, s in peers if cond is None)
    for cond, r, s in peers:
        if cond is not None:
            awaited = awaited + cond.astype(jnp.int32)
    pl.semaphore_wait(barrier, awaited)


def exchange(place, ident, jobs):
    kinds = set().union(*[job.kinds for job in jobs])
    n_in = sum(len(job.ins) for job in jobs)
    n_out = sum(len(job.outs) for job in jobs)
    sems = 24 + sum(12 + 2 * place.Q + place.R * place.Q for job in jobs)
    arrays, in_specs, outs, aliases = [], [], [], {}
    for job in jobs:
        for k, o in job.aliases:
            aliases[len(arrays) + k] = len(outs) + o
        for k, value in enumerate(job.ins):
            arrays.append(value)
            in_specs.append(pl.BlockSpec(memory_space=pltpu.VMEM if k in job.vmem else pl.ANY))
        outs.extend(job.outs)

    def body(*refs):
        at = place.here()
        ins, results = refs[:n_in], refs[n_in : n_in + n_out]
        copies = Copies(refs[n_in + n_out], refs[n_in + n_out + 1])
        meet(at, kinds)
        runs, i, o = [], 0, 0
        for job in jobs:
            runs.append(
                job.run(at, copies, ins[i : i + len(job.ins)], results[o : o + len(job.outs)])
            )
            i, o = i + len(job.ins), o + len(job.outs)
        pairs = list(zip(jobs, runs))
        relays = together([steps for job, steps in pairs if job.relay])
        for steps in [steps for job, steps in pairs if not job.relay and not job.late]:
            next(steps)
        next(relays, "done")
        next(relays, "done")
        for steps in [steps for job, steps in pairs if job.late]:
            next(steps)
        for _ in relays:
            pass
        for steps in [steps for job, steps in pairs if not job.relay]:
            for _ in steps:
                pass
        copies.drain()

    results = pl.pallas_call(
        body,
        out_shape=tuple(outs),
        in_specs=in_specs,
        out_specs=tuple(pl.BlockSpec(memory_space=pl.ANY) for _ in outs),
        scratch_shapes=[pltpu.SemaphoreType.DMA((sems,)), pltpu.SemaphoreType.DMA((sems,))],
        input_output_aliases=aliases,
        compiler_params=pltpu.CompilerParams(collective_id=ident, has_side_effects=True),
        name="exchange_%d" % ident,
    )(*arrays)
    given, o = [], 0
    for job in jobs:
        given.append(results[o : o + len(job.outs)])
        o += len(job.outs)
    return given


def like(shape, dtype=BF):
    return jax.ShapeDtypeStruct(shape, dtype)


def gather_plane(value):
    def run(at, copies, ins, outs):
        slots = [copies.slot() for _ in range(TP - 1)]
        for j in range(1, TP):
            peer = at.q * TP + lax.rem(at.p + j, TP)
            copies.push(ins[0], outs[0].at[at.p], slots[j - 1], (at.r, peer))
        copies.local(ins[0], outs[0].at[at.p])
        yield "go"
        for j in range(1, TP):
            origin = lax.rem(at.p + TP - j, TP)
            copies.arrived(outs[0].at[origin], slots[j - 1], (at.r, at.s))

    return Job([value], [like((TP,) + value.shape, value.dtype)], run, {"plane"}, vmem=(0,))


def swap_plane(value):
    def run(at, copies, ins, outs):
        slots = [copies.slot() for _ in range(TP - 1)]
        for j in range(1, TP):
            other = lax.rem(at.p + j, TP)
            copies.push(
                ins[0].at[other], outs[0].at[at.p], slots[j - 1], (at.r, at.q * TP + other)
            )
        yield "go"
        for j in range(1, TP):
            origin = lax.rem(at.p + TP - j, TP)
            copies.arrived(outs[0].at[origin], slots[j - 1], (at.r, at.s))

    return Job([value], [like(value.shape, value.dtype)], run, {"plane"})


def swap_core(value):
    def run(at, copies, ins, outs):
        slots = [copies.slot() for _ in range(at.R - 1)]
        for j in range(1, at.R):
            other = lax.rem(at.r + j, at.R)
            copies.push(ins[0].at[other], outs[0].at[at.r], slots[j - 1], (other, at.s))
        yield "go"
        for j in range(1, at.R):
            origin = lax.rem(at.r + at.R - j, at.R)
            copies.arrived(outs[0].at[origin], slots[j - 1], (at.r, at.s))

    return Job([value], [like(value.shape, value.dtype)], run, {"core"})


def swap_line(value):
    def run(at, copies, ins, outs):
        slots = [copies.slot() for _ in range(at.Q - 1)]
        for j in range(1, at.Q):
            other = lax.rem(at.q + j, at.Q)
            copies.push(
                ins[0].at[other], outs[0].at[at.q], slots[j - 1], (at.r, other * TP + at.p)
            )
        yield "go"
        for j in range(1, at.Q):
            origin = lax.rem(at.q + at.Q - j, at.Q)
            copies.arrived(outs[0].at[origin], slots[j - 1], (at.r, at.s))

    return Job([value], [like(value.shape, value.dtype)], run, {"zall"})


def window_forward(place, value):
    reach = place.Q // 2

    def run(at, copies, ins, outs):
        slots = [copies.slot() for _ in range(reach)]
        for j in range(1, reach + 1):
            target = (at.q + j) * TP + at.p
            copies.push(ins[0], outs[0].at[j], slots[j - 1], (at.r, target), at.q + j < at.Q)
        copies.local(ins[0], outs[0].at[0])
        yield "go"
        for j in range(1, reach + 1):
            copies.arrived(outs[0].at[j], slots[j - 1], (at.r, at.s), at.q >= j)

    shape = (reach + 1,) + value.shape
    return Job([value], [like(shape, value.dtype)], run, {"zall"}, vmem=(0,))


def window_backward(place, value):
    reach = place.Q // 2

    def run(at, copies, ins, outs):
        slots = [copies.slot() for _ in range(reach)]
        for j in range(1, reach + 1):
            target = (at.q - j) * TP + at.p
            copies.push(
                ins[0].at[j], outs[0].at[j - 1], slots[j - 1], (at.r, target), at.q >= j
            )
        yield "go"
        for j in range(1, reach + 1):
            copies.arrived(outs[0].at[j - 1], slots[j - 1], (at.r, at.s), at.q + j < at.Q)

    shape = (reach,) + value.shape[1:]
    return Job([value], [like(shape, value.dtype)], run, {"zall"})


def halo_tokens(value):
    rows = value.shape[0]

    def run(at, copies, ins, outs):
        ahead = [copies.slot() for _ in range(TP)]
        back = [copies.slot() for _ in range(TP)]
        first = (at.p == 0) & (at.q > 0)
        last = (at.p == TP - 1) & (at.q < at.Q - 1)
        for j in range(TP):
            tail = ins[0].at[pl.ds(rows - HALO, HALO)]
            there = (at.r, (at.q + 1) * TP + j)
            copies.push(tail, outs[0], ahead[j], there, last, ahead[0])
            head = ins[0].at[pl.ds(0, HALO)]
            there = (at.r, (at.q - 1) * TP + j)
            copies.push(head, outs[1], back[j], there, first, back[0])
        yield "go"
        copies.arrived(outs[0], ahead[0], (at.r, at.s), at.q > 0)
        copies.arrived(outs[1], back[0], (at.r, at.s), at.q < at.Q - 1)

    shape = (HALO,) + value.shape[1:]
    outs = [like(shape, value.dtype), like(shape, value.dtype)]
    return Job([value], outs, run, {"halo"}, vmem=(0,))


def spread_run(place, at, copies, source, held, lead):
    mine = at.r * at.S + at.s
    slots = [copies.slot() for _ in range(TP - 1)]

    def slot_of(shard):
        return held.at[shard] if lead is None else held.at[:, shard]

    for j in range(1, TP):
        other = lax.rem(at.p + j, TP)
        copies.push(source.at[other], slot_of(mine), slots[j - 1], (at.r, at.q * TP + other))
    copy = pltpu.make_async_copy(source.at[at.p], slot_of(mine), copies.recv.at[copies.slot()])
    copy.start()
    yield "go"
    copy.wait()
    for j in range(1, TP):
        origin = at.r * at.S + at.q * TP + lax.rem(at.p + TP - j, TP)
        copies.arrived(slot_of(origin), slots[j - 1], (at.r, at.s))


def chain_run(at, copies, held):
    def block(r, q):
        return held.at[pl.ds((r * at.Q + q) * TP, TP)]

    right = [copies.slot() for _ in range(at.Q - 1)]
    left = [copies.slot() for _ in range(at.Q - 1)]
    across = [[copies.slot() for _ in range(at.Q)] for _ in range(at.R - 1)]

    def cross(q, index, cond):
        for j in range(1, at.R):
            other = lax.rem(at.r + j, at.R)
            copies.push(block(at.r, q), block(at.r, q), across[j - 1][index], (other, at.s), cond)

    copies.push(
        block(at.r, at.q), block(at.r, at.q), right[0], (at.r, at.s + TP), at.q < at.Q - 1
    )
    copies.push(block(at.r, at.q), block(at.r, at.q), left[0], (at.r, at.s - TP), at.q > 0)
    cross(at.q, 0, None)
    index = 0
    spots = {}
    for hop in range(1, at.Q):
        yield "go"
        from_left, from_right = at.q >= hop, at.q + hop < at.Q
        copies.arrived(block(at.r, at.q - hop), right[hop - 1], (at.r, at.s), from_left)
        if hop < at.Q - 1:
            copies.push(
                block(at.r, at.q - hop),
                block(at.r, at.q - hop),
                right[hop],
                (at.r, at.s + TP),
                from_left & (at.q < at.Q - 1),
            )
        copies.arrived(block(at.r, at.q + hop), left[hop - 1], (at.r, at.s), from_right)
        if hop < at.Q - 1:
            copies.push(
                block(at.r, at.q + hop),
                block(at.r, at.q + hop),
                left[hop],
                (at.r, at.s - TP),
                from_right & (at.q > 0),
            )
        for side, sign in ((from_left, -1), (from_right, 1)):
            spots[(hop, sign)] = [copies.slot() for _ in range(at.R - 1)]
            for j in range(1, at.R):
                other = lax.rem(at.r + j, at.R)
                piece = block(at.r, at.q + sign * hop)
                copies.push(piece, piece, spots[(hop, sign)][j - 1], (other, at.s), side)
    yield "go"
    for j in range(1, at.R):
        source = lax.rem(at.r + at.R - j, at.R)
        copies.arrived(block(source, at.q), across[j - 1][0], (at.r, at.s))
        for hop in range(1, at.Q):
            for sign in (-1, 1):
                there = at.q + sign * hop
                copies.arrived(
                    block(source, there),
                    spots[(hop, sign)][j - 1],
                    (at.r, at.s),
                    at.q >= hop if sign < 0 else there < at.Q,
                )


def spread(place, source, lead=None, chained=False):
    total = place.R * place.S
    inner = source.shape[1:]
    shape = (total,) + inner if lead is None else (lead, total) + inner[1:]

    def run(at, copies, ins, outs):
        yield from spread_run(place, at, copies, ins[0], outs[0], lead)
        if chained:
            yield from chain_run(at, copies, outs[0])

    kinds = {"plane"} | ({"chain", "core"} if chained else set())
    outs = [like(shape, source.dtype)]
    return Job([source], outs, run, kinds, vmem=(0,), relay=chained, late=not chained)


def chain(held, parts=None):
    def run(at, copies, ins, outs):
        pieces = [outs[0]] if parts is None else [outs[0].at[part] for part in parts]
        yield from together([chain_run(at, copies, piece) for piece in pieces])

    kinds = {"chain", "core"}
    return Job([held], [like(held.shape, held.dtype)], run, kinds, ((0, 0),), relay=True)


def doc_info(positions, lengths):
    doc_ends = jnp.cumsum(lengths, dtype=jnp.int32)
    passed = positions[:, None] >= doc_ends[None, :]
    segment = jnp.sum(passed.astype(jnp.int32), axis=1, dtype=jnp.int32)
    opening = jnp.sum(jnp.where(passed, lengths[None, :], 0), axis=1, dtype=jnp.int32)
    return (segment, positions - opening)


def inverse_rms(values):
    return lax.rsqrt(jnp.mean(values * values, axis=-1, keepdims=True) + EPSILON)


def rms_pull(upstream, values, inverse, norm_gain):
    scaled = upstream * norm_gain
    product_mean = jnp.mean(scaled * values, axis=-1, keepdims=True)
    return inverse * scaled - values * (inverse * inverse * inverse) * product_mean


def rope_tables(relative):
    half_size = HD // 2
    frequency = jnp.exp(
        jnp.arange(half_size, dtype=F32) * (-2.0 * math.log(THETA) / HD)
    )
    angles = relative.astype(F32)[:, None] * frequency[None, :]
    return (jnp.cos(angles)[:, None, :], jnp.sin(angles)[:, None, :])


def rope_apply(values, cosine, sine):
    front, back = values[..., : HD // 2], values[..., HD // 2 :]
    return jnp.concatenate([front * cosine - back * sine, back * cosine + front * sine], axis=-1)


def rope_revert(values, cosine, sine):
    front, back = values[..., : HD // 2], values[..., HD // 2 :]
    return jnp.concatenate([front * cosine + back * sine, back * cosine - front * sine], axis=-1)


def settle(own, arrived, p):
    index = jnp.arange(TP, dtype=jnp.int32)[:, None, None]
    others = jnp.where(index == p, 0.0, arrived.astype(F32))
    mine = lax.dynamic_index_in_dim(own, p, 0, keepdims=False)
    return mine + jnp.sum(others, axis=0)


def per_device(
    place,
    tokens,
    doc_lengths,
    cotangent,
    gain_conv,
    w_in,
    kernel,
    w_mix,
    gain_ffa,
    gate_a,
    up_a,
    down_a,
    gain_att,
    w_query,
    w_key,
    w_value,
    head_gains,
    w_attout,
    gain_ffb,
    gate_b,
    up_b,
    down_b,
):
    R, S, Q = place.R, place.S, place.Q
    n, D = tokens.shape[1], tokens.shape[2]
    shard = w_in.shape[0]
    FS = gate_a.shape[1] // TP
    CS = D // TP
    QS, KS = H * HD // TP, KVH * HD // TP
    taps = kernel.shape[0]
    N = n * TP
    r, s = lax.axis_index("rows"), lax.axis_index("seq")
    q, p = s // TP, lax.rem(s, TP)
    lengths = doc_lengths[0]

    def slices(weight):
        return weight.reshape(shard, TP, -1).transpose(1, 0, 2)

    in_cut = w_in.reshape(shard, 3, TP, CS).transpose(2, 0, 1, 3).reshape(TP, shard, 3 * CS)

    def ffn_cut(gate, up, down):
        return jnp.stack([slices(gate), slices(up), slices(down.T)], axis=1)

    att_cut = jnp.concatenate(
        [slices(w_query), slices(w_key), slices(w_value), slices(w_attout.T)], axis=2
    )
    small = jnp.stack([gain_conv, gain_ffa, gain_att, gain_ffb] + [kernel[i] for i in range(taps)])
    small = jnp.pad(small, ((0, 16 - 4 - taps), (0, 128 - shard)))
    small = jnp.broadcast_to(small[None], (TP, 16, 128))
    mix_full = lax.all_gather(w_mix, ("rows", "seq"), axis=0, tiled=True)

    mine = tokens[0]
    (tok_g,), (halo_a, halo_b), (in_g,), (small_g,), (ffa_g,), (att_g,), (ffb_g,) = exchange(
        place,
        0,
        [
            gather_plane(mine),
            halo_tokens(mine),
            spread(place, in_cut, chained=True),
            spread(place, small, chained=True),
            spread(place, ffn_cut(gate_a, up_a, down_a), lead=3),
            spread(place, att_cut),
            spread(place, ffn_cut(gate_b, up_b, down_b), lead=3),
        ],
    )
    vectors = small_g[:, : 4 + taps, :shard].transpose(1, 0, 2).reshape(4 + taps, D).astype(F32)
    g_conv, g_ffa, g_att, g_ffb = (vectors[i] for i in range(4))
    kernel_f = lax.dynamic_slice_in_dim(vectors[4:], p * CS, CS, 1)
    w_in_s = in_g.reshape(D, 3 * CS)
    w_mix_s = lax.dynamic_slice_in_dim(mix_full, p * CS, CS, 0)

    def by_row(grads):
        return grads.astype(BF).reshape(R, S, shard, -1)

    def own(parts, index):
        return lax.dynamic_index_in_dim(parts, index, 0, keepdims=False).astype(F32)

    def collect(parts, came, index):
        slot = jnp.arange(came.shape[0], dtype=jnp.int32).reshape((-1,) + (1,) * (came.ndim - 1))
        mine_part = lax.dynamic_index_in_dim(parts, index, 0, keepdims=True).astype(F32)
        return jnp.sum(jnp.where(slot == index, mine_part, came.astype(F32)), axis=0)

    def after_core(parts, came):
        summed = collect(parts, came, r)
        return summed.reshape((Q, TP) + summed.shape[1:])

    def after_line(parts, came):
        return collect(parts, came, q)

    def after_plane(full, came):
        slot = jnp.arange(TP, dtype=jnp.int32).reshape((TP,) + (1,) * (full.ndim - 1))
        mine_part = lax.dynamic_index_in_dim(full, p, 0, keepdims=True)
        return jnp.where(slot == p, mine_part, came.astype(F32))

    def low(parts):
        return [part.astype(BF) for part in parts]

    total = S * n
    pos_ext = q * N - HALO + jnp.arange(N + 2 * HALO, dtype=jnp.int32)
    seg_ext, rel_ext = doc_info(pos_ext, lengths)
    valid = ((pos_ext >= 0) & (pos_ext < total))[:, None]
    x_ext = jnp.concatenate([halo_a, tok_g.reshape(N, D), halo_b], axis=0)
    x_ext = jnp.where(valid, x_ext, jnp.zeros_like(x_ext)).astype(F32)
    r0_ext = inverse_rms(x_ext)
    n1_ext = (x_ext * r0_ext * g_conv).astype(BF)
    z_ext = dot(n1_ext, w_in_s)
    b_ext, c_ext, v_ext = z_ext[:, :CS], z_ext[:, CS : 2 * CS], z_ext[:, 2 * CS :]
    u_ext = lax.optimization_barrier((b_ext * v_ext).astype(BF)).astype(F32)
    span = slice(HALO, HALO + N)
    same = [
        (seg_ext[HALO - 2 + k : HALO - 2 + k + N] == seg_ext[span]).astype(F32)[:, None]
        for k in range(taps)
    ]
    near = [u_ext[HALO - 2 + k : HALO - 2 + k + N] for k in range(taps)]
    conv = kernel_f[0] * near[0] * same[0]
    for k in range(1, taps):
        conv = conv + kernel_f[k] * near[k] * same[k]
    m_bf = (c_ext[span] * conv).astype(BF)
    part = dot(m_bf, w_mix_s).reshape(TP, n, D)
    (got,), (ffa_g,) = exchange(
        place, 1, [swap_plane(part.astype(BF)), chain(ffa_g, (0, 1))]
    )
    x0 = mine.astype(F32)
    h1 = x0 + settle(part, got, p)

    r1 = inverse_rms(h1)
    a1 = (h1 * r1 * g_ffa).astype(BF)
    (a1_g,), (ffa_g,) = exchange(place, 2, [gather_plane(a1), chain(ffa_g, (2,))])
    a1_g = a1_g.reshape(N, D)
    wa = ffa_g.reshape(3, D, FS)

    def ffn(a, w):
        gate, up = dot(a, w[0]), dot(a, w[1])
        act = (jax.nn.silu(gate) * up).astype(BF)
        return gate, up, act, dot_nt(act, w[2]).reshape(TP, n, D)

    gate1, up1, act1, part = ffn(a1_g, wa)
    (got,), (att_g,) = exchange(place, 3, [swap_plane(part.astype(BF)), chain(att_g)])
    h2 = h1 + settle(part, got, p)

    r2 = inverse_rms(h2)
    n3 = (h2 * r2 * g_att).astype(BF)
    (n3_g,), (ffb_g,) = exchange(place, 4, [gather_plane(n3), chain(ffb_g, (0,))])
    n3_g = n3_g.reshape(N, D)
    w_att = att_g.reshape(D, 2 * QS + 2 * KS)
    w_qkv, w_out = w_att[:, : QS + 2 * KS], w_att[:, QS + 2 * KS :]
    qkv = dot(n3_g, w_qkv)
    heads, kv_heads = QS // HD, KS // HD
    groups = heads // kv_heads
    q_pre = qkv[:, :QS].reshape(N, heads, HD)
    k_pre = qkv[:, QS : QS + KS].reshape(N, kv_heads, HD)
    head_f = head_gains.astype(F32)
    cosine, sine = rope_tables(rel_ext[span])
    q_inv, k_inv = inverse_rms(q_pre), inverse_rms(k_pre)
    q_bf = rope_apply(q_pre * q_inv * head_f[0], cosine, sine).astype(BF)
    k_bf = rope_apply(k_pre * k_inv * head_f[1], cosine, sine).astype(BF).reshape(N, KS)
    v_bf = qkv[:, QS + KS :].astype(BF)
    (kv_w,), (ffb_g,) = exchange(
        place,
        5,
        [window_forward(place, jnp.concatenate([k_bf, v_bf], axis=1)), chain(ffb_g, (1,))],
    )
    reach = Q // 2 + 1
    q_pos = pos_ext[span]
    key_pos = (q_pos[None, :] - N * jnp.arange(reach, dtype=jnp.int32)[:, None]).reshape(-1)
    key_seg, _ = doc_info(key_pos, lengths)
    kv_all = kv_w.reshape(reach * N, 2 * KS)
    kv_all = jnp.where((key_pos >= 0)[:, None], kv_all, jnp.zeros_like(kv_all))
    allowed = (
        (seg_ext[span][:, None] == key_seg[None, :])
        & (key_pos[None, :] <= q_pos[:, None])
        & (key_pos[None, :] >= 0)
    )
    k_all = kv_all[:, :KS].reshape(reach * N, kv_heads, HD)
    v_all = kv_all[:, KS:].reshape(reach * N, kv_heads, HD)
    q_grp = q_bf.reshape(N, kv_heads, groups, HD)
    factor = 1.0 / math.sqrt(HD)
    raw = jnp.einsum("qkgd,tkd->kgqt", q_grp, k_all, preferred_element_type=F32)
    scores = jnp.where(allowed[None, None], raw * factor, MASKED)
    shares = jax.nn.softmax(scores, axis=-1)
    shares_bf = shares.astype(BF)
    o_bf = (
        jnp.einsum("kgqt,tkd->qkgd", shares_bf, v_all, preferred_element_type=F32)
        .reshape(N, QS)
        .astype(BF)
    )
    part = dot_nt(o_bf, w_out).reshape(TP, n, D)
    (got,), (ffb_g,) = exchange(place, 6, [swap_plane(part.astype(BF)), chain(ffb_g, (2,))])
    h3 = h2 + settle(part, got, p)

    r3 = inverse_rms(h3)
    a2 = (h3 * r3 * g_ffb).astype(BF)
    e_bf = cotangent[0]
    (a2_g,), (e_g,) = exchange(place, 7, [gather_plane(a2), gather_plane(e_bf)])
    a2_g, e_g = a2_g.reshape(N, D), e_g.reshape(N, D)
    wb = ffb_g.reshape(3, D, FS)
    gate2, up2, act2, part = ffn(a2_g, wb)

    def ffn_back(e, a, gate, up, act, w):
        d_down = dot_tn(e, act)
        d_act = dot(e, w[2])
        sigma = jax.nn.sigmoid(gate)
        d_gate = (d_act * up * sigma * (1.0 + gate * (1.0 - sigma))).astype(BF)
        d_up = (d_act * (gate * sigma)).astype(BF)
        grads = [by_row(dot_tn(a, d_gate)), by_row(dot_tn(a, d_up)), by_row(d_down)]
        d_normed = dot_nt(d_gate, w[0]) + dot_nt(d_up, w[1])
        return grads, d_normed.reshape(TP, n, D)

    grads_b, part_b = ffn_back(e_g, a2_g, gate2, up2, act2, wb)

    (got,), (got_b,), *core_b = exchange(
        place,
        8,
        [swap_plane(part.astype(BF)), swap_plane(part_b.astype(BF))]
        + [swap_core(rows) for rows in grads_b],
    )
    h4 = h3 + settle(part, got, p)
    mixed = h4.astype(BF)[None]
    d_gain = {}
    d_normed = settle(part_b, got_b, p)
    d_gain["ffb"] = jnp.sum(d_normed * h3 * r3, axis=0)
    g4 = e_bf.astype(F32)
    g3 = g4 + rms_pull(d_normed, h3, r3, g_ffb)

    line_b = [after_core(rows, came[0]) for rows, came in zip(grads_b, core_b)]
    sent_b = low(line_b)
    (g3_g,), (got_l0,) = exchange(
        place, 9, [gather_plane(g3.astype(BF)), swap_line(sent_b[0])]
    )
    g3_g = g3_g.reshape(N, D)
    d_out = dot_tn(g3_g, o_bf)
    d_o = dot(g3_g, w_out).astype(BF).reshape(N, kv_heads, groups, HD)
    d_shares = jnp.einsum("qkgd,tkd->kgqt", d_o, v_all, preferred_element_type=F32)
    delta = jnp.sum(shares * d_shares, axis=-1, keepdims=True)
    d_scores = (shares * (d_shares - delta)).astype(BF)
    d_q = factor * jnp.einsum("kgqt,tkd->qkgd", d_scores, k_all, preferred_element_type=F32)
    d_k = factor * jnp.einsum("kgqt,qkgd->tkd", d_scores, q_grp, preferred_element_type=F32)
    d_v = jnp.einsum("kgqt,qkgd->tkd", shares_bf, d_o, preferred_element_type=F32)
    d_kv = jnp.concatenate(
        [d_k.reshape(reach, N, KS), d_v.reshape(reach, N, KS)], axis=-1
    )
    (got_kv,), (got_l1,) = exchange(
        place,
        10,
        [window_backward(place, d_kv.astype(BF)), swap_line(sent_b[1])],
    )
    there = (q + 1 + jnp.arange(reach - 1, dtype=jnp.int32) < Q)[:, None, None]
    d_kv = d_kv[0] + jnp.sum(jnp.where(there, got_kv.astype(F32), 0.0), axis=0)
    dv_bf = d_kv[:, KS:].astype(BF)
    dk_norm = rope_revert(d_kv[:, :KS].reshape(N, kv_heads, HD), cosine, sine)
    dq_norm = rope_revert(d_q.reshape(N, heads, HD), cosine, sine)
    dk_pre = rms_pull(dk_norm, k_pre, k_inv, head_f[1]).reshape(N, KS)
    dq_pre = rms_pull(dq_norm, q_pre, q_inv, head_f[0]).reshape(N, QS)
    d_heads = jnp.stack(
        [
            jnp.sum(dq_norm * q_pre * q_inv, axis=(0, 1)),
            jnp.sum(dk_norm * k_pre * k_inv, axis=(0, 1)),
        ]
    )
    d_qkv = jnp.concatenate([dq_pre.astype(BF), dk_pre.astype(BF), dv_bf], axis=1)
    part = dot_nt(d_qkv, w_qkv).reshape(TP, n, D)
    rows_att = by_row(jnp.concatenate([dot_tn(n3_g, d_qkv), d_out], axis=1))
    (got,), (got_l2,), (core_att,) = exchange(
        place,
        11,
        [
            swap_plane(part.astype(BF)),
            swap_line(sent_b[2]),
            swap_core(rows_att),
        ],
    )
    d_normed = settle(part, got, p)
    d_gain["att"] = jnp.sum(d_normed * h2 * r2, axis=0)
    g2 = g3 + rms_pull(d_normed, h2, r2, g_att)

    full_b = [after_line(x, y) for x, y in zip(sent_b, [got_l0, got_l1, got_l2])]
    line_att = after_core(rows_att, core_att)
    sent_att = line_att.astype(BF)
    (g2_g,), (line_att_got,), *plane_b = exchange(
        place,
        12,
        [gather_plane(g2.astype(BF)), swap_line(sent_att)]
        + [swap_plane(full) for full in low(full_b)],
    )
    g2_g = g2_g.reshape(N, D)
    grads_a, part = ffn_back(g2_g, a1_g, gate1, up1, act1, wa)
    full_att = after_line(sent_att, line_att_got)
    (got,), (plane_att,), *core_a = exchange(
        place,
        13,
        [swap_plane(part.astype(BF)), swap_plane(full_att.astype(BF))]
        + [swap_core(rows) for rows in grads_a],
    )
    d_normed = settle(part, got, p)
    d_gain["ffa"] = jnp.sum(d_normed * h1 * r1, axis=0)
    g1 = g2 + rms_pull(d_normed, h1, r1, g_ffa)

    sent_a = low([after_core(rows, came[0]) for rows, came in zip(grads_a, core_a)])
    g1_bf = g1.astype(BF)
    (g1_g,), (_, g1_halo), (got_a0,) = exchange(
        place,
        14,
        [
            gather_plane(g1_bf),
            halo_tokens(g1_bf),
            swap_line(sent_a[0]),
        ],
    )
    g1_halo = jnp.where(q < Q - 1, g1_halo, jnp.zeros_like(g1_halo))
    g1_ext = jnp.concatenate([g1_g.reshape(N, D), g1_halo], axis=0)
    d_m = dot_nt(g1_ext, w_mix_s)
    d_mix_s = dot_tn(m_bf, g1_ext[:N])
    d_c = d_m[:N] * conv
    d_conv = lax.optimization_barrier((d_m * c_ext[HALO:]).astype(BF)).astype(F32)
    d_kernel = jnp.stack(
        [jnp.sum(d_conv[:N] * near[k] * same[k], axis=0) for k in range(taps)]
    )
    d_u = jnp.zeros((N, CS), F32)
    for k in range(taps):
        ahead = taps - 1 - k
        match = (seg_ext[HALO + ahead : HALO + ahead + N] == seg_ext[span]).astype(F32)[:, None]
        d_u = d_u + kernel_f[k] * d_conv[ahead : ahead + N] * match
    d_z = jnp.concatenate([d_u * v_ext[span], d_c, d_u * b_ext[span]], axis=1).astype(BF)
    grads_in = dot_tn(n1_ext[span], d_z)
    d_n1 = dot_nt(d_z, w_in_s)
    d_gain["conv"] = jnp.sum(d_n1 * x_ext[span] * r0_ext[span], axis=0)
    part = d_n1.reshape(TP, n, D)
    d_taps = lax.dynamic_update_slice(jnp.zeros((taps, D), F32), d_kernel, (0, p * CS))
    lanes = jnp.concatenate(
        [jnp.stack([d_gain["conv"], d_gain["ffa"], d_gain["att"], d_gain["ffb"]]), d_taps]
    )
    lanes = lanes.reshape(4 + taps, R * S, shard).transpose(1, 0, 2)
    lanes = jnp.pad(lanes, ((0, 0), (0, 0), (0, 128 - shard)))
    heads_row = jnp.broadcast_to(d_heads.reshape(1, 1, 2 * HD), (R * S, 1, 2 * HD))
    tiny = jnp.concatenate([lanes, heads_row], axis=1)
    mix_rows = lax.dynamic_update_slice(jnp.zeros((D, D), BF), d_mix_s.astype(BF), (p * CS, 0))
    mix_rows = lax.psum_scatter(mix_rows, ("rows", "seq"), scatter_dimension=0, tiled=True)
    rows_in = by_row(grads_in)
    tiny_rows = tiny.reshape(R, S, 4 + taps + 1, 128)
    (got,), (core_in,), (core_t,), (got_a1,) = exchange(
        place,
        15,
        [
            swap_plane(part.astype(BF)),
            swap_core(rows_in),
            swap_core(tiny_rows),
            swap_line(sent_a[1]),
        ],
    )
    d_normed = settle(part, got, p)
    g0 = g1 + rms_pull(d_normed, x0, inverse_rms(x0), g_conv)
    d_tokens = g0.astype(BF)[None]

    sent_in = after_core(rows_in, core_in).astype(BF)
    tiny_line = after_core(tiny_rows, core_t)
    (got_a2,), (line_in_got,), (line_t,) = exchange(
        place, 16, [swap_line(sent_a[2]), swap_line(sent_in), swap_line(tiny_line)]
    )
    full_a = [after_line(x, y) for x, y in zip(sent_a, [got_a0, got_a1, got_a2])]
    full_in = after_line(sent_in, line_in_got)
    tiny_full = after_line(tiny_line, line_t)
    (plane_in,), (plane_t,), *plane_a = exchange(
        place,
        17,
        [swap_plane(full_in.astype(BF)), swap_plane(tiny_full)]
        + [swap_plane(full) for full in low(full_a)],
    )
    tiny_sum = jnp.sum(after_plane(tiny_full, plane_t), axis=0)
    d_heads = tiny_sum[4 + taps].reshape(2, HD)

    def back(value):
        return value.transpose(1, 0, 2).reshape(shard, -1)

    out_in = after_plane(full_in, plane_in)
    out_in = out_in.reshape(TP, shard, 3, CS).transpose(1, 2, 0, 3).reshape(shard, 3 * D)
    out_att = after_plane(full_att, plane_att)
    out_a = [back(after_plane(x, y[0])) for x, y in zip(full_a, plane_a)]
    out_b = [back(after_plane(x, y[0])) for x, y in zip(full_b, plane_b)]
    return (
        mixed,
        d_tokens,
        tiny_sum[0, :shard],
        out_in,
        tiny_sum[4 : 4 + taps, :shard],
        mix_rows.astype(F32),
        tiny_sum[1, :shard],
        out_a[0],
        out_a[1],
        out_a[2].T,
        tiny_sum[2, :shard],
        back(out_att[..., :QS]),
        back(out_att[..., QS : QS + KS]),
        back(out_att[..., QS + KS : QS + 2 * KS]),
        d_heads,
        back(out_att[..., QS + 2 * KS :]).T,
        tiny_sum[3, :shard],
        out_b[0],
        out_b[1],
        out_b[2].T,
    )


def solution(mesh):
    place = Place(mesh.shape["rows"], mesh.shape["seq"])
    whole = ("rows", "seq")
    wide, first, second = P("rows", "seq", None), P(whole, None), P(None, whole)
    in_specs = (
        (wide, P("rows", None), wide, P(whole), first, second, first)
        + (P(whole), first, first, second)
        + (P(whole), first, first, first, P(), second)
        + (P(whole), first, first, second)
    )
    out_specs = (
        (wide, wide, P(whole), first, second, first)
        + (P(whole), first, first, second)
        + (P(whole), first, first, first, P(), second)
        + (P(whole), first, first, second)
    )
    return jax.shard_map(
        functools.partial(per_device, place),
        mesh=mesh,
        in_specs=in_specs,
        out_specs=out_specs,
        check_vma=False,
    )
```

```python
import functools
import math

import jax
import jax.numpy as jnp
from jax import lax
from jax.experimental import pallas as pl
from jax.experimental.pallas import tpu as pltpu
from jax.sharding import PartitionSpec as P

H = 16
KVH = 8
HD = 64
TP = 4
HALO = 16

EPSILON = 1e-05
THETA = 1000000.0
MASKED = -1e30
MESH_ID = pl.DeviceIdType.MESH
BF = jnp.bfloat16
F32 = jnp.float32


def dot(left, right):
    return jnp.dot(left, right, preferred_element_type=F32)


def dot_tn(left, right):
    return lax.dot_general(left, right, (((0,), (0,)), ((), ())), preferred_element_type=F32)


def dot_nt(left, right):
    return lax.dot_general(left, right, (((1,), (1,)), ((), ())), preferred_element_type=F32)


class Place:
    def __init__(self, rows, seq):
        self.R, self.S = rows, seq
        self.Q = seq // TP

    def here(self):
        here = Place(self.R, self.S)
        here.r = lax.axis_index("rows")
        here.s = lax.axis_index("seq")
        here.q = here.s // TP
        here.p = lax.rem(here.s, TP)
        return here


class Copies:
    def __init__(self, send, recv):
        self.send, self.recv, self.count, self.sent = send, recv, 0, []

    def slot(self):
        self.count += 1
        return self.count - 1

    def remote(self, src, dst, slot, where, recv_slot=None):
        return pltpu.make_async_remote_copy(
            src_ref=src,
            dst_ref=dst,
            send_sem=self.send.at[slot],
            recv_sem=self.recv.at[slot if recv_slot is None else recv_slot],
            device_id=where,
            device_id_type=MESH_ID,
        )

    def push(self, src, dst, slot, where, cond=None, recv_slot=None):
        copy = self.remote(src, dst, slot, where, recv_slot)
        when(cond, copy.start)
        self.sent.append((copy.wait_send, cond))

    def arrived(self, dst, slot, where, cond=None):
        copy = self.remote(dst, dst, slot, where)
        when(cond, copy.wait_recv)

    def local(self, src, dst):
        slot = self.slot()
        copy = pltpu.make_async_copy(src, dst, self.recv.at[slot])
        copy.start()
        self.sent.append((copy.wait, None))

    def drain(self):
        for wait, cond in self.sent:
            when(cond, wait)


def when(cond, action):
    if cond is None:
        action()
    else:
        pl.when(cond)(lambda: action())


class Job:
    def __init__(self, ins, outs, run, kinds, aliases=(), vmem=(), relay=False, late=False):
        self.ins, self.outs, self.run, self.kinds = ins, outs, run, kinds
        self.aliases, self.vmem, self.relay, self.late = aliases, vmem, relay, late


def together(runs):
    while runs:
        runs = [steps for steps in runs if next(steps, "done") != "done"]
        yield "go"


def partners(at, kinds):
    found = []
    if "plane" in kinds:
        for j in range(1, TP):
            found.append((None, at.r, at.q * TP + lax.rem(at.p + j, TP)))
    if "core" in kinds:
        for j in range(1, at.R):
            found.append((None, lax.rem(at.r + j, at.R), at.s))
    if "zall" in kinds:
        for j in range(1, at.Q):
            found.append((None, at.r, lax.rem(at.q + j, at.Q) * TP + at.p))
    elif "chain" in kinds:
        found.append((at.q > 0, at.r, at.s - TP))
        found.append((at.q < at.Q - 1, at.r, at.s + TP))
    if "halo" in kinds:
        found.append((at.q > 0, at.r, (at.q - 1) * TP + TP - 1))
        found.append((at.q < at.Q - 1, at.r, (at.q + 1) * TP))
        for j in range(TP):
            found.append(((at.p == TP - 1) & (at.q < at.Q - 1), at.r, (at.q + 1) * TP + j))
            found.append(((at.p == 0) & (at.q > 0), at.r, (at.q - 1) * TP + j))
    return found


def meet(at, kinds):
    barrier = pltpu.get_barrier_semaphore()
    peers = partners(at, kinds)
    for cond, r, s in peers:
        when(
            cond,
            functools.partial(
                pl.semaphore_signal, barrier, inc=1, device_id=(r, s), device_id_type=MESH_ID
            ),
        )
    awaited = sum(1 for cond, r, s in peers if cond is None)
    for cond, r, s in peers:
        if cond is not None:
            awaited = awaited + cond.astype(jnp.int32)
    pl.semaphore_wait(barrier, awaited)


def exchange(place, ident, jobs):
    kinds = set().union(*[job.kinds for job in jobs])
    n_in = sum(len(job.ins) for job in jobs)
    n_out = sum(len(job.outs) for job in jobs)
    sems = 24 + sum(12 + 2 * place.Q + place.R * place.Q for job in jobs)
    arrays, in_specs, outs, aliases = [], [], [], {}
    for job in jobs:
        for k, o in job.aliases:
            aliases[len(arrays) + k] = len(outs) + o
        for k, value in enumerate(job.ins):
            arrays.append(value)
            in_specs.append(pl.BlockSpec(memory_space=pltpu.VMEM if k in job.vmem else pl.ANY))
        outs.extend(job.outs)

    def body(*refs):
        at = place.here()
        ins, results = refs[:n_in], refs[n_in : n_in + n_out]
        copies = Copies(refs[n_in + n_out], refs[n_in + n_out + 1])
        meet(at, kinds)
        runs, i, o = [], 0, 0
        for job in jobs:
            runs.append(
                job.run(at, copies, ins[i : i + len(job.ins)], results[o : o + len(job.outs)])
            )
            i, o = i + len(job.ins), o + len(job.outs)
        pairs = list(zip(jobs, runs))
        relays = together([steps for job, steps in pairs if job.relay])
        for steps in [steps for job, steps in pairs if not job.relay and not job.late]:
            next(steps)
        next(relays, "done")
        next(relays, "done")
        for steps in [steps for job, steps in pairs if job.late]:
            next(steps)
        for _ in relays:
            pass
        for steps in [steps for job, steps in pairs if not job.relay]:
            for _ in steps:
                pass
        copies.drain()

    results = pl.pallas_call(
        body,
        out_shape=tuple(outs),
        in_specs=in_specs,
        out_specs=tuple(pl.BlockSpec(memory_space=pl.ANY) for _ in outs),
        scratch_shapes=[pltpu.SemaphoreType.DMA((sems,)), pltpu.SemaphoreType.DMA((sems,))],
        input_output_aliases=aliases,
        compiler_params=pltpu.CompilerParams(collective_id=ident, has_side_effects=True),
        name="exchange_%d" % ident,
    )(*arrays)
    given, o = [], 0
    for job in jobs:
        given.append(results[o : o + len(job.outs)])
        o += len(job.outs)
    return given


def like(shape, dtype=BF):
    return jax.ShapeDtypeStruct(shape, dtype)


def gather_plane(value):
    def run(at, copies, ins, outs):
        slots = [copies.slot() for _ in range(TP - 1)]
        for j in range(1, TP):
            peer = at.q * TP + lax.rem(at.p + j, TP)
            copies.push(ins[0], outs[0].at[at.p], slots[j - 1], (at.r, peer))
        copies.local(ins[0], outs[0].at[at.p])
        yield "go"
        for j in range(1, TP):
            origin = lax.rem(at.p + TP - j, TP)
            copies.arrived(outs[0].at[origin], slots[j - 1], (at.r, at.s))

    return Job([value], [like((TP,) + value.shape, value.dtype)], run, {"plane"}, vmem=(0,))


def swap_plane(value):
    def run(at, copies, ins, outs):
        slots = [copies.slot() for _ in range(TP - 1)]
        for j in range(1, TP):
            other = lax.rem(at.p + j, TP)
            copies.push(
                ins[0].at[other], outs[0].at[at.p], slots[j - 1], (at.r, at.q * TP + other)
            )
        yield "go"
        for j in range(1, TP):
            origin = lax.rem(at.p + TP - j, TP)
            copies.arrived(outs[0].at[origin], slots[j - 1], (at.r, at.s))

    return Job([value], [like(value.shape, value.dtype)], run, {"plane"})


def swap_core(value):
    def run(at, copies, ins, outs):
        slots = [copies.slot() for _ in range(at.R - 1)]
        for j in range(1, at.R):
            other = lax.rem(at.r + j, at.R)
            copies.push(ins[0].at[other], outs[0].at[at.r], slots[j - 1], (other, at.s))
        yield "go"
        for j in range(1, at.R):
            origin = lax.rem(at.r + at.R - j, at.R)
            copies.arrived(outs[0].at[origin], slots[j - 1], (at.r, at.s))

    return Job([value], [like(value.shape, value.dtype)], run, {"core"})


def swap_line(value):
    def run(at, copies, ins, outs):
        slots = [copies.slot() for _ in range(at.Q - 1)]
        for j in range(1, at.Q):
            other = lax.rem(at.q + j, at.Q)
            copies.push(
                ins[0].at[other], outs[0].at[at.q], slots[j - 1], (at.r, other * TP + at.p)
            )
        yield "go"
        for j in range(1, at.Q):
            origin = lax.rem(at.q + at.Q - j, at.Q)
            copies.arrived(outs[0].at[origin], slots[j - 1], (at.r, at.s))

    return Job([value], [like(value.shape, value.dtype)], run, {"zall"})


def window_forward(place, value):
    reach = place.Q // 2

    def run(at, copies, ins, outs):
        slots = [copies.slot() for _ in range(reach)]
        for j in range(1, reach + 1):
            target = (at.q + j) * TP + at.p
            copies.push(ins[0], outs[0].at[j], slots[j - 1], (at.r, target), at.q + j < at.Q)
        copies.local(ins[0], outs[0].at[0])
        yield "go"
        for j in range(1, reach + 1):
            copies.arrived(outs[0].at[j], slots[j - 1], (at.r, at.s), at.q >= j)

    shape = (reach + 1,) + value.shape
    return Job([value], [like(shape, value.dtype)], run, {"zall"}, vmem=(0,))


def window_backward(place, value):
    reach = place.Q // 2

    def run(at, copies, ins, outs):
        slots = [copies.slot() for _ in range(reach)]
        for j in range(1, reach + 1):
            target = (at.q - j) * TP + at.p
            copies.push(
                ins[0].at[j], outs[0].at[j - 1], slots[j - 1], (at.r, target), at.q >= j
            )
        yield "go"
        for j in range(1, reach + 1):
            copies.arrived(outs[0].at[j - 1], slots[j - 1], (at.r, at.s), at.q + j < at.Q)

    shape = (reach,) + value.shape[1:]
    return Job([value], [like(shape, value.dtype)], run, {"zall"})


def halo_tokens(value):
    rows = value.shape[0]

    def run(at, copies, ins, outs):
        ahead = [copies.slot() for _ in range(TP)]
        back = [copies.slot() for _ in range(TP)]
        first = (at.p == 0) & (at.q > 0)
        last = (at.p == TP - 1) & (at.q < at.Q - 1)
        for j in range(TP):
            tail = ins[0].at[pl.ds(rows - HALO, HALO)]
            there = (at.r, (at.q + 1) * TP + j)
            copies.push(tail, outs[0], ahead[j], there, last, ahead[0])
            head = ins[0].at[pl.ds(0, HALO)]
            there = (at.r, (at.q - 1) * TP + j)
            copies.push(head, outs[1], back[j], there, first, back[0])
        yield "go"
        copies.arrived(outs[0], ahead[0], (at.r, at.s), at.q > 0)
        copies.arrived(outs[1], back[0], (at.r, at.s), at.q < at.Q - 1)

    shape = (HALO,) + value.shape[1:]
    outs = [like(shape, value.dtype), like(shape, value.dtype)]
    return Job([value], outs, run, {"halo"}, vmem=(0,))


def spread_run(at, copies, source, held, first):
    slots = [copies.slot() for _ in range(TP - 1)]
    for j in range(1, TP):
        other = lax.rem(at.p + j, TP)
        copies.push(
            source.at[other], held.at[first + at.p], slots[j - 1], (at.r, at.q * TP + other)
        )
    copy = pltpu.make_async_copy(
        source.at[at.p], held.at[first + at.p], copies.recv.at[copies.slot()]
    )
    copy.start()
    yield "go"
    copy.wait()
    for j in range(1, TP):
        origin = lax.rem(at.p + TP - j, TP)
        copies.arrived(held.at[first + origin], slots[j - 1], (at.r, at.s))


def chain_run(at, copies, held):
    def block(r, q):
        return held.at[pl.ds((r * at.Q + q) * TP, TP)]

    right = [copies.slot() for _ in range(at.Q - 1)]
    left = [copies.slot() for _ in range(at.Q - 1)]
    across = [[copies.slot() for _ in range(at.Q)] for _ in range(at.R - 1)]

    def cross(q, index, cond):
        for j in range(1, at.R):
            other = lax.rem(at.r + j, at.R)
            copies.push(block(at.r, q), block(at.r, q), across[j - 1][index], (other, at.s), cond)

    copies.push(
        block(at.r, at.q), block(at.r, at.q), right[0], (at.r, at.s + TP), at.q < at.Q - 1
    )
    copies.push(block(at.r, at.q), block(at.r, at.q), left[0], (at.r, at.s - TP), at.q > 0)
    cross(at.q, 0, None)
    index = 0
    spots = {}
    for hop in range(1, at.Q):
        yield "go"
        from_left, from_right = at.q >= hop, at.q + hop < at.Q
        copies.arrived(block(at.r, at.q - hop), right[hop - 1], (at.r, at.s), from_left)
        if hop < at.Q - 1:
            copies.push(
                block(at.r, at.q - hop),
                block(at.r, at.q - hop),
                right[hop],
                (at.r, at.s + TP),
                from_left & (at.q < at.Q - 1),
            )
        copies.arrived(block(at.r, at.q + hop), left[hop - 1], (at.r, at.s), from_right)
        if hop < at.Q - 1:
            copies.push(
                block(at.r, at.q + hop),
                block(at.r, at.q + hop),
                left[hop],
                (at.r, at.s - TP),
                from_right & (at.q > 0),
            )
        for side, sign in ((from_left, -1), (from_right, 1)):
            spots[(hop, sign)] = [copies.slot() for _ in range(at.R - 1)]
            for j in range(1, at.R):
                other = lax.rem(at.r + j, at.R)
                piece = block(at.r, at.q + sign * hop)
                copies.push(piece, piece, spots[(hop, sign)][j - 1], (other, at.s), side)
    yield "go"
    for j in range(1, at.R):
        source = lax.rem(at.r + at.R - j, at.R)
        copies.arrived(block(source, at.q), across[j - 1][0], (at.r, at.s))
        for hop in range(1, at.Q):
            for sign in (-1, 1):
                there = at.q + sign * hop
                copies.arrived(
                    block(source, there),
                    spots[(hop, sign)][j - 1],
                    (at.r, at.s),
                    at.q >= hop if sign < 0 else there < at.Q,
                )


def spread(source):
    def run(at, copies, ins, outs):
        yield from spread_run(at, copies, ins[0], outs[0], 0)

    outs = [like(source.shape, source.dtype)]
    return Job([source], outs, run, {"plane"}, vmem=(0,), late=True)


def spread_all(place, source):
    def run(at, copies, ins, outs):
        yield from spread_run(at, copies, ins[0], outs[0], (at.r * at.Q + at.q) * TP)
        yield from chain_run(at, copies, outs[0])

    outs = [like((place.R * place.S,) + source.shape[1:], source.dtype)]
    return Job([source], outs, run, {"plane", "chain", "core"}, vmem=(0,), relay=True)


def doc_info(positions, lengths):
    doc_ends = jnp.cumsum(lengths, dtype=jnp.int32)
    passed = positions[:, None] >= doc_ends[None, :]
    segment = jnp.sum(passed.astype(jnp.int32), axis=1, dtype=jnp.int32)
    opening = jnp.sum(jnp.where(passed, lengths[None, :], 0), axis=1, dtype=jnp.int32)
    return (segment, positions - opening)


def inverse_rms(values):
    return lax.rsqrt(jnp.mean(values * values, axis=-1, keepdims=True) + EPSILON)


def rms_pull(upstream, values, inverse, norm_gain):
    scaled = upstream * norm_gain
    product_mean = jnp.mean(scaled * values, axis=-1, keepdims=True)
    return inverse * scaled - values * (inverse * inverse * inverse) * product_mean


def rope_tables(relative):
    half_size = HD // 2
    frequency = jnp.exp(
        jnp.arange(half_size, dtype=F32) * (-2.0 * math.log(THETA) / HD)
    )
    angles = relative.astype(F32)[:, None] * frequency[None, :]
    return (jnp.cos(angles)[:, None, :], jnp.sin(angles)[:, None, :])


def rope_apply(values, cosine, sine):
    front, back = values[..., : HD // 2], values[..., HD // 2 :]
    return jnp.concatenate([front * cosine - back * sine, back * cosine + front * sine], axis=-1)


def rope_revert(values, cosine, sine):
    front, back = values[..., : HD // 2], values[..., HD // 2 :]
    return jnp.concatenate([front * cosine + back * sine, back * cosine - front * sine], axis=-1)


def settle(own, arrived, p):
    index = jnp.arange(TP, dtype=jnp.int32)[:, None, None]
    others = jnp.where(index == p, 0.0, arrived.astype(F32))
    mine = lax.dynamic_index_in_dim(own, p, 0, keepdims=False)
    return mine + jnp.sum(others, axis=0)


def per_device(
    place,
    tokens,
    doc_lengths,
    cotangent,
    gain_conv,
    w_in,
    kernel,
    w_mix,
    gain_ffa,
    gate_a,
    up_a,
    down_a,
    gain_att,
    w_query,
    w_key,
    w_value,
    head_gains,
    w_attout,
    gain_ffb,
    gate_b,
    up_b,
    down_b,
):
    R, S, Q = place.R, place.S, place.Q
    n, D = tokens.shape[1], tokens.shape[2]
    shard = w_in.shape[0]
    FS = gate_a.shape[1] // TP
    CS = D // TP
    QS, KS = H * HD // TP, KVH * HD // TP
    taps = kernel.shape[0]
    N = n * TP
    r, s = lax.axis_index("rows"), lax.axis_index("seq")
    q, p = s // TP, lax.rem(s, TP)
    lengths = doc_lengths[0]

    def slices(weight):
        return weight.reshape(shard, TP, -1).transpose(1, 0, 2)

    def joined(*weights):
        return jnp.concatenate([slices(weight) for weight in weights], axis=2)

    columns = [[a * S + b * TP + c for a in range(R) for b in range(Q)] for c in range(TP)]
    lines = [[b * TP + c for b in range(Q)] for c in range(TP)]

    def gather_rest(plane):
        flat = plane.reshape(TP * shard, -1)
        return lax.all_gather(
            flat, ("rows", "seq"), axis=0, tiled=True, axis_index_groups=columns
        )

    def reduce_rest(grads):
        grads = grads.astype(BF)
        half = lax.psum_scatter(grads, "rows", scatter_dimension=0, tiled=True)
        part = lax.psum_scatter(
            half, "seq", scatter_dimension=0, tiled=True, axis_index_groups=lines
        )
        return part.reshape(-1, shard, part.shape[1])

    in_cut = w_in.reshape(shard, 3, TP, CS).transpose(2, 0, 1, 3).reshape(TP, shard, 3 * CS)
    small = jnp.stack([gain_conv, gain_ffa, gain_att, gain_ffb] + [kernel[i] for i in range(taps)])
    small = jnp.pad(small, ((0, 16 - 4 - taps), (0, 128 - shard)))
    small = jnp.broadcast_to(small[None], (TP, 16, 128))

    per_slice = R * Q
    homes = []
    for d in range(R * S):
        k = d % per_slice
        homes.append((d, (k // Q) * S + (k % Q) * TP + d // per_slice))
    w_mix_s = lax.all_gather(
        lax.ppermute(w_mix, ("rows", "seq"), homes),
        ("rows", "seq"),
        axis=0,
        tiled=True,
        axis_index_groups=columns,
    )

    mine = tokens[0]
    (tok_g,), (halo_a, halo_b), (in_g,), (small_g,), (ffa_p,) = exchange(
        place,
        0,
        [
            gather_plane(mine),
            halo_tokens(mine),
            spread_all(place, in_cut),
            spread_all(place, small),
            spread(joined(gate_a, up_a, down_a.T)),
        ],
    )
    wa = gather_rest(ffa_p)
    vectors = small_g[:, : 4 + taps, :shard].transpose(1, 0, 2).reshape(4 + taps, D).astype(F32)
    g_conv, g_ffa, g_att, g_ffb = (vectors[i] for i in range(4))
    kernel_f = lax.dynamic_slice_in_dim(vectors[4:], p * CS, CS, 1)
    w_in_s = in_g.reshape(D, 3 * CS)

    def own(parts, index):
        return lax.dynamic_index_in_dim(parts, index, 0, keepdims=False).astype(F32)

    def collect(parts, came, index):
        slot = jnp.arange(came.shape[0], dtype=jnp.int32).reshape((-1,) + (1,) * (came.ndim - 1))
        mine_part = lax.dynamic_index_in_dim(parts, index, 0, keepdims=True).astype(F32)
        return jnp.sum(jnp.where(slot == index, mine_part, came.astype(F32)), axis=0)

    def after_core(parts, came):
        summed = collect(parts, came, r)
        return summed.reshape((Q, TP) + summed.shape[1:])

    def after_line(parts, came):
        return collect(parts, came, q)

    def after_plane(full, came):
        slot = jnp.arange(TP, dtype=jnp.int32).reshape((TP,) + (1,) * (full.ndim - 1))
        mine_part = lax.dynamic_index_in_dim(full, p, 0, keepdims=True)
        return jnp.where(slot == p, mine_part, came.astype(F32))

    total = S * n
    pos_ext = q * N - HALO + jnp.arange(N + 2 * HALO, dtype=jnp.int32)
    seg_ext, rel_ext = doc_info(pos_ext, lengths)
    valid = ((pos_ext >= 0) & (pos_ext < total))[:, None]
    x_ext = jnp.concatenate([halo_a, tok_g.reshape(N, D), halo_b], axis=0)
    x_ext = jnp.where(valid, x_ext, jnp.zeros_like(x_ext)).astype(F32)
    r0_ext = inverse_rms(x_ext)
    n1_ext = (x_ext * r0_ext * g_conv).astype(BF)
    z_ext = dot(n1_ext, w_in_s)
    b_ext, c_ext, v_ext = z_ext[:, :CS], z_ext[:, CS : 2 * CS], z_ext[:, 2 * CS :]
    u_ext = lax.optimization_barrier((b_ext * v_ext).astype(BF)).astype(F32)
    span = slice(HALO, HALO + N)
    same = [
        (seg_ext[HALO - 2 + k : HALO - 2 + k + N] == seg_ext[span]).astype(F32)[:, None]
        for k in range(taps)
    ]
    near = [u_ext[HALO - 2 + k : HALO - 2 + k + N] for k in range(taps)]
    conv = kernel_f[0] * near[0] * same[0]
    for k in range(1, taps):
        conv = conv + kernel_f[k] * near[k] * same[k]
    m_bf = (c_ext[span] * conv).astype(BF)
    part = dot(m_bf, w_mix_s).reshape(TP, n, D)
    (got,), (att_p,), (ffb_p,) = exchange(
        place,
        1,
        [
            swap_plane(part.astype(BF)),
            spread(joined(w_query, w_key, w_value, w_attout.T)),
            spread(joined(gate_b, up_b, down_b.T)),
        ],
    )
    w_att = gather_rest(att_p)
    wb = gather_rest(ffb_p)
    x0 = mine.astype(F32)
    h1 = x0 + settle(part, got, p)

    r1 = inverse_rms(h1)
    a1 = (h1 * r1 * g_ffa).astype(BF)
    ((a1_g,),) = exchange(place, 2, [gather_plane(a1)])
    a1_g = a1_g.reshape(N, D)

    def ffn(a, w):
        both = dot(a, w[:, : 2 * FS])
        gate, up = both[:, :FS], both[:, FS:]
        act = (jax.nn.silu(gate) * up).astype(BF)
        return gate, up, act, dot_nt(act, w[:, 2 * FS :]).reshape(TP, n, D)

    gate1, up1, act1, part = ffn(a1_g, wa)
    ((got,),) = exchange(place, 3, [swap_plane(part.astype(BF))])
    h2 = h1 + settle(part, got, p)

    r2 = inverse_rms(h2)
    n3 = (h2 * r2 * g_att).astype(BF)
    ((n3_g,),) = exchange(place, 4, [gather_plane(n3)])
    n3_g = n3_g.reshape(N, D)
    w_qkv, w_out = w_att[:, : QS + 2 * KS], w_att[:, QS + 2 * KS :]
    qkv = dot(n3_g, w_qkv)
    heads, kv_heads = QS // HD, KS // HD
    groups = heads // kv_heads
    q_pre = qkv[:, :QS].reshape(N, heads, HD)
    k_pre = qkv[:, QS : QS + KS].reshape(N, kv_heads, HD)
    head_f = head_gains.astype(F32)
    cosine, sine = rope_tables(rel_ext[span])
    q_inv, k_inv = inverse_rms(q_pre), inverse_rms(k_pre)
    q_bf = rope_apply(q_pre * q_inv * head_f[0], cosine, sine).astype(BF)
    k_bf = rope_apply(k_pre * k_inv * head_f[1], cosine, sine).astype(BF).reshape(N, KS)
    v_bf = qkv[:, QS + KS :].astype(BF)
    ((kv_w,),) = exchange(
        place, 5, [window_forward(place, jnp.concatenate([k_bf, v_bf], axis=1))]
    )
    reach = Q // 2 + 1
    q_pos = pos_ext[span]
    key_pos = (q_pos[None, :] - N * jnp.arange(reach, dtype=jnp.int32)[:, None]).reshape(-1)
    key_seg, _ = doc_info(key_pos, lengths)
    kv_all = kv_w.reshape(reach * N, 2 * KS)
    kv_all = jnp.where((key_pos >= 0)[:, None], kv_all, jnp.zeros_like(kv_all))
    allowed = (
        (seg_ext[span][:, None] == key_seg[None, :])
        & (key_pos[None, :] <= q_pos[:, None])
        & (key_pos[None, :] >= 0)
    )
    k_all = kv_all[:, :KS].reshape(reach * N, kv_heads, HD)
    v_all = kv_all[:, KS:].reshape(reach * N, kv_heads, HD)
    q_grp = q_bf.reshape(N, kv_heads, groups, HD)
    factor = 1.0 / math.sqrt(HD)
    raw = jnp.einsum("qkgd,tkd->kgqt", q_grp, k_all, preferred_element_type=F32)
    scores = jnp.where(allowed[None, None], raw * factor, MASKED)
    shares = jax.nn.softmax(scores, axis=-1)
    shares_bf = shares.astype(BF)
    o_bf = (
        jnp.einsum("kgqt,tkd->qkgd", shares_bf, v_all, preferred_element_type=F32)
        .reshape(N, QS)
        .astype(BF)
    )
    part = dot_nt(o_bf, w_out).reshape(TP, n, D)
    ((got,),) = exchange(place, 6, [swap_plane(part.astype(BF))])
    h3 = h2 + settle(part, got, p)

    r3 = inverse_rms(h3)
    a2 = (h3 * r3 * g_ffb).astype(BF)
    e_bf = cotangent[0]
    (a2_g,), (e_g,) = exchange(place, 7, [gather_plane(a2), gather_plane(e_bf)])
    a2_g, e_g = a2_g.reshape(N, D), e_g.reshape(N, D)
    gate2, up2, act2, part = ffn(a2_g, wb)

    def ffn_back(e, a, gate, up, act, w):
        d_down = dot_tn(e, act)
        d_act = dot(e, w[:, 2 * FS :])
        sigma = jax.nn.sigmoid(gate)
        d_gate = (d_act * up * sigma * (1.0 + gate * (1.0 - sigma))).astype(BF)
        d_up = (d_act * (gate * sigma)).astype(BF)
        d_both = jnp.concatenate([d_gate, d_up], axis=1)
        grads = jnp.concatenate([dot_tn(a, d_both).astype(BF), d_down.astype(BF)], axis=1)
        d_normed = dot_nt(d_both, w[:, : 2 * FS])
        return grads, d_normed.reshape(TP, n, D)

    grads_b, part_b = ffn_back(e_g, a2_g, gate2, up2, act2, wb)

    full_b = reduce_rest(grads_b)
    (got,), (got_b,) = exchange(
        place, 8, [swap_plane(part.astype(BF)), swap_plane(part_b.astype(BF))]
    )
    h4 = h3 + settle(part, got, p)
    mixed = h4.astype(BF)[None]
    d_gain = {}
    d_normed = settle(part_b, got_b, p)
    d_gain["ffb"] = jnp.sum(d_normed * h3 * r3, axis=0)
    g4 = e_bf.astype(F32)
    g3 = g4 + rms_pull(d_normed, h3, r3, g_ffb)

    ((g3_g,),) = exchange(place, 9, [gather_plane(g3.astype(BF))])
    g3_g = g3_g.reshape(N, D)
    d_out = dot_tn(g3_g, o_bf)
    d_o = dot(g3_g, w_out).astype(BF).reshape(N, kv_heads, groups, HD)
    d_shares = jnp.einsum("qkgd,tkd->kgqt", d_o, v_all, preferred_element_type=F32)
    delta = jnp.sum(shares * d_shares, axis=-1, keepdims=True)
    d_scores = (shares * (d_shares - delta)).astype(BF)
    d_q = factor * jnp.einsum("kgqt,tkd->qkgd", d_scores, k_all, preferred_element_type=F32)
    d_k = factor * jnp.einsum("kgqt,qkgd->tkd", d_scores, q_grp, preferred_element_type=F32)
    d_v = jnp.einsum("kgqt,qkgd->tkd", shares_bf, d_o, preferred_element_type=F32)
    d_kv = jnp.concatenate(
        [d_k.reshape(reach, N, KS), d_v.reshape(reach, N, KS)], axis=-1
    )
    ((got_kv,),) = exchange(place, 10, [window_backward(place, d_kv.astype(BF))])
    there = (q + 1 + jnp.arange(reach - 1, dtype=jnp.int32) < Q)[:, None, None]
    d_kv = d_kv[0] + jnp.sum(jnp.where(there, got_kv.astype(F32), 0.0), axis=0)
    dv_bf = d_kv[:, KS:].astype(BF)
    dk_norm = rope_revert(d_kv[:, :KS].reshape(N, kv_heads, HD), cosine, sine)
    dq_norm = rope_revert(d_q.reshape(N, heads, HD), cosine, sine)
    dk_pre = rms_pull(dk_norm, k_pre, k_inv, head_f[1]).reshape(N, KS)
    dq_pre = rms_pull(dq_norm, q_pre, q_inv, head_f[0]).reshape(N, QS)
    d_heads = jnp.stack(
        [
            jnp.sum(dq_norm * q_pre * q_inv, axis=(0, 1)),
            jnp.sum(dk_norm * k_pre * k_inv, axis=(0, 1)),
        ]
    )
    d_qkv = jnp.concatenate([dq_pre.astype(BF), dk_pre.astype(BF), dv_bf], axis=1)
    part = dot_nt(d_qkv, w_qkv).reshape(TP, n, D)
    full_att = reduce_rest(
        jnp.concatenate([dot_tn(n3_g, d_qkv).astype(BF), d_out.astype(BF)], axis=1)
    )
    ((got,),) = exchange(place, 11, [swap_plane(part.astype(BF))])
    d_normed = settle(part, got, p)
    d_gain["att"] = jnp.sum(d_normed * h2 * r2, axis=0)
    g2 = g3 + rms_pull(d_normed, h2, r2, g_att)

    ((g2_g,),) = exchange(place, 12, [gather_plane(g2.astype(BF))])
    g2_g = g2_g.reshape(N, D)
    grads_a, part = ffn_back(g2_g, a1_g, gate1, up1, act1, wa)
    full_a = reduce_rest(grads_a)
    (got,), (plane_b,) = exchange(
        place, 13, [swap_plane(part.astype(BF)), swap_plane(full_b)]
    )
    d_normed = settle(part, got, p)
    d_gain["ffa"] = jnp.sum(d_normed * h1 * r1, axis=0)
    g1 = g2 + rms_pull(d_normed, h1, r1, g_ffa)

    g1_bf = g1.astype(BF)
    (g1_g,), (_, g1_halo), (plane_att,) = exchange(
        place, 14, [gather_plane(g1_bf), halo_tokens(g1_bf), swap_plane(full_att)]
    )
    g1_halo = jnp.where(q < Q - 1, g1_halo, jnp.zeros_like(g1_halo))
    g1_ext = jnp.concatenate([g1_g.reshape(N, D), g1_halo], axis=0)
    d_m = dot_nt(g1_ext, w_mix_s)
    d_mix_s = dot_tn(m_bf, g1_ext[:N])
    d_c = d_m[:N] * conv
    d_conv = lax.optimization_barrier((d_m * c_ext[HALO:]).astype(BF)).astype(F32)
    d_kernel = jnp.stack(
        [jnp.sum(d_conv[:N] * near[k] * same[k], axis=0) for k in range(taps)]
    )
    d_u = jnp.zeros((N, CS), F32)
    for k in range(taps):
        ahead = taps - 1 - k
        match = (seg_ext[HALO + ahead : HALO + ahead + N] == seg_ext[span]).astype(F32)[:, None]
        d_u = d_u + kernel_f[k] * d_conv[ahead : ahead + N] * match
    d_z = jnp.concatenate([d_u * v_ext[span], d_c, d_u * b_ext[span]], axis=1).astype(BF)
    full_in = reduce_rest(dot_tn(n1_ext[span], d_z))
    full_mix = reduce_rest(d_mix_s).reshape(shard, D)
    out_mix = lax.ppermute(full_mix, ("rows", "seq"), [(b, a) for a, b in homes])
    d_n1 = dot_nt(d_z, w_in_s)
    d_gain["conv"] = jnp.sum(d_n1 * x_ext[span] * r0_ext[span], axis=0)
    part = d_n1.reshape(TP, n, D)
    d_taps = lax.dynamic_update_slice(jnp.zeros((taps, D), F32), d_kernel, (0, p * CS))
    lanes = jnp.concatenate(
        [jnp.stack([d_gain["conv"], d_gain["ffa"], d_gain["att"], d_gain["ffb"]]), d_taps]
    )
    lanes = lanes.reshape(4 + taps, R * S, shard).transpose(1, 0, 2)
    lanes = jnp.pad(lanes, ((0, 0), (0, 0), (0, 128 - shard)))
    heads_row = jnp.broadcast_to(d_heads.reshape(1, 1, 2 * HD), (R * S, 1, 2 * HD))
    tiny = jnp.concatenate([lanes, heads_row], axis=1)
    tiny_rows = tiny.reshape(R, S, 4 + taps + 1, 128)
    (got,), (core_t,) = exchange(
        place, 15, [swap_plane(part.astype(BF)), swap_core(tiny_rows)]
    )
    d_normed = settle(part, got, p)
    g0 = g1 + rms_pull(d_normed, x0, inverse_rms(x0), g_conv)
    d_tokens = g0.astype(BF)[None]

    tiny_line = after_core(tiny_rows, core_t)
    ((line_t,),) = exchange(place, 16, [swap_line(tiny_line)])
    tiny_full = after_line(tiny_line, line_t)
    (plane_in,), (plane_t,), (plane_a,) = exchange(
        place, 17, [swap_plane(full_in), swap_plane(tiny_full), swap_plane(full_a)]
    )
    tiny_sum = jnp.sum(after_plane(tiny_full, plane_t), axis=0)
    d_heads = tiny_sum[4 + taps].reshape(2, HD)

    def back(value):
        return value.transpose(1, 0, 2).reshape(shard, -1)

    out_in = after_plane(full_in, plane_in)
    out_in = out_in.reshape(TP, shard, 3, CS).transpose(1, 2, 0, 3).reshape(shard, 3 * D)
    out_att = after_plane(full_att, plane_att)
    out_a = after_plane(full_a, plane_a)
    out_b = after_plane(full_b, plane_b)
    return (
        mixed,
        d_tokens,
        tiny_sum[0, :shard],
        out_in,
        tiny_sum[4 : 4 + taps, :shard],
        out_mix.astype(F32),
        tiny_sum[1, :shard],
        back(out_a[..., 0 * FS : 1 * FS]),
        back(out_a[..., 1 * FS : 2 * FS]),
        back(out_a[..., 2 * FS : 3 * FS]).T,
        tiny_sum[2, :shard],
        back(out_att[..., :QS]),
        back(out_att[..., QS : QS + KS]),
        back(out_att[..., QS + KS : QS + 2 * KS]),
        d_heads,
        back(out_att[..., QS + 2 * KS :]).T,
        tiny_sum[3, :shard],
        back(out_b[..., 0 * FS : 1 * FS]),
        back(out_b[..., 1 * FS : 2 * FS]),
        back(out_b[..., 2 * FS : 3 * FS]).T,
    )


def solution(mesh):
    place = Place(mesh.shape["rows"], mesh.shape["seq"])
    whole = ("rows", "seq")
    wide, first, second = P("rows", "seq", None), P(whole, None), P(None, whole)
    in_specs = (
        (wide, P("rows", None), wide, P(whole), first, second, first)
        + (P(whole), first, first, second)
        + (P(whole), first, first, first, P(), second)
        + (P(whole), first, first, second)
    )
    out_specs = (
        (wide, wide, P(whole), first, second, first)
        + (P(whole), first, first, second)
        + (P(whole), first, first, first, P(), second)
        + (P(whole), first, first, second)
    )
    return jax.shard_map(
        functools.partial(per_device, place),
        mesh=mesh,
        in_specs=in_specs,
        out_specs=out_specs,
        check_vma=False,
    )
```

```python
import functools
import math

import jax
import jax.numpy as jnp
from jax import lax
from jax.experimental import pallas as pl
from jax.experimental.pallas import tpu as pltpu
from jax.sharding import PartitionSpec as P

H = 16
KVH = 8
HD = 64
TP = 4
HALO = 16
COST = 1_000_000

EPSILON = 1e-05
THETA = 1000000.0
MASKED = -1e30
MESH_ID = pl.DeviceIdType.MESH
BF = jnp.bfloat16
F32 = jnp.float32


def dot(left, right):
    return jnp.dot(left, right, preferred_element_type=F32)


def dot_tn(left, right):
    return lax.dot_general(left, right, (((0,), (0,)), ((), ())), preferred_element_type=F32)


def dot_nt(left, right):
    return lax.dot_general(left, right, (((1,), (1,)), ((), ())), preferred_element_type=F32)


class Place:
    def __init__(self, rows, seq):
        self.R, self.S = rows, seq
        self.Q = seq // TP

    def here(self):
        here = Place(self.R, self.S)
        here.r = lax.axis_index("rows")
        here.s = lax.axis_index("seq")
        here.q = here.s // TP
        here.p = lax.rem(here.s, TP)
        return here


class Copies:
    def __init__(self, send, recv):
        self.send, self.recv, self.count, self.sent = send, recv, 0, []

    def slot(self):
        self.count += 1
        return self.count - 1

    def remote(self, src, dst, slot, where, recv_slot=None):
        return pltpu.make_async_remote_copy(
            src_ref=src,
            dst_ref=dst,
            send_sem=self.send.at[slot],
            recv_sem=self.recv.at[slot if recv_slot is None else recv_slot],
            device_id=where,
            device_id_type=MESH_ID,
        )

    def push(self, src, dst, slot, where, cond=None, recv_slot=None):
        copy = self.remote(src, dst, slot, where, recv_slot)
        when(cond, copy.start)
        self.sent.append((copy.wait_send, cond))

    def arrived(self, dst, slot, where, cond=None):
        copy = self.remote(dst, dst, slot, where)
        when(cond, copy.wait_recv)

    def local(self, src, dst):
        slot = self.slot()
        copy = pltpu.make_async_copy(src, dst, self.recv.at[slot])
        copy.start()
        self.sent.append((copy.wait, None))

    def drain(self):
        for wait, cond in self.sent:
            when(cond, wait)


def when(cond, action):
    if cond is None:
        action()
    else:
        pl.when(cond)(lambda: action())


class Job:
    def __init__(self, ins, outs, run, kinds, aliases=(), vmem=(), relay=False, late=False):
        self.ins, self.outs, self.run, self.kinds = ins, outs, run, kinds
        self.aliases, self.vmem, self.relay, self.late = aliases, vmem, relay, late


def together(runs):
    while runs:
        runs = [steps for steps in runs if next(steps, "done") != "done"]
        yield "go"


def partners(at, kinds):
    found = []
    if "plane" in kinds:
        for j in range(1, TP):
            found.append((None, at.r, at.q * TP + lax.rem(at.p + j, TP)))
    if "core" in kinds:
        for j in range(1, at.R):
            found.append((None, lax.rem(at.r + j, at.R), at.s))
    if "zall" in kinds:
        for j in range(1, at.Q):
            found.append((None, at.r, lax.rem(at.q + j, at.Q) * TP + at.p))
    elif "chain" in kinds:
        found.append((at.q > 0, at.r, at.s - TP))
        found.append((at.q < at.Q - 1, at.r, at.s + TP))
    if "home" in kinds:
        r, s, _, same = home_of(at)
        found.append((same == 0, r, s))
        r, s, same = visitor_of(at)
        found.append((same == 0, r, s))
    if "halo" in kinds:
        found.append((at.q > 0, at.r, (at.q - 1) * TP + TP - 1))
        found.append((at.q < at.Q - 1, at.r, (at.q + 1) * TP))
        for j in range(TP):
            found.append(((at.p == TP - 1) & (at.q < at.Q - 1), at.r, (at.q + 1) * TP + j))
            found.append(((at.p == 0) & (at.q > 0), at.r, (at.q - 1) * TP + j))
    return found


def home_of(at):
    k = lax.rem(at.r * at.S + at.s, at.R * at.Q)
    r, s = k // at.Q, lax.rem(k, at.Q) * TP + (at.r * at.S + at.s) // (at.R * at.Q)
    return r, s, k, ((r == at.r) & (s == at.s)).astype(jnp.int32)


def visitor_of(at):
    d = at.p * (at.R * at.Q) + at.r * at.Q + at.q
    r, s = d // at.S, lax.rem(d, at.S)
    return r, s, ((r == at.r) & (s == at.s)).astype(jnp.int32)


def meet(at, kinds):
    barrier = pltpu.get_barrier_semaphore()
    peers = partners(at, kinds)
    for cond, r, s in peers:
        when(
            cond,
            functools.partial(
                pl.semaphore_signal, barrier, inc=1, device_id=(r, s), device_id_type=MESH_ID
            ),
        )
    awaited = sum(1 for cond, r, s in peers if cond is None)
    for cond, r, s in peers:
        if cond is not None:
            awaited = awaited + cond.astype(jnp.int32)
    pl.semaphore_wait(barrier, awaited)


def exchange(place, ident, jobs):
    kinds = set().union(*[job.kinds for job in jobs])
    n_in = sum(len(job.ins) for job in jobs)
    n_out = sum(len(job.outs) for job in jobs)
    sems = 24 + sum(12 + 2 * place.Q + place.R * place.Q * 2 for job in jobs)
    arrays, in_specs, outs, aliases = [], [], [], {}
    for job in jobs:
        for k, o in job.aliases:
            aliases[len(arrays) + k] = len(outs) + o
        for k, value in enumerate(job.ins):
            arrays.append(value)
            in_specs.append(pl.BlockSpec(memory_space=pltpu.VMEM if k in job.vmem else pl.ANY))
        outs.extend(job.outs)

    def body(*refs):
        at = place.here()
        ins, results = refs[:n_in], refs[n_in : n_in + n_out]
        copies = Copies(refs[n_in + n_out], refs[n_in + n_out + 1])
        meet(at, kinds)
        runs, i, o = [], 0, 0
        for job in jobs:
            runs.append(
                job.run(at, copies, ins[i : i + len(job.ins)], results[o : o + len(job.outs)])
            )
            i, o = i + len(job.ins), o + len(job.outs)
        pairs = list(zip(jobs, runs))
        relays = together([steps for job, steps in pairs if job.relay])
        next(relays, "done")
        for steps in [steps for job, steps in pairs if not job.relay and not job.late]:
            next(steps)
        next(relays, "done")
        for steps in [steps for job, steps in pairs if job.late]:
            next(steps)
        for _ in relays:
            pass
        for steps in [steps for job, steps in pairs if not job.relay]:
            for _ in steps:
                pass
        copies.drain()

    results = pl.pallas_call(
        body,
        out_shape=tuple(outs),
        in_specs=in_specs,
        out_specs=tuple(pl.BlockSpec(memory_space=pl.ANY) for _ in outs),
        scratch_shapes=[pltpu.SemaphoreType.DMA((sems,)), pltpu.SemaphoreType.DMA((sems,))],
        input_output_aliases=aliases,
        compiler_params=pltpu.CompilerParams(collective_id=ident, has_side_effects=True),
        cost_estimate=pl.CostEstimate(flops=0, bytes_accessed=COST, transcendentals=0),
        name="exchange_%d" % ident,
    )(*arrays)
    given, o = [], 0
    for job in jobs:
        given.append(results[o : o + len(job.outs)])
        o += len(job.outs)
    return given


def like(shape, dtype=BF):
    return jax.ShapeDtypeStruct(shape, dtype)


def gather_plane(value):
    def run(at, copies, ins, outs):
        slots = [copies.slot() for _ in range(TP - 1)]
        for j in range(1, TP):
            peer = at.q * TP + lax.rem(at.p + j, TP)
            copies.push(ins[0], outs[0].at[at.p], slots[j - 1], (at.r, peer))
        copies.local(ins[0], outs[0].at[at.p])
        yield "go"
        for j in range(1, TP):
            origin = lax.rem(at.p + TP - j, TP)
            copies.arrived(outs[0].at[origin], slots[j - 1], (at.r, at.s))

    return Job([value], [like((TP,) + value.shape, value.dtype)], run, {"plane"}, vmem=(0,))


def swap_plane(value):
    def run(at, copies, ins, outs):
        slots = [copies.slot() for _ in range(TP - 1)]
        for j in range(1, TP):
            other = lax.rem(at.p + j, TP)
            copies.push(
                ins[0].at[other], outs[0].at[at.p], slots[j - 1], (at.r, at.q * TP + other)
            )
        yield "go"
        for j in range(1, TP):
            origin = lax.rem(at.p + TP - j, TP)
            copies.arrived(outs[0].at[origin], slots[j - 1], (at.r, at.s))

    return Job([value], [like(value.shape, value.dtype)], run, {"plane"})


def swap_core(value):
    def run(at, copies, ins, outs):
        slots = [copies.slot() for _ in range(at.R - 1)]
        for j in range(1, at.R):
            other = lax.rem(at.r + j, at.R)
            copies.push(ins[0].at[other], outs[0].at[at.r], slots[j - 1], (other, at.s))
        yield "go"
        for j in range(1, at.R):
            origin = lax.rem(at.r + at.R - j, at.R)
            copies.arrived(outs[0].at[origin], slots[j - 1], (at.r, at.s))

    return Job([value], [like(value.shape, value.dtype)], run, {"core"})


def swap_line(value):
    def run(at, copies, ins, outs):
        slots = [copies.slot() for _ in range(at.Q - 1)]
        for j in range(1, at.Q):
            other = lax.rem(at.q + j, at.Q)
            copies.push(
                ins[0].at[other], outs[0].at[at.q], slots[j - 1], (at.r, other * TP + at.p)
            )
        yield "go"
        for j in range(1, at.Q):
            origin = lax.rem(at.q + at.Q - j, at.Q)
            copies.arrived(outs[0].at[origin], slots[j - 1], (at.r, at.s))

    return Job([value], [like(value.shape, value.dtype)], run, {"zall"})


def window_forward(place, value):
    reach = place.Q // 2

    def run(at, copies, ins, outs):
        slots = [copies.slot() for _ in range(reach)]
        for j in range(1, reach + 1):
            target = (at.q + j) * TP + at.p
            there = outs[0].at[reach - j]
            copies.push(ins[0], there, slots[j - 1], (at.r, target), at.q + j < at.Q)
        copies.local(ins[0], outs[0].at[reach])
        yield "go"
        for j in range(1, reach + 1):
            copies.arrived(outs[0].at[reach - j], slots[j - 1], (at.r, at.s), at.q >= j)

    shape = (reach + 1,) + value.shape
    return Job([value], [like(shape, value.dtype)], run, {"zall"}, vmem=(0,))


def window_backward(place, value):
    reach = place.Q // 2

    def run(at, copies, ins, outs):
        slots = [copies.slot() for _ in range(reach)]
        for j in range(1, reach + 1):
            target = (at.q - j) * TP + at.p
            copies.push(
                ins[0].at[reach - j], outs[0].at[j - 1], slots[j - 1], (at.r, target), at.q >= j
            )
        yield "go"
        for j in range(1, reach + 1):
            copies.arrived(outs[0].at[j - 1], slots[j - 1], (at.r, at.s), at.q + j < at.Q)

    shape = (reach,) + value.shape[1:]
    return Job([value], [like(shape, value.dtype)], run, {"zall"})


def halo_tokens(value):
    rows = value.shape[0]

    def run(at, copies, ins, outs):
        ahead = [copies.slot() for _ in range(TP)]
        back = [copies.slot() for _ in range(TP)]
        first = (at.p == 0) & (at.q > 0)
        last = (at.p == TP - 1) & (at.q < at.Q - 1)
        for j in range(TP):
            tail = ins[0].at[pl.ds(rows - HALO, HALO)]
            there = (at.r, (at.q + 1) * TP + j)
            copies.push(tail, outs[0], ahead[j], there, last, ahead[0])
            head = ins[0].at[pl.ds(0, HALO)]
            there = (at.r, (at.q - 1) * TP + j)
            copies.push(head, outs[1], back[j], there, first, back[0])
        yield "go"
        copies.arrived(outs[0], ahead[0], (at.r, at.s), at.q > 0)
        copies.arrived(outs[1], back[0], (at.r, at.s), at.q < at.Q - 1)

    shape = (HALO,) + value.shape[1:]
    outs = [like(shape, value.dtype), like(shape, value.dtype)]
    return Job([value], outs, run, {"halo"}, vmem=(0,))


def spread_run(at, copies, source, held, first):
    slots = [copies.slot() for _ in range(TP - 1)]
    for j in range(1, TP):
        other = lax.rem(at.p + j, TP)
        copies.push(
            source.at[other], held.at[first + at.p], slots[j - 1], (at.r, at.q * TP + other)
        )
    copy = pltpu.make_async_copy(
        source.at[at.p], held.at[first + at.p], copies.recv.at[copies.slot()]
    )
    copy.start()
    yield "go"
    copy.wait()
    for j in range(1, TP):
        origin = lax.rem(at.p + TP - j, TP)
        copies.arrived(held.at[first + origin], slots[j - 1], (at.r, at.s))


def chain_run(at, copies, held, unit=TP):
    def block(r, q):
        return held.at[pl.ds((r * at.Q + q) * unit, unit)]

    right = [copies.slot() for _ in range(at.Q - 1)]
    left = [copies.slot() for _ in range(at.Q - 1)]
    across = [[copies.slot() for _ in range(at.Q)] for _ in range(at.R - 1)]

    def cross(q, index, cond):
        for j in range(1, at.R):
            other = lax.rem(at.r + j, at.R)
            copies.push(block(at.r, q), block(at.r, q), across[j - 1][index], (other, at.s), cond)

    copies.push(
        block(at.r, at.q), block(at.r, at.q), right[0], (at.r, at.s + TP), at.q < at.Q - 1
    )
    copies.push(block(at.r, at.q), block(at.r, at.q), left[0], (at.r, at.s - TP), at.q > 0)
    cross(at.q, 0, None)
    index = 0
    spots = {}
    for hop in range(1, at.Q):
        yield "go"
        from_left, from_right = at.q >= hop, at.q + hop < at.Q
        copies.arrived(block(at.r, at.q - hop), right[hop - 1], (at.r, at.s), from_left)
        if hop < at.Q - 1:
            copies.push(
                block(at.r, at.q - hop),
                block(at.r, at.q - hop),
                right[hop],
                (at.r, at.s + TP),
                from_left & (at.q < at.Q - 1),
            )
        copies.arrived(block(at.r, at.q + hop), left[hop - 1], (at.r, at.s), from_right)
        if hop < at.Q - 1:
            copies.push(
                block(at.r, at.q + hop),
                block(at.r, at.q + hop),
                left[hop],
                (at.r, at.s - TP),
                from_right & (at.q > 0),
            )
        for side, sign in ((from_left, -1), (from_right, 1)):
            spots[(hop, sign)] = [copies.slot() for _ in range(at.R - 1)]
            for j in range(1, at.R):
                other = lax.rem(at.r + j, at.R)
                piece = block(at.r, at.q + sign * hop)
                copies.push(piece, piece, spots[(hop, sign)][j - 1], (other, at.s), side)
    yield "go"
    for j in range(1, at.R):
        source = lax.rem(at.r + at.R - j, at.R)
        copies.arrived(block(source, at.q), across[j - 1][0], (at.r, at.s))
        for hop in range(1, at.Q):
            for sign in (-1, 1):
                there = at.q + sign * hop
                copies.arrived(
                    block(source, there),
                    spots[(hop, sign)][j - 1],
                    (at.r, at.s),
                    at.q >= hop if sign < 0 else there < at.Q,
                )


def spread(source):
    def run(at, copies, ins, outs):
        yield from spread_run(at, copies, ins[0], outs[0], 0)

    outs = [like(source.shape, source.dtype)]
    return Job([source], outs, run, {"plane"}, vmem=(0,), late=True)


def spread_all(place, source):
    def run(at, copies, ins, outs):
        yield from spread_run(at, copies, ins[0], outs[0], (at.r * at.Q + at.q) * TP)
        yield from chain_run(at, copies, outs[0])

    outs = [like((place.R * place.S,) + source.shape[1:], source.dtype)]
    return Job([source], outs, run, {"plane", "chain", "core"}, vmem=(0,), relay=True)


def home_all(place, source):
    def run(at, copies, ins, outs):
        r, s, slot, here = home_of(at)
        _, _, own = visitor_of(at)
        index = copies.slot()
        copies.push(ins[0], outs[0].at[slot], index, (r, s), here == 0)
        copy = pltpu.make_async_copy(ins[0], outs[0].at[slot], copies.recv.at[copies.slot()])
        when(here == 1, copy.start)
        yield "go"
        when(here == 1, copy.wait)
        copies.arrived(outs[0].at[at.r * at.Q + at.q], index, (at.r, at.s), own == 0)
        yield from chain_run(at, copies, outs[0], 1)

    outs = [like((place.R * place.Q,) + source.shape, source.dtype)]
    return Job([source], outs, run, {"home", "chain", "core"}, vmem=(0,), relay=True)


FACTOR = 1.0 / math.sqrt(HD)


def masked_keys(kv_ref, first, kv_s):
    index = lax.broadcasted_iota(jnp.int32, kv_ref.shape, 0)
    kv_s[...] = jnp.where(index >= first, kv_ref[...].astype(F32), 0.0).astype(BF)


def attend_forward(q, kv, q_seg, key_seg, first, block):
    N, QS = q.shape
    M, KS = kv.shape[0], kv.shape[1] // 2
    ahead = M - N
    span = ahead + block
    kv_heads = KS // HD
    groups = QS // KS

    def body(first_ref, q_ref, kv_ref, qs_ref, ks_ref, o_ref, kv_s):
        masked_keys(kv_ref, first_ref[0], kv_s)

        @pl.loop(0, N // block)
        def _(i):
            start = pl.multiple_of(i * block, block)
            here, keys = pl.ds(start, block), pl.ds(start, span)
            row = lax.broadcasted_iota(jnp.int32, (block, span), 0) + ahead
            col = lax.broadcasted_iota(jnp.int32, (block, span), 1)
            open_ = (qs_ref[here, :1] == ks_ref[:1, keys]) & (col <= row)
            open_ = open_ & (col + start >= first_ref[0])
            open_ = jnp.concatenate([open_] * groups, axis=0)
            queries = q_ref[here, :]
            done = []
            for k in range(kv_heads):
                mine = [
                    queries[:, (k * groups + g) * HD : (k * groups + g + 1) * HD]
                    for g in range(groups)
                ]
                key = kv_s[keys, k * HD : (k + 1) * HD]
                value = kv_s[keys, KS + k * HD : KS + (k + 1) * HD]
                score = jnp.where(open_, dot_nt(jnp.concatenate(mine, axis=0), key) * FACTOR, MASKED)
                weight = jnp.exp(score - jnp.max(score, axis=-1, keepdims=True))
                weight = weight / jnp.sum(weight, axis=-1, keepdims=True)
                out = dot(weight.astype(BF), value).astype(BF)
                done.extend(out[g * block : (g + 1) * block] for g in range(groups))
            o_ref[here, :] = jnp.concatenate(done, axis=1)

    return attend_call(
        body, like((N, QS)), [pltpu.VMEM(kv.shape, BF)], 4 * N * span * QS, first, q, kv, q_seg, key_seg
    )


def attend_call(body, outs, scratch, flops, first, *arrays):
    return pl.pallas_call(
        body,
        out_shape=outs,
        in_specs=[pl.BlockSpec(memory_space=pltpu.SMEM)]
        + [pl.BlockSpec(memory_space=pltpu.VMEM) for _ in arrays],
        out_specs=jax.tree.map(lambda _: pl.BlockSpec(memory_space=pltpu.VMEM), outs),
        scratch_shapes=scratch,
        cost_estimate=pl.CostEstimate(flops=flops, bytes_accessed=COST, transcendentals=0),
    )(first, *arrays)


def attend_backward(q, kv, d_o, q_seg, key_seg, first, block):
    N, QS = q.shape
    M, KS = kv.shape[0], kv.shape[1] // 2
    ahead = M - N
    span = ahead + block
    kv_heads = KS // HD
    groups = QS // KS

    def body(first_ref, q_ref, kv_ref, do_ref, qs_ref, ks_ref, dq_ref, dkv_ref, kv_s, *sums):
        masked_keys(kv_ref, first_ref[0], kv_s)
        for total in sums:
            total[...] = jnp.zeros_like(total)

        @pl.loop(0, N // block)
        def _(i):
            start = pl.multiple_of(i * block, block)
            here, keys = pl.ds(start, block), pl.ds(start, span)
            row = lax.broadcasted_iota(jnp.int32, (span, block), 0)
            col = lax.broadcasted_iota(jnp.int32, (span, block), 1) + ahead
            open_ = (ks_ref[keys, :1] == qs_ref[:1, here]) & (row <= col)
            open_ = open_ & (row + start >= first_ref[0])
            open_ = jnp.concatenate([open_] * groups, axis=1)
            queries, pulls = q_ref[here, :], do_ref[here, :]

            def heads_of(values, k):
                return jnp.concatenate(
                    [
                        values[:, (k * groups + g) * HD : (k * groups + g + 1) * HD]
                        for g in range(groups)
                    ],
                    axis=0,
                )

            done = []
            for k in range(kv_heads):
                mine, pull = heads_of(queries, k), heads_of(pulls, k)
                key = kv_s[keys, k * HD : (k + 1) * HD]
                value = kv_s[keys, KS + k * HD : KS + (k + 1) * HD]
                score = jnp.where(open_, dot_nt(key, mine) * FACTOR, MASKED)
                weight = jnp.exp(score - jnp.max(score, axis=0, keepdims=True))
                weight = weight / jnp.sum(weight, axis=0, keepdims=True)
                d_weight = dot_nt(value, pull)
                delta = jnp.sum(weight * d_weight, axis=0, keepdims=True)
                d_score = (weight * (d_weight - delta)).astype(BF)
                sums[k][keys, :] += dot(d_score, mine) * FACTOR
                sums[kv_heads + k][keys, :] += dot(weight.astype(BF), pull)
                dq = dot_tn(d_score, key) * FACTOR
                done.extend(dq[g * block : (g + 1) * block] for g in range(groups))
            dq_ref[here, :] = jnp.concatenate(done, axis=1)

        dkv_ref[...] = jnp.concatenate([total[...] for total in sums], axis=1)

    return attend_call(
        body,
        (like((N, QS), F32), like((M, 2 * KS), F32)),
        [pltpu.VMEM(kv.shape, BF)] + [pltpu.VMEM((M, HD), F32) for _ in range(2 * kv_heads)],
        10 * N * span * QS,
        first,
        q,
        kv,
        d_o,
        q_seg,
        key_seg,
    )


def doc_info(positions, lengths):
    doc_ends = jnp.cumsum(lengths, dtype=jnp.int32)
    passed = positions[:, None] >= doc_ends[None, :]
    segment = jnp.sum(passed.astype(jnp.int32), axis=1, dtype=jnp.int32)
    opening = jnp.sum(jnp.where(passed, lengths[None, :], 0), axis=1, dtype=jnp.int32)
    return (segment, positions - opening)


def inverse_rms(values):
    return lax.rsqrt(jnp.mean(values * values, axis=-1, keepdims=True) + EPSILON)


def rms_pull(upstream, values, inverse, norm_gain):
    scaled = upstream * norm_gain
    product_mean = jnp.mean(scaled * values, axis=-1, keepdims=True)
    return inverse * scaled - values * (inverse * inverse * inverse) * product_mean


def rope_tables(relative):
    half_size = HD // 2
    frequency = jnp.exp(
        jnp.arange(half_size, dtype=F32) * (-2.0 * math.log(THETA) / HD)
    )
    angles = relative.astype(F32)[:, None] * frequency[None, :]
    return (jnp.cos(angles)[:, None, :], jnp.sin(angles)[:, None, :])


def rope_apply(values, cosine, sine):
    front, back = values[..., : HD // 2], values[..., HD // 2 :]
    return jnp.concatenate([front * cosine - back * sine, back * cosine + front * sine], axis=-1)


def rope_revert(values, cosine, sine):
    front, back = values[..., : HD // 2], values[..., HD // 2 :]
    return jnp.concatenate([front * cosine + back * sine, back * cosine - front * sine], axis=-1)


def settle(own, arrived, p):
    index = jnp.arange(TP, dtype=jnp.int32)[:, None, None]
    others = jnp.where(index == p, 0.0, arrived.astype(F32))
    mine = lax.dynamic_index_in_dim(own, p, 0, keepdims=False)
    return mine + jnp.sum(others, axis=0)


def per_device(
    place,
    tokens,
    doc_lengths,
    cotangent,
    gain_conv,
    w_in,
    kernel,
    w_mix,
    gain_ffa,
    gate_a,
    up_a,
    down_a,
    gain_att,
    w_query,
    w_key,
    w_value,
    head_gains,
    w_attout,
    gain_ffb,
    gate_b,
    up_b,
    down_b,
):
    R, S, Q = place.R, place.S, place.Q
    n, D = tokens.shape[1], tokens.shape[2]
    shard = w_in.shape[0]
    FS = gate_a.shape[1] // TP
    CS = D // TP
    QS, KS = H * HD // TP, KVH * HD // TP
    taps = kernel.shape[0]
    N = n * TP
    r, s = lax.axis_index("rows"), lax.axis_index("seq")
    q, p = s // TP, lax.rem(s, TP)
    lengths = doc_lengths[0]

    def slices(weight):
        return weight.reshape(shard, TP, -1).transpose(1, 0, 2)

    def joined(*weights):
        return jnp.concatenate([slices(weight) for weight in weights], axis=2)

    columns = [[a * S + b * TP + c for a in range(R) for b in range(Q)] for c in range(TP)]
    lines = [[b * TP + c for b in range(Q)] for c in range(TP)]

    def gather_rest(plane):
        flat = plane.reshape(TP * shard, -1)
        return lax.all_gather(
            flat, ("rows", "seq"), axis=0, tiled=True, axis_index_groups=columns
        )

    def by_row(grads):
        return grads.astype(BF).reshape(R, S * shard, -1)

    def own_rows(rows, came, *later):
        return lax.optimization_barrier((collect(rows, came, r).astype(BF),) + later)

    def reduce_line(half):
        part = lax.psum_scatter(
            half, "seq", scatter_dimension=0, tiled=True, axis_index_groups=lines
        )
        return part.reshape(TP, shard, part.shape[1])

    in_cut = w_in.reshape(shard, 3, TP, CS).transpose(2, 0, 1, 3).reshape(TP, shard, 3 * CS)
    small = jnp.stack([gain_conv, gain_ffa, gain_att, gain_ffb] + [kernel[i] for i in range(taps)])
    small = jnp.pad(small, ((0, 16 - 4 - taps), (0, 128 - shard)))
    small = jnp.broadcast_to(small[None], (TP, 16, 128))

    per_slice = R * Q
    homes = []
    for d in range(R * S):
        k = d % per_slice
        homes.append((d, (k // Q) * S + (k % Q) * TP + d // per_slice))
    mine = tokens[0]
    (tok_g,), (halo_a, halo_b), (in_g,), (mix_g,), (small_g,), (ffa_p,) = exchange(
        place,
        0,
        [
            gather_plane(mine),
            halo_tokens(mine),
            spread_all(place, in_cut),
            home_all(place, w_mix),
            spread_all(place, small),
            spread(joined(gate_a, up_a, down_a.T)),
        ],
    )
    wa = gather_rest(ffa_p)
    w_mix_s = mix_g.reshape(CS, D)
    vectors = small_g[:, : 4 + taps, :shard].transpose(1, 0, 2).reshape(4 + taps, D).astype(F32)
    g_conv, g_ffa, g_att, g_ffb = (vectors[i] for i in range(4))
    kernel_f = lax.dynamic_slice_in_dim(vectors[4:], p * CS, CS, 1)
    w_in_s = in_g.reshape(D, 3 * CS)

    def own(parts, index):
        return lax.dynamic_index_in_dim(parts, index, 0, keepdims=False).astype(F32)

    def collect(parts, came, index):
        slot = jnp.arange(came.shape[0], dtype=jnp.int32).reshape((-1,) + (1,) * (came.ndim - 1))
        mine_part = lax.dynamic_index_in_dim(parts, index, 0, keepdims=True).astype(F32)
        return jnp.sum(jnp.where(slot == index, mine_part, came.astype(F32)), axis=0)

    def after_core(parts, came):
        summed = collect(parts, came, r)
        return summed.reshape((Q, TP) + summed.shape[1:])

    def after_line(parts, came):
        return collect(parts, came, q)

    def after_plane(full, came):
        slot = jnp.arange(TP, dtype=jnp.int32).reshape((TP,) + (1,) * (full.ndim - 1))
        mine_part = lax.dynamic_index_in_dim(full, p, 0, keepdims=True)
        return jnp.where(slot == p, mine_part, came.astype(F32))

    total = S * n
    pos_ext = q * N - HALO + jnp.arange(N + 2 * HALO, dtype=jnp.int32)
    seg_ext, rel_ext = doc_info(pos_ext, lengths)
    valid = ((pos_ext >= 0) & (pos_ext < total))[:, None]
    x_ext = jnp.concatenate([halo_a, tok_g.reshape(N, D), halo_b], axis=0)
    x_ext = jnp.where(valid, x_ext, jnp.zeros_like(x_ext)).astype(F32)
    r0_ext = inverse_rms(x_ext)
    n1_ext = (x_ext * r0_ext * g_conv).astype(BF)
    z_ext = dot(n1_ext, w_in_s)
    b_ext, c_ext, v_ext = z_ext[:, :CS], z_ext[:, CS : 2 * CS], z_ext[:, 2 * CS :]
    u_ext = lax.optimization_barrier((b_ext * v_ext).astype(BF)).astype(F32)
    span = slice(HALO, HALO + N)
    same = [
        (seg_ext[HALO - 2 + k : HALO - 2 + k + N] == seg_ext[span]).astype(F32)[:, None]
        for k in range(taps)
    ]
    near = [u_ext[HALO - 2 + k : HALO - 2 + k + N] for k in range(taps)]
    conv = kernel_f[0] * near[0] * same[0]
    for k in range(1, taps):
        conv = conv + kernel_f[k] * near[k] * same[k]
    m_bf = (c_ext[span] * conv).astype(BF)
    part = dot(m_bf, w_mix_s).reshape(TP, n, D)
    (got,), (att_p,), (ffb_p,) = exchange(
        place,
        1,
        [
            swap_plane(part.astype(BF)),
            spread(joined(w_query, w_key, w_value, w_attout.T)),
            spread(joined(gate_b, up_b, down_b.T)),
        ],
    )
    w_att = gather_rest(att_p)
    wb = gather_rest(ffb_p)
    x0 = mine.astype(F32)
    h1 = x0 + settle(part, got, p)

    r1 = inverse_rms(h1)
    a1 = (h1 * r1 * g_ffa).astype(BF)
    ((a1_g,),) = exchange(place, 2, [gather_plane(a1)])
    a1_g = a1_g.reshape(N, D)

    def ffn(a, w):
        both = dot(a, w[:, : 2 * FS])
        gate, up = both[:, :FS], both[:, FS:]
        act = (jax.nn.silu(gate) * up).astype(BF)
        return gate, up, act, dot_nt(act, w[:, 2 * FS :]).reshape(TP, n, D)

    gate1, up1, act1, part = ffn(a1_g, wa)
    ((got,),) = exchange(place, 3, [swap_plane(part.astype(BF))])
    h2 = h1 + settle(part, got, p)

    r2 = inverse_rms(h2)
    n3 = (h2 * r2 * g_att).astype(BF)
    ((n3_g,),) = exchange(place, 4, [gather_plane(n3)])
    n3_g = n3_g.reshape(N, D)
    w_qkv, w_out = w_att[:, : QS + 2 * KS], w_att[:, QS + 2 * KS :]
    qkv = dot(n3_g, w_qkv)
    heads, kv_heads = QS // HD, KS // HD
    groups = heads // kv_heads
    q_pre = qkv[:, :QS].reshape(N, heads, HD)
    k_pre = qkv[:, QS : QS + KS].reshape(N, kv_heads, HD)
    head_f = head_gains.astype(F32)
    cosine, sine = rope_tables(rel_ext[span])
    q_inv, k_inv = inverse_rms(q_pre), inverse_rms(k_pre)
    q_bf = rope_apply(q_pre * q_inv * head_f[0], cosine, sine).astype(BF)
    k_bf = rope_apply(k_pre * k_inv * head_f[1], cosine, sine).astype(BF).reshape(N, KS)
    v_bf = qkv[:, QS + KS :].astype(BF)
    e_bf = cotangent[0]
    (kv_w,), (e_g,) = exchange(
        place,
        5,
        [window_forward(place, jnp.concatenate([k_bf, v_bf], axis=1)), gather_plane(e_bf)],
    )
    reach = Q // 2 + 1
    kv_all = kv_w.reshape(reach * N, 2 * KS)
    q_seg = seg_ext[span]
    key_seg, _ = doc_info((q - reach + 1) * N + jnp.arange(reach * N, dtype=jnp.int32), lengths)
    first = jnp.maximum((reach - 1 - q) * N, 0).astype(jnp.int32).reshape(1)
    q_bf = q_bf.reshape(N, QS)
    seg_col, seg_row = (jnp.broadcast_to(q_seg[:, None], (N, 128)), jnp.broadcast_to(q_seg, (8, N)))
    key_col = jnp.broadcast_to(key_seg[:, None], (reach * N, 128))
    key_row = jnp.broadcast_to(key_seg, (8, reach * N))
    o_bf = attend_forward(q_bf, kv_all, seg_col, key_row, first, 128)
    part = dot_nt(o_bf, w_out).reshape(TP, n, D)
    ((got,),) = exchange(place, 6, [swap_plane(part.astype(BF))])
    h3 = h2 + settle(part, got, p)

    r3 = inverse_rms(h3)
    a2 = (h3 * r3 * g_ffb).astype(BF)
    ((a2_g,),) = exchange(place, 7, [gather_plane(a2)])
    a2_g, e_g = a2_g.reshape(N, D), e_g.reshape(N, D)
    gate2, up2, act2, part_o = ffn(a2_g, wb)

    def ffn_back(e, a, gate, up, act, w):
        d_down = dot_tn(e, act)
        d_act = dot(e, w[:, 2 * FS :])
        sigma = jax.nn.sigmoid(gate)
        d_gate = (d_act * up * sigma * (1.0 + gate * (1.0 - sigma))).astype(BF)
        d_up = (d_act * (gate * sigma)).astype(BF)
        d_both = jnp.concatenate([d_gate, d_up], axis=1)
        grads = jnp.concatenate([dot_tn(a, d_both).astype(BF), d_down.astype(BF)], axis=1)
        d_normed = dot_nt(d_both, w[:, : 2 * FS])
        return grads, d_normed.reshape(TP, n, D)

    grads_b, part_b = ffn_back(e_g, a2_g, gate2, up2, act2, wb)

    rows_b = by_row(grads_b)
    (got_b,), (core_b,) = exchange(
        place, 8, [swap_plane(part_b.astype(BF)), swap_core(rows_b)]
    )
    d_gain = {}
    d_normed = settle(part_b, got_b, p)
    d_gain["ffb"] = jnp.sum(d_normed * h3 * r3, axis=0)
    g4 = e_bf.astype(F32)
    g3 = g4 + rms_pull(d_normed, h3, r3, g_ffb)

    ((g3_g,),) = exchange(place, 9, [gather_plane(g3.astype(BF))])
    g3_g = g3_g.reshape(N, D)
    d_out = dot_tn(g3_g, o_bf)
    d_o = dot(g3_g, w_out).astype(BF)
    d_q, d_kv = attend_backward(q_bf, kv_all, d_o, seg_row, key_col, first, 128)
    d_kv = d_kv.reshape(reach, N, 2 * KS)
    (got_kv,), (got_o,) = exchange(
        place, 10, [window_backward(place, d_kv.astype(BF)), swap_plane(part_o.astype(BF))]
    )
    h4 = h3 + settle(part_o, got_o, p)
    mixed = h4.astype(BF)[None]
    there = (q + 1 + jnp.arange(reach - 1, dtype=jnp.int32) < Q)[:, None, None]
    d_kv = d_kv[-1] + jnp.sum(jnp.where(there, got_kv.astype(F32), 0.0), axis=0)
    half_b, d_kv = own_rows(rows_b, core_b, d_kv)
    full_b = reduce_line(half_b)
    dv_bf = d_kv[:, KS:].astype(BF)
    dk_norm = rope_revert(d_kv[:, :KS].reshape(N, kv_heads, HD), cosine, sine)
    dq_norm = rope_revert(d_q.reshape(N, heads, HD), cosine, sine)
    dk_pre = rms_pull(dk_norm, k_pre, k_inv, head_f[1]).reshape(N, KS)
    dq_pre = rms_pull(dq_norm, q_pre, q_inv, head_f[0]).reshape(N, QS)
    d_heads = jnp.stack(
        [
            jnp.sum(dq_norm * q_pre * q_inv, axis=(0, 1)),
            jnp.sum(dk_norm * k_pre * k_inv, axis=(0, 1)),
        ]
    )
    d_qkv = jnp.concatenate([dq_pre.astype(BF), dk_pre.astype(BF), dv_bf], axis=1)
    part = dot_nt(d_qkv, w_qkv).reshape(TP, n, D)
    rows_att = by_row(
        jnp.concatenate([dot_tn(n3_g, d_qkv).astype(BF), d_out.astype(BF)], axis=1)
    )
    (got,), (core_att,) = exchange(
        place, 11, [swap_plane(part.astype(BF)), swap_core(rows_att)]
    )
    d_normed = settle(part, got, p)
    d_gain["att"] = jnp.sum(d_normed * h2 * r2, axis=0)
    g2 = g3 + rms_pull(d_normed, h2, r2, g_att)

    half_att, g2_bf = own_rows(rows_att, core_att, g2.astype(BF))
    full_att = reduce_line(half_att)
    ((g2_g,),) = exchange(place, 12, [gather_plane(g2_bf)])
    g2_g = g2_g.reshape(N, D)
    grads_a, part = ffn_back(g2_g, a1_g, gate1, up1, act1, wa)
    rows_a = by_row(grads_a)
    full_b, rows_a = lax.optimization_barrier((full_b, rows_a))
    (got,), (core_a,) = exchange(place, 13, [swap_plane(part.astype(BF)), swap_core(rows_a)])
    d_normed = settle(part, got, p)
    d_gain["ffa"] = jnp.sum(d_normed * h1 * r1, axis=0)
    g1 = g2 + rms_pull(d_normed, h1, r1, g_ffa)

    half_a, g1_bf = own_rows(rows_a, core_a, g1.astype(BF))
    full_a = reduce_line(half_a)
    (g1_g,), (_, g1_halo) = exchange(place, 14, [gather_plane(g1_bf), halo_tokens(g1_bf)])
    g1_halo = jnp.where(q < Q - 1, g1_halo, jnp.zeros_like(g1_halo))
    g1_ext = jnp.concatenate([g1_g.reshape(N, D), g1_halo], axis=0)
    d_m = dot_nt(g1_ext, w_mix_s)
    d_mix_s = dot_tn(m_bf, g1_ext[:N])
    d_c = d_m[:N] * conv
    d_conv = lax.optimization_barrier((d_m * c_ext[HALO:]).astype(BF)).astype(F32)
    d_kernel = jnp.stack(
        [jnp.sum(d_conv[:N] * near[k] * same[k], axis=0) for k in range(taps)]
    )
    d_u = jnp.zeros((N, CS), F32)
    for k in range(taps):
        ahead = taps - 1 - k
        match = (seg_ext[HALO + ahead : HALO + ahead + N] == seg_ext[span]).astype(F32)[:, None]
        d_u = d_u + kernel_f[k] * d_conv[ahead : ahead + N] * match
    d_z = jnp.concatenate([d_u * v_ext[span], d_c, d_u * b_ext[span]], axis=1).astype(BF)
    rows_in = dot_tn(n1_ext[span], d_z).astype(BF).reshape(R, S, shard, 3 * CS)
    rows_mix = d_mix_s.astype(BF).reshape(R, Q, shard, D)
    d_n1 = dot_nt(d_z, w_in_s)
    d_gain["conv"] = jnp.sum(d_n1 * x_ext[span] * r0_ext[span], axis=0)
    part = d_n1.reshape(TP, n, D)
    d_taps = lax.dynamic_update_slice(jnp.zeros((taps, D), F32), d_kernel, (0, p * CS))
    lanes = jnp.concatenate(
        [jnp.stack([d_gain["conv"], d_gain["ffa"], d_gain["att"], d_gain["ffb"]]), d_taps]
    )
    lanes = lanes.reshape(4 + taps, R * S, shard).transpose(1, 0, 2)
    lanes = jnp.pad(lanes, ((0, 0), (0, 0), (0, 128 - shard)))
    heads_row = jnp.broadcast_to(d_heads.reshape(1, 1, 2 * HD), (R * S, 1, 2 * HD))
    tiny = jnp.concatenate([lanes, heads_row], axis=1)
    tiny_rows = tiny.reshape(R, S, 4 + taps + 1, 128)
    (got,), (core_in,), (core_mix,), (core_t,) = exchange(
        place,
        15,
        [
            swap_plane(part.astype(BF)),
            swap_core(rows_in),
            swap_core(rows_mix),
            swap_core(tiny_rows),
        ],
    )
    d_normed = settle(part, got, p)
    g0 = g1 + rms_pull(d_normed, x0, inverse_rms(x0), g_conv)
    d_tokens = g0.astype(BF)[None]

    tiny_line = after_core(tiny_rows, core_t)
    line_in = after_core(rows_in, core_in).astype(BF)
    line_mix = collect(rows_mix, core_mix, r).astype(BF)
    (got_in,), (got_mix,), (line_t,), (plane_b,), (plane_att,) = exchange(
        place,
        16,
        [
            swap_line(line_in),
            swap_line(line_mix),
            swap_line(tiny_line),
            swap_plane(full_b),
            swap_plane(full_att),
        ],
    )
    tiny_full = after_line(tiny_line, line_t)
    full_in = after_line(line_in, got_in).astype(BF)
    full_mix = after_line(line_mix, got_mix).astype(BF)
    out_mix = lax.ppermute(full_mix, ("rows", "seq"), [(b, a) for a, b in homes])
    (plane_in,), (plane_t,), (plane_a,) = exchange(
        place, 17, [swap_plane(full_in), swap_plane(tiny_full), swap_plane(full_a)]
    )
    tiny_sum = jnp.sum(after_plane(tiny_full, plane_t), axis=0)
    d_heads = tiny_sum[4 + taps].reshape(2, HD)

    def back(value):
        return value.transpose(1, 0, 2).reshape(shard, -1)

    out_in = after_plane(full_in, plane_in)
    out_in = out_in.reshape(TP, shard, 3, CS).transpose(1, 2, 0, 3).reshape(shard, 3 * D)
    out_att = after_plane(full_att, plane_att)
    out_a = after_plane(full_a, plane_a)
    out_b = after_plane(full_b, plane_b)
    return (
        mixed,
        d_tokens,
        tiny_sum[0, :shard],
        out_in,
        tiny_sum[4 : 4 + taps, :shard],
        out_mix.astype(F32),
        tiny_sum[1, :shard],
        back(out_a[..., 0 * FS : 1 * FS]),
        back(out_a[..., 1 * FS : 2 * FS]),
        back(out_a[..., 2 * FS : 3 * FS]).T,
        tiny_sum[2, :shard],
        back(out_att[..., :QS]),
        back(out_att[..., QS : QS + KS]),
        back(out_att[..., QS + KS : QS + 2 * KS]),
        d_heads,
        back(out_att[..., QS + 2 * KS :]).T,
        tiny_sum[3, :shard],
        back(out_b[..., 0 * FS : 1 * FS]),
        back(out_b[..., 1 * FS : 2 * FS]),
        back(out_b[..., 2 * FS : 3 * FS]).T,
    )


def solution(mesh):
    place = Place(mesh.shape["rows"], mesh.shape["seq"])
    whole = ("rows", "seq")
    wide, first, second = P("rows", "seq", None), P(whole, None), P(None, whole)
    in_specs = (
        (wide, P("rows", None), wide, P(whole), first, second, first)
        + (P(whole), first, first, second)
        + (P(whole), first, first, first, P(), second)
        + (P(whole), first, first, second)
    )
    out_specs = (
        (wide, wide, P(whole), first, second, first)
        + (P(whole), first, first, second)
        + (P(whole), first, first, first, P(), second)
        + (P(whole), first, first, second)
    )
    return jax.shard_map(
        functools.partial(per_device, place),
        mesh=mesh,
        in_specs=in_specs,
        out_specs=out_specs,
        check_vma=False,
    )
```

```python
import functools
import math

import jax
import jax.numpy as jnp
from jax import lax
from jax.experimental import pallas as pl
from jax.experimental.pallas import tpu as pltpu
from jax.sharding import PartitionSpec as P

H = 16
KVH = 8
HD = 64
TP = 4
HALO = 16
COST = 1_000_000

EPSILON = 1e-05
THETA = 1000000.0
MASKED = -1e30
MESH_ID = pl.DeviceIdType.MESH
BF = jnp.bfloat16
F32 = jnp.float32


def dot(left, right):
    return jnp.dot(left, right, preferred_element_type=F32)


def dot_tn(left, right):
    return lax.dot_general(left, right, (((0,), (0,)), ((), ())), preferred_element_type=F32)


def dot_nt(left, right):
    return lax.dot_general(left, right, (((1,), (1,)), ((), ())), preferred_element_type=F32)


class Place:
    def __init__(self, rows, seq):
        self.R, self.S = rows, seq
        self.Q = seq // TP

    def here(self):
        here = Place(self.R, self.S)
        here.r = lax.axis_index("rows")
        here.s = lax.axis_index("seq")
        here.q = here.s // TP
        here.p = lax.rem(here.s, TP)
        return here


class Copies:
    def __init__(self, send, recv):
        self.send, self.recv, self.count, self.sent = send, recv, 0, []

    def slot(self):
        self.count += 1
        return self.count - 1

    def remote(self, src, dst, slot, where, recv_slot=None):
        return pltpu.make_async_remote_copy(
            src_ref=src,
            dst_ref=dst,
            send_sem=self.send.at[slot],
            recv_sem=self.recv.at[slot if recv_slot is None else recv_slot],
            device_id=where,
            device_id_type=MESH_ID,
        )

    def push(self, src, dst, slot, where, cond=None, recv_slot=None):
        copy = self.remote(src, dst, slot, where, recv_slot)
        when(cond, copy.start)
        self.sent.append((copy.wait_send, cond))

    def arrived(self, dst, slot, where, cond=None):
        copy = self.remote(dst, dst, slot, where)
        when(cond, copy.wait_recv)

    def local(self, src, dst):
        slot = self.slot()
        copy = pltpu.make_async_copy(src, dst, self.recv.at[slot])
        copy.start()
        self.sent.append((copy.wait, None))

    def drain(self):
        for wait, cond in self.sent:
            when(cond, wait)


def when(cond, action):
    if cond is None:
        action()
    else:
        pl.when(cond)(lambda: action())


class Job:
    def __init__(self, ins, outs, run, kinds, aliases=(), vmem=(), relay=False, late=False):
        self.ins, self.outs, self.run, self.kinds = ins, outs, run, kinds
        self.aliases, self.vmem, self.relay, self.late = aliases, vmem, relay, late


def together(runs):
    while runs:
        runs = [steps for steps in runs if next(steps, "done") != "done"]
        yield "go"


def partners(at, kinds):
    found = []
    if "plane" in kinds:
        for j in range(1, TP):
            found.append((None, at.r, at.q * TP + lax.rem(at.p + j, TP)))
    if "core" in kinds:
        for j in range(1, at.R):
            found.append((None, lax.rem(at.r + j, at.R), at.s))
    if "zall" in kinds:
        for j in range(1, at.Q):
            found.append((None, at.r, lax.rem(at.q + j, at.Q) * TP + at.p))
    elif "chain" in kinds:
        found.append((at.q > 0, at.r, at.s - TP))
        found.append((at.q < at.Q - 1, at.r, at.s + TP))
    if "home" in kinds:
        r, s, _, same = home_of(at)
        found.append((same == 0, r, s))
        r, s, same = visitor_of(at)
        found.append((same == 0, r, s))
    if "back" in kinds:
        found.append((at.q < at.Q - 1, at.r, (at.q + 1) * TP))
        for j in range(TP):
            found.append(((at.p == 0) & (at.q > 0), at.r, (at.q - 1) * TP + j))
    if "halo" in kinds:
        found.append((at.q > 0, at.r, (at.q - 1) * TP + TP - 1))
        found.append((at.q < at.Q - 1, at.r, (at.q + 1) * TP))
        for j in range(TP):
            found.append(((at.p == TP - 1) & (at.q < at.Q - 1), at.r, (at.q + 1) * TP + j))
            found.append(((at.p == 0) & (at.q > 0), at.r, (at.q - 1) * TP + j))
    return found


def home_of(at):
    k = lax.rem(at.r * at.S + at.s, at.R * at.Q)
    r, s = k // at.Q, lax.rem(k, at.Q) * TP + (at.r * at.S + at.s) // (at.R * at.Q)
    return r, s, k, ((r == at.r) & (s == at.s)).astype(jnp.int32)


def visitor_of(at):
    d = at.p * (at.R * at.Q) + at.r * at.Q + at.q
    r, s = d // at.S, lax.rem(d, at.S)
    return r, s, ((r == at.r) & (s == at.s)).astype(jnp.int32)


def meet(at, kinds):
    barrier = pltpu.get_barrier_semaphore()
    peers = partners(at, kinds)
    for cond, r, s in peers:
        when(
            cond,
            functools.partial(
                pl.semaphore_signal, barrier, inc=1, device_id=(r, s), device_id_type=MESH_ID
            ),
        )
    awaited = sum(1 for cond, r, s in peers if cond is None)
    for cond, r, s in peers:
        if cond is not None:
            awaited = awaited + cond.astype(jnp.int32)
    pl.semaphore_wait(barrier, awaited)


def exchange(place, ident, jobs):
    kinds = set().union(*[job.kinds for job in jobs])
    n_in = sum(len(job.ins) for job in jobs)
    n_out = sum(len(job.outs) for job in jobs)
    sems = 24 + sum(12 + 2 * place.Q + place.R * place.Q * 2 for job in jobs)
    arrays, in_specs, outs, aliases = [], [], [], {}
    for job in jobs:
        for k, o in job.aliases:
            aliases[len(arrays) + k] = len(outs) + o
        for k, value in enumerate(job.ins):
            arrays.append(value)
            in_specs.append(pl.BlockSpec(memory_space=pltpu.VMEM if k in job.vmem else pl.ANY))
        outs.extend(job.outs)

    def body(*refs):
        at = place.here()
        ins, results = refs[:n_in], refs[n_in : n_in + n_out]
        copies = Copies(refs[n_in + n_out], refs[n_in + n_out + 1])
        meet(at, kinds)
        runs, i, o = [], 0, 0
        for job in jobs:
            runs.append(
                job.run(at, copies, ins[i : i + len(job.ins)], results[o : o + len(job.outs)])
            )
            i, o = i + len(job.ins), o + len(job.outs)
        pairs = list(zip(jobs, runs))
        relays = together([steps for job, steps in pairs if job.relay])
        next(relays, "done")
        for steps in [steps for job, steps in pairs if not job.relay and not job.late]:
            next(steps)
        next(relays, "done")
        for steps in [steps for job, steps in pairs if job.late]:
            next(steps)
        for _ in relays:
            pass
        for steps in [steps for job, steps in pairs if not job.relay]:
            for _ in steps:
                pass
        copies.drain()

    results = pl.pallas_call(
        body,
        out_shape=tuple(outs),
        in_specs=in_specs,
        out_specs=tuple(pl.BlockSpec(memory_space=pl.ANY) for _ in outs),
        scratch_shapes=[pltpu.SemaphoreType.DMA((sems,)), pltpu.SemaphoreType.DMA((sems,))],
        input_output_aliases=aliases,
        compiler_params=pltpu.CompilerParams(collective_id=ident, has_side_effects=True),
        cost_estimate=pl.CostEstimate(flops=0, bytes_accessed=COST, transcendentals=0),
        name="exchange_%d" % ident,
    )(*arrays)
    given, o = [], 0
    for job in jobs:
        given.append(results[o : o + len(job.outs)])
        o += len(job.outs)
    return given


def like(shape, dtype=BF):
    return jax.ShapeDtypeStruct(shape, dtype)


def gather_plane(value):
    def run(at, copies, ins, outs):
        slots = [copies.slot() for _ in range(TP - 1)]
        for j in range(1, TP):
            peer = at.q * TP + lax.rem(at.p + j, TP)
            copies.push(ins[0], outs[0].at[at.p], slots[j - 1], (at.r, peer))
        copies.local(ins[0], outs[0].at[at.p])
        yield "go"
        for j in range(1, TP):
            origin = lax.rem(at.p + TP - j, TP)
            copies.arrived(outs[0].at[origin], slots[j - 1], (at.r, at.s))

    return Job([value], [like((TP,) + value.shape, value.dtype)], run, {"plane"}, vmem=(0,))


def swap_plane(value):
    def run(at, copies, ins, outs):
        slots = [copies.slot() for _ in range(TP - 1)]
        for j in range(1, TP):
            other = lax.rem(at.p + j, TP)
            copies.push(
                ins[0].at[other], outs[0].at[at.p], slots[j - 1], (at.r, at.q * TP + other)
            )
        yield "go"
        for j in range(1, TP):
            origin = lax.rem(at.p + TP - j, TP)
            copies.arrived(outs[0].at[origin], slots[j - 1], (at.r, at.s))

    return Job([value], [like(value.shape, value.dtype)], run, {"plane"})


def swap_core(value):
    def run(at, copies, ins, outs):
        slots = [copies.slot() for _ in range(at.R - 1)]
        for j in range(1, at.R):
            other = lax.rem(at.r + j, at.R)
            copies.push(ins[0].at[other], outs[0].at[at.r], slots[j - 1], (other, at.s))
        yield "go"
        for j in range(1, at.R):
            origin = lax.rem(at.r + at.R - j, at.R)
            copies.arrived(outs[0].at[origin], slots[j - 1], (at.r, at.s))

    return Job([value], [like(value.shape, value.dtype)], run, {"core"})


def swap_line(value):
    def run(at, copies, ins, outs):
        slots = [copies.slot() for _ in range(at.Q - 1)]
        for j in range(1, at.Q):
            other = lax.rem(at.q + j, at.Q)
            copies.push(
                ins[0].at[other], outs[0].at[at.q], slots[j - 1], (at.r, other * TP + at.p)
            )
        yield "go"
        for j in range(1, at.Q):
            origin = lax.rem(at.q + at.Q - j, at.Q)
            copies.arrived(outs[0].at[origin], slots[j - 1], (at.r, at.s))

    return Job([value], [like(value.shape, value.dtype)], run, {"zall"})


def window_forward(place, value):
    reach = place.Q // 2

    def run(at, copies, ins, outs):
        slots = [copies.slot() for _ in range(reach)]
        for j in range(1, reach + 1):
            target = (at.q + j) * TP + at.p
            there = outs[0].at[reach - j]
            copies.push(ins[0], there, slots[j - 1], (at.r, target), at.q + j < at.Q)
        copies.local(ins[0], outs[0].at[reach])
        yield "go"
        for j in range(1, reach + 1):
            copies.arrived(outs[0].at[reach - j], slots[j - 1], (at.r, at.s), at.q >= j)

    shape = (reach + 1,) + value.shape
    return Job([value], [like(shape, value.dtype)], run, {"zall"}, vmem=(0,))


def window_backward(place, value):
    reach = place.Q // 2

    def run(at, copies, ins, outs):
        slots = [copies.slot() for _ in range(reach)]
        for j in range(1, reach + 1):
            target = (at.q - j) * TP + at.p
            copies.push(
                ins[0].at[reach - j], outs[0].at[j - 1], slots[j - 1], (at.r, target), at.q >= j
            )
        yield "go"
        for j in range(1, reach + 1):
            copies.arrived(outs[0].at[j - 1], slots[j - 1], (at.r, at.s), at.q + j < at.Q)

    shape = (reach,) + value.shape[1:]
    return Job([value], [like(shape, value.dtype)], run, {"zall"})


def halo_tokens(value):
    rows = value.shape[0]

    def run(at, copies, ins, outs):
        ahead = [copies.slot() for _ in range(TP)]
        back = [copies.slot() for _ in range(TP)]
        first = (at.p == 0) & (at.q > 0)
        last = (at.p == TP - 1) & (at.q < at.Q - 1)
        for j in range(TP):
            tail = ins[0].at[pl.ds(rows - HALO, HALO)]
            there = (at.r, (at.q + 1) * TP + j)
            copies.push(tail, outs[0], ahead[j], there, last, ahead[0])
            head = ins[0].at[pl.ds(0, HALO)]
            there = (at.r, (at.q - 1) * TP + j)
            copies.push(head, outs[1], back[j], there, first, back[0])
        yield "go"
        copies.arrived(outs[0], ahead[0], (at.r, at.s), at.q > 0)
        copies.arrived(outs[1], back[0], (at.r, at.s), at.q < at.Q - 1)

    shape = (HALO,) + value.shape[1:]
    outs = [like(shape, value.dtype), like(shape, value.dtype)]
    return Job([value], outs, run, {"halo"}, vmem=(0,))


def spread_run(at, copies, source, held, first):
    slots = [copies.slot() for _ in range(TP - 1)]
    for j in range(1, TP):
        other = lax.rem(at.p + j, TP)
        copies.push(
            source.at[other], held.at[first + at.p], slots[j - 1], (at.r, at.q * TP + other)
        )
    copy = pltpu.make_async_copy(
        source.at[at.p], held.at[first + at.p], copies.recv.at[copies.slot()]
    )
    copy.start()
    yield "go"
    copy.wait()
    for j in range(1, TP):
        origin = lax.rem(at.p + TP - j, TP)
        copies.arrived(held.at[first + origin], slots[j - 1], (at.r, at.s))


def chain_run(at, copies, held, unit=TP):
    def block(r, q):
        return held.at[pl.ds((r * at.Q + q) * unit, unit)]

    right = [copies.slot() for _ in range(at.Q - 1)]
    left = [copies.slot() for _ in range(at.Q - 1)]
    across = [[copies.slot() for _ in range(at.Q)] for _ in range(at.R - 1)]

    def cross(q, index, cond):
        for j in range(1, at.R):
            other = lax.rem(at.r + j, at.R)
            copies.push(block(at.r, q), block(at.r, q), across[j - 1][index], (other, at.s), cond)

    copies.push(
        block(at.r, at.q), block(at.r, at.q), right[0], (at.r, at.s + TP), at.q < at.Q - 1
    )
    copies.push(block(at.r, at.q), block(at.r, at.q), left[0], (at.r, at.s - TP), at.q > 0)
    cross(at.q, 0, None)
    index = 0
    spots = {}
    for hop in range(1, at.Q):
        yield "go"
        from_left, from_right = at.q >= hop, at.q + hop < at.Q
        copies.arrived(block(at.r, at.q - hop), right[hop - 1], (at.r, at.s), from_left)
        if hop < at.Q - 1:
            copies.push(
                block(at.r, at.q - hop),
                block(at.r, at.q - hop),
                right[hop],
                (at.r, at.s + TP),
                from_left & (at.q < at.Q - 1),
            )
        copies.arrived(block(at.r, at.q + hop), left[hop - 1], (at.r, at.s), from_right)
        if hop < at.Q - 1:
            copies.push(
                block(at.r, at.q + hop),
                block(at.r, at.q + hop),
                left[hop],
                (at.r, at.s - TP),
                from_right & (at.q > 0),
            )
        for side, sign in ((from_left, -1), (from_right, 1)):
            spots[(hop, sign)] = [copies.slot() for _ in range(at.R - 1)]
            for j in range(1, at.R):
                other = lax.rem(at.r + j, at.R)
                piece = block(at.r, at.q + sign * hop)
                copies.push(piece, piece, spots[(hop, sign)][j - 1], (other, at.s), side)
    yield "go"
    for j in range(1, at.R):
        source = lax.rem(at.r + at.R - j, at.R)
        copies.arrived(block(source, at.q), across[j - 1][0], (at.r, at.s))
        for hop in range(1, at.Q):
            for sign in (-1, 1):
                there = at.q + sign * hop
                copies.arrived(
                    block(source, there),
                    spots[(hop, sign)][j - 1],
                    (at.r, at.s),
                    at.q >= hop if sign < 0 else there < at.Q,
                )


def spread(source):
    def run(at, copies, ins, outs):
        yield from spread_run(at, copies, ins[0], outs[0], 0)

    outs = [like(source.shape, source.dtype)]
    return Job([source], outs, run, {"plane"}, vmem=(0,), late=True)


def spread_all(place, source):
    def run(at, copies, ins, outs):
        yield from spread_run(at, copies, ins[0], outs[0], (at.r * at.Q + at.q) * TP)
        yield from chain_run(at, copies, outs[0])

    outs = [like((place.R * place.S,) + source.shape[1:], source.dtype)]
    return Job([source], outs, run, {"plane", "chain", "core"}, vmem=(0,), relay=True)


def home_all(place, source):
    def run(at, copies, ins, outs):
        r, s, slot, here = home_of(at)
        _, _, own = visitor_of(at)
        index = copies.slot()
        copies.push(ins[0], outs[0].at[slot], index, (r, s), here == 0)
        copy = pltpu.make_async_copy(ins[0], outs[0].at[slot], copies.recv.at[copies.slot()])
        when(here == 1, copy.start)
        yield "go"
        when(here == 1, copy.wait)
        copies.arrived(outs[0].at[at.r * at.Q + at.q], index, (at.r, at.s), own == 0)
        yield from chain_run(at, copies, outs[0], 1)

    outs = [like((place.R * place.Q,) + source.shape, source.dtype)]
    return Job([source], outs, run, {"home", "chain", "core"}, vmem=(0,), relay=True)


FACTOR = 1.0 / math.sqrt(HD)


def masked_keys(kv_ref, first, kv_s):
    index = lax.broadcasted_iota(jnp.int32, kv_ref.shape, 0)
    kv_s[...] = jnp.where(index >= first, kv_ref[...].astype(F32), 0.0).astype(BF)


def attend_forward(q, kv, q_seg, key_seg, first, block):
    N, QS = q.shape
    M, KS = kv.shape[0], kv.shape[1] // 2
    ahead = M - N
    span = ahead + block
    kv_heads = KS // HD
    groups = QS // KS

    def body(first_ref, q_ref, kv_ref, qs_ref, ks_ref, o_ref, kv_s):
        masked_keys(kv_ref, first_ref[0], kv_s)

        @pl.loop(0, N // block)
        def _(i):
            start = pl.multiple_of(i * block, block)
            here, keys = pl.ds(start, block), pl.ds(start, span)
            row = lax.broadcasted_iota(jnp.int32, (block, span), 0) + ahead
            col = lax.broadcasted_iota(jnp.int32, (block, span), 1)
            open_ = (qs_ref[here, :1] == ks_ref[:1, keys]) & (col <= row)
            open_ = open_ & (col + start >= first_ref[0])
            open_ = jnp.concatenate([open_] * groups, axis=0)
            queries = q_ref[here, :]
            done = []
            for k in range(kv_heads):
                mine = [
                    queries[:, (k * groups + g) * HD : (k * groups + g + 1) * HD]
                    for g in range(groups)
                ]
                key = kv_s[keys, k * HD : (k + 1) * HD]
                value = kv_s[keys, KS + k * HD : KS + (k + 1) * HD]
                score = jnp.where(open_, dot_nt(jnp.concatenate(mine, axis=0), key) * FACTOR, MASKED)
                weight = jnp.exp(score - jnp.max(score, axis=-1, keepdims=True))
                weight = weight / jnp.sum(weight, axis=-1, keepdims=True)
                out = dot(weight.astype(BF), value).astype(BF)
                done.extend(out[g * block : (g + 1) * block] for g in range(groups))
            o_ref[here, :] = jnp.concatenate(done, axis=1)

    return attend_call(
        body, like((N, QS)), [pltpu.VMEM(kv.shape, BF)], 4 * N * span * QS, first, q, kv, q_seg, key_seg
    )


def attend_call(body, outs, scratch, flops, first, *arrays):
    return pl.pallas_call(
        body,
        out_shape=outs,
        in_specs=[pl.BlockSpec(memory_space=pltpu.SMEM)]
        + [pl.BlockSpec(memory_space=pltpu.VMEM) for _ in arrays],
        out_specs=jax.tree.map(lambda _: pl.BlockSpec(memory_space=pltpu.VMEM), outs),
        scratch_shapes=scratch,
        cost_estimate=pl.CostEstimate(flops=flops, bytes_accessed=COST, transcendentals=0),
    )(first, *arrays)


def attend_backward(q, kv, d_o, q_seg, key_seg, first, block):
    N, QS = q.shape
    M, KS = kv.shape[0], kv.shape[1] // 2
    ahead = M - N
    span = ahead + block
    kv_heads = KS // HD
    groups = QS // KS

    def body(first_ref, q_ref, kv_ref, do_ref, qs_ref, ks_ref, dq_ref, dkv_ref, kv_s, *sums):
        masked_keys(kv_ref, first_ref[0], kv_s)
        for total in sums:
            total[...] = jnp.zeros_like(total)

        @pl.loop(0, N // block)
        def _(i):
            start = pl.multiple_of(i * block, block)
            here, keys = pl.ds(start, block), pl.ds(start, span)
            row = lax.broadcasted_iota(jnp.int32, (span, block), 0)
            col = lax.broadcasted_iota(jnp.int32, (span, block), 1) + ahead
            open_ = (ks_ref[keys, :1] == qs_ref[:1, here]) & (row <= col)
            open_ = open_ & (row + start >= first_ref[0])
            open_ = jnp.concatenate([open_] * groups, axis=1)
            queries, pulls = q_ref[here, :], do_ref[here, :]

            def heads_of(values, k):
                return jnp.concatenate(
                    [
                        values[:, (k * groups + g) * HD : (k * groups + g + 1) * HD]
                        for g in range(groups)
                    ],
                    axis=0,
                )

            done = []
            for k in range(kv_heads):
                mine, pull = heads_of(queries, k), heads_of(pulls, k)
                key = kv_s[keys, k * HD : (k + 1) * HD]
                value = kv_s[keys, KS + k * HD : KS + (k + 1) * HD]
                score = jnp.where(open_, dot_nt(key, mine) * FACTOR, MASKED)
                weight = jnp.exp(score - jnp.max(score, axis=0, keepdims=True))
                weight = weight / jnp.sum(weight, axis=0, keepdims=True)
                d_weight = dot_nt(value, pull)
                delta = jnp.sum(weight * d_weight, axis=0, keepdims=True)
                d_score = (weight * (d_weight - delta)).astype(BF)
                sums[k][keys, :] += dot(d_score, mine) * FACTOR
                sums[kv_heads + k][keys, :] += dot(weight.astype(BF), pull)
                dq = dot_tn(d_score, key) * FACTOR
                done.extend(dq[g * block : (g + 1) * block] for g in range(groups))
            dq_ref[here, :] = jnp.concatenate(done, axis=1)

        dkv_ref[...] = jnp.concatenate([total[...] for total in sums], axis=1)

    return attend_call(
        body,
        (like((N, QS), F32), like((M, 2 * KS), F32)),
        [pltpu.VMEM(kv.shape, BF)] + [pltpu.VMEM((M, HD), F32) for _ in range(2 * kv_heads)],
        10 * N * span * QS,
        first,
        q,
        kv,
        d_o,
        q_seg,
        key_seg,
    )


class Plane:
    def __init__(self, at, copies):
        self.at, self.copies = at, copies

    def swap(self, send, recv):
        at, slots = self.at, [self.copies.slot() for _ in range(TP - 1)]
        for j in range(1, TP):
            other = lax.rem(at.p + j, TP)
            there = (at.r, at.q * TP + other)
            self.copies.push(send.at[other], recv.at[at.p], slots[j - 1], there)
        return functools.partial(self.arrive, recv, slots)

    def gather(self, held):
        at, slots = self.at, [self.copies.slot() for _ in range(TP - 1)]
        for j in range(1, TP):
            there = (at.r, at.q * TP + lax.rem(at.p + j, TP))
            self.copies.push(held.at[at.p], held.at[at.p], slots[j - 1], there)
        return functools.partial(self.arrive, held, slots)

    def arrive(self, held, slots):
        at = self.at
        for j in range(1, TP):
            origin = lax.rem(at.p + TP - j, TP)
            self.copies.arrived(held.at[origin], slots[j - 1], (at.r, at.s))

    def settle(self, own, recv, n):
        total = own[pl.ds(pl.multiple_of(self.at.p * n, n), n), :]
        for j in range(1, TP):
            total = total + recv[lax.rem(self.at.p + j, TP)].astype(F32)
        return total


def columns_of(count, width, action):
    @pl.loop(0, count)
    def _(c):
        action(pl.ds(pl.multiple_of(c * width, width), width))


def activate(gu, act, N, FS):
    @pl.loop(0, N // 64)
    def _(i):
        rows = pl.ds(pl.multiple_of(i * 64, 64), 64)
        gate, up = gu[rows, :FS], gu[rows, FS:]
        act[rows, :] = (jax.nn.silu(gate) * up).astype(BF)


def deactivate(gu, d_act, dgu, N, FS):
    @pl.loop(0, N // 64)
    def _(i):
        rows = pl.ds(pl.multiple_of(i * 64, 64), 64)
        gate, up, pull = gu[rows, :FS], gu[rows, FS:], d_act[rows, :]
        sigma = jax.nn.sigmoid(gate)
        dgu[rows, :FS] = (pull * up * sigma * (1.0 + gate * (1.0 - sigma))).astype(BF)
        dgu[rows, FS:] = (pull * (gate * sigma)).astype(BF)


def feed_up(held, weights, gu, N, D, FS):
    values = held[...].reshape(N, D)

    def go(cols):
        gu[:, cols] = dot(values, weights[:, cols])

    columns_of(3, 2 * FS // 3, go)


def project(left, weights, first, width, part, send, n):
    step = 256

    def go(cols):
        out = dot_nt(left[...], weights[cols, first : first + width])
        part[:, cols] = out
        send[:, :, cols] = out.reshape(TP, n, step).astype(BF)

    columns_of(weights.shape[0] // step, step, go)


def feed_kernel(place, ident, mode, arrays, D, FS, n, side=0):
    N = n * TP
    R = place.R
    half = D // R
    W = 3 * FS
    forward, backward = mode in ("fwd", "both"), mode in ("both", "bwd")
    VM, HB = pltpu.VMEM, pl.ANY
    ins, scratch, outs = {}, {}, {}
    ins["weights"] = HB
    if mode == "fwd":
        ins.update(a_g=VM, h_in=VM, gain_next=VM)
        outs.update(
            h_out=((n, D), F32, VM), next_g=((TP, n, D), BF, VM), gu_out=((N, 2 * FS), F32, HB)
        )
    else:
        ins.update(first_part=VM, h_in=VM, gain=VM)
        outs.update(
            g_out=((n, D), F32, VM),
            next_g=((TP, n, D), BF, VM),
            d_gain=((1, D), F32, VM),
            half_out=((half, W), BF, VM),
        )
        scratch.update(
            first_send=((TP, n, D), BF),
            first_got=((TP, n, D), BF),
            a_v=((TP, n, D), BF),
            e_v=((TP, n, D), BF),
            d_act=((N, FS), F32),
            dgu=((N, 2 * FS), BF),
            grad_send=((R - 1, half, W), BF),
            grad_got=((R - 1, half, W), BF),
        )
    if mode == "both":
        ins.update(e_g=HB, e_own=VM)
        outs.update(mid_out=((n, D), F32, VM), o_send=((TP, n, D), BF, VM), o_base=((n, D), F32, VM))
    if mode == "bwd":
        ins.update(a_g=HB, gu_in=HB, g_in=VM, h_before=VM, gain_before=VM)
        piece = (half // place.Q, side)
        ins.update(side_in=VM)
        outs.update(
            d_gain_before=((1, D), F32, VM),
            halo=((HALO, D), BF, VM),
            side_out=((place.Q,) + piece, BF, VM),
        )
        scratch.update(side_got=((R - 1, half, side), BF), side_half=((place.Q,) + piece, BF))
    scratch.update(
        w=((D, W), BF),
        gu=((N, 2 * FS), F32),
        act=((N, FS), BF),
        part=((N, D), F32),
        send=((TP, n, D), BF),
        got=((TP, n, D), BF),
    )
    in_names, out_names, scratch_names = list(ins), list(outs), list(scratch)
    kinds = {"plane"}
    if backward:
        kinds.add("core")
    if mode == "bwd":
        kinds.update({"back", "zall"})
    sems = 32 + 2 * R + place.Q

    def body(*refs):
        names = in_names + out_names + scratch_names
        v = dict(zip(names, refs))
        at = place.here()
        copies = Copies(refs[len(names)], refs[len(names) + 1])
        plane = Plane(at, copies)
        loads = refs[len(names) + 2]
        pending = {}

        def load(name, src, dst):
            pending[name] = pltpu.make_async_copy(src, dst, loads.at[len(pending)])
            pending[name].start()

        load("w", v["weights"], v["w"])
        if mode == "both":
            load("e", v["e_g"], v["e_v"])
        if mode == "bwd":
            load("a", v["a_g"], v["a_v"])
            load("gu", v["gu_in"], v["gu"])
        meet(at, kinds)
        w, gu, act, part, send, got = (v[k] for k in ("w", "gu", "act", "part", "send", "got"))

        if mode != "fwd":
            first = v["first_part"]
            v["first_send"][...] = first[...].reshape(TP, n, D).astype(BF)
            wait = plane.swap(v["first_send"], v["first_got"])
        if mode == "fwd":
            pending["w"].wait()
            feed_up(v["a_g"], w, gu, N, D, FS)
            save = pltpu.make_async_copy(gu, v["gu_out"], loads.at[len(pending)])
            save.start()
            activate(gu, act, N, FS)
            project(act, w, 2 * FS, FS, part, send, n)
            wait = plane.swap(send, got)
            wait()
            h_out = v["h_in"][...] + plane.settle(part, got, n)
            v["h_out"][...] = h_out
            v["next_g"][at.p] = (h_out * inverse_rms(h_out) * v["gain_next"][...]).astype(BF)
            wait = plane.gather(v["next_g"])
            wait()
            save.wait()
            copies.drain()
            return
        if mode == "both":
            wait()
            h = v["h_in"][...] + plane.settle(first, v["first_got"], n)
            v["mid_out"][...] = h
            v["a_v"][at.p] = (h * inverse_rms(h) * v["gain"][...]).astype(BF)
            wait = plane.gather(v["a_v"])
            pending["w"].wait()
            pending["e"].wait()
        else:
            side_slots = [copies.slot() for _ in range(R - 1)]
            for j in range(1, R):
                other = lax.rem(at.r + j, R)
                copies.push(
                    v["side_in"].at[other], v["side_got"].at[j - 1], side_slots[j - 1], (other, at.s)
                )
            wait()
            h = v["h_in"][...]
            before = v["h_before"][...]
            r_before = inverse_rms(before)
            d_normed = plane.settle(first, v["first_got"], n)
            v["d_gain_before"][...] = jnp.sum(d_normed * before * r_before, axis=0, keepdims=True)
            g_mid = v["g_in"][...] + rms_pull(d_normed, before, r_before, v["gain_before"][...])
            v["g_out"][...] = g_mid
            v["e_v"][at.p] = g_mid.astype(BF)
            wait = plane.gather(v["e_v"])
            pending["gu"].wait()
            activate(gu, act, N, FS)
            pending["w"].wait()
            pending["a"].wait()
        if mode == "both":
            pull_in(v["e_v"], w, v["d_act"], N, D, FS)
            wait()
            feed_up(v["a_v"], w, gu, N, D, FS)
            activate(gu, act, N, FS)
        else:
            total = v["side_in"][at.r].astype(F32)
            for j in range(1, R):
                copies.arrived(v["side_got"].at[j - 1], side_slots[j - 1], (at.r, at.s))
                total = total + v["side_got"][j - 1].astype(F32)
            v["side_half"][...] = total.astype(BF).reshape(v["side_half"].shape)
            line_slots = [copies.slot() for _ in range(at.Q - 1)]
            for j in range(1, at.Q):
                other = lax.rem(at.q + j, at.Q)
                copies.push(
                    v["side_half"].at[other],
                    v["side_out"].at[at.q],
                    line_slots[j - 1],
                    (at.r, other * TP + at.p),
                )
            v["side_out"][at.q] = v["side_half"][at.q]
            wait()
            pull_in(v["e_v"], w, v["d_act"], N, D, FS)
        deactivate(gu, v["d_act"], v["dgu"], N, FS)
        project(v["dgu"], w, 0, 2 * FS, part, send, n)
        wait = plane.swap(send, got)
        values, pulls = v["a_v"], v["e_v"]

        def grads(j):
            first_col = lax.rem(at.r + j, R) * half
            cols = pl.ds(pl.multiple_of(first_col, 128), half)
            left = values[:, :, cols].reshape(N, half).astype(F32).T.astype(BF)
            right = pulls[:, :, cols].reshape(N, half).astype(F32).T.astype(BF)
            return left, right

        slots = [copies.slot() for _ in range(R - 1)]
        for j in range(1, R):
            left, right = grads(j)

            def put(cols, left=left, j=j):
                v["grad_send"][j - 1, :, cols] = dot(left, v["dgu"][:, cols]).astype(BF)

            columns_of(3, 2 * FS // 3, put)
            v["grad_send"][j - 1, :, 2 * FS :] = dot(right, act[...]).astype(BF)
            other = lax.rem(at.r + j, R)
            copies.push(
                v["grad_send"].at[j - 1], v["grad_got"].at[j - 1], slots[j - 1], (other, at.s)
            )
        wait()
        if mode == "both":
            d_normed = plane.settle(part, got, n)
            r = inverse_rms(h)
            base = v["e_own"][...].astype(F32)
        else:
            d_normed = plane.settle(part, got, n)
            r = inverse_rms(h)
            base = v["g_out"][...]
        v["d_gain"][...] = jnp.sum(d_normed * h * r, axis=0, keepdims=True)
        g_new = base + rms_pull(d_normed, h, r, v["gain"][...])
        v["g_out"][...] = g_new
        v["next_g"][at.p] = g_new.astype(BF)
        wait = plane.gather(v["next_g"])
        if mode == "bwd":
            back = [copies.slot() for _ in range(TP)]
            for j in range(TP):
                copies.push(
                    v["next_g"].at[at.p, pl.ds(0, HALO)],
                    v["halo"],
                    back[j],
                    (at.r, (at.q - 1) * TP + j),
                    (at.p == 0) & (at.q > 0),
                    back[0],
                )
        if mode == "both":
            project(act, w, 2 * FS, FS, part, v["o_send"], n)
            v["o_base"][...] = h + part[pl.ds(pl.multiple_of(at.p * n, n), n), :]
        left, right = grads(0)
        for j in range(1, R):
            copies.arrived(v["grad_got"].at[j - 1], slots[j - 1], (at.r, at.s))

        def finish(cols):
            total = dot(left, v["dgu"][:, cols])
            for j in range(1, R):
                total = total + v["grad_got"][j - 1, :, cols].astype(F32)
            v["half_out"][:, cols] = total.astype(BF)

        columns_of(3, 2 * FS // 3, finish)
        total = dot(right, act[...])
        for j in range(1, R):
            total = total + v["grad_got"][j - 1, :, 2 * FS :].astype(F32)
        v["half_out"][:, 2 * FS :] = total.astype(BF)
        wait()
        if mode == "bwd":
            copies.arrived(v["halo"], back[0], (at.r, at.s), at.q < at.Q - 1)
            for j in range(1, at.Q):
                origin = lax.rem(at.q + at.Q - j, at.Q)
                copies.arrived(v["side_out"].at[origin], line_slots[j - 1], (at.r, at.s))
        copies.drain()

    results = pl.pallas_call(
        body,
        out_shape=tuple(like(outs[k][0], outs[k][1]) for k in out_names),
        in_specs=[pl.BlockSpec(memory_space=ins[k]) for k in in_names],
        out_specs=tuple(pl.BlockSpec(memory_space=outs[k][2]) for k in out_names),
        scratch_shapes=[pltpu.VMEM(*scratch[k]) for k in scratch_names]
        + [pltpu.SemaphoreType.DMA((sems,)), pltpu.SemaphoreType.DMA((sems,))]
        + [pltpu.SemaphoreType.DMA((4,))],
        compiler_params=pltpu.CompilerParams(collective_id=ident, has_side_effects=True),
        cost_estimate=pl.CostEstimate(flops=0, bytes_accessed=COST, transcendentals=0),
        name="feed_%s" % mode,
    )(*[arrays[k] for k in in_names])
    return dict(zip(out_names, results))


def pull_in(pulls, weights, d_act, N, D, FS):
    values = pulls[...].reshape(N, D)

    def go(cols):
        d_act[:, cols] = dot(values, weights[:, pl.ds(pl.multiple_of(2 * FS + cols.start, 128), cols.size)])

    columns_of(3, FS // 3, go)


def doc_info(positions, lengths):
    doc_ends = jnp.cumsum(lengths, dtype=jnp.int32)
    passed = positions[:, None] >= doc_ends[None, :]
    segment = jnp.sum(passed.astype(jnp.int32), axis=1, dtype=jnp.int32)
    opening = jnp.sum(jnp.where(passed, lengths[None, :], 0), axis=1, dtype=jnp.int32)
    return (segment, positions - opening)


def inverse_rms(values):
    return lax.rsqrt(jnp.mean(values * values, axis=-1, keepdims=True) + EPSILON)


def rms_pull(upstream, values, inverse, norm_gain):
    scaled = upstream * norm_gain
    product_mean = jnp.mean(scaled * values, axis=-1, keepdims=True)
    return inverse * scaled - values * (inverse * inverse * inverse) * product_mean


def rope_tables(relative):
    half_size = HD // 2
    frequency = jnp.exp(
        jnp.arange(half_size, dtype=F32) * (-2.0 * math.log(THETA) / HD)
    )
    angles = relative.astype(F32)[:, None] * frequency[None, :]
    return (jnp.cos(angles)[:, None, :], jnp.sin(angles)[:, None, :])


def rope_apply(values, cosine, sine):
    front, back = values[..., : HD // 2], values[..., HD // 2 :]
    return jnp.concatenate([front * cosine - back * sine, back * cosine + front * sine], axis=-1)


def rope_revert(values, cosine, sine):
    front, back = values[..., : HD // 2], values[..., HD // 2 :]
    return jnp.concatenate([front * cosine + back * sine, back * cosine - front * sine], axis=-1)


def settle(own, arrived, p):
    index = jnp.arange(TP, dtype=jnp.int32)[:, None, None]
    others = jnp.where(index == p, 0.0, arrived.astype(F32))
    mine = lax.dynamic_index_in_dim(own, p, 0, keepdims=False)
    return mine + jnp.sum(others, axis=0)


def per_device(
    place,
    tokens,
    doc_lengths,
    cotangent,
    gain_conv,
    w_in,
    kernel,
    w_mix,
    gain_ffa,
    gate_a,
    up_a,
    down_a,
    gain_att,
    w_query,
    w_key,
    w_value,
    head_gains,
    w_attout,
    gain_ffb,
    gate_b,
    up_b,
    down_b,
):
    R, S, Q = place.R, place.S, place.Q
    n, D = tokens.shape[1], tokens.shape[2]
    shard = w_in.shape[0]
    FS = gate_a.shape[1] // TP
    CS = D // TP
    QS, KS = H * HD // TP, KVH * HD // TP
    taps = kernel.shape[0]
    N = n * TP
    r, s = lax.axis_index("rows"), lax.axis_index("seq")
    q, p = s // TP, lax.rem(s, TP)
    lengths = doc_lengths[0]

    def slices(weight):
        return weight.reshape(shard, TP, -1).transpose(1, 0, 2)

    def joined(*weights):
        return jnp.concatenate([slices(weight) for weight in weights], axis=2)

    columns = [[a * S + b * TP + c for a in range(R) for b in range(Q)] for c in range(TP)]
    lines = [[b * TP + c for b in range(Q)] for c in range(TP)]

    def gather_rest(plane):
        flat = plane.reshape(TP * shard, -1)
        return lax.all_gather(
            flat, ("rows", "seq"), axis=0, tiled=True, axis_index_groups=columns
        )

    def by_row(grads):
        return grads.astype(BF).reshape(R, S * shard, -1)

    def own_rows(rows, came, *later):
        return lax.optimization_barrier((collect(rows, came, r).astype(BF),) + later)

    def reduce_line(half):
        part = lax.psum_scatter(
            half, "seq", scatter_dimension=0, tiled=True, axis_index_groups=lines
        )
        return part.reshape(TP, shard, part.shape[1])

    in_cut = w_in.reshape(shard, 3, TP, CS).transpose(2, 0, 1, 3).reshape(TP, shard, 3 * CS)
    small = jnp.stack([gain_conv, gain_ffa, gain_att, gain_ffb] + [kernel[i] for i in range(taps)])
    small = jnp.pad(small, ((0, 16 - 4 - taps), (0, 128 - shard)))
    small = jnp.broadcast_to(small[None], (TP, 16, 128))

    per_slice = R * Q
    homes = []
    for d in range(R * S):
        k = d % per_slice
        homes.append((d, (k // Q) * S + (k % Q) * TP + d // per_slice))
    mine = tokens[0]
    (tok_g,), (halo_a, halo_b), (in_g,), (mix_g,), (small_g,), (ffa_p,) = exchange(
        place,
        0,
        [
            gather_plane(mine),
            halo_tokens(mine),
            spread_all(place, in_cut),
            home_all(place, w_mix),
            spread_all(place, small),
            spread(joined(gate_a, up_a, down_a.T)),
        ],
    )
    wa = gather_rest(ffa_p)
    w_mix_s = mix_g.reshape(CS, D)
    vectors = small_g[:, : 4 + taps, :shard].transpose(1, 0, 2).reshape(4 + taps, D).astype(F32)
    g_conv, g_ffa, g_att, g_ffb = (vectors[i] for i in range(4))
    kernel_f = lax.dynamic_slice_in_dim(vectors[4:], p * CS, CS, 1)
    w_in_s = in_g.reshape(D, 3 * CS)

    def own(parts, index):
        return lax.dynamic_index_in_dim(parts, index, 0, keepdims=False).astype(F32)

    def collect(parts, came, index):
        slot = jnp.arange(came.shape[0], dtype=jnp.int32).reshape((-1,) + (1,) * (came.ndim - 1))
        mine_part = lax.dynamic_index_in_dim(parts, index, 0, keepdims=True).astype(F32)
        return jnp.sum(jnp.where(slot == index, mine_part, came.astype(F32)), axis=0)

    def after_core(parts, came):
        summed = collect(parts, came, r)
        return summed.reshape((Q, TP) + summed.shape[1:])

    def after_line(parts, came):
        return collect(parts, came, q)

    def after_plane(full, came):
        slot = jnp.arange(TP, dtype=jnp.int32).reshape((TP,) + (1,) * (full.ndim - 1))
        mine_part = lax.dynamic_index_in_dim(full, p, 0, keepdims=True)
        return jnp.where(slot == p, mine_part, came.astype(F32))

    total = S * n
    pos_ext = q * N - HALO + jnp.arange(N + 2 * HALO, dtype=jnp.int32)
    seg_ext, rel_ext = doc_info(pos_ext, lengths)
    valid = ((pos_ext >= 0) & (pos_ext < total))[:, None]
    x_ext = jnp.concatenate([halo_a, tok_g.reshape(N, D), halo_b], axis=0)
    x_ext = jnp.where(valid, x_ext, jnp.zeros_like(x_ext)).astype(F32)
    r0_ext = inverse_rms(x_ext)
    n1_ext = (x_ext * r0_ext * g_conv).astype(BF)
    z_ext = dot(n1_ext, w_in_s)
    b_ext, c_ext, v_ext = z_ext[:, :CS], z_ext[:, CS : 2 * CS], z_ext[:, 2 * CS :]
    u_ext = lax.optimization_barrier((b_ext * v_ext).astype(BF)).astype(F32)
    span = slice(HALO, HALO + N)
    same = [
        (seg_ext[HALO - 2 + k : HALO - 2 + k + N] == seg_ext[span]).astype(F32)[:, None]
        for k in range(taps)
    ]
    near = [u_ext[HALO - 2 + k : HALO - 2 + k + N] for k in range(taps)]
    conv = kernel_f[0] * near[0] * same[0]
    for k in range(1, taps):
        conv = conv + kernel_f[k] * near[k] * same[k]
    m_bf = (c_ext[span] * conv).astype(BF)
    part = dot(m_bf, w_mix_s).reshape(TP, n, D)
    (got,), (att_p,), (ffb_p,) = exchange(
        place,
        1,
        [
            swap_plane(part.astype(BF)),
            spread(joined(w_query, w_key, w_value, w_attout.T)),
            spread(joined(gate_b, up_b, down_b.T)),
        ],
    )
    w_att = gather_rest(att_p)
    wb = gather_rest(ffb_p)
    x0 = mine.astype(F32)
    h1 = x0 + settle(part, got, p)

    r1 = inverse_rms(h1)
    a1 = (h1 * r1 * g_ffa).astype(BF)
    ((a1_g,),) = exchange(place, 2, [gather_plane(a1)])
    a1_g = a1_g.reshape(N, D)

    g_row = {name: value[None] for name, value in
             (("ffa", g_ffa), ("att", g_att), ("ffb", g_ffb))}
    fed = feed_kernel(
        place,
        3,
        "fwd",
        {"weights": wa, "a_g": a1_g.reshape(TP, n, D), "h_in": h1, "gain_next": g_row["att"]},
        D,
        FS,
        n,
    )
    h2, n3_g, gu1 = fed["h_out"], fed["next_g"], fed["gu_out"]

    n3_g = n3_g.reshape(N, D)
    w_qkv, w_out = w_att[:, : QS + 2 * KS], w_att[:, QS + 2 * KS :]
    qkv = dot(n3_g, w_qkv)
    heads, kv_heads = QS // HD, KS // HD
    groups = heads // kv_heads
    q_pre = qkv[:, :QS].reshape(N, heads, HD)
    k_pre = qkv[:, QS : QS + KS].reshape(N, kv_heads, HD)
    head_f = head_gains.astype(F32)
    cosine, sine = rope_tables(rel_ext[span])
    q_inv, k_inv = inverse_rms(q_pre), inverse_rms(k_pre)
    q_bf = rope_apply(q_pre * q_inv * head_f[0], cosine, sine).astype(BF)
    k_bf = rope_apply(k_pre * k_inv * head_f[1], cosine, sine).astype(BF).reshape(N, KS)
    v_bf = qkv[:, QS + KS :].astype(BF)
    e_bf = cotangent[0]
    (kv_w,), (e_g,) = exchange(
        place,
        5,
        [window_forward(place, jnp.concatenate([k_bf, v_bf], axis=1)), gather_plane(e_bf)],
    )
    reach = Q // 2 + 1
    kv_all = kv_w.reshape(reach * N, 2 * KS)
    q_seg = seg_ext[span]
    key_seg, _ = doc_info((q - reach + 1) * N + jnp.arange(reach * N, dtype=jnp.int32), lengths)
    first = jnp.maximum((reach - 1 - q) * N, 0).astype(jnp.int32).reshape(1)
    q_bf = q_bf.reshape(N, QS)
    seg_col, seg_row = (jnp.broadcast_to(q_seg[:, None], (N, 128)), jnp.broadcast_to(q_seg, (8, N)))
    key_col = jnp.broadcast_to(key_seg[:, None], (reach * N, 128))
    key_row = jnp.broadcast_to(key_seg, (8, reach * N))
    o_bf = attend_forward(q_bf, kv_all, seg_col, key_row, first, 128)
    fed = feed_kernel(
        place,
        8,
        "both",
        {
            "weights": wb,
            "first_part": dot_nt(o_bf, w_out),
            "h_in": h2,
            "gain": g_row["ffb"],
            "e_g": e_g.reshape(TP, n, D),
            "e_own": e_bf,
        },
        D,
        FS,
        n,
    )
    h3, g3, g3_g, half_b = fed["mid_out"], fed["g_out"], fed["next_g"], fed["half_out"]
    d_gain = {}
    d_gain["ffb"] = fed["d_gain"][0]

    g3_g = g3_g.reshape(N, D)
    d_out = dot_tn(g3_g, o_bf)
    d_o = dot(g3_g, w_out).astype(BF)
    d_q, d_kv = attend_backward(q_bf, kv_all, d_o, seg_row, key_col, first, 128)
    d_kv = d_kv.reshape(reach, N, 2 * KS)
    (got_kv,), (got_o,) = exchange(
        place, 10, [window_backward(place, d_kv.astype(BF)), swap_plane(fed["o_send"])]
    )
    index = jnp.arange(TP, dtype=jnp.int32)[:, None, None]
    h4 = fed["o_base"] + jnp.sum(jnp.where(index == p, 0.0, got_o.astype(F32)), axis=0)
    mixed = h4.astype(BF)[None]
    there = (q + 1 + jnp.arange(reach - 1, dtype=jnp.int32) < Q)[:, None, None]
    d_kv = d_kv[-1] + jnp.sum(jnp.where(there, got_kv.astype(F32), 0.0), axis=0)
    half_b, d_kv = lax.optimization_barrier((half_b, d_kv))
    full_b = reduce_line(half_b)
    dv_bf = d_kv[:, KS:].astype(BF)
    dk_norm = rope_revert(d_kv[:, :KS].reshape(N, kv_heads, HD), cosine, sine)
    dq_norm = rope_revert(d_q.reshape(N, heads, HD), cosine, sine)
    dk_pre = rms_pull(dk_norm, k_pre, k_inv, head_f[1]).reshape(N, KS)
    dq_pre = rms_pull(dq_norm, q_pre, q_inv, head_f[0]).reshape(N, QS)
    d_heads = jnp.stack(
        [
            jnp.sum(dq_norm * q_pre * q_inv, axis=(0, 1)),
            jnp.sum(dk_norm * k_pre * k_inv, axis=(0, 1)),
        ]
    )
    d_qkv = jnp.concatenate([dq_pre.astype(BF), dk_pre.astype(BF), dv_bf], axis=1)
    rows_att = by_row(
        jnp.concatenate([dot_tn(n3_g, d_qkv).astype(BF), d_out.astype(BF)], axis=1)
    )
    fed = feed_kernel(
        place,
        13,
        "bwd",
        {
            "weights": wa,
            "first_part": dot_nt(d_qkv, w_qkv),
            "h_in": h1,
            "gain": g_row["ffa"],
            "a_g": a1_g.reshape(TP, n, D),
            "gu_in": gu1,
            "g_in": g3,
            "h_before": h2,
            "gain_before": g_row["att"],
            "side_in": rows_att,
        },
        D,
        FS,
        n,
        rows_att.shape[2],
    )
    full_att = jnp.sum(fed["side_out"].astype(F32), axis=0).astype(BF).reshape(TP, shard, -1)
    g1, g1_g, g1_halo = fed["g_out"], fed["next_g"], fed["halo"]
    d_gain["att"], d_gain["ffa"] = fed["d_gain_before"][0], fed["d_gain"][0]
    full_a = reduce_line(fed["half_out"])

    g1_halo = jnp.where(q < Q - 1, g1_halo, jnp.zeros_like(g1_halo))
    g1_ext = jnp.concatenate([g1_g.reshape(N, D), g1_halo], axis=0)
    d_m = dot_nt(g1_ext, w_mix_s)
    d_mix_s = dot_tn(m_bf, g1_ext[:N])
    d_c = d_m[:N] * conv
    d_conv = lax.optimization_barrier((d_m * c_ext[HALO:]).astype(BF)).astype(F32)
    d_kernel = jnp.stack(
        [jnp.sum(d_conv[:N] * near[k] * same[k], axis=0) for k in range(taps)]
    )
    d_u = jnp.zeros((N, CS), F32)
    for k in range(taps):
        ahead = taps - 1 - k
        match = (seg_ext[HALO + ahead : HALO + ahead + N] == seg_ext[span]).astype(F32)[:, None]
        d_u = d_u + kernel_f[k] * d_conv[ahead : ahead + N] * match
    d_z = jnp.concatenate([d_u * v_ext[span], d_c, d_u * b_ext[span]], axis=1).astype(BF)
    rows_in = dot_tn(n1_ext[span], d_z).astype(BF).reshape(R, S, shard, 3 * CS)
    rows_mix = d_mix_s.astype(BF).reshape(R, Q, shard, D)
    d_n1 = dot_nt(d_z, w_in_s)
    d_gain["conv"] = jnp.sum(d_n1 * x_ext[span] * r0_ext[span], axis=0)
    part = d_n1.reshape(TP, n, D)
    d_taps = lax.dynamic_update_slice(jnp.zeros((taps, D), F32), d_kernel, (0, p * CS))
    lanes = jnp.concatenate(
        [jnp.stack([d_gain["conv"], d_gain["ffa"], d_gain["att"], d_gain["ffb"]]), d_taps]
    )
    lanes = lanes.reshape(4 + taps, R * S, shard).transpose(1, 0, 2)
    lanes = jnp.pad(lanes, ((0, 0), (0, 0), (0, 128 - shard)))
    heads_row = jnp.broadcast_to(d_heads.reshape(1, 1, 2 * HD), (R * S, 1, 2 * HD))
    tiny = jnp.concatenate([lanes, heads_row], axis=1)
    tiny_rows = tiny.reshape(R, S, 4 + taps + 1, 128)
    (got,), (core_in,), (core_mix,), (core_t,) = exchange(
        place,
        15,
        [
            swap_plane(part.astype(BF)),
            swap_core(rows_in),
            swap_core(rows_mix),
            swap_core(tiny_rows),
        ],
    )
    d_normed = settle(part, got, p)
    g0 = g1 + rms_pull(d_normed, x0, inverse_rms(x0), g_conv)
    d_tokens = g0.astype(BF)[None]

    tiny_line = after_core(tiny_rows, core_t)
    line_in = after_core(rows_in, core_in).astype(BF)
    line_mix = collect(rows_mix, core_mix, r).astype(BF)
    (got_in,), (got_mix,), (line_t,), (plane_b,), (plane_att,) = exchange(
        place,
        16,
        [
            swap_line(line_in),
            swap_line(line_mix),
            swap_line(tiny_line),
            swap_plane(full_b),
            swap_plane(full_att),
        ],
    )
    tiny_full = after_line(tiny_line, line_t)
    full_in = after_line(line_in, got_in).astype(BF)
    full_mix = after_line(line_mix, got_mix).astype(BF)
    out_mix = lax.ppermute(full_mix, ("rows", "seq"), [(b, a) for a, b in homes])
    (plane_in,), (plane_t,), (plane_a,) = exchange(
        place, 17, [swap_plane(full_in), swap_plane(tiny_full), swap_plane(full_a)]
    )
    tiny_sum = jnp.sum(after_plane(tiny_full, plane_t), axis=0)
    d_heads = tiny_sum[4 + taps].reshape(2, HD)

    def back(value):
        return value.transpose(1, 0, 2).reshape(shard, -1)

    out_in = after_plane(full_in, plane_in)
    out_in = out_in.reshape(TP, shard, 3, CS).transpose(1, 2, 0, 3).reshape(shard, 3 * D)
    out_att = after_plane(full_att, plane_att)
    out_a = after_plane(full_a, plane_a)
    out_b = after_plane(full_b, plane_b)
    return (
        mixed,
        d_tokens,
        tiny_sum[0, :shard],
        out_in,
        tiny_sum[4 : 4 + taps, :shard],
        out_mix.astype(F32),
        tiny_sum[1, :shard],
        back(out_a[..., 0 * FS : 1 * FS]),
        back(out_a[..., 1 * FS : 2 * FS]),
        back(out_a[..., 2 * FS : 3 * FS]).T,
        tiny_sum[2, :shard],
        back(out_att[..., :QS]),
        back(out_att[..., QS : QS + KS]),
        back(out_att[..., QS + KS : QS + 2 * KS]),
        d_heads,
        back(out_att[..., QS + 2 * KS :]).T,
        tiny_sum[3, :shard],
        back(out_b[..., 0 * FS : 1 * FS]),
        back(out_b[..., 1 * FS : 2 * FS]),
        back(out_b[..., 2 * FS : 3 * FS]).T,
    )


def solution(mesh):
    place = Place(mesh.shape["rows"], mesh.shape["seq"])
    whole = ("rows", "seq")
    wide, first, second = P("rows", "seq", None), P(whole, None), P(None, whole)
    in_specs = (
        (wide, P("rows", None), wide, P(whole), first, second, first)
        + (P(whole), first, first, second)
        + (P(whole), first, first, first, P(), second)
        + (P(whole), first, first, second)
    )
    out_specs = (
        (wide, wide, P(whole), first, second, first)
        + (P(whole), first, first, second)
        + (P(whole), first, first, first, P(), second)
        + (P(whole), first, first, second)
    )
    return jax.shard_map(
        functools.partial(per_device, place),
        mesh=mesh,
        in_specs=in_specs,
        out_specs=out_specs,
        check_vma=False,
    )
```

```python
import functools
import math

import jax
import jax.numpy as jnp
from jax import lax
from jax.experimental import pallas as pl
from jax.experimental.pallas import tpu as pltpu
from jax.sharding import PartitionSpec as P

H = 16
KVH = 8
HD = 64
TP = 4
HALO = 16
COST = 1_000_000

EPSILON = 1e-05
THETA = 1000000.0
MASKED = -1e30
MESH_ID = pl.DeviceIdType.MESH
BF = jnp.bfloat16
F32 = jnp.float32


def dot(left, right):
    return jnp.dot(left, right, preferred_element_type=F32)


def dot_tn(left, right):
    return lax.dot_general(left, right, (((0,), (0,)), ((), ())), preferred_element_type=F32)


def dot_nt(left, right):
    return lax.dot_general(left, right, (((1,), (1,)), ((), ())), preferred_element_type=F32)


class Place:
    def __init__(self, rows, seq):
        self.R, self.S = rows, seq
        self.Q = seq // TP

    def here(self):
        here = Place(self.R, self.S)
        here.r = lax.axis_index("rows")
        here.s = lax.axis_index("seq")
        here.q = here.s // TP
        here.p = lax.rem(here.s, TP)
        return here


class Copies:
    def __init__(self, send, recv):
        self.send, self.recv, self.count, self.sent = send, recv, 0, []

    def slot(self):
        self.count += 1
        return self.count - 1

    def remote(self, src, dst, slot, where, recv_slot=None):
        return pltpu.make_async_remote_copy(
            src_ref=src,
            dst_ref=dst,
            send_sem=self.send.at[slot],
            recv_sem=self.recv.at[slot if recv_slot is None else recv_slot],
            device_id=where,
            device_id_type=MESH_ID,
        )

    def push(self, src, dst, slot, where, cond=None, recv_slot=None):
        copy = self.remote(src, dst, slot, where, recv_slot)
        when(cond, copy.start)
        self.sent.append((copy.wait_send, cond))

    def arrived(self, dst, slot, where, cond=None):
        copy = self.remote(dst, dst, slot, where)
        when(cond, copy.wait_recv)

    def local(self, src, dst):
        slot = self.slot()
        copy = pltpu.make_async_copy(src, dst, self.recv.at[slot])
        copy.start()
        self.sent.append((copy.wait, None))

    def drain(self):
        for wait, cond in self.sent:
            when(cond, wait)


def when(cond, action):
    if cond is None:
        action()
    else:
        pl.when(cond)(lambda: action())


class Job:
    def __init__(
        self, ins, outs, run, kinds, aliases=(), vmem=(), relay=False, late=False
    ):
        self.ins, self.outs, self.run, self.kinds = ins, outs, run, kinds
        self.aliases, self.vmem, self.relay, self.late = aliases, vmem, relay, late


def together(runs):
    while runs:
        runs = [steps for steps in runs if next(steps, "done") != "done"]
        yield "go"


def partners(at, kinds):
    found = []
    if "plane" in kinds:
        for j in range(1, TP):
            found.append((None, at.r, at.q * TP + lax.rem(at.p + j, TP)))
    if "core" in kinds:
        for j in range(1, at.R):
            found.append((None, lax.rem(at.r + j, at.R), at.s))
    if "zall" in kinds:
        for j in range(1, at.Q):
            found.append((None, at.r, lax.rem(at.q + j, at.Q) * TP + at.p))
    elif "chain" in kinds:
        found.append((at.q > 0, at.r, at.s - TP))
        found.append((at.q < at.Q - 1, at.r, at.s + TP))
    if "home" in kinds:
        r, s, _, same = home_of(at)
        found.append((same == 0, r, s))
        r, s, same = visitor_of(at)
        found.append((same == 0, r, s))
    if "back" in kinds:
        found.append((at.q < at.Q - 1, at.r, (at.q + 1) * TP))
        for j in range(TP):
            found.append(((at.p == 0) & (at.q > 0), at.r, (at.q - 1) * TP + j))
    if "halo" in kinds:
        found.append((at.q > 0, at.r, (at.q - 1) * TP + TP - 1))
        found.append((at.q < at.Q - 1, at.r, (at.q + 1) * TP))
        for j in range(TP):
            found.append(((at.p == TP - 1) & (at.q < at.Q - 1), at.r, (at.q + 1) * TP + j))
            found.append(((at.p == 0) & (at.q > 0), at.r, (at.q - 1) * TP + j))
    return found


def home_of(at):
    k = lax.rem(at.r * at.S + at.s, at.R * at.Q)
    r, s = k // at.Q, lax.rem(k, at.Q) * TP + (at.r * at.S + at.s) // (at.R * at.Q)
    return r, s, k, ((r == at.r) & (s == at.s)).astype(jnp.int32)


def visitor_of(at):
    d = at.p * (at.R * at.Q) + at.r * at.Q + at.q
    r, s = d // at.S, lax.rem(d, at.S)
    return r, s, ((r == at.r) & (s == at.s)).astype(jnp.int32)


def meet(at, kinds):
    barrier = pltpu.get_barrier_semaphore()
    peers = partners(at, kinds)
    for cond, r, s in peers:
        when(
            cond,
            functools.partial(
                pl.semaphore_signal, barrier, inc=1, device_id=(r, s), device_id_type=MESH_ID
            ),
        )
    awaited = sum(1 for cond, r, s in peers if cond is None)
    for cond, r, s in peers:
        if cond is not None:
            awaited = awaited + cond.astype(jnp.int32)
    pl.semaphore_wait(barrier, awaited)


def exchange(place, ident, jobs):
    kinds = set().union(*[job.kinds for job in jobs])
    n_in = sum(len(job.ins) for job in jobs)
    n_out = sum(len(job.outs) for job in jobs)
    sems = 24 + sum(12 + 2 * place.Q + place.R * place.Q * 2 for job in jobs)
    arrays, in_specs, outs, aliases = [], [], [], {}
    for job in jobs:
        for k, o in job.aliases:
            aliases[len(arrays) + k] = len(outs) + o
        for k, value in enumerate(job.ins):
            arrays.append(value)
            in_specs.append(pl.BlockSpec(memory_space=pltpu.VMEM if k in job.vmem else pl.ANY))
        outs.extend(job.outs)

    def body(*refs):
        at = place.here()
        ins, results = refs[:n_in], refs[n_in : n_in + n_out]
        copies = Copies(refs[n_in + n_out], refs[n_in + n_out + 1])
        meet(at, kinds)
        runs, i, o = [], 0, 0
        for job in jobs:
            mine = results[o : o + len(job.outs)]
            runs.append(job.run(at, copies, ins[i : i + len(job.ins)], mine))
            i, o = i + len(job.ins), o + len(job.outs)
        pairs = list(zip(jobs, runs))
        relays = together([steps for job, steps in pairs if job.relay])
        next(relays, "done")
        for steps in [steps for job, steps in pairs if not job.relay and not job.late]:
            next(steps)
        next(relays, "done")
        for steps in [steps for job, steps in pairs if job.late]:
            next(steps)
        for _ in relays:
            pass
        for steps in [steps for job, steps in pairs if not job.relay]:
            for _ in steps:
                pass
        copies.drain()

    results = pl.pallas_call(
        body,
        out_shape=tuple(outs),
        in_specs=in_specs,
        out_specs=tuple(pl.BlockSpec(memory_space=pl.ANY) for _ in outs),
        scratch_shapes=[pltpu.SemaphoreType.DMA((sems,)), pltpu.SemaphoreType.DMA((sems,))],
        input_output_aliases=aliases,
        compiler_params=pltpu.CompilerParams(collective_id=ident, has_side_effects=True),
        cost_estimate=pl.CostEstimate(flops=0, bytes_accessed=COST, transcendentals=0),
        name="exchange_%d" % ident,
    )(*arrays)
    given, o = [], 0
    for job in jobs:
        given.append(results[o : o + len(job.outs)])
        o += len(job.outs)
    return given


def like(shape, dtype=BF):
    return jax.ShapeDtypeStruct(shape, dtype)


def gather_plane(value):
    def run(at, copies, ins, outs):
        slots = [copies.slot() for _ in range(TP - 1)]
        for j in range(1, TP):
            peer = at.q * TP + lax.rem(at.p + j, TP)
            copies.push(ins[0], outs[0].at[at.p], slots[j - 1], (at.r, peer))
        copies.local(ins[0], outs[0].at[at.p])
        yield "go"
        for j in range(1, TP):
            origin = lax.rem(at.p + TP - j, TP)
            copies.arrived(outs[0].at[origin], slots[j - 1], (at.r, at.s))

    return Job([value], [like((TP,) + value.shape, value.dtype)], run, {"plane"}, vmem=(0,))


def swap_plane(value):
    def run(at, copies, ins, outs):
        slots = [copies.slot() for _ in range(TP - 1)]
        for j in range(1, TP):
            other = lax.rem(at.p + j, TP)
            copies.push(
                ins[0].at[other], outs[0].at[at.p], slots[j - 1], (at.r, at.q * TP + other)
            )
        yield "go"
        for j in range(1, TP):
            origin = lax.rem(at.p + TP - j, TP)
            copies.arrived(outs[0].at[origin], slots[j - 1], (at.r, at.s))

    return Job([value], [like(value.shape, value.dtype)], run, {"plane"})


def home_back(value):
    def run(at, copies, ins, outs):
        r, s, own = visitor_of(at)
        _, _, _, here = home_of(at)
        slot = copies.slot()
        copies.push(ins[0], outs[0], slot, (r, s), own == 0)
        yield "go"
        copies.arrived(outs[0], slot, (at.r, at.s), here == 0)

    return Job([value], [like(value.shape, value.dtype)], run, {"home"})


def finish(place, at, sliced, tiny, mix, taps):
    shard, D = mix[0].shape
    shapes = [shape for _, _, _, outs in sliced for shape in outs]
    tiny_shapes = [(1, shard)] * 4 + [(taps, shard), (2, HD)]
    arrays = [x for own, came, _, _ in sliced for x in (own, came)] + [*tiny, *mix]
    where = jnp.stack([at.p, home_of(at)[3]]).astype(jnp.int32)

    def body(where_ref, *refs):
        ins, outs = refs[: len(arrays)], refs[len(arrays) :]

        def pick(index, k):
            return jnp.where(where_ref[0] == k, ins[index][k], ins[index + 1][k]).astype(F32)

        first = 0
        for n, (_, _, parts, made) in enumerate(sliced):
            for k in range(TP):
                piece = pick(2 * n, k)
                for start, width, out, base in parts:
                    there = slice(base + k * width, base + (k + 1) * width)
                    outs[first + out][:, there] = piece[:, start : start + width]
            first += len(made)
        n = 2 * len(sliced)
        total = pick(n, 0)
        for k in range(1, TP):
            total = total + pick(n, k)
        for k in range(4):
            outs[first + k][...] = total[k : k + 1, :shard]
        outs[first + 4][...] = total[4 : 4 + taps, :shard]
        row = total[4 + taps : 5 + taps, :]
        outs[first + 5][0:1, :] = row[:, :HD]
        outs[first + 5][1:2, :] = row[:, HD:]
        whole = jnp.where(where_ref[1] == 1, ins[n + 2][...], ins[n + 3][...])
        outs[first + 6][...] = whole.astype(F32)

    outs = [like(shape, F32) for shape in shapes + tiny_shapes + [(shard, D)]]
    return plain_call(body, tuple(outs), (), where, *arrays, smem=1)


def swap_core(value):
    def run(at, copies, ins, outs):
        slots = [copies.slot() for _ in range(at.R - 1)]
        for j in range(1, at.R):
            other = lax.rem(at.r + j, at.R)
            copies.push(ins[0].at[other], outs[0].at[at.r], slots[j - 1], (other, at.s))
        yield "go"
        for j in range(1, at.R):
            origin = lax.rem(at.r + at.R - j, at.R)
            copies.arrived(outs[0].at[origin], slots[j - 1], (at.r, at.s))

    return Job([value], [like(value.shape, value.dtype)], run, {"core"})


def swap_line(value):
    def run(at, copies, ins, outs):
        slots = [copies.slot() for _ in range(at.Q - 1)]
        for j in range(1, at.Q):
            other = lax.rem(at.q + j, at.Q)
            copies.push(
                ins[0].at[other], outs[0].at[at.q], slots[j - 1], (at.r, other * TP + at.p)
            )
        yield "go"
        for j in range(1, at.Q):
            origin = lax.rem(at.q + at.Q - j, at.Q)
            copies.arrived(outs[0].at[origin], slots[j - 1], (at.r, at.s))

    return Job([value], [like(value.shape, value.dtype)], run, {"zall"})


def window_forward(place, value):
    reach = place.Q // 2

    def run(at, copies, ins, outs):
        slots = [copies.slot() for _ in range(reach)]
        there = (at.r, at.s + TP)
        copies.push(ins[0], outs[0].at[reach - 1], slots[0], there, at.q + 1 < at.Q)
        copies.local(ins[0], outs[0].at[reach])
        for j in range(1, reach + 1):
            yield "go"
            came = outs[0].at[reach - j]
            copies.arrived(came, slots[j - 1], (at.r, at.s), at.q >= j)
            if j < reach:
                passes = (at.q >= j) & (at.q + 1 < at.Q)
                copies.push(came, outs[0].at[reach - j - 1], slots[j], there, passes)

    shape = (reach + 1,) + value.shape
    outs = [like(shape, value.dtype)]
    return Job([value], outs, run, {"chain"}, vmem=(0,), relay=True)


def window_backward(place, value):
    reach = place.Q // 2

    def run(at, copies, ins, outs):
        slots = [copies.slot() for _ in range(reach)]
        for j in range(1, reach + 1):
            target = (at.q - j) * TP + at.p
            copies.push(
                ins[0].at[reach - j], outs[0].at[j - 1], slots[j - 1], (at.r, target), at.q >= j
            )
        yield "go"
        for j in range(1, reach + 1):
            copies.arrived(outs[0].at[j - 1], slots[j - 1], (at.r, at.s), at.q + j < at.Q)

    shape = (reach,) + value.shape[1:]
    return Job([value], [like(shape, value.dtype)], run, {"zall"})


def halo_tokens(value):
    rows = value.shape[0]

    def run(at, copies, ins, outs):
        ahead = [copies.slot() for _ in range(TP)]
        back = [copies.slot() for _ in range(TP)]
        first = (at.p == 0) & (at.q > 0)
        last = (at.p == TP - 1) & (at.q < at.Q - 1)
        for j in range(TP):
            tail = ins[0].at[pl.ds(rows - HALO, HALO)]
            there = (at.r, (at.q + 1) * TP + j)
            copies.push(tail, outs[0], ahead[j], there, last, ahead[0])
            head = ins[0].at[pl.ds(0, HALO)]
            there = (at.r, (at.q - 1) * TP + j)
            copies.push(head, outs[1], back[j], there, first, back[0])
        yield "go"
        copies.arrived(outs[0], ahead[0], (at.r, at.s), at.q > 0)
        copies.arrived(outs[1], back[0], (at.r, at.s), at.q < at.Q - 1)

    shape = (HALO,) + value.shape[1:]
    outs = [like(shape, value.dtype), like(shape, value.dtype)]
    return Job([value], outs, run, {"halo"}, vmem=(0,))


def spread_run(at, copies, source, held, first):
    slots = [copies.slot() for _ in range(TP - 1)]
    for j in range(1, TP):
        other = lax.rem(at.p + j, TP)
        copies.push(
            source.at[other], held.at[first + at.p], slots[j - 1], (at.r, at.q * TP + other)
        )
    copy = pltpu.make_async_copy(
        source.at[at.p], held.at[first + at.p], copies.recv.at[copies.slot()]
    )
    copy.start()
    yield "go"
    copy.wait()
    for j in range(1, TP):
        origin = lax.rem(at.p + TP - j, TP)
        copies.arrived(held.at[first + origin], slots[j - 1], (at.r, at.s))


def chain_run(at, copies, held, unit=TP):
    def block(r, q):
        return held.at[pl.ds((r * at.Q + q) * unit, unit)]

    right = [copies.slot() for _ in range(at.Q - 1)]
    left = [copies.slot() for _ in range(at.Q - 1)]
    across = [[copies.slot() for _ in range(at.Q)] for _ in range(at.R - 1)]

    def cross(q, index, cond):
        for j in range(1, at.R):
            other = lax.rem(at.r + j, at.R)
            copies.push(block(at.r, q), block(at.r, q), across[j - 1][index], (other, at.s), cond)

    copies.push(
        block(at.r, at.q), block(at.r, at.q), right[0], (at.r, at.s + TP), at.q < at.Q - 1
    )
    copies.push(block(at.r, at.q), block(at.r, at.q), left[0], (at.r, at.s - TP), at.q > 0)
    cross(at.q, 0, None)
    index = 0
    spots = {}
    for hop in range(1, at.Q):
        yield "go"
        from_left, from_right = at.q >= hop, at.q + hop < at.Q
        copies.arrived(block(at.r, at.q - hop), right[hop - 1], (at.r, at.s), from_left)
        if hop < at.Q - 1:
            copies.push(
                block(at.r, at.q - hop),
                block(at.r, at.q - hop),
                right[hop],
                (at.r, at.s + TP),
                from_left & (at.q < at.Q - 1),
            )
        copies.arrived(block(at.r, at.q + hop), left[hop - 1], (at.r, at.s), from_right)
        if hop < at.Q - 1:
            copies.push(
                block(at.r, at.q + hop),
                block(at.r, at.q + hop),
                left[hop],
                (at.r, at.s - TP),
                from_right & (at.q > 0),
            )
        for side, sign in ((from_left, -1), (from_right, 1)):
            spots[(hop, sign)] = [copies.slot() for _ in range(at.R - 1)]
            for j in range(1, at.R):
                other = lax.rem(at.r + j, at.R)
                piece = block(at.r, at.q + sign * hop)
                copies.push(piece, piece, spots[(hop, sign)][j - 1], (other, at.s), side)
    yield "go"
    for j in range(1, at.R):
        source = lax.rem(at.r + at.R - j, at.R)
        copies.arrived(block(source, at.q), across[j - 1][0], (at.r, at.s))
        for hop in range(1, at.Q):
            for sign in (-1, 1):
                there = at.q + sign * hop
                copies.arrived(
                    block(source, there),
                    spots[(hop, sign)][j - 1],
                    (at.r, at.s),
                    at.q >= hop if sign < 0 else there < at.Q,
                )


def spread(source):
    def run(at, copies, ins, outs):
        yield from spread_run(at, copies, ins[0], outs[0], 0)

    outs = [like(source.shape, source.dtype)]
    return Job([source], outs, run, {"plane"}, vmem=(0,), late=True)


def spread_all(place, source):
    def run(at, copies, ins, outs):
        yield from spread_run(at, copies, ins[0], outs[0], (at.r * at.Q + at.q) * TP)
        yield from chain_run(at, copies, outs[0])

    outs = [like((place.R * place.S,) + source.shape[1:], source.dtype)]
    return Job([source], outs, run, {"plane", "chain", "core"}, vmem=(0,), relay=True)


def home_all(place, source):
    def run(at, copies, ins, outs):
        r, s, slot, here = home_of(at)
        _, _, own = visitor_of(at)
        index = copies.slot()
        copies.push(ins[0], outs[0].at[slot], index, (r, s), here == 0)
        copy = pltpu.make_async_copy(ins[0], outs[0].at[slot], copies.recv.at[copies.slot()])
        when(here == 1, copy.start)
        yield "go"
        when(here == 1, copy.wait)
        copies.arrived(outs[0].at[at.r * at.Q + at.q], index, (at.r, at.s), own == 0)
        yield from chain_run(at, copies, outs[0], 1)

    outs = [like((place.R * place.Q,) + source.shape, source.dtype)]
    return Job([source], outs, run, {"home", "chain", "core"}, vmem=(0,), relay=True)


FACTOR = 1.0 / math.sqrt(HD)


def masked_keys(kv_ref, first, kv_s):
    index = lax.broadcasted_iota(jnp.int32, kv_ref.shape, 0)
    kv_s[...] = jnp.where(index >= first, kv_ref[...].astype(F32), 0.0).astype(BF)


def attend_forward(q, kv, q_seg, key_seg, first, block):
    N, QS = q.shape
    M, KS = kv.shape[0], kv.shape[1] // 2
    ahead = M - N
    span = ahead + block
    kv_heads = KS // HD
    groups = QS // KS

    def body(first_ref, q_ref, kv_ref, qs_ref, ks_ref, o_ref, kv_s):
        masked_keys(kv_ref, first_ref[0], kv_s)

        @pl.loop(0, N // block)
        def _(i):
            start = pl.multiple_of(i * block, block)
            here, keys = pl.ds(start, block), pl.ds(start, span)
            row = lax.broadcasted_iota(jnp.int32, (block, span), 0) + ahead
            col = lax.broadcasted_iota(jnp.int32, (block, span), 1)
            open_ = (qs_ref[here, :1] == ks_ref[:1, keys]) & (col <= row)
            open_ = open_ & (col + start >= first_ref[0])
            open_ = jnp.concatenate([open_] * groups, axis=0)
            queries = q_ref[here, :]
            done = []
            for k in range(kv_heads):
                mine = [
                    queries[:, (k * groups + g) * HD : (k * groups + g + 1) * HD]
                    for g in range(groups)
                ]
                key = kv_s[keys, k * HD : (k + 1) * HD]
                value = kv_s[keys, KS + k * HD : KS + (k + 1) * HD]
                score = jnp.where(open_, dot_nt(jnp.concatenate(mine, axis=0), key) * FACTOR, MASKED)
                weight = jnp.exp(score - jnp.max(score, axis=-1, keepdims=True))
                weight = weight / jnp.sum(weight, axis=-1, keepdims=True)
                out = dot(weight.astype(BF), value).astype(BF)
                done.extend(out[g * block : (g + 1) * block] for g in range(groups))
            o_ref[here, :] = jnp.concatenate(done, axis=1)

    return attend_call(
        body, like((N, QS)), [pltpu.VMEM(kv.shape, BF)], 4 * N * span * QS, first, q, kv, q_seg, key_seg
    )


def attend_call(body, outs, scratch, flops, first, *arrays):
    return pl.pallas_call(
        body,
        out_shape=outs,
        in_specs=[pl.BlockSpec(memory_space=pltpu.SMEM)]
        + [pl.BlockSpec(memory_space=pltpu.VMEM) for _ in arrays],
        out_specs=jax.tree.map(lambda _: pl.BlockSpec(memory_space=pltpu.VMEM), outs),
        scratch_shapes=scratch,
        cost_estimate=pl.CostEstimate(flops=flops, bytes_accessed=COST, transcendentals=0),
    )(first, *arrays)


def attend_backward(q, kv, d_o, q_seg, key_seg, first, block):
    N, QS = q.shape
    M, KS = kv.shape[0], kv.shape[1] // 2
    ahead = M - N
    span = ahead + block
    kv_heads = KS // HD
    groups = QS // KS

    def body(first_ref, q_ref, kv_ref, do_ref, qs_ref, ks_ref, dq_ref, dkv_ref, kv_s, *sums):
        masked_keys(kv_ref, first_ref[0], kv_s)
        for total in sums:
            total[...] = jnp.zeros_like(total)

        @pl.loop(0, N // block)
        def _(i):
            start = pl.multiple_of(i * block, block)
            here, keys = pl.ds(start, block), pl.ds(start, span)
            row = lax.broadcasted_iota(jnp.int32, (span, block), 0)
            col = lax.broadcasted_iota(jnp.int32, (span, block), 1) + ahead
            open_ = (ks_ref[keys, :1] == qs_ref[:1, here]) & (row <= col)
            open_ = open_ & (row + start >= first_ref[0])
            open_ = jnp.concatenate([open_] * groups, axis=1)
            queries, pulls = q_ref[here, :], do_ref[here, :]

            def heads_of(values, k):
                return jnp.concatenate(
                    [
                        values[:, (k * groups + g) * HD : (k * groups + g + 1) * HD]
                        for g in range(groups)
                    ],
                    axis=0,
                )

            done = []
            for k in range(kv_heads):
                mine, pull = heads_of(queries, k), heads_of(pulls, k)
                key = kv_s[keys, k * HD : (k + 1) * HD]
                value = kv_s[keys, KS + k * HD : KS + (k + 1) * HD]
                score = jnp.where(open_, dot_nt(key, mine) * FACTOR, MASKED)
                weight = jnp.exp(score - jnp.max(score, axis=0, keepdims=True))
                weight = weight / jnp.sum(weight, axis=0, keepdims=True)
                d_weight = dot_nt(value, pull)
                delta = jnp.sum(weight * d_weight, axis=0, keepdims=True)
                d_score = (weight * (d_weight - delta)).astype(BF)
                sums[k][keys, :] += dot(d_score, mine) * FACTOR
                sums[kv_heads + k][keys, :] += dot(weight.astype(BF), pull)
                dq = dot_tn(d_score, key) * FACTOR
                done.extend(dq[g * block : (g + 1) * block] for g in range(groups))
            dq_ref[here, :] = jnp.concatenate(done, axis=1)

        dkv_ref[...] = jnp.concatenate([total[...] for total in sums], axis=1)

    return attend_call(
        body,
        (like((N, QS), F32), like((M, 2 * KS), F32)),
        [pltpu.VMEM(kv.shape, BF)] + [pltpu.VMEM((M, HD), F32) for _ in range(2 * kv_heads)],
        10 * N * span * QS,
        first,
        q,
        kv,
        d_o,
        q_seg,
        key_seg,
    )


def turned(values, cosine, sine):
    lane = lax.broadcasted_iota(jnp.int32, values.shape, 1)
    ahead = pltpu.roll(values, 2 * HD - HD // 2, 1)
    behind = pltpu.roll(values, HD // 2, 1)
    other = jnp.where(lax.rem(lane, HD) < HD // 2, ahead, behind)
    return values * cosine + other * sine


def head_means(values):
    lane = lax.broadcasted_iota(jnp.int32, values.shape, 1)
    front = lane < HD
    first = jnp.sum(jnp.where(front, values, 0.0), axis=-1, keepdims=True)
    second = jnp.sum(jnp.where(front, 0.0, values), axis=-1, keepdims=True)
    return jnp.where(front, first, second) * (1.0 / HD)


def pairs_of(width):
    return [slice(c, c + 2 * HD) for c in range(0, width, 2 * HD)]


def heads_forward(n3, w, gains, cosine, sine, QS, KS):
    N = n3.shape[0]

    def body(n3_ref, w_ref, gains_ref, cos_ref, sin_ref, pre_ref, q_ref, kv_ref):
        pre_ref[...] = dot(n3_ref[...], w_ref[:, : QS + 2 * KS])

        def normed(cols, row):
            values = pre_ref[:, cols]
            inverse = lax.rsqrt(head_means(values * values) + EPSILON)
            values = values * inverse * gains_ref[row : row + 1, :]
            return turned(values, cos_ref[...], sin_ref[...]).astype(BF)

        for cols in pairs_of(QS):
            q_ref[:, cols] = normed(cols, 0)
        for cols in pairs_of(KS):
            kv_ref[:, cols] = normed(slice(QS + cols.start, QS + cols.stop), 1)
        kv_ref[:, KS:] = pre_ref[:, QS + KS :].astype(BF)

    outs = (like((N, QS + 2 * KS), F32), like((N, QS)), like((N, 2 * KS)))
    return plain_call(body, outs, (), n3, w, gains, cosine, sine)


def heads_backward(d_q, d_kv, got, count, pre, gains, cosine, sine, n3, g3, o, w):
    N, QS = d_q.shape
    KS = d_kv.shape[1] // 2
    D = n3.shape[1]
    W = QS + 2 * KS
    step = 256

    def body(
        count_ref, dq_ref, dkv_ref, got_ref, pre_ref, gains_ref, cos_ref, sin_ref, n3_ref, g3_ref,
        o_ref, w_ref, part_ref, rows_ref, heads_ref, all_ref,
    ):
        d_kv_sum = dkv_ref[...]
        for j in range(got_ref.shape[0]):
            d_kv_sum = d_kv_sum + jnp.where(j < count_ref[0], got_ref[j].astype(F32), 0.0)
        all_ref[:, QS + KS :] = d_kv_sum[:, KS:].astype(BF)

        def back(pull, cols, row):
            values = pre_ref[:, cols]
            inverse = lax.rsqrt(head_means(values * values) + EPSILON)
            pull = turned(pull, cos_ref[...], -sin_ref[...])
            scaled = pull * gains_ref[row : row + 1, :]
            mean = head_means(scaled * values)
            d_values = inverse * scaled - values * (inverse * inverse * inverse) * mean
            all_ref[:, cols] = d_values.astype(BF)
            return jnp.sum(pull * values * inverse, axis=0, keepdims=True)

        of_queries = [back(dq_ref[:, cols], cols, 0) for cols in pairs_of(QS)]
        of_keys = [
            back(d_kv_sum[:, cols], slice(QS + cols.start, QS + cols.stop), 1)
            for cols in pairs_of(KS)
        ]
        heads_ref[0:1, :] = sum(of_queries[1:], of_queries[0])
        heads_ref[1:2, :] = sum(of_keys[1:], of_keys[0])
        values, outputs = all_ref[...], o_ref[...]

        @pl.loop(0, D // step)
        def _(c):
            cols = pl.ds(pl.multiple_of(c * step, step), step)
            part_ref[:, cols] = dot_nt(values, w_ref[cols, :W])
            left = n3_ref[:, cols].astype(F32).T.astype(BF)
            rows_ref[cols, :W] = dot(left, values).astype(BF)
            right = g3_ref[:, cols].astype(F32).T.astype(BF)
            rows_ref[cols, W:] = dot(right, outputs).astype(BF)

    outs = (like((N, D), F32), like((D, W + QS)), like((2, 2 * HD), F32))
    return plain_call(
        body, outs, [pltpu.VMEM((N, W), BF)],
        count, d_q, d_kv, got, pre, gains, cosine, sine, n3, g3, o, w, smem=1,
    )


def plain_call(body, outs, scratch, *arrays, smem=0):
    return pl.pallas_call(
        body,
        out_shape=outs,
        in_specs=[
            pl.BlockSpec(memory_space=pltpu.SMEM if k < smem else pltpu.VMEM)
            for k in range(len(arrays))
        ],
        out_specs=tuple(pl.BlockSpec(memory_space=pltpu.VMEM) for _ in outs),
        scratch_shapes=scratch,
        cost_estimate=pl.CostEstimate(flops=0, bytes_accessed=COST, transcendentals=0),
    )(*arrays)


class Plane:
    def __init__(self, at, copies):
        self.at, self.copies = at, copies

    def swap(self, send, recv):
        at, slots = self.at, [self.copies.slot() for _ in range(TP - 1)]
        for j in range(1, TP):
            other = lax.rem(at.p + j, TP)
            there = (at.r, at.q * TP + other)
            self.copies.push(send.at[other], recv.at[at.p], slots[j - 1], there)
        return functools.partial(self.arrive, recv, slots)

    def gather(self, held):
        at, slots = self.at, [self.copies.slot() for _ in range(TP - 1)]
        for j in range(1, TP):
            there = (at.r, at.q * TP + lax.rem(at.p + j, TP))
            self.copies.push(held.at[at.p], held.at[at.p], slots[j - 1], there)
        return functools.partial(self.arrive, held, slots)

    def arrive(self, held, slots):
        at = self.at
        for j in range(1, TP):
            origin = lax.rem(at.p + TP - j, TP)
            self.copies.arrived(held.at[origin], slots[j - 1], (at.r, at.s))

    def settle(self, own, recv, n):
        total = own[pl.ds(pl.multiple_of(self.at.p * n, n), n), :]
        for j in range(1, TP):
            total = total + recv[lax.rem(self.at.p + j, TP)].astype(F32)
        return total


def columns_of(count, width, action):
    @pl.loop(0, count)
    def _(c):
        action(pl.ds(pl.multiple_of(c * width, width), width))


def activate(gu, act, N, FS):
    @pl.loop(0, N // 64)
    def _(i):
        rows = pl.ds(pl.multiple_of(i * 64, 64), 64)
        gate, up = gu[rows, :FS], gu[rows, FS:]
        act[rows, :] = (jax.nn.silu(gate) * up).astype(BF)


def deactivate(gu, d_act, dgu, N, FS):
    @pl.loop(0, N // 64)
    def _(i):
        rows = pl.ds(pl.multiple_of(i * 64, 64), 64)
        gate, up, pull = gu[rows, :FS], gu[rows, FS:], d_act[rows, :]
        sigma = jax.nn.sigmoid(gate)
        dgu[rows, :FS] = (pull * up * sigma * (1.0 + gate * (1.0 - sigma))).astype(BF)
        dgu[rows, FS:] = (pull * (gate * sigma)).astype(BF)


def feed_up(held, weights, gu, N, D, FS):
    values = held[...].reshape(N, D)

    def go(cols):
        gu[:, cols] = dot(values, weights[:, cols])

    columns_of(3, 2 * FS // 3, go)


def project(left, weights, first, width, part, send, n):
    step = 256

    def go(cols):
        out = dot_nt(left[...], weights[cols, first : first + width])
        part[:, cols] = out
        send[:, :, cols] = out.reshape(TP, n, step).astype(BF)

    columns_of(weights.shape[0] // step, step, go)


def feed_kernel(place, ident, mode, arrays, D, FS, n, side=0):
    N = n * TP
    R = place.R
    half = D // R
    W = 3 * FS
    forward, backward = mode in ("fwd", "both"), mode in ("both", "bwd")
    VM, HB = pltpu.VMEM, pl.ANY
    ins, scratch, outs = {}, {}, {}
    ins["weights"] = HB
    if mode == "fwd":
        ins.update(a_g=VM, h_in=VM, gain_next=VM)
        outs.update(
            h_out=((n, D), F32, VM), next_g=((TP, n, D), BF, VM), gu_out=((N, 2 * FS), F32, HB)
        )
    else:
        ins.update(first_part=VM, h_in=VM, gain=VM)
        outs.update(
            g_out=((n, D), F32, VM),
            next_g=((TP, n, D), BF, VM),
            d_gain=((1, D), F32, VM),
            half_out=((half, W), BF, VM),
        )
        scratch.update(
            first_send=((TP, n, D), BF),
            first_got=((TP, n, D), BF),
            a_v=((TP, n, D), BF),
            e_v=((TP, n, D), BF),
            d_act=((N, FS), F32),
            dgu=((N, 2 * FS), BF),
            grad_send=((R - 1, half, W), BF),
            grad_got=((R - 1, half, W), BF),
        )
    if mode == "both":
        ins.update(e_g=HB, e_own=VM)
        outs.update(mid_out=((n, D), F32, VM), o_send=((TP, n, D), BF, VM), o_base=((n, D), F32, VM))
    if mode == "bwd":
        ins.update(a_g=HB, gu_in=HB, g_in=VM, h_before=VM, gain_before=VM)
        piece = (half // place.Q, side)
        ins.update(side_in=VM)
        outs.update(
            d_gain_before=((1, D), F32, VM),
            halo=((HALO, D), BF, VM),
            side_out=((place.Q,) + piece, BF, VM),
        )
        scratch.update(side_got=((R - 1, half, side), BF), side_half=((place.Q,) + piece, BF))
    scratch.update(
        w=((D, W), BF),
        gu=((N, 2 * FS), F32),
        act=((N, FS), BF),
        part=((N, D), F32),
        send=((TP, n, D), BF),
        got=((TP, n, D), BF),
    )
    in_names, out_names, scratch_names = list(ins), list(outs), list(scratch)
    kinds = {"plane"}
    if backward:
        kinds.add("core")
    if mode == "bwd":
        kinds.update({"back", "zall"})
    sems = 32 + 2 * R + place.Q

    def body(*refs):
        names = in_names + out_names + scratch_names
        v = dict(zip(names, refs))
        at = place.here()
        copies = Copies(refs[len(names)], refs[len(names) + 1])
        plane = Plane(at, copies)
        loads = refs[len(names) + 2]
        pending = {}

        def load(name, src, dst):
            pending[name] = pltpu.make_async_copy(src, dst, loads.at[len(pending)])
            pending[name].start()

        load("w", v["weights"], v["w"])
        if mode == "both":
            load("e", v["e_g"], v["e_v"])
        if mode == "bwd":
            load("a", v["a_g"], v["a_v"])
            load("gu", v["gu_in"], v["gu"])
        meet(at, kinds)
        w, gu, act, part, send, got = (v[k] for k in ("w", "gu", "act", "part", "send", "got"))

        if mode != "fwd":
            first = v["first_part"]
            v["first_send"][...] = first[...].reshape(TP, n, D).astype(BF)
            wait = plane.swap(v["first_send"], v["first_got"])
        if mode == "fwd":
            pending["w"].wait()
            feed_up(v["a_g"], w, gu, N, D, FS)
            save = pltpu.make_async_copy(gu, v["gu_out"], loads.at[len(pending)])
            save.start()
            activate(gu, act, N, FS)
            project(act, w, 2 * FS, FS, part, send, n)
            wait = plane.swap(send, got)
            wait()
            h_out = v["h_in"][...] + plane.settle(part, got, n)
            v["h_out"][...] = h_out
            v["next_g"][at.p] = (h_out * inverse_rms(h_out) * v["gain_next"][...]).astype(BF)
            wait = plane.gather(v["next_g"])
            wait()
            save.wait()
            copies.drain()
            return
        if mode == "both":
            wait()
            h = v["h_in"][...] + plane.settle(first, v["first_got"], n)
            v["mid_out"][...] = h
            v["a_v"][at.p] = (h * inverse_rms(h) * v["gain"][...]).astype(BF)
            wait = plane.gather(v["a_v"])
            pending["w"].wait()
            pending["e"].wait()
        else:
            side_slots = [copies.slot() for _ in range(R - 1)]
            for j in range(1, R):
                other = lax.rem(at.r + j, R)
                copies.push(
                    v["side_in"].at[other], v["side_got"].at[j - 1], side_slots[j - 1], (other, at.s)
                )
            wait()
            h = v["h_in"][...]
            before = v["h_before"][...]
            r_before = inverse_rms(before)
            d_normed = plane.settle(first, v["first_got"], n)
            v["d_gain_before"][...] = jnp.sum(d_normed * before * r_before, axis=0, keepdims=True)
            g_mid = v["g_in"][...] + rms_pull(d_normed, before, r_before, v["gain_before"][...])
            v["g_out"][...] = g_mid
            v["e_v"][at.p] = g_mid.astype(BF)
            wait = plane.gather(v["e_v"])
            pending["gu"].wait()
            activate(gu, act, N, FS)
            pending["w"].wait()
            pending["a"].wait()
        if mode == "both":
            pull_in(v["e_v"], w, v["d_act"], N, D, FS)
            wait()
            feed_up(v["a_v"], w, gu, N, D, FS)
            activate(gu, act, N, FS)
        else:
            total = v["side_in"][at.r].astype(F32)
            for j in range(1, R):
                copies.arrived(v["side_got"].at[j - 1], side_slots[j - 1], (at.r, at.s))
                total = total + v["side_got"][j - 1].astype(F32)
            v["side_half"][...] = total.astype(BF).reshape(v["side_half"].shape)
            line_slots = [copies.slot() for _ in range(at.Q - 1)]
            for j in range(1, at.Q):
                other = lax.rem(at.q + j, at.Q)
                copies.push(
                    v["side_half"].at[other],
                    v["side_out"].at[at.q],
                    line_slots[j - 1],
                    (at.r, other * TP + at.p),
                )
            v["side_out"][at.q] = v["side_half"][at.q]
            wait()
            pull_in(v["e_v"], w, v["d_act"], N, D, FS)
        deactivate(gu, v["d_act"], v["dgu"], N, FS)
        project(v["dgu"], w, 0, 2 * FS, part, send, n)
        wait = plane.swap(send, got)
        values, pulls = v["a_v"], v["e_v"]

        def grads(j):
            first_col = lax.rem(at.r + j, R) * half
            cols = pl.ds(pl.multiple_of(first_col, 128), half)
            left = values[:, :, cols].reshape(N, half).astype(F32).T.astype(BF)
            right = pulls[:, :, cols].reshape(N, half).astype(F32).T.astype(BF)
            return left, right

        slots = [copies.slot() for _ in range(R - 1)]
        for j in range(1, R):
            left, right = grads(j)

            def put(cols, left=left, j=j):
                v["grad_send"][j - 1, :, cols] = dot(left, v["dgu"][:, cols]).astype(BF)

            columns_of(3, 2 * FS // 3, put)
            v["grad_send"][j - 1, :, 2 * FS :] = dot(right, act[...]).astype(BF)
            other = lax.rem(at.r + j, R)
            copies.push(
                v["grad_send"].at[j - 1], v["grad_got"].at[j - 1], slots[j - 1], (other, at.s)
            )
        wait()
        if mode == "both":
            d_normed = plane.settle(part, got, n)
            r = inverse_rms(h)
            base = v["e_own"][...].astype(F32)
        else:
            d_normed = plane.settle(part, got, n)
            r = inverse_rms(h)
            base = v["g_out"][...]
        v["d_gain"][...] = jnp.sum(d_normed * h * r, axis=0, keepdims=True)
        g_new = base + rms_pull(d_normed, h, r, v["gain"][...])
        v["g_out"][...] = g_new
        v["next_g"][at.p] = g_new.astype(BF)
        wait = plane.gather(v["next_g"])
        if mode == "bwd":
            back = [copies.slot() for _ in range(TP)]
            for j in range(TP):
                copies.push(
                    v["next_g"].at[at.p, pl.ds(0, HALO)],
                    v["halo"],
                    back[j],
                    (at.r, (at.q - 1) * TP + j),
                    (at.p == 0) & (at.q > 0),
                    back[0],
                )
        if mode == "both":
            project(act, w, 2 * FS, FS, part, v["o_send"], n)
            v["o_base"][...] = h + part[pl.ds(pl.multiple_of(at.p * n, n), n), :]
        left, right = grads(0)
        for j in range(1, R):
            copies.arrived(v["grad_got"].at[j - 1], slots[j - 1], (at.r, at.s))

        def finish(cols):
            total = dot(left, v["dgu"][:, cols])
            for j in range(1, R):
                total = total + v["grad_got"][j - 1, :, cols].astype(F32)
            v["half_out"][:, cols] = total.astype(BF)

        columns_of(3, 2 * FS // 3, finish)
        total = dot(right, act[...])
        for j in range(1, R):
            total = total + v["grad_got"][j - 1, :, 2 * FS :].astype(F32)
        v["half_out"][:, 2 * FS :] = total.astype(BF)
        wait()
        if mode == "bwd":
            copies.arrived(v["halo"], back[0], (at.r, at.s), at.q < at.Q - 1)
            for j in range(1, at.Q):
                origin = lax.rem(at.q + at.Q - j, at.Q)
                copies.arrived(v["side_out"].at[origin], line_slots[j - 1], (at.r, at.s))
        copies.drain()

    results = pl.pallas_call(
        body,
        out_shape=tuple(like(outs[k][0], outs[k][1]) for k in out_names),
        in_specs=[pl.BlockSpec(memory_space=ins[k]) for k in in_names],
        out_specs=tuple(pl.BlockSpec(memory_space=outs[k][2]) for k in out_names),
        scratch_shapes=[pltpu.VMEM(*scratch[k]) for k in scratch_names]
        + [pltpu.SemaphoreType.DMA((sems,)), pltpu.SemaphoreType.DMA((sems,))]
        + [pltpu.SemaphoreType.DMA((4,))],
        compiler_params=pltpu.CompilerParams(collective_id=ident, has_side_effects=True),
        cost_estimate=pl.CostEstimate(flops=0, bytes_accessed=COST, transcendentals=0),
        name="feed_%s" % mode,
    )(*[arrays[k] for k in in_names])
    return dict(zip(out_names, results))


def pull_in(pulls, weights, d_act, N, D, FS):
    values = pulls[...].reshape(N, D)

    def go(cols):
        d_act[:, cols] = dot(values, weights[:, pl.ds(pl.multiple_of(2 * FS + cols.start, 128), cols.size)])

    columns_of(3, FS // 3, go)


def doc_info(positions, lengths):
    doc_ends = jnp.cumsum(lengths, dtype=jnp.int32)
    passed = positions[:, None] >= doc_ends[None, :]
    segment = jnp.sum(passed.astype(jnp.int32), axis=1, dtype=jnp.int32)
    opening = jnp.sum(jnp.where(passed, lengths[None, :], 0), axis=1, dtype=jnp.int32)
    return (segment, positions - opening)


def inverse_rms(values):
    return lax.rsqrt(jnp.mean(values * values, axis=-1, keepdims=True) + EPSILON)


def rms_pull(upstream, values, inverse, norm_gain):
    scaled = upstream * norm_gain
    product_mean = jnp.mean(scaled * values, axis=-1, keepdims=True)
    return inverse * scaled - values * (inverse * inverse * inverse) * product_mean


def settle(own, arrived, p):
    index = jnp.arange(TP, dtype=jnp.int32)[:, None, None]
    others = jnp.where(index == p, 0.0, arrived.astype(F32))
    mine = lax.dynamic_index_in_dim(own, p, 0, keepdims=False)
    return mine + jnp.sum(others, axis=0)


def per_device(
    place,
    tokens,
    doc_lengths,
    cotangent,
    gain_conv,
    w_in,
    kernel,
    w_mix,
    gain_ffa,
    gate_a,
    up_a,
    down_a,
    gain_att,
    w_query,
    w_key,
    w_value,
    head_gains,
    w_attout,
    gain_ffb,
    gate_b,
    up_b,
    down_b,
):
    R, S, Q = place.R, place.S, place.Q
    n, D = tokens.shape[1], tokens.shape[2]
    shard = w_in.shape[0]
    FS = gate_a.shape[1] // TP
    CS = D // TP
    QS, KS = H * HD // TP, KVH * HD // TP
    taps = kernel.shape[0]
    N = n * TP
    r, s = lax.axis_index("rows"), lax.axis_index("seq")
    q, p = s // TP, lax.rem(s, TP)
    lengths = doc_lengths[0]

    def slices(weight):
        return weight.reshape(shard, TP, -1).transpose(1, 0, 2)

    def joined(*weights):
        return jnp.concatenate([slices(weight) for weight in weights], axis=2)

    columns = [[a * S + b * TP + c for a in range(R) for b in range(Q)] for c in range(TP)]
    lines = [[b * TP + c for b in range(Q)] for c in range(TP)]

    def gather_rest(plane):
        flat = plane.reshape(TP * shard, -1)
        return lax.all_gather(
            flat, ("rows", "seq"), axis=0, tiled=True, axis_index_groups=columns
        )

    def by_row(grads):
        return grads.astype(BF).reshape(R, S * shard, -1)

    def own_rows(rows, came, *later):
        return lax.optimization_barrier((collect(rows, came, r).astype(BF),) + later)

    def reduce_line(half):
        part = lax.psum_scatter(
            half, "seq", scatter_dimension=0, tiled=True, axis_index_groups=lines
        )
        return part.reshape(TP, shard, part.shape[1])

    in_cut = w_in.reshape(shard, 3, TP, CS).transpose(2, 0, 1, 3).reshape(TP, shard, 3 * CS)
    small = jnp.stack([gain_conv, gain_ffa, gain_att, gain_ffb] + [kernel[i] for i in range(taps)])
    small = jnp.pad(small, ((0, 16 - 4 - taps), (0, 128 - shard)))
    small = jnp.broadcast_to(small[None], (TP, 16, 128))

    mine = tokens[0]
    (tok_g,), (halo_a, halo_b), (in_g,), (mix_g,), (small_g,), (ffa_p,) = exchange(
        place,
        0,
        [
            gather_plane(mine),
            halo_tokens(mine),
            spread_all(place, in_cut),
            home_all(place, w_mix),
            spread_all(place, small),
            spread(joined(gate_a, up_a, down_a.T)),
        ],
    )
    wa = gather_rest(ffa_p)
    w_mix_s = mix_g.reshape(CS, D)
    vectors = small_g[:, : 4 + taps, :shard].transpose(1, 0, 2).reshape(4 + taps, D).astype(F32)
    g_conv, g_ffa, g_att, g_ffb = (vectors[i] for i in range(4))
    kernel_f = lax.dynamic_slice_in_dim(vectors[4:], p * CS, CS, 1)
    w_in_s = in_g.reshape(D, 3 * CS)

    def own(parts, index):
        return lax.dynamic_index_in_dim(parts, index, 0, keepdims=False).astype(F32)

    def collect(parts, came, index):
        slot = jnp.arange(came.shape[0], dtype=jnp.int32).reshape((-1,) + (1,) * (came.ndim - 1))
        mine_part = lax.dynamic_index_in_dim(parts, index, 0, keepdims=True).astype(F32)
        return jnp.sum(jnp.where(slot == index, mine_part, came.astype(F32)), axis=0)

    def after_core(parts, came):
        summed = collect(parts, came, r)
        return summed.reshape((Q, TP) + summed.shape[1:])

    def after_line(parts, came):
        return collect(parts, came, q)

    total = S * n
    pos_ext = q * N - HALO + jnp.arange(N + 2 * HALO, dtype=jnp.int32)
    seg_ext, rel_ext = doc_info(pos_ext, lengths)
    valid = ((pos_ext >= 0) & (pos_ext < total))[:, None]
    x_ext = jnp.concatenate([halo_a, tok_g.reshape(N, D), halo_b], axis=0)
    x_ext = jnp.where(valid, x_ext, jnp.zeros_like(x_ext)).astype(F32)
    r0_ext = inverse_rms(x_ext)
    n1_ext = (x_ext * r0_ext * g_conv).astype(BF)
    z_ext = dot(n1_ext, w_in_s)
    b_ext, c_ext, v_ext = z_ext[:, :CS], z_ext[:, CS : 2 * CS], z_ext[:, 2 * CS :]
    u_ext = lax.optimization_barrier((b_ext * v_ext).astype(BF)).astype(F32)
    span = slice(HALO, HALO + N)
    same = [
        (seg_ext[HALO - 2 + k : HALO - 2 + k + N] == seg_ext[span]).astype(F32)[:, None]
        for k in range(taps)
    ]
    near = [u_ext[HALO - 2 + k : HALO - 2 + k + N] for k in range(taps)]
    conv = kernel_f[0] * near[0] * same[0]
    for k in range(1, taps):
        conv = conv + kernel_f[k] * near[k] * same[k]
    m_bf = (c_ext[span] * conv).astype(BF)
    part = dot(m_bf, w_mix_s).reshape(TP, n, D)
    (got,), (att_p,), (ffb_p,) = exchange(
        place,
        1,
        [
            swap_plane(part.astype(BF)),
            spread(joined(w_query, w_key, w_value, w_attout.T)),
            spread(joined(gate_b, up_b, down_b.T)),
        ],
    )
    w_att = gather_rest(att_p)
    wb = gather_rest(ffb_p)
    x0 = mine.astype(F32)
    h1 = x0 + settle(part, got, p)

    r1 = inverse_rms(h1)
    a1 = (h1 * r1 * g_ffa).astype(BF)
    ((a1_g,),) = exchange(place, 2, [gather_plane(a1)])
    a1_g = a1_g.reshape(N, D)

    g_row = {name: value[None] for name, value in
             (("ffa", g_ffa), ("att", g_att), ("ffb", g_ffb))}
    fed = feed_kernel(
        place,
        3,
        "fwd",
        {"weights": wa, "a_g": a1_g.reshape(TP, n, D), "h_in": h1, "gain_next": g_row["att"]},
        D,
        FS,
        n,
    )
    h2, n3_g, gu1 = fed["h_out"], fed["next_g"], fed["gu_out"]

    n3_g = n3_g.reshape(N, D)
    w_out = w_att[:, QS + 2 * KS :]
    lane = jnp.arange(2 * HD, dtype=jnp.int32)
    frequency = jnp.exp(jnp.arange(HD // 2, dtype=F32) * (-2.0 * math.log(THETA) / HD))
    angles = rel_ext[span].astype(F32)[:, None] * jnp.tile(frequency, 4)[None, :]
    cosine = jnp.cos(angles)
    sine = jnp.sin(angles) * jnp.where(lane % HD < HD // 2, -1.0, 1.0)
    head_rows = jnp.tile(head_gains.astype(F32), (1, 2))
    pre, q_bf, kv_bf = heads_forward(n3_g, w_att, head_rows, cosine, sine, QS, KS)
    e_bf = cotangent[0]
    (kv_w,), (e_g,) = exchange(
        place,
        5,
        [window_forward(place, kv_bf), gather_plane(e_bf)],
    )
    reach = Q // 2 + 1
    kv_all = kv_w.reshape(reach * N, 2 * KS)
    q_seg = seg_ext[span]
    key_seg, _ = doc_info((q - reach + 1) * N + jnp.arange(reach * N, dtype=jnp.int32), lengths)
    first = jnp.maximum((reach - 1 - q) * N, 0).astype(jnp.int32).reshape(1)
    seg_col, seg_row = (jnp.broadcast_to(q_seg[:, None], (N, 128)), jnp.broadcast_to(q_seg, (8, N)))
    key_col = jnp.broadcast_to(key_seg[:, None], (reach * N, 128))
    key_row = jnp.broadcast_to(key_seg, (8, reach * N))
    o_bf = attend_forward(q_bf, kv_all, seg_col, key_row, first, 128)
    fed = feed_kernel(
        place,
        8,
        "both",
        {
            "weights": wb,
            "first_part": dot_nt(o_bf, w_out),
            "h_in": h2,
            "gain": g_row["ffb"],
            "e_g": e_g.reshape(TP, n, D),
            "e_own": e_bf,
        },
        D,
        FS,
        n,
    )
    h3, g3, g3_g, half_b = fed["mid_out"], fed["g_out"], fed["next_g"], fed["half_out"]
    d_gain = {}
    d_gain["ffb"] = fed["d_gain"][0]

    g3_g = g3_g.reshape(N, D)
    d_o = dot(g3_g, w_out).astype(BF)
    d_q, d_kv = attend_backward(q_bf, kv_all, d_o, seg_row, key_col, first, 128)
    d_kv = d_kv.reshape(reach, N, 2 * KS)
    (got_kv,), (got_o,) = exchange(
        place, 10, [window_backward(place, d_kv.astype(BF)), swap_plane(fed["o_send"])]
    )
    index = jnp.arange(TP, dtype=jnp.int32)[:, None, None]
    h4 = fed["o_base"] + jnp.sum(jnp.where(index == p, 0.0, got_o.astype(F32)), axis=0)
    mixed = h4.astype(BF)[None]
    count = jnp.clip(Q - 1 - q, 0, reach - 1).astype(jnp.int32).reshape(1)
    half_b, got_kv = lax.optimization_barrier((half_b, got_kv))
    full_b = reduce_line(half_b)
    part, rows_att, d_heads = heads_backward(
        d_q, d_kv[-1], got_kv, count, pre, head_rows, cosine, sine, n3_g, g3_g, o_bf, w_att
    )
    d_heads = jnp.sum(d_heads.reshape(2, 2, HD), axis=1)
    rows_att = by_row(rows_att)
    fed = feed_kernel(
        place,
        13,
        "bwd",
        {
            "weights": wa,
            "first_part": part,
            "h_in": h1,
            "gain": g_row["ffa"],
            "a_g": a1_g.reshape(TP, n, D),
            "gu_in": gu1,
            "g_in": g3,
            "h_before": h2,
            "gain_before": g_row["att"],
            "side_in": rows_att,
        },
        D,
        FS,
        n,
        rows_att.shape[2],
    )
    full_att = jnp.sum(fed["side_out"].astype(F32), axis=0).astype(BF).reshape(TP, shard, -1)
    g1, g1_g, g1_halo = fed["g_out"], fed["next_g"], fed["halo"]
    d_gain["att"], d_gain["ffa"] = fed["d_gain_before"][0], fed["d_gain"][0]
    full_a = reduce_line(fed["half_out"])

    g1_halo = jnp.where(q < Q - 1, g1_halo, jnp.zeros_like(g1_halo))
    g1_ext = jnp.concatenate([g1_g.reshape(N, D), g1_halo], axis=0)
    d_m = dot_nt(g1_ext, w_mix_s)
    d_mix_s = dot_tn(m_bf, g1_ext[:N])
    d_c = d_m[:N] * conv
    d_conv = lax.optimization_barrier((d_m * c_ext[HALO:]).astype(BF)).astype(F32)
    d_kernel = jnp.stack(
        [jnp.sum(d_conv[:N] * near[k] * same[k], axis=0) for k in range(taps)]
    )
    d_u = jnp.zeros((N, CS), F32)
    for k in range(taps):
        ahead = taps - 1 - k
        match = (seg_ext[HALO + ahead : HALO + ahead + N] == seg_ext[span]).astype(F32)[:, None]
        d_u = d_u + kernel_f[k] * d_conv[ahead : ahead + N] * match
    d_z = jnp.concatenate([d_u * v_ext[span], d_c, d_u * b_ext[span]], axis=1).astype(BF)
    rows_in = dot_tn(n1_ext[span], d_z).astype(BF).reshape(R, S, shard, 3 * CS)
    rows_mix = d_mix_s.astype(BF).reshape(R, Q, shard, D)
    d_n1 = dot_nt(d_z, w_in_s)
    d_gain["conv"] = jnp.sum(d_n1 * x_ext[span] * r0_ext[span], axis=0)
    part = d_n1.reshape(TP, n, D)
    d_taps = lax.dynamic_update_slice(jnp.zeros((taps, D), F32), d_kernel, (0, p * CS))
    lanes = jnp.concatenate(
        [jnp.stack([d_gain["conv"], d_gain["ffa"], d_gain["att"], d_gain["ffb"]]), d_taps]
    )
    lanes = lanes.reshape(4 + taps, R * S, shard).transpose(1, 0, 2)
    lanes = jnp.pad(lanes, ((0, 0), (0, 0), (0, 128 - shard)))
    heads_row = jnp.broadcast_to(d_heads.reshape(1, 1, 2 * HD), (R * S, 1, 2 * HD))
    tiny = jnp.concatenate([lanes, heads_row], axis=1)
    tiny_rows = tiny.reshape(R, S, 4 + taps + 1, 128)
    (got,), (core_in,), (core_mix,), (core_t,) = exchange(
        place,
        15,
        [
            swap_plane(part.astype(BF)),
            swap_core(rows_in),
            swap_core(rows_mix),
            swap_core(tiny_rows),
        ],
    )
    d_normed = settle(part, got, p)
    g0 = g1 + rms_pull(d_normed, x0, inverse_rms(x0), g_conv)
    d_tokens = g0.astype(BF)[None]

    tiny_line = after_core(tiny_rows, core_t)
    line_in = after_core(rows_in, core_in).astype(BF)
    line_mix = collect(rows_mix, core_mix, r).astype(BF)
    FF = TP * FS
    by_weight = [(k * FS, FS, k, 0) for k in range(3)]
    by_head = [(0, QS, 0, 0), (QS, KS, 1, 0), (QS + KS, KS, 2, 0), (QS + 2 * KS, QS, 3, 0)]
    (got_in,), (got_mix,), (line_t,), (plane_b,), (plane_att,) = exchange(
        place,
        16,
        [
            swap_line(line_in),
            swap_line(line_mix),
            swap_line(tiny_line),
            swap_plane(full_b),
            swap_plane(full_att),
        ],
    )
    tiny_full = after_line(tiny_line, line_t)
    full_in = after_line(line_in, got_in).astype(BF)
    full_mix = after_line(line_mix, got_mix).astype(BF)
    (plane_in,), (plane_a,), (plane_t,), (mix_back,) = exchange(
        place,
        17,
        [swap_plane(full_in), swap_plane(full_a), swap_plane(tiny_full), home_back(full_mix)],
    )
    FF = TP * FS
    by_weight = [(k * FS, FS, k, 0) for k in range(3)]
    by_gate = [(k * CS, CS, 0, k * D) for k in range(3)]
    by_head = [(0, QS, 0, 0), (QS, KS, 1, 0), (QS + KS, KS, 2, 0), (QS + 2 * KS, QS, 3, 0)]
    ready = finish(
        place,
        place.here(),
        [
            (full_b, plane_b, by_weight, [(shard, FF)] * 3),
            (full_att, plane_att, by_head, [(shard, TP * k) for k in (QS, KS, KS, QS)]),
            (full_a, plane_a, by_weight, [(shard, FF)] * 3),
            (full_in, plane_in, by_gate, [(shard, 3 * D)]),
        ],
        (tiny_full, plane_t),
        (full_mix, mix_back),
        taps,
    )
    out_b, out_att, out_a, (out_in,) = ready[:3], ready[3:7], ready[7:10], ready[10:11]
    of_conv, of_ffa, of_att, of_ffb, of_taps, d_heads, out_mix = ready[11:]
    return (
        mixed,
        d_tokens,
        of_conv[0],
        out_in,
        of_taps,
        out_mix,
        of_ffa[0],
        out_a[0],
        out_a[1],
        out_a[2].T,
        of_att[0],
        out_att[0],
        out_att[1],
        out_att[2],
        d_heads,
        out_att[3].T,
        of_ffb[0],
        out_b[0],
        out_b[1],
        out_b[2].T,
    )


def solution(mesh):
    place = Place(mesh.shape["rows"], mesh.shape["seq"])
    whole = ("rows", "seq")
    wide, first, second = P("rows", "seq", None), P(whole, None), P(None, whole)
    in_specs = (
        (wide, P("rows", None), wide, P(whole), first, second, first)
        + (P(whole), first, first, second)
        + (P(whole), first, first, first, P(), second)
        + (P(whole), first, first, second)
    )
    out_specs = (
        (wide, wide, P(whole), first, second, first)
        + (P(whole), first, first, second)
        + (P(whole), first, first, first, P(), second)
        + (P(whole), first, first, second)
    )
    return jax.shard_map(
        functools.partial(per_device, place),
        mesh=mesh,
        in_specs=in_specs,
        out_specs=out_specs,
        check_vma=False,
    )
```

```python
import functools
import math

import jax
import jax.numpy as jnp
from jax import lax
from jax.experimental import pallas as pl
from jax.experimental.pallas import tpu as pltpu
from jax.sharding import PartitionSpec as P

H = 16
KVH = 8
HD = 64
TP = 4
HALO = 16
COST = 1_000_000

EPSILON = 1e-05
THETA = 1000000.0
MASKED = -1e30
MESH_ID = pl.DeviceIdType.MESH
BF = jnp.bfloat16
F32 = jnp.float32


def dot(left, right):
    return jnp.dot(left, right, preferred_element_type=F32)


def dot_tn(left, right):
    return lax.dot_general(left, right, (((0,), (0,)), ((), ())), preferred_element_type=F32)


def dot_nt(left, right):
    return lax.dot_general(left, right, (((1,), (1,)), ((), ())), preferred_element_type=F32)


class Place:
    def __init__(self, rows, seq):
        self.R, self.S = rows, seq
        self.Q = seq // TP

    def here(self):
        here = Place(self.R, self.S)
        here.r = lax.axis_index("rows")
        here.s = lax.axis_index("seq")
        here.q = here.s // TP
        here.p = lax.rem(here.s, TP)
        return here


class Copies:
    def __init__(self, send, recv):
        self.send, self.recv, self.count, self.sent = send, recv, 0, []

    def slot(self):
        self.count += 1
        return self.count - 1

    def remote(self, src, dst, slot, where, recv_slot=None):
        return pltpu.make_async_remote_copy(
            src_ref=src,
            dst_ref=dst,
            send_sem=self.send.at[slot],
            recv_sem=self.recv.at[slot if recv_slot is None else recv_slot],
            device_id=where,
            device_id_type=MESH_ID,
        )

    def push(self, src, dst, slot, where, cond=None, recv_slot=None):
        copy = self.remote(src, dst, slot, where, recv_slot)
        when(cond, copy.start)
        self.sent.append((copy.wait_send, cond))

    def arrived(self, dst, slot, where, cond=None):
        copy = self.remote(dst, dst, slot, where)
        when(cond, copy.wait_recv)

    def local(self, src, dst):
        slot = self.slot()
        copy = pltpu.make_async_copy(src, dst, self.recv.at[slot])
        copy.start()
        self.sent.append((copy.wait, None))

    def drain(self):
        for wait, cond in self.sent:
            when(cond, wait)


def when(cond, action):
    if cond is None:
        action()
    else:
        pl.when(cond)(lambda: action())


class Job:
    def __init__(
        self, ins, outs, run, kinds, aliases=(), vmem=(), relay=False, late=False
    ):
        self.ins, self.outs, self.run, self.kinds = ins, outs, run, kinds
        self.aliases, self.vmem, self.relay, self.late = aliases, vmem, relay, late


def together(runs):
    while runs:
        runs = [steps for steps in runs if next(steps, "done") != "done"]
        yield "go"


def partners(at, kinds):
    found = []
    if "plane" in kinds:
        for j in range(1, TP):
            found.append((None, at.r, at.q * TP + lax.rem(at.p + j, TP)))
    if "core" in kinds:
        for j in range(1, at.R):
            found.append((None, lax.rem(at.r + j, at.R), at.s))
    if "zall" in kinds:
        for j in range(1, at.Q):
            found.append((None, at.r, lax.rem(at.q + j, at.Q) * TP + at.p))
    elif "chain" in kinds:
        found.append((at.q > 0, at.r, at.s - TP))
        found.append((at.q < at.Q - 1, at.r, at.s + TP))
    if "home" in kinds:
        r, s, _, same = home_of(at)
        found.append((same == 0, r, s))
        r, s, same = visitor_of(at)
        found.append((same == 0, r, s))
    if "back" in kinds:
        found.append((at.q < at.Q - 1, at.r, (at.q + 1) * TP))
        for j in range(TP):
            found.append(((at.p == 0) & (at.q > 0), at.r, (at.q - 1) * TP + j))
    if "halo" in kinds:
        found.append((at.q > 0, at.r, (at.q - 1) * TP + TP - 1))
        found.append((at.q < at.Q - 1, at.r, (at.q + 1) * TP))
        for j in range(TP):
            found.append(((at.p == TP - 1) & (at.q < at.Q - 1), at.r, (at.q + 1) * TP + j))
            found.append(((at.p == 0) & (at.q > 0), at.r, (at.q - 1) * TP + j))
    return found


def home_of(at):
    k = lax.rem(at.r * at.S + at.s, at.R * at.Q)
    r, s = k // at.Q, lax.rem(k, at.Q) * TP + (at.r * at.S + at.s) // (at.R * at.Q)
    return r, s, k, ((r == at.r) & (s == at.s)).astype(jnp.int32)


def visitor_of(at):
    d = at.p * (at.R * at.Q) + at.r * at.Q + at.q
    r, s = d // at.S, lax.rem(d, at.S)
    return r, s, ((r == at.r) & (s == at.s)).astype(jnp.int32)


def meet(at, kinds):
    barrier = pltpu.get_barrier_semaphore()
    peers = partners(at, kinds)
    for cond, r, s in peers:
        when(
            cond,
            functools.partial(
                pl.semaphore_signal, barrier, inc=1, device_id=(r, s), device_id_type=MESH_ID
            ),
        )
    awaited = sum(1 for cond, r, s in peers if cond is None)
    for cond, r, s in peers:
        if cond is not None:
            awaited = awaited + cond.astype(jnp.int32)
    pl.semaphore_wait(barrier, awaited)


def exchange(place, ident, jobs):
    kinds = set().union(*[job.kinds for job in jobs])
    n_in = sum(len(job.ins) for job in jobs)
    n_out = sum(len(job.outs) for job in jobs)
    sems = 24 + sum(12 + 2 * place.Q + place.R * place.Q * 2 for job in jobs)
    arrays, in_specs, outs, aliases = [], [], [], {}
    for job in jobs:
        for k, o in job.aliases:
            aliases[len(arrays) + k] = len(outs) + o
        for k, value in enumerate(job.ins):
            arrays.append(value)
            in_specs.append(pl.BlockSpec(memory_space=pltpu.VMEM if k in job.vmem else pl.ANY))
        outs.extend(job.outs)

    def body(*refs):
        at = place.here()
        ins, results = refs[:n_in], refs[n_in : n_in + n_out]
        copies = Copies(refs[n_in + n_out], refs[n_in + n_out + 1])
        meet(at, kinds)
        runs, i, o = [], 0, 0
        for job in jobs:
            mine = results[o : o + len(job.outs)]
            runs.append(job.run(at, copies, ins[i : i + len(job.ins)], mine))
            i, o = i + len(job.ins), o + len(job.outs)
        pairs = list(zip(jobs, runs))
        relays = together([steps for job, steps in pairs if job.relay])
        next(relays, "done")
        for steps in [steps for job, steps in pairs if not job.relay and not job.late]:
            next(steps)
        next(relays, "done")
        for steps in [steps for job, steps in pairs if job.late]:
            next(steps)
        for _ in relays:
            pass
        for steps in [steps for job, steps in pairs if not job.relay]:
            for _ in steps:
                pass
        copies.drain()

    results = pl.pallas_call(
        body,
        out_shape=tuple(outs),
        in_specs=in_specs,
        out_specs=tuple(pl.BlockSpec(memory_space=pl.ANY) for _ in outs),
        scratch_shapes=[pltpu.SemaphoreType.DMA((sems,)), pltpu.SemaphoreType.DMA((sems,))],
        input_output_aliases=aliases,
        compiler_params=pltpu.CompilerParams(collective_id=ident, has_side_effects=True),
        cost_estimate=pl.CostEstimate(flops=0, bytes_accessed=COST, transcendentals=0),
        name="exchange_%d" % ident,
    )(*arrays)
    given, o = [], 0
    for job in jobs:
        given.append(results[o : o + len(job.outs)])
        o += len(job.outs)
    return given


def like(shape, dtype=BF):
    return jax.ShapeDtypeStruct(shape, dtype)


def gather_plane(value):
    def run(at, copies, ins, outs):
        slots = [copies.slot() for _ in range(TP - 1)]
        for j in range(1, TP):
            peer = at.q * TP + lax.rem(at.p + j, TP)
            copies.push(ins[0], outs[0].at[at.p], slots[j - 1], (at.r, peer))
        copies.local(ins[0], outs[0].at[at.p])
        yield "go"
        for j in range(1, TP):
            origin = lax.rem(at.p + TP - j, TP)
            copies.arrived(outs[0].at[origin], slots[j - 1], (at.r, at.s))

    return Job([value], [like((TP,) + value.shape, value.dtype)], run, {"plane"}, vmem=(0,))


def swap_plane(value):
    def run(at, copies, ins, outs):
        slots = [copies.slot() for _ in range(TP - 1)]
        for j in range(1, TP):
            other = lax.rem(at.p + j, TP)
            copies.push(
                ins[0].at[other], outs[0].at[at.p], slots[j - 1], (at.r, at.q * TP + other)
            )
        yield "go"
        for j in range(1, TP):
            origin = lax.rem(at.p + TP - j, TP)
            copies.arrived(outs[0].at[origin], slots[j - 1], (at.r, at.s))

    return Job([value], [like(value.shape, value.dtype)], run, {"plane"})


def home_back(value):
    def run(at, copies, ins, outs):
        r, s, own = visitor_of(at)
        _, _, _, here = home_of(at)
        slot = copies.slot()
        copies.push(ins[0], outs[0], slot, (r, s), own == 0)
        yield "go"
        copies.arrived(outs[0], slot, (at.r, at.s), here == 0)

    return Job([value], [like(value.shape, value.dtype)], run, {"home"})


def finish(place, at, sliced, tiny, mix, taps):
    shard, D = mix[0].shape
    shapes = [shape for _, _, _, outs in sliced for shape in outs]
    tiny_shapes = [(1, shard)] * 4 + [(taps, shard), (2, HD)]
    arrays = [x for own, came, _, _ in sliced for x in (own, came)] + [*tiny, *mix]
    where = jnp.stack([at.p, home_of(at)[3]]).astype(jnp.int32)

    def body(where_ref, *refs):
        ins, outs = refs[: len(arrays)], refs[len(arrays) :]

        def pick(index, k):
            return jnp.where(where_ref[0] == k, ins[index][k], ins[index + 1][k]).astype(F32)

        first = 0
        for n, (_, _, parts, made) in enumerate(sliced):
            for k in range(TP):
                piece = pick(2 * n, k)
                for start, width, out, base in parts:
                    there = slice(base + k * width, base + (k + 1) * width)
                    outs[first + out][:, there] = piece[:, start : start + width]
            first += len(made)
        n = 2 * len(sliced)
        total = pick(n, 0)
        for k in range(1, TP):
            total = total + pick(n, k)
        for k in range(4):
            outs[first + k][...] = total[k : k + 1, :shard]
        outs[first + 4][...] = total[4 : 4 + taps, :shard]
        row = total[4 + taps : 5 + taps, :]
        outs[first + 5][0:1, :] = row[:, :HD]
        outs[first + 5][1:2, :] = row[:, HD:]
        whole = jnp.where(where_ref[1] == 1, ins[n + 2][...], ins[n + 3][...])
        outs[first + 6][...] = whole.astype(F32)

    outs = [like(shape, F32) for shape in shapes + tiny_shapes + [(shard, D)]]
    return plain_call(body, tuple(outs), (), where, *arrays, smem=1)


def swap_core(value):
    def run(at, copies, ins, outs):
        slots = [copies.slot() for _ in range(at.R - 1)]
        for j in range(1, at.R):
            other = lax.rem(at.r + j, at.R)
            copies.push(ins[0].at[other], outs[0].at[at.r], slots[j - 1], (other, at.s))
        yield "go"
        for j in range(1, at.R):
            origin = lax.rem(at.r + at.R - j, at.R)
            copies.arrived(outs[0].at[origin], slots[j - 1], (at.r, at.s))

    return Job([value], [like(value.shape, value.dtype)], run, {"core"})


def swap_line(value):
    def run(at, copies, ins, outs):
        slots = [copies.slot() for _ in range(at.Q - 1)]
        for j in range(1, at.Q):
            other = lax.rem(at.q + j, at.Q)
            copies.push(
                ins[0].at[other], outs[0].at[at.q], slots[j - 1], (at.r, other * TP + at.p)
            )
        yield "go"
        for j in range(1, at.Q):
            origin = lax.rem(at.q + at.Q - j, at.Q)
            copies.arrived(outs[0].at[origin], slots[j - 1], (at.r, at.s))

    return Job([value], [like(value.shape, value.dtype)], run, {"zall"})


def window_forward(place, value):
    reach = place.Q // 2

    def run(at, copies, ins, outs):
        slots = [copies.slot() for _ in range(reach)]
        there = (at.r, at.s + TP)
        copies.push(ins[0], outs[0].at[reach - 1], slots[0], there, at.q + 1 < at.Q)
        copies.local(ins[0], outs[0].at[reach])
        for j in range(1, reach + 1):
            yield "go"
            came = outs[0].at[reach - j]
            copies.arrived(came, slots[j - 1], (at.r, at.s), at.q >= j)
            if j < reach:
                passes = (at.q >= j) & (at.q + 1 < at.Q)
                copies.push(came, outs[0].at[reach - j - 1], slots[j], there, passes)

    shape = (reach + 1,) + value.shape
    outs = [like(shape, value.dtype)]
    return Job([value], outs, run, {"chain"}, vmem=(0,), relay=True)


def window_backward(place, value):
    reach = place.Q // 2

    def run(at, copies, ins, outs):
        slots = [copies.slot() for _ in range(reach)]
        for j in range(1, reach + 1):
            target = (at.q - j) * TP + at.p
            copies.push(
                ins[0].at[reach - j], outs[0].at[j - 1], slots[j - 1], (at.r, target), at.q >= j
            )
        yield "go"
        for j in range(1, reach + 1):
            copies.arrived(outs[0].at[j - 1], slots[j - 1], (at.r, at.s), at.q + j < at.Q)

    shape = (reach,) + value.shape[1:]
    return Job([value], [like(shape, value.dtype)], run, {"zall"})


def halo_tokens(value):
    rows = value.shape[0]

    def run(at, copies, ins, outs):
        ahead = [copies.slot() for _ in range(TP)]
        back = [copies.slot() for _ in range(TP)]
        first = (at.p == 0) & (at.q > 0)
        last = (at.p == TP - 1) & (at.q < at.Q - 1)
        for j in range(TP):
            tail = ins[0].at[pl.ds(rows - HALO, HALO)]
            there = (at.r, (at.q + 1) * TP + j)
            copies.push(tail, outs[0], ahead[j], there, last, ahead[0])
            head = ins[0].at[pl.ds(0, HALO)]
            there = (at.r, (at.q - 1) * TP + j)
            copies.push(head, outs[1], back[j], there, first, back[0])
        yield "go"
        copies.arrived(outs[0], ahead[0], (at.r, at.s), at.q > 0)
        copies.arrived(outs[1], back[0], (at.r, at.s), at.q < at.Q - 1)

    shape = (HALO,) + value.shape[1:]
    outs = [like(shape, value.dtype), like(shape, value.dtype)]
    return Job([value], outs, run, {"halo"}, vmem=(0,))


def spread_run(at, copies, source, held, first):
    slots = [copies.slot() for _ in range(TP - 1)]
    for j in range(1, TP):
        other = lax.rem(at.p + j, TP)
        copies.push(
            source.at[other], held.at[first + at.p], slots[j - 1], (at.r, at.q * TP + other)
        )
    copy = pltpu.make_async_copy(
        source.at[at.p], held.at[first + at.p], copies.recv.at[copies.slot()]
    )
    copy.start()
    yield "go"
    copy.wait()
    for j in range(1, TP):
        origin = lax.rem(at.p + TP - j, TP)
        copies.arrived(held.at[first + origin], slots[j - 1], (at.r, at.s))


def chain_run(at, copies, held, unit=TP):
    def block(r, q):
        return held.at[pl.ds(pl.multiple_of((r * at.Q + q) * unit, unit), unit)]

    right = [copies.slot() for _ in range(at.Q - 1)]
    left = [copies.slot() for _ in range(at.Q - 1)]
    across = [[copies.slot() for _ in range(at.Q)] for _ in range(at.R - 1)]

    def cross(q, index, cond):
        for j in range(1, at.R):
            other = lax.rem(at.r + j, at.R)
            copies.push(block(at.r, q), block(at.r, q), across[j - 1][index], (other, at.s), cond)

    copies.push(
        block(at.r, at.q), block(at.r, at.q), right[0], (at.r, at.s + TP), at.q < at.Q - 1
    )
    copies.push(block(at.r, at.q), block(at.r, at.q), left[0], (at.r, at.s - TP), at.q > 0)
    cross(at.q, 0, None)
    index = 0
    spots = {}
    for hop in range(1, at.Q):
        yield "go"
        from_left, from_right = at.q >= hop, at.q + hop < at.Q
        copies.arrived(block(at.r, at.q - hop), right[hop - 1], (at.r, at.s), from_left)
        if hop < at.Q - 1:
            copies.push(
                block(at.r, at.q - hop),
                block(at.r, at.q - hop),
                right[hop],
                (at.r, at.s + TP),
                from_left & (at.q < at.Q - 1),
            )
        copies.arrived(block(at.r, at.q + hop), left[hop - 1], (at.r, at.s), from_right)
        if hop < at.Q - 1:
            copies.push(
                block(at.r, at.q + hop),
                block(at.r, at.q + hop),
                left[hop],
                (at.r, at.s - TP),
                from_right & (at.q > 0),
            )
        for side, sign in ((from_left, -1), (from_right, 1)):
            spots[(hop, sign)] = [copies.slot() for _ in range(at.R - 1)]
            for j in range(1, at.R):
                other = lax.rem(at.r + j, at.R)
                piece = block(at.r, at.q + sign * hop)
                copies.push(piece, piece, spots[(hop, sign)][j - 1], (other, at.s), side)
    yield "go"
    for j in range(1, at.R):
        source = lax.rem(at.r + at.R - j, at.R)
        copies.arrived(block(source, at.q), across[j - 1][0], (at.r, at.s))
        for hop in range(1, at.Q):
            for sign in (-1, 1):
                there = at.q + sign * hop
                copies.arrived(
                    block(source, there),
                    spots[(hop, sign)][j - 1],
                    (at.r, at.s),
                    at.q >= hop if sign < 0 else there < at.Q,
                )


def spread(source):
    def run(at, copies, ins, outs):
        yield from spread_run(at, copies, ins[0], outs[0], 0)

    outs = [like(source.shape, source.dtype)]
    return Job([source], outs, run, {"plane"}, vmem=(0,), late=True)


def spread_all(place, source):
    def run(at, copies, ins, outs):
        yield from spread_run(at, copies, ins[0], outs[0], (at.r * at.Q + at.q) * TP)
        yield from chain_run(at, copies, outs[0])

    outs = [like((place.R * place.S,) + source.shape[1:], source.dtype)]
    return Job([source], outs, run, {"plane", "chain", "core"}, vmem=(0,), relay=True)


def home_all(place, source):
    def run(at, copies, ins, outs):
        r, s, slot, here = home_of(at)
        _, _, own = visitor_of(at)
        index = copies.slot()
        copies.push(ins[0], outs[0].at[slot], index, (r, s), here == 0)
        copy = pltpu.make_async_copy(ins[0], outs[0].at[slot], copies.recv.at[copies.slot()])
        when(here == 1, copy.start)
        yield "go"
        when(here == 1, copy.wait)
        copies.arrived(outs[0].at[at.r * at.Q + at.q], index, (at.r, at.s), own == 0)
        yield from chain_run(at, copies, outs[0], 1)

    outs = [like((place.R * place.Q,) + source.shape, source.dtype)]
    return Job([source], outs, run, {"home", "chain", "core"}, vmem=(0,), relay=True)


FACTOR = 1.0 / math.sqrt(HD)


def masked_keys(kv_ref, first, kv_s):
    index = lax.broadcasted_iota(jnp.int32, kv_ref.shape, 0)
    kv_s[...] = jnp.where(index >= first, kv_ref[...].astype(F32), 0.0).astype(BF)


def attend_forward(q, kv, q_seg, key_seg, first, block):
    N, QS = q.shape
    M, KS = kv.shape[0], kv.shape[1] // 2
    ahead = M - N
    span = ahead + block
    kv_heads = KS // HD
    groups = QS // KS

    def body(first_ref, q_ref, kv_ref, qs_ref, ks_ref, o_ref, kv_s):
        masked_keys(kv_ref, first_ref[0], kv_s)

        @pl.loop(0, N // block)
        def _(i):
            start = pl.multiple_of(i * block, block)
            here, keys = pl.ds(start, block), pl.ds(start, span)
            row = lax.broadcasted_iota(jnp.int32, (block, span), 0) + ahead
            col = lax.broadcasted_iota(jnp.int32, (block, span), 1)
            open_ = (qs_ref[here, :1] == ks_ref[:1, keys]) & (col <= row)
            open_ = open_ & (col + start >= first_ref[0])
            open_ = jnp.concatenate([open_] * groups, axis=0)
            queries = q_ref[here, :]
            done = []
            for k in range(kv_heads):
                mine = [
                    queries[:, (k * groups + g) * HD : (k * groups + g + 1) * HD]
                    for g in range(groups)
                ]
                key = kv_s[keys, k * HD : (k + 1) * HD]
                value = kv_s[keys, KS + k * HD : KS + (k + 1) * HD]
                score = jnp.where(open_, dot_nt(jnp.concatenate(mine, axis=0), key) * FACTOR, MASKED)
                weight = jnp.exp(score - jnp.max(score, axis=-1, keepdims=True))
                weight = weight / jnp.sum(weight, axis=-1, keepdims=True)
                out = dot(weight.astype(BF), value).astype(BF)
                done.extend(out[g * block : (g + 1) * block] for g in range(groups))
            o_ref[here, :] = jnp.concatenate(done, axis=1)

    return attend_call(
        body, like((N, QS)), [pltpu.VMEM(kv.shape, BF)], 4 * N * span * QS, first, q, kv, q_seg, key_seg
    )


def attend_call(body, outs, scratch, flops, first, *arrays):
    return pl.pallas_call(
        body,
        out_shape=outs,
        in_specs=[pl.BlockSpec(memory_space=pltpu.SMEM)]
        + [pl.BlockSpec(memory_space=pltpu.VMEM) for _ in arrays],
        out_specs=jax.tree.map(lambda _: pl.BlockSpec(memory_space=pltpu.VMEM), outs),
        scratch_shapes=scratch,
        cost_estimate=pl.CostEstimate(flops=flops, bytes_accessed=COST, transcendentals=0),
    )(first, *arrays)


def attend_backward(q, kv, d_o, q_seg, key_seg, first, block):
    N, QS = q.shape
    M, KS = kv.shape[0], kv.shape[1] // 2
    ahead = M - N
    span = ahead + block
    kv_heads = KS // HD
    groups = QS // KS

    def body(first_ref, q_ref, kv_ref, do_ref, qs_ref, ks_ref, dq_ref, dkv_ref, kv_s, *sums):
        masked_keys(kv_ref, first_ref[0], kv_s)
        for total in sums:
            total[...] = jnp.zeros_like(total)

        @pl.loop(0, N // block)
        def _(i):
            start = pl.multiple_of(i * block, block)
            here, keys = pl.ds(start, block), pl.ds(start, span)
            row = lax.broadcasted_iota(jnp.int32, (span, block), 0)
            col = lax.broadcasted_iota(jnp.int32, (span, block), 1) + ahead
            open_ = (ks_ref[keys, :1] == qs_ref[:1, here]) & (row <= col)
            open_ = open_ & (row + start >= first_ref[0])
            open_ = jnp.concatenate([open_] * groups, axis=1)
            queries, pulls = q_ref[here, :], do_ref[here, :]

            def heads_of(values, k):
                return jnp.concatenate(
                    [
                        values[:, (k * groups + g) * HD : (k * groups + g + 1) * HD]
                        for g in range(groups)
                    ],
                    axis=0,
                )

            done = []
            for k in range(kv_heads):
                mine, pull = heads_of(queries, k), heads_of(pulls, k)
                key = kv_s[keys, k * HD : (k + 1) * HD]
                value = kv_s[keys, KS + k * HD : KS + (k + 1) * HD]
                score = jnp.where(open_, dot_nt(key, mine) * FACTOR, MASKED)
                weight = jnp.exp(score - jnp.max(score, axis=0, keepdims=True))
                weight = weight / jnp.sum(weight, axis=0, keepdims=True)
                d_weight = dot_nt(value, pull)
                delta = jnp.sum(weight * d_weight, axis=0, keepdims=True)
                d_score = (weight * (d_weight - delta)).astype(BF)
                sums[k][keys, :] += dot(d_score, mine) * FACTOR
                sums[kv_heads + k][keys, :] += dot(weight.astype(BF), pull)
                dq = dot_tn(d_score, key) * FACTOR
                done.extend(dq[g * block : (g + 1) * block] for g in range(groups))
            dq_ref[here, :] = jnp.concatenate(done, axis=1)

        dkv_ref[...] = jnp.concatenate([total[...] for total in sums], axis=1)

    return attend_call(
        body,
        (like((N, QS), F32), like((M, 2 * KS), F32)),
        [pltpu.VMEM(kv.shape, BF)] + [pltpu.VMEM((M, HD), F32) for _ in range(2 * kv_heads)],
        10 * N * span * QS,
        first,
        q,
        kv,
        d_o,
        q_seg,
        key_seg,
    )


def turned(values, cosine, sine):
    lane = lax.broadcasted_iota(jnp.int32, values.shape, 1)
    ahead = pltpu.roll(values, 2 * HD - HD // 2, 1)
    behind = pltpu.roll(values, HD // 2, 1)
    other = jnp.where(lax.rem(lane, HD) < HD // 2, ahead, behind)
    return values * cosine + other * sine


def head_means(values):
    lane = lax.broadcasted_iota(jnp.int32, values.shape, 1)
    front = lane < HD
    first = jnp.sum(jnp.where(front, values, 0.0), axis=-1, keepdims=True)
    second = jnp.sum(jnp.where(front, 0.0, values), axis=-1, keepdims=True)
    return jnp.where(front, first, second) * (1.0 / HD)


def pairs_of(width):
    return [slice(c, c + 2 * HD) for c in range(0, width, 2 * HD)]


def heads_forward(n3, w, gains, cosine, sine, QS, KS):
    N = n3.shape[0]

    def body(n3_ref, w_ref, gains_ref, cos_ref, sin_ref, pre_ref, q_ref, kv_ref):
        pre_ref[...] = dot(n3_ref[...], w_ref[:, : QS + 2 * KS])

        def normed(cols, row):
            values = pre_ref[:, cols]
            inverse = lax.rsqrt(head_means(values * values) + EPSILON)
            values = values * inverse * gains_ref[row : row + 1, :]
            return turned(values, cos_ref[...], sin_ref[...]).astype(BF)

        for cols in pairs_of(QS):
            q_ref[:, cols] = normed(cols, 0)
        for cols in pairs_of(KS):
            kv_ref[:, cols] = normed(slice(QS + cols.start, QS + cols.stop), 1)
        kv_ref[:, KS:] = pre_ref[:, QS + KS :].astype(BF)

    outs = (like((N, QS + 2 * KS), F32), like((N, QS)), like((N, 2 * KS)))
    return plain_call(body, outs, (), n3, w, gains, cosine, sine)


def heads_backward(d_q, d_kv, got, count, pre, gains, cosine, sine, n3, g3, o, w):
    N, QS = d_q.shape
    KS = d_kv.shape[1] // 2
    D = n3.shape[1]
    W = QS + 2 * KS
    step = 256

    def body(
        count_ref, dq_ref, dkv_ref, got_ref, pre_ref, gains_ref, cos_ref, sin_ref, n3_ref, g3_ref,
        o_ref, w_ref, part_ref, rows_ref, heads_ref, all_ref,
    ):
        d_kv_sum = dkv_ref[...]
        for j in range(got_ref.shape[0]):
            d_kv_sum = d_kv_sum + jnp.where(j < count_ref[0], got_ref[j].astype(F32), 0.0)
        all_ref[:, QS + KS :] = d_kv_sum[:, KS:].astype(BF)

        def back(pull, cols, row):
            values = pre_ref[:, cols]
            inverse = lax.rsqrt(head_means(values * values) + EPSILON)
            pull = turned(pull, cos_ref[...], -sin_ref[...])
            scaled = pull * gains_ref[row : row + 1, :]
            mean = head_means(scaled * values)
            d_values = inverse * scaled - values * (inverse * inverse * inverse) * mean
            all_ref[:, cols] = d_values.astype(BF)
            return jnp.sum(pull * values * inverse, axis=0, keepdims=True)

        of_queries = [back(dq_ref[:, cols], cols, 0) for cols in pairs_of(QS)]
        of_keys = [
            back(d_kv_sum[:, cols], slice(QS + cols.start, QS + cols.stop), 1)
            for cols in pairs_of(KS)
        ]
        heads_ref[0:1, :] = sum(of_queries[1:], of_queries[0])
        heads_ref[1:2, :] = sum(of_keys[1:], of_keys[0])
        values, outputs = all_ref[...], o_ref[...]

        @pl.loop(0, D // step)
        def _(c):
            cols = pl.ds(pl.multiple_of(c * step, step), step)
            part_ref[:, cols] = dot_nt(values, w_ref[cols, :W])
            left = n3_ref[:, cols].astype(F32).T.astype(BF)
            rows_ref[cols, :W] = dot(left, values).astype(BF)
            right = g3_ref[:, cols].astype(F32).T.astype(BF)
            rows_ref[cols, W:] = dot(right, outputs).astype(BF)

    outs = (like((N, D), F32), like((D, W + QS)), like((2, 2 * HD), F32))
    return plain_call(
        body, outs, [pltpu.VMEM((N, W), BF)],
        count, d_q, d_kv, got, pre, gains, cosine, sine, n3, g3, o, w, smem=1,
    )


def plain_call(body, outs, scratch, *arrays, smem=0):
    return pl.pallas_call(
        body,
        out_shape=outs,
        in_specs=[
            pl.BlockSpec(memory_space=pltpu.SMEM if k < smem else pltpu.VMEM)
            for k in range(len(arrays))
        ],
        out_specs=tuple(pl.BlockSpec(memory_space=pltpu.VMEM) for _ in outs),
        scratch_shapes=scratch,
        cost_estimate=pl.CostEstimate(flops=0, bytes_accessed=COST, transcendentals=0),
    )(*arrays)


class Plane:
    def __init__(self, at, copies):
        self.at, self.copies = at, copies

    def swap(self, send, recv):
        at, slots = self.at, [self.copies.slot() for _ in range(TP - 1)]
        for j in range(1, TP):
            other = lax.rem(at.p + j, TP)
            there = (at.r, at.q * TP + other)
            self.copies.push(send.at[other], recv.at[at.p], slots[j - 1], there)
        return functools.partial(self.arrive, recv, slots)

    def gather(self, held):
        at, slots = self.at, [self.copies.slot() for _ in range(TP - 1)]
        for j in range(1, TP):
            there = (at.r, at.q * TP + lax.rem(at.p + j, TP))
            self.copies.push(held.at[at.p], held.at[at.p], slots[j - 1], there)
        return functools.partial(self.arrive, held, slots)

    def mate(self, k):
        p = self.at.p
        if k == 1:
            return p + 1 - 2 * lax.rem(p, 2)
        if k == 2:
            return p + 2 - 4 * (p // 2)
        return TP - 1 - p if k == TP - 1 else p

    def to_mate(self, source, held, k):
        at, slot = self.at, self.copies.slot()
        there = (at.r, at.q * TP + self.mate(k))
        self.copies.push(source, held.at[k], slot, there)
        return functools.partial(self.copies.arrived, held.at[k], slot, (at.r, at.s))

    def spread_mates(self, held):
        return [self.to_mate(held.at[0], held, k) for k in range(1, TP)]

    def sum_mates(self, own, recv):
        for k in range(1, TP):
            own = own + recv[k].astype(F32)
        return own

    def arrive(self, held, slots):
        at = self.at
        for j in range(1, TP):
            origin = lax.rem(at.p + TP - j, TP)
            self.copies.arrived(held.at[origin], slots[j - 1], (at.r, at.s))

    def settle(self, own, recv, n):
        total = own[pl.ds(pl.multiple_of(self.at.p * n, n), n), :]
        for j in range(1, TP):
            total = total + recv[lax.rem(self.at.p + j, TP)].astype(F32)
        return total


def columns_of(count, width, action):
    @pl.loop(0, count)
    def _(c):
        action(pl.ds(pl.multiple_of(c * width, width), width))


def rows_of(span, action):
    first, count = span

    @pl.loop(0, count // 64)
    def _(i):
        action(pl.ds(pl.multiple_of(first + i * 64, 64), 64))


def activate(gu, act, span, FS):
    def go(rows):
        gate, up = gu[rows, :FS], gu[rows, FS:]
        act[rows, :] = (jax.nn.silu(gate) * up).astype(BF)

    rows_of(span, go)


def deactivate(gu, d_act, dgu, span, FS):
    def go(rows):
        gate, up, pull = gu[rows, :FS], gu[rows, FS:], d_act[rows, :]
        sigma = jax.nn.sigmoid(gate)
        dgu[rows, :FS] = (pull * up * sigma * (1.0 + gate * (1.0 - sigma))).astype(BF)
        dgu[rows, FS:] = (pull * (gate * sigma)).astype(BF)

    rows_of(span, go)


def multiply(held, weights, out, span, parts):
    first, count = span
    n, D = held.shape[1:]
    values = held[first // n : (first + count) // n].reshape(count, D)
    rows = pl.ds(first, count)

    def go(cols):
        out[rows, cols] = dot(values, weights[:, cols])

    columns_of(parts, weights.shape[1] // parts, go)


def project(left, weights, part, span, send=None, order=None):
    first, count = span
    step = 256
    rows = pl.ds(first, count)
    n = send.shape[1] if send is not None else count

    def go(cols):
        out = dot_nt(left[rows, :], weights[cols, :])
        part[rows, cols] = out
        if send is not None:
            for k in range(first // n, (first + count) // n):
                block = out[k * n - first : (k + 1) * n - first].astype(BF)
                send[k if order is None else order[k], :, cols] = block

    columns_of(weights.shape[0] // step, step, go)


def feed_kernel(place, ident, mode, arrays, D, FS, n, side=0):
    N = n * TP
    R = place.R
    half = D // R
    W = 2 * FS if mode == "both" else 3 * FS
    forward, backward = mode in ("fwd", "both"), mode in ("both", "bwd")
    VM, HB = pltpu.VMEM, pl.ANY
    ins, scratch, outs = {}, {}, {}
    ins["weights"] = HB
    if mode == "fwd":
        ins.update(a_g=VM, h_in=VM, gain_next=VM)
        outs.update(
            h_out=((n, D), F32, VM), next_g=((TP, n, D), BF, VM), gu_out=((N, 2 * FS), F32, HB)
        )
    else:
        ins.update(first_part=VM, h_in=VM, gain=VM)
        outs.update(
            g_out=((n, D), F32, VM),
            next_g=((TP, n, D), BF, VM),
            d_gain=((1, D), F32, VM),
            half_out=((half, W), BF, VM),
        )
        scratch.update(
            first_send=((TP, n, D), BF),
            first_got=((TP, n, D), BF),
            a_v=((TP, n, D), BF),
            e_v=((TP, n, D), BF),
            d_act=((N, FS), F32),
            dgu=((N, 2 * FS), BF),
            grad_send=((R - 1, half, W), BF),
            grad_got=((R - 1, half, W), BF),
        )
    if mode == "both":
        ins.update(e_g=HB, e_own=VM, down=HB)
        down_piece = (half // place.Q, FS)
        outs.update(
            mid_out=((n, D), F32, VM),
            o_send=((TP, n, D), BF, VM),
            o_base=((n, D), F32, VM),
            down_out=((place.Q,) + down_piece, BF, VM),
        )
        scratch.update(
            down_send=((R - 1, half, FS), BF),
            down_got=((R - 1, half, FS), BF),
            down_half=((place.Q,) + down_piece, BF),
        )
    if mode == "bwd":
        ins.update(a_g=HB, gu_in=HB, g_in=VM, h_before=VM, gain_before=VM)
        piece = (half // place.Q, side)
        ins.update(side_in=VM)
        outs.update(
            d_gain_before=((1, D), F32, VM),
            halo=((HALO, D), BF, VM),
            side_out=((place.Q,) + piece, BF, VM),
        )
        scratch.update(side_got=((R - 1, half, side), BF), side_half=((place.Q,) + piece, BF))
    scratch.update(
        w=((D, 2 * FS), BF),
        wd=((D, FS), BF),
        gu=((N, 2 * FS), F32),
        act=((N, FS), BF),
        part=((N, D), F32),
        send=((TP, n, D), BF),
        got=((TP, n, D), BF),
    )
    in_names, out_names, scratch_names = list(ins), list(outs), list(scratch)
    kinds = {"plane"}
    if backward:
        kinds.add("core")
    if mode == "bwd":
        kinds.update({"back", "zall"})
    if mode == "both":
        kinds.add("zall")
    unit = D // (R * place.Q)
    sems = 32 + 3 * R + 4 * place.Q + 3 * R * place.Q

    def body(*refs):
        names = in_names + out_names + scratch_names
        v = dict(zip(names, refs))
        at = place.here()
        copies = Copies(refs[len(names)], refs[len(names) + 1])
        plane = Plane(at, copies)
        loads = refs[len(names) + 2]
        pending = {}

        def load(name, src, dst):
            pending[name] = pltpu.make_async_copy(src, dst, loads.at[len(pending)])
            pending[name].start()

        def load_blocks(name, source, target):
            for k in range(TP):
                load(name + str(k), source.at[plane.mate(k)], target.at[k])

        def loaded(*names):
            for name in names:
                pending[name].wait()

        def loaded_blocks(name):
            loaded(*[name + str(k) for k in range(TP)])

        if mode == "both":
            load("w", v["weights"], v["w"])
            load_blocks("e", v["e_g"], v["e_v"])
            own_rows = pl.ds(pl.multiple_of((at.r * at.Q + at.q) * unit, unit), unit)
            load("wd", v["down"], v["wd"].at[own_rows])
        else:
            load("w", v["weights"].at[:, : 2 * FS], v["w"])
            load("wd", v["weights"].at[:, 2 * FS :], v["wd"])
        if mode == "bwd":
            for k in range(TP):
                rows = pl.ds(pl.multiple_of(plane.mate(k) * n, n), n)
                load("gu%d" % k, v["gu_in"].at[rows], v["gu"].at[pl.ds(k * n, n)])
            load_blocks("a", v["a_g"], v["a_v"])
        meet(at, kinds)
        w, wd, gu, act = (v[k] for k in ("w", "wd", "gu", "act"))
        part, send, got = (v[k] for k in ("part", "send", "got"))

        def along_line(source, target):
            slots = [copies.slot() for _ in range(at.Q - 1)]
            for j in range(1, at.Q):
                other = lax.rem(at.q + j, at.Q)
                there = (at.r, other * TP + at.p)
                copies.push(source.at[other], target.at[at.q], slots[j - 1], there)
            target[at.q] = source[at.q]
            return slots

        def line_done(target, slots):
            for j in range(1, at.Q):
                origin = lax.rem(at.q + at.Q - j, at.Q)
                copies.arrived(target.at[origin], slots[j - 1], (at.r, at.s))

        def turned_rows(held, j):
            first_col = lax.rem(at.r + j, R) * half
            cols = pl.ds(pl.multiple_of(first_col, 128), half)
            return held[:, :, cols].reshape(N, half).astype(F32).T.astype(BF)

        if mode != "fwd":
            first = v["first_part"]
            mine = [pl.ds(pl.multiple_of(plane.mate(k) * n, n), n) for k in range(TP)]
            waits = []
            for k in range(1, TP):
                v["first_send"][k] = first[mine[k], :].astype(BF)
                waits.append(plane.to_mate(v["first_send"].at[k], v["first_got"], k))
        if mode == "fwd":
            pending["w"].wait()
            multiply(v["a_g"], w, gu, (0, N), 3)
            save = pltpu.make_async_copy(gu, v["gu_out"], loads.at[len(pending)])
            save.start()
            activate(gu, act, (0, N), FS)
            pending["wd"].wait()
            project(act, wd, part, (0, N), send)
            wait = plane.swap(send, got)
            wait()
            h_out = v["h_in"][...] + plane.settle(part, got, n)
            v["h_out"][...] = h_out
            v["next_g"][at.p] = (h_out * inverse_rms(h_out) * v["gain_next"][...]).astype(BF)
            wait = plane.gather(v["next_g"])
            wait()
            save.wait()
            copies.drain()
            return
        everything, own, near, far = (0, N), (0, n), (n, 2 * n), (3 * n, n)
        d_act, dgu = v["d_act"], v["dgu"]
        if mode == "both":
            loaded("wd")
            steps = chain_run(at, copies, wd, unit)
            next(steps)
            next(steps)
            for wait in waits:
                wait()
            h = v["h_in"][...] + plane.sum_mates(first[mine[0], :], v["first_got"])
            v["mid_out"][...] = h
            v["a_v"][0] = (h * inverse_rms(h) * v["gain"][...]).astype(BF)
            waits = plane.spread_mates(v["a_v"])
            for _ in range(at.Q - 3):
                next(steps)
            loaded("w")
            loaded_blocks("e")
            for span, awaited in ((own, ()), (near, waits[:2]), (far, waits[2:])):
                for wait in awaited:
                    wait()
                multiply(v["a_v"], w, gu, span, 3)
                activate(gu, act, span, FS)
            for _ in steps:
                pass
            down_slots = [copies.slot() for _ in range(R - 1)]
            for j in range(1, R):
                v["down_send"][j - 1] = dot(turned_rows(v["e_v"], j), act[...]).astype(BF)
                there = (lax.rem(at.r + j, R), at.s)
                copies.push(v["down_send"].at[j - 1], v["down_got"].at[j - 1], down_slots[j - 1], there)
            total = dot(turned_rows(v["e_v"], 0), act[...])
            for j in range(1, R):
                copies.arrived(v["down_got"].at[j - 1], down_slots[j - 1], (at.r, at.s))
                total = total + v["down_got"][j - 1].astype(F32)
            v["down_half"][...] = total.astype(BF).reshape(v["down_half"].shape)
            line_slots = along_line(v["down_half"], v["down_out"])
            multiply(v["e_v"], wd, d_act, everything, 3)
            waits = []
            for span, slots in ((near, (1, 2)), (far, (3,))):
                deactivate(gu, d_act, dgu, span, FS)
                project(dgu, w, part, span, send)
                waits.extend(plane.to_mate(send.at[k], got, k) for k in slots)
            deactivate(gu, d_act, dgu, own, FS)
            project(dgu, w, part, own)
        else:
            side_slots = [copies.slot() for _ in range(R - 1)]
            for j in range(1, R):
                other = lax.rem(at.r + j, R)
                copies.push(
                    v["side_in"].at[other], v["side_got"].at[j - 1], side_slots[j - 1], (other, at.s)
                )
            loaded_blocks("gu")
            activate(gu, act, everything, FS)
            for wait in waits:
                wait()
            h = v["h_in"][...]
            before = v["h_before"][...]
            r_before = inverse_rms(before)
            d_normed = plane.sum_mates(first[mine[0], :], v["first_got"])
            v["d_gain_before"][...] = jnp.sum(d_normed * before * r_before, axis=0, keepdims=True)
            g_mid = v["g_in"][...] + rms_pull(d_normed, before, r_before, v["gain_before"][...])
            v["g_out"][...] = g_mid
            v["e_v"][0] = g_mid.astype(BF)
            waits = plane.spread_mates(v["e_v"])
            loaded("w", "wd")
            loaded_blocks("a")
            total = v["side_in"][at.r].astype(F32)
            for j in range(1, R):
                copies.arrived(v["side_got"].at[j - 1], side_slots[j - 1], (at.r, at.s))
                total = total + v["side_got"][j - 1].astype(F32)
            v["side_half"][...] = total.astype(BF).reshape(v["side_half"].shape)
            line_slots = along_line(v["side_half"], v["side_out"])
            returns = []
            for span, awaited, slots in (
                (own, (), ()),
                (near, waits[:2], (1, 2)),
                (far, waits[2:], (3,)),
            ):
                for wait in awaited:
                    wait()
                multiply(v["e_v"], wd, d_act, span, 3)
                deactivate(gu, d_act, dgu, span, FS)
                project(dgu, w, part, span, send if slots else None)
                returns.extend(plane.to_mate(send.at[k], got, k) for k in slots)
            waits = returns
        values, pulls = v["a_v"], v["e_v"]

        slots = [copies.slot() for _ in range(R - 1)]
        for j in range(1, R):
            left = turned_rows(values, j)

            def put(cols, left=left, j=j):
                v["grad_send"][j - 1, :, cols] = dot(left, v["dgu"][:, cols]).astype(BF)

            columns_of(3, 2 * FS // 3, put)
            if mode == "bwd":
                v["grad_send"][j - 1, :, 2 * FS :] = dot(turned_rows(pulls, j), act[...]).astype(BF)
            other = lax.rem(at.r + j, R)
            copies.push(
                v["grad_send"].at[j - 1], v["grad_got"].at[j - 1], slots[j - 1], (other, at.s)
            )
        for wait in waits:
            wait()
        d_normed = plane.sum_mates(part[:n, :], got)
        r = inverse_rms(h)
        base = v["e_own"][...].astype(F32) if mode == "both" else v["g_out"][...]
        v["d_gain"][...] = jnp.sum(d_normed * h * r, axis=0, keepdims=True)
        g_new = base + rms_pull(d_normed, h, r, v["gain"][...])
        v["g_out"][...] = g_new
        v["next_g"][at.p] = g_new.astype(BF)
        wait = plane.gather(v["next_g"])
        if mode == "bwd":
            back = [copies.slot() for _ in range(TP)]
            for j in range(TP):
                copies.push(
                    v["next_g"].at[at.p, pl.ds(0, HALO)],
                    v["halo"],
                    back[j],
                    (at.r, (at.q - 1) * TP + j),
                    (at.p == 0) & (at.q > 0),
                    back[0],
                )
        if mode == "both":
            project(act, wd, part, everything, v["o_send"], [plane.mate(k) for k in range(TP)])
            v["o_base"][...] = h + part[:n, :]
        left = turned_rows(values, 0)
        for j in range(1, R):
            copies.arrived(v["grad_got"].at[j - 1], slots[j - 1], (at.r, at.s))

        def finish(cols):
            total = dot(left, v["dgu"][:, cols])
            for j in range(1, R):
                total = total + v["grad_got"][j - 1, :, cols].astype(F32)
            v["half_out"][:, cols] = total.astype(BF)

        columns_of(3, 2 * FS // 3, finish)
        if mode == "bwd":
            total = dot(turned_rows(pulls, 0), act[...])
            for j in range(1, R):
                total = total + v["grad_got"][j - 1, :, 2 * FS :].astype(F32)
            v["half_out"][:, 2 * FS :] = total.astype(BF)
        wait()
        if mode == "bwd":
            copies.arrived(v["halo"], back[0], (at.r, at.s), at.q < at.Q - 1)
            line_done(v["side_out"], line_slots)
        if mode == "both":
            line_done(v["down_out"], line_slots)
        copies.drain()

    results = pl.pallas_call(
        body,
        out_shape=tuple(like(outs[k][0], outs[k][1]) for k in out_names),
        in_specs=[pl.BlockSpec(memory_space=ins[k]) for k in in_names],
        out_specs=tuple(pl.BlockSpec(memory_space=outs[k][2]) for k in out_names),
        scratch_shapes=[pltpu.VMEM(*scratch[k]) for k in scratch_names]
        + [pltpu.SemaphoreType.DMA((sems,)), pltpu.SemaphoreType.DMA((sems,))]
        + [pltpu.SemaphoreType.DMA((12,))],
        compiler_params=pltpu.CompilerParams(collective_id=ident, has_side_effects=True),
        cost_estimate=pl.CostEstimate(flops=0, bytes_accessed=COST, transcendentals=0),
        name="feed_%s" % mode,
    )(*[arrays[k] for k in in_names])
    return dict(zip(out_names, results))


def doc_info(positions, lengths):
    doc_ends = jnp.cumsum(lengths, dtype=jnp.int32)
    passed = positions[:, None] >= doc_ends[None, :]
    segment = jnp.sum(passed.astype(jnp.int32), axis=1, dtype=jnp.int32)
    opening = jnp.sum(jnp.where(passed, lengths[None, :], 0), axis=1, dtype=jnp.int32)
    return (segment, positions - opening)


def inverse_rms(values):
    return lax.rsqrt(jnp.mean(values * values, axis=-1, keepdims=True) + EPSILON)


def rms_pull(upstream, values, inverse, norm_gain):
    scaled = upstream * norm_gain
    product_mean = jnp.mean(scaled * values, axis=-1, keepdims=True)
    return inverse * scaled - values * (inverse * inverse * inverse) * product_mean


def settle(own, arrived, p):
    index = jnp.arange(TP, dtype=jnp.int32)[:, None, None]
    others = jnp.where(index == p, 0.0, arrived.astype(F32))
    mine = lax.dynamic_index_in_dim(own, p, 0, keepdims=False)
    return mine + jnp.sum(others, axis=0)


def per_device(
    place,
    tokens,
    doc_lengths,
    cotangent,
    gain_conv,
    w_in,
    kernel,
    w_mix,
    gain_ffa,
    gate_a,
    up_a,
    down_a,
    gain_att,
    w_query,
    w_key,
    w_value,
    head_gains,
    w_attout,
    gain_ffb,
    gate_b,
    up_b,
    down_b,
):
    R, S, Q = place.R, place.S, place.Q
    n, D = tokens.shape[1], tokens.shape[2]
    shard = w_in.shape[0]
    FS = gate_a.shape[1] // TP
    CS = D // TP
    QS, KS = H * HD // TP, KVH * HD // TP
    taps = kernel.shape[0]
    N = n * TP
    r, s = lax.axis_index("rows"), lax.axis_index("seq")
    q, p = s // TP, lax.rem(s, TP)
    lengths = doc_lengths[0]

    def slices(weight):
        return weight.reshape(shard, TP, -1).transpose(1, 0, 2)

    def joined(*weights):
        return jnp.concatenate([slices(weight) for weight in weights], axis=2)

    columns = [[a * S + b * TP + c for a in range(R) for b in range(Q)] for c in range(TP)]
    lines = [[b * TP + c for b in range(Q)] for c in range(TP)]

    def gather_rest(plane):
        flat = plane.reshape(TP * shard, -1)
        return lax.all_gather(
            flat, ("rows", "seq"), axis=0, tiled=True, axis_index_groups=columns
        )

    def by_row(grads):
        return grads.astype(BF).reshape(R, S * shard, -1)

    def own_rows(rows, came, *later):
        return lax.optimization_barrier((collect(rows, came, r).astype(BF),) + later)

    def reduce_line(half):
        part = lax.psum_scatter(
            half, "seq", scatter_dimension=0, tiled=True, axis_index_groups=lines
        )
        return part.reshape(TP, shard, part.shape[1])

    in_cut = w_in.reshape(shard, 3, TP, CS).transpose(2, 0, 1, 3).reshape(TP, shard, 3 * CS)
    small = jnp.stack([gain_conv, gain_ffa, gain_att, gain_ffb] + [kernel[i] for i in range(taps)])
    small = jnp.pad(small, ((0, 16 - 4 - taps), (0, 128 - shard)))
    small = jnp.broadcast_to(small[None], (TP, 16, 128))

    mine = tokens[0]
    (tok_g,), (halo_a, halo_b), (in_g,), (mix_g,), (small_g,), (ffa_p,) = exchange(
        place,
        0,
        [
            gather_plane(mine),
            halo_tokens(mine),
            spread_all(place, in_cut),
            home_all(place, w_mix),
            spread_all(place, small),
            spread(joined(gate_a, up_a, down_a.T)),
        ],
    )
    wa = gather_rest(ffa_p)
    w_mix_s = mix_g.reshape(CS, D)
    vectors = small_g[:, : 4 + taps, :shard].transpose(1, 0, 2).reshape(4 + taps, D).astype(F32)
    g_conv, g_ffa, g_att, g_ffb = (vectors[i] for i in range(4))
    kernel_f = lax.dynamic_slice_in_dim(vectors[4:], p * CS, CS, 1)
    w_in_s = in_g.reshape(D, 3 * CS)

    def own(parts, index):
        return lax.dynamic_index_in_dim(parts, index, 0, keepdims=False).astype(F32)

    def collect(parts, came, index):
        slot = jnp.arange(came.shape[0], dtype=jnp.int32).reshape((-1,) + (1,) * (came.ndim - 1))
        mine_part = lax.dynamic_index_in_dim(parts, index, 0, keepdims=True).astype(F32)
        return jnp.sum(jnp.where(slot == index, mine_part, came.astype(F32)), axis=0)

    def after_core(parts, came):
        summed = collect(parts, came, r)
        return summed.reshape((Q, TP) + summed.shape[1:])

    def after_line(parts, came):
        return collect(parts, came, q)

    total = S * n
    pos_ext = q * N - HALO + jnp.arange(N + 2 * HALO, dtype=jnp.int32)
    seg_ext, rel_ext = doc_info(pos_ext, lengths)
    valid = ((pos_ext >= 0) & (pos_ext < total))[:, None]
    x_ext = jnp.concatenate([halo_a, tok_g.reshape(N, D), halo_b], axis=0)
    x_ext = jnp.where(valid, x_ext, jnp.zeros_like(x_ext)).astype(F32)
    r0_ext = inverse_rms(x_ext)
    n1_ext = (x_ext * r0_ext * g_conv).astype(BF)
    z_ext = dot(n1_ext, w_in_s)
    b_ext, c_ext, v_ext = z_ext[:, :CS], z_ext[:, CS : 2 * CS], z_ext[:, 2 * CS :]
    u_ext = lax.optimization_barrier((b_ext * v_ext).astype(BF)).astype(F32)
    span = slice(HALO, HALO + N)
    same = [
        (seg_ext[HALO - 2 + k : HALO - 2 + k + N] == seg_ext[span]).astype(F32)[:, None]
        for k in range(taps)
    ]
    near = [u_ext[HALO - 2 + k : HALO - 2 + k + N] for k in range(taps)]
    conv = kernel_f[0] * near[0] * same[0]
    for k in range(1, taps):
        conv = conv + kernel_f[k] * near[k] * same[k]
    m_bf = (c_ext[span] * conv).astype(BF)
    part = dot(m_bf, w_mix_s).reshape(TP, n, D)
    (got,), (att_p,), (ffb_p,), (down_p,) = exchange(
        place,
        1,
        [
            swap_plane(part.astype(BF)),
            spread(joined(w_query, w_key, w_value, w_attout.T)),
            spread(joined(gate_b, up_b)),
            spread(joined(down_b.T)),
        ],
    )
    w_att = gather_rest(att_p)
    wb = gather_rest(ffb_p)
    x0 = mine.astype(F32)
    h1 = x0 + settle(part, got, p)

    r1 = inverse_rms(h1)
    a1 = (h1 * r1 * g_ffa).astype(BF)
    ((a1_g,),) = exchange(place, 2, [gather_plane(a1)])
    a1_g = a1_g.reshape(N, D)

    g_row = {name: value[None] for name, value in
             (("ffa", g_ffa), ("att", g_att), ("ffb", g_ffb))}
    fed = feed_kernel(
        place,
        3,
        "fwd",
        {"weights": wa, "a_g": a1_g.reshape(TP, n, D), "h_in": h1, "gain_next": g_row["att"]},
        D,
        FS,
        n,
    )
    h2, n3_g, gu1 = fed["h_out"], fed["next_g"], fed["gu_out"]

    n3_g = n3_g.reshape(N, D)
    w_out = w_att[:, QS + 2 * KS :]
    lane = jnp.arange(2 * HD, dtype=jnp.int32)
    frequency = jnp.exp(jnp.arange(HD // 2, dtype=F32) * (-2.0 * math.log(THETA) / HD))
    angles = rel_ext[span].astype(F32)[:, None] * jnp.tile(frequency, 4)[None, :]
    cosine = jnp.cos(angles)
    sine = jnp.sin(angles) * jnp.where(lane % HD < HD // 2, -1.0, 1.0)
    head_rows = jnp.tile(head_gains.astype(F32), (1, 2))
    pre, q_bf, kv_bf = heads_forward(n3_g, w_att, head_rows, cosine, sine, QS, KS)
    e_bf = cotangent[0]
    (kv_w,), (e_g,) = exchange(
        place,
        5,
        [window_forward(place, kv_bf), gather_plane(e_bf)],
    )
    reach = Q // 2 + 1
    kv_all = kv_w.reshape(reach * N, 2 * KS)
    q_seg = seg_ext[span]
    key_seg, _ = doc_info((q - reach + 1) * N + jnp.arange(reach * N, dtype=jnp.int32), lengths)
    first = jnp.maximum((reach - 1 - q) * N, 0).astype(jnp.int32).reshape(1)
    seg_col, seg_row = (jnp.broadcast_to(q_seg[:, None], (N, 128)), jnp.broadcast_to(q_seg, (8, N)))
    key_col = jnp.broadcast_to(key_seg[:, None], (reach * N, 128))
    key_row = jnp.broadcast_to(key_seg, (8, reach * N))
    o_bf = attend_forward(q_bf, kv_all, seg_col, key_row, first, 128)
    fed = feed_kernel(
        place,
        8,
        "both",
        {
            "weights": wb,
            "down": down_p.reshape(TP * shard, FS),
            "first_part": dot_nt(o_bf, w_out),
            "h_in": h2,
            "gain": g_row["ffb"],
            "e_g": e_g.reshape(TP, n, D),
            "e_own": e_bf,
        },
        D,
        FS,
        n,
    )
    full_down = jnp.sum(fed["down_out"].astype(F32), axis=0).astype(BF).reshape(TP, shard, FS)
    h3, g3, g3_g, half_b = fed["mid_out"], fed["g_out"], fed["next_g"], fed["half_out"]
    d_gain = {}
    d_gain["ffb"] = fed["d_gain"][0]

    g3_g = g3_g.reshape(N, D)
    d_o = dot(g3_g, w_out).astype(BF)
    d_q, d_kv = attend_backward(q_bf, kv_all, d_o, seg_row, key_col, first, 128)
    d_kv = d_kv.reshape(reach, N, 2 * KS)
    (got_kv,), (got_o,) = exchange(
        place, 10, [window_backward(place, d_kv.astype(BF)), swap_plane(fed["o_send"])]
    )
    index = jnp.arange(TP, dtype=jnp.int32)[:, None, None]
    h4 = fed["o_base"] + jnp.sum(jnp.where(index == p, 0.0, got_o.astype(F32)), axis=0)
    mixed = h4.astype(BF)[None]
    count = jnp.clip(Q - 1 - q, 0, reach - 1).astype(jnp.int32).reshape(1)
    half_b, got_kv = lax.optimization_barrier((half_b, got_kv))
    full_b = reduce_line(half_b)
    part, rows_att, d_heads = heads_backward(
        d_q, d_kv[-1], got_kv, count, pre, head_rows, cosine, sine, n3_g, g3_g, o_bf, w_att
    )
    d_heads = jnp.sum(d_heads.reshape(2, 2, HD), axis=1)
    rows_att = by_row(rows_att)
    fed = feed_kernel(
        place,
        13,
        "bwd",
        {
            "weights": wa,
            "first_part": part,
            "h_in": h1,
            "gain": g_row["ffa"],
            "a_g": a1_g.reshape(TP, n, D),
            "gu_in": gu1,
            "g_in": g3,
            "h_before": h2,
            "gain_before": g_row["att"],
            "side_in": rows_att,
        },
        D,
        FS,
        n,
        rows_att.shape[2],
    )
    full_att = jnp.sum(fed["side_out"].astype(F32), axis=0).astype(BF).reshape(TP, shard, -1)
    g1, g1_g, g1_halo = fed["g_out"], fed["next_g"], fed["halo"]
    d_gain["att"], d_gain["ffa"] = fed["d_gain_before"][0], fed["d_gain"][0]
    full_a = reduce_line(fed["half_out"])

    g1_halo = jnp.where(q < Q - 1, g1_halo, jnp.zeros_like(g1_halo))
    g1_ext = jnp.concatenate([g1_g.reshape(N, D), g1_halo], axis=0)
    d_m = dot_nt(g1_ext, w_mix_s)
    d_mix_s = dot_tn(m_bf, g1_ext[:N])
    d_c = d_m[:N] * conv
    d_conv = lax.optimization_barrier((d_m * c_ext[HALO:]).astype(BF)).astype(F32)
    d_kernel = jnp.stack(
        [jnp.sum(d_conv[:N] * near[k] * same[k], axis=0) for k in range(taps)]
    )
    d_u = jnp.zeros((N, CS), F32)
    for k in range(taps):
        ahead = taps - 1 - k
        match = (seg_ext[HALO + ahead : HALO + ahead + N] == seg_ext[span]).astype(F32)[:, None]
        d_u = d_u + kernel_f[k] * d_conv[ahead : ahead + N] * match
    d_z = jnp.concatenate([d_u * v_ext[span], d_c, d_u * b_ext[span]], axis=1).astype(BF)
    rows_in = dot_tn(n1_ext[span], d_z).astype(BF).reshape(R, S, shard, 3 * CS)
    rows_mix = d_mix_s.astype(BF).reshape(R, Q, shard, D)
    d_n1 = dot_nt(d_z, w_in_s)
    d_gain["conv"] = jnp.sum(d_n1 * x_ext[span] * r0_ext[span], axis=0)
    part = d_n1.reshape(TP, n, D)
    d_taps = lax.dynamic_update_slice(jnp.zeros((taps, D), F32), d_kernel, (0, p * CS))
    lanes = jnp.concatenate(
        [jnp.stack([d_gain["conv"], d_gain["ffa"], d_gain["att"], d_gain["ffb"]]), d_taps]
    )
    lanes = lanes.reshape(4 + taps, R * S, shard).transpose(1, 0, 2)
    lanes = jnp.pad(lanes, ((0, 0), (0, 0), (0, 128 - shard)))
    heads_row = jnp.broadcast_to(d_heads.reshape(1, 1, 2 * HD), (R * S, 1, 2 * HD))
    tiny = jnp.concatenate([lanes, heads_row], axis=1)
    tiny_rows = tiny.reshape(R, S, 4 + taps + 1, 128)
    (got,), (core_in,), (core_mix,), (core_t,) = exchange(
        place,
        15,
        [
            swap_plane(part.astype(BF)),
            swap_core(rows_in),
            swap_core(rows_mix),
            swap_core(tiny_rows),
        ],
    )
    d_normed = settle(part, got, p)
    g0 = g1 + rms_pull(d_normed, x0, inverse_rms(x0), g_conv)
    d_tokens = g0.astype(BF)[None]

    tiny_line = after_core(tiny_rows, core_t)
    line_in = after_core(rows_in, core_in).astype(BF)
    line_mix = collect(rows_mix, core_mix, r).astype(BF)
    FF = TP * FS
    by_weight = [(k * FS, FS, k, 0) for k in range(3)]
    by_head = [(0, QS, 0, 0), (QS, KS, 1, 0), (QS + KS, KS, 2, 0), (QS + 2 * KS, QS, 3, 0)]
    (got_in,), (got_mix,), (line_t,), (plane_b,), (plane_down,), (plane_att,) = exchange(
        place,
        16,
        [
            swap_line(line_in),
            swap_line(line_mix),
            swap_line(tiny_line),
            swap_plane(full_b),
            swap_plane(full_down),
            swap_plane(full_att),
        ],
    )
    tiny_full = after_line(tiny_line, line_t)
    full_in = after_line(line_in, got_in).astype(BF)
    full_mix = after_line(line_mix, got_mix).astype(BF)
    (plane_in,), (plane_a,), (plane_t,), (mix_back,) = exchange(
        place,
        17,
        [swap_plane(full_in), swap_plane(full_a), swap_plane(tiny_full), home_back(full_mix)],
    )
    FF = TP * FS
    by_weight = [(k * FS, FS, k, 0) for k in range(3)]
    by_gate = [(k * CS, CS, 0, k * D) for k in range(3)]
    by_head = [(0, QS, 0, 0), (QS, KS, 1, 0), (QS + KS, KS, 2, 0), (QS + 2 * KS, QS, 3, 0)]
    ready = finish(
        place,
        place.here(),
        [
            (full_b, plane_b, by_weight[:2], [(shard, FF)] * 2),
            (full_down, plane_down, by_weight[:1], [(shard, FF)]),
            (full_att, plane_att, by_head, [(shard, TP * k) for k in (QS, KS, KS, QS)]),
            (full_a, plane_a, by_weight, [(shard, FF)] * 3),
            (full_in, plane_in, by_gate, [(shard, 3 * D)]),
        ],
        (tiny_full, plane_t),
        (full_mix, mix_back),
        taps,
    )
    out_b, out_att, out_a, (out_in,) = ready[:3], ready[3:7], ready[7:10], ready[10:11]
    of_conv, of_ffa, of_att, of_ffb, of_taps, d_heads, out_mix = ready[11:]
    return (
        mixed,
        d_tokens,
        of_conv[0],
        out_in,
        of_taps,
        out_mix,
        of_ffa[0],
        out_a[0],
        out_a[1],
        out_a[2].T,
        of_att[0],
        out_att[0],
        out_att[1],
        out_att[2],
        d_heads,
        out_att[3].T,
        of_ffb[0],
        out_b[0],
        out_b[1],
        out_b[2].T,
    )


def solution(mesh):
    place = Place(mesh.shape["rows"], mesh.shape["seq"])
    whole = ("rows", "seq")
    wide, first, second = P("rows", "seq", None), P(whole, None), P(None, whole)
    in_specs = (
        (wide, P("rows", None), wide, P(whole), first, second, first)
        + (P(whole), first, first, second)
        + (P(whole), first, first, first, P(), second)
        + (P(whole), first, first, second)
    )
    out_specs = (
        (wide, wide, P(whole), first, second, first)
        + (P(whole), first, first, second)
        + (P(whole), first, first, first, P(), second)
        + (P(whole), first, first, second)
    )
    return jax.shard_map(
        functools.partial(per_device, place),
        mesh=mesh,
        in_specs=in_specs,
        out_specs=out_specs,
        check_vma=False,
    )
```

```python
import functools
import math

import jax
import jax.numpy as jnp
from jax import lax
from jax.experimental import pallas as pl
from jax.experimental.pallas import tpu as pltpu
from jax.sharding import PartitionSpec as P

H = 16
KVH = 8
HD = 64
TP = 4
HALO = 16
COST = 1_000_000

EPSILON = 1e-05
THETA = 1000000.0
MASKED = -1e30
MESH_ID = pl.DeviceIdType.MESH
BF = jnp.bfloat16
F32 = jnp.float32


def dot(left, right):
    return jnp.dot(left, right, preferred_element_type=F32)


def dot_tn(left, right):
    return lax.dot_general(left, right, (((0,), (0,)), ((), ())), preferred_element_type=F32)


def dot_nt(left, right):
    return lax.dot_general(left, right, (((1,), (1,)), ((), ())), preferred_element_type=F32)


class Place:
    def __init__(self, rows, seq):
        self.R, self.S = rows, seq
        self.Q = seq // TP

    def here(self):
        here = Place(self.R, self.S)
        here.r = lax.axis_index("rows")
        here.s = lax.axis_index("seq")
        here.q = here.s // TP
        here.p = lax.rem(here.s, TP)
        return here


class Copies:
    def __init__(self, send, recv):
        self.send, self.recv, self.count, self.sent = send, recv, 0, []

    def slot(self):
        self.count += 1
        return self.count - 1

    def remote(self, src, dst, slot, where, recv_slot=None):
        return pltpu.make_async_remote_copy(
            src_ref=src,
            dst_ref=dst,
            send_sem=self.send.at[slot],
            recv_sem=self.recv.at[slot if recv_slot is None else recv_slot],
            device_id=where,
            device_id_type=MESH_ID,
        )

    def push(self, src, dst, slot, where, cond=None, recv_slot=None):
        copy = self.remote(src, dst, slot, where, recv_slot)
        when(cond, copy.start)
        self.sent.append((copy.wait_send, cond))

    def arrived(self, dst, slot, where, cond=None):
        copy = self.remote(dst, dst, slot, where)
        when(cond, copy.wait_recv)

    def local(self, src, dst):
        slot = self.slot()
        copy = pltpu.make_async_copy(src, dst, self.recv.at[slot])
        copy.start()
        self.sent.append((copy.wait, None))

    def drain(self):
        for wait, cond in self.sent:
            when(cond, wait)


def when(cond, action):
    if cond is None:
        action()
    else:
        pl.when(cond)(lambda: action())


class Job:
    def __init__(
        self, ins, outs, run, kinds, aliases=(), vmem=(), relay=False, late=False, scratch=()
    ):
        self.ins, self.outs, self.run, self.kinds = ins, outs, run, kinds
        self.aliases, self.vmem, self.relay, self.late = aliases, vmem, relay, late
        self.scratch = scratch


def together(runs):
    while runs:
        runs = [steps for steps in runs if next(steps, "done") != "done"]
        yield "go"


def partners(at, kinds):
    found = []
    if "plane" in kinds:
        for j in range(1, TP):
            found.append((None, at.r, at.q * TP + lax.rem(at.p + j, TP)))
    if "core" in kinds:
        for j in range(1, at.R):
            found.append((None, lax.rem(at.r + j, at.R), at.s))
    if "zall" in kinds:
        for j in range(1, at.Q):
            found.append((None, at.r, lax.rem(at.q + j, at.Q) * TP + at.p))
    elif "chain" in kinds:
        found.append((at.q > 0, at.r, at.s - TP))
        found.append((at.q < at.Q - 1, at.r, at.s + TP))
    if "home" in kinds:
        r, s, _, same = home_of(at)
        found.append((same == 0, r, s))
        r, s, same = visitor_of(at)
        found.append((same == 0, r, s))
    if "back" in kinds:
        found.append((at.q < at.Q - 1, at.r, (at.q + 1) * TP))
        for j in range(TP):
            found.append(((at.p == 0) & (at.q > 0), at.r, (at.q - 1) * TP + j))
    if "halo" in kinds:
        found.append((at.q > 0, at.r, (at.q - 1) * TP + TP - 1))
        found.append((at.q < at.Q - 1, at.r, (at.q + 1) * TP))
        for j in range(TP):
            found.append(((at.p == TP - 1) & (at.q < at.Q - 1), at.r, (at.q + 1) * TP + j))
            found.append(((at.p == 0) & (at.q > 0), at.r, (at.q - 1) * TP + j))
    return found


def home_of(at):
    k = lax.rem(at.r * at.S + at.s, at.R * at.Q)
    r, s = k // at.Q, lax.rem(k, at.Q) * TP + (at.r * at.S + at.s) // (at.R * at.Q)
    return r, s, k, ((r == at.r) & (s == at.s)).astype(jnp.int32)


def visitor_of(at):
    d = at.p * (at.R * at.Q) + at.r * at.Q + at.q
    r, s = d // at.S, lax.rem(d, at.S)
    return r, s, ((r == at.r) & (s == at.s)).astype(jnp.int32)


def meet(at, kinds):
    barrier = pltpu.get_barrier_semaphore()
    peers = partners(at, kinds)
    for cond, r, s in peers:
        when(
            cond,
            functools.partial(
                pl.semaphore_signal, barrier, inc=1, device_id=(r, s), device_id_type=MESH_ID
            ),
        )
    awaited = sum(1 for cond, r, s in peers if cond is None)
    for cond, r, s in peers:
        if cond is not None:
            awaited = awaited + cond.astype(jnp.int32)
    pl.semaphore_wait(barrier, awaited)


def exchange(place, ident, jobs):
    kinds = set().union(*[job.kinds for job in jobs])
    n_in = sum(len(job.ins) for job in jobs)
    n_out = sum(len(job.outs) for job in jobs)
    sems = 24 + sum(12 + 2 * place.Q + place.R * place.Q * 2 for job in jobs)
    arrays, in_specs, outs, aliases = [], [], [], {}
    for job in jobs:
        for k, o in job.aliases:
            aliases[len(arrays) + k] = len(outs) + o
        for k, value in enumerate(job.ins):
            arrays.append(value)
            in_specs.append(pl.BlockSpec(memory_space=pltpu.VMEM if k in job.vmem else pl.ANY))
        outs.extend(job.outs)

    def body(*refs):
        at = place.here()
        ins, results = refs[:n_in], refs[n_in : n_in + n_out]
        copies = Copies(refs[n_in + n_out], refs[n_in + n_out + 1])
        held = refs[n_in + n_out + 2 :]
        meet(at, kinds)
        runs, i, o, h = [], 0, 0, 0
        for job in jobs:
            mine = list(results[o : o + len(job.outs)]) + list(held[h : h + len(job.scratch)])
            runs.append(job.run(at, copies, ins[i : i + len(job.ins)], mine))
            i, o, h = i + len(job.ins), o + len(job.outs), h + len(job.scratch)
        pairs = list(zip(jobs, runs))
        relays = together([steps for job, steps in pairs if job.relay])
        next(relays, "done")
        for steps in [steps for job, steps in pairs if not job.relay and not job.late]:
            next(steps)
        next(relays, "done")
        for steps in [steps for job, steps in pairs if job.late]:
            next(steps)
        for _ in relays:
            pass
        for steps in [steps for job, steps in pairs if not job.relay]:
            for _ in steps:
                pass
        copies.drain()

    results = pl.pallas_call(
        body,
        out_shape=tuple(outs),
        in_specs=in_specs,
        out_specs=tuple(
            pl.BlockSpec(memory_space=pltpu.VMEM if job.scratch else pl.ANY)
            for job in jobs
            for _ in job.outs
        ),
        scratch_shapes=[pltpu.SemaphoreType.DMA((sems,)), pltpu.SemaphoreType.DMA((sems,))]
        + [pltpu.VMEM(*shape) for job in jobs for shape in job.scratch],
        input_output_aliases=aliases,
        compiler_params=pltpu.CompilerParams(collective_id=ident, has_side_effects=True),
        cost_estimate=pl.CostEstimate(flops=0, bytes_accessed=COST, transcendentals=0),
        name="exchange_%d" % ident,
    )(*arrays)
    given, o = [], 0
    for job in jobs:
        given.append(results[o : o + len(job.outs)])
        o += len(job.outs)
    return given


def like(shape, dtype=BF):
    return jax.ShapeDtypeStruct(shape, dtype)


def gather_plane(value):
    def run(at, copies, ins, outs):
        slots = [copies.slot() for _ in range(TP - 1)]
        for j in range(1, TP):
            peer = at.q * TP + lax.rem(at.p + j, TP)
            copies.push(ins[0], outs[0].at[at.p], slots[j - 1], (at.r, peer))
        copies.local(ins[0], outs[0].at[at.p])
        yield "go"
        for j in range(1, TP):
            origin = lax.rem(at.p + TP - j, TP)
            copies.arrived(outs[0].at[origin], slots[j - 1], (at.r, at.s))

    return Job([value], [like((TP,) + value.shape, value.dtype)], run, {"plane"}, vmem=(0,))


def swap_plane(value):
    def run(at, copies, ins, outs):
        slots = [copies.slot() for _ in range(TP - 1)]
        for j in range(1, TP):
            other = lax.rem(at.p + j, TP)
            copies.push(
                ins[0].at[other], outs[0].at[at.p], slots[j - 1], (at.r, at.q * TP + other)
            )
        yield "go"
        for j in range(1, TP):
            origin = lax.rem(at.p + TP - j, TP)
            copies.arrived(outs[0].at[origin], slots[j - 1], (at.r, at.s))

    return Job([value], [like(value.shape, value.dtype)], run, {"plane"})


def line_sum(at, copies, source, held):
    slots = [copies.slot() for _ in range(at.Q - 1)]
    for j in range(1, at.Q):
        other = lax.rem(at.q + j, at.Q)
        there = (at.r, other * TP + at.p)
        copies.push(source.at[other], held.at[at.q], slots[j - 1], there)
    held[at.q] = source[at.q]
    yield "go"
    yield "go"
    for j in range(1, at.Q):
        origin = lax.rem(at.q + at.Q - j, at.Q)
        copies.arrived(held.at[origin], slots[j - 1], (at.r, at.s))
    total = held[0].astype(F32)
    for k in range(1, at.Q):
        total = total + held[k].astype(F32)
    return total


def line_plane(value):
    def run(at, copies, ins, outs):
        held, summed = outs[1:]
        total = yield from line_sum(at, copies, ins[0], held)
        summed[...] = total.astype(summed.dtype)
        slots = [copies.slot() for _ in range(TP - 1)]
        for j in range(1, TP):
            other = lax.rem(at.p + j, TP)
            there = (at.r, at.q * TP + other)
            copies.push(summed.at[other], outs[0].at[at.p], slots[j - 1], there)
        outs[0][at.p] = summed[at.p]
        yield "go"
        for j in range(1, TP):
            origin = lax.rem(at.p + TP - j, TP)
            copies.arrived(outs[0].at[origin], slots[j - 1], (at.r, at.s))

    scratch = ((value.shape, value.dtype), (value.shape[1:], value.dtype))
    outs = [like(value.shape[1:], value.dtype)]
    kinds = {"zall", "plane"}
    return Job([value], outs, run, kinds, vmem=(0,), relay=True, scratch=scratch)


def line_home(value):
    def run(at, copies, ins, outs):
        held, summed, got = outs[1:]
        total = yield from line_sum(at, copies, ins[0], held)
        summed[...] = total.astype(summed.dtype)
        r, s, own = visitor_of(at)
        _, _, _, here = home_of(at)
        slot = copies.slot()
        copies.push(summed, got, slot, (r, s), own == 0)
        yield "go"
        copies.arrived(got, slot, (at.r, at.s), here == 0)

        @pl.when(here == 0)
        def _():
            outs[0][...] = got[...]

        @pl.when(here == 1)
        def _():
            outs[0][...] = summed[...]

    one = (value.shape[1:], value.dtype)
    outs = [like(*one)]
    kinds = {"zall", "home"}
    return Job([value], outs, run, kinds, vmem=(0,), relay=True, scratch=((value.shape, value.dtype), one, one))


def finish(place, at, sliced, tiny, mix, taps):
    shard, D = mix.shape
    shapes = [shape for _, _, _, outs in sliced for shape in outs]
    tiny_shapes = [(1, shard)] * 4 + [(taps, shard), (2, HD)]
    arrays = [x for own, came, _, _ in sliced for x in (own, came) if x is not None] + [tiny, mix]
    where = at.p.astype(jnp.int32).reshape(1)

    def body(where_ref, *refs):
        ins, outs = refs[: len(arrays)], refs[len(arrays) :]

        ins = list(ins)
        first = 0
        for own, _, parts, made in sliced:
            mine = None if own is None else ins.pop(0)
            came = ins.pop(0)
            for k in range(TP):
                piece = came[k]
                if mine is not None:
                    piece = jnp.where(where_ref[0] == k, mine[k], piece)
                piece = piece.astype(F32)
                for start, width, out, base in parts:
                    there = slice(base + k * width, base + (k + 1) * width)
                    outs[first + out][:, there] = piece[:, start : start + width]
            first += len(made)
        total = ins[0][0]
        for k in range(1, TP):
            total = total + ins[0][k]
        for k in range(4):
            outs[first + k][...] = total[k : k + 1, :shard]
        outs[first + 4][...] = total[4 : 4 + taps, :shard]
        row = total[4 + taps : 5 + taps, :]
        outs[first + 5][0:1, :] = row[:, :HD]
        outs[first + 5][1:2, :] = row[:, HD:]
        outs[first + 6][...] = ins[1][...].astype(F32)

    outs = [like(shape, F32) for shape in shapes + tiny_shapes + [(shard, D)]]
    return plain_call(body, tuple(outs), (), where, *arrays, smem=1)


def swap_core(value):
    def run(at, copies, ins, outs):
        slots = [copies.slot() for _ in range(at.R - 1)]
        for j in range(1, at.R):
            other = lax.rem(at.r + j, at.R)
            copies.push(ins[0].at[other], outs[0].at[at.r], slots[j - 1], (other, at.s))
        yield "go"
        for j in range(1, at.R):
            origin = lax.rem(at.r + at.R - j, at.R)
            copies.arrived(outs[0].at[origin], slots[j - 1], (at.r, at.s))

    return Job([value], [like(value.shape, value.dtype)], run, {"core"})


def window_forward(place, value):
    reach = place.Q // 2

    def run(at, copies, ins, outs):
        slots = [copies.slot() for _ in range(reach)]
        there = (at.r, at.s + TP)
        copies.push(ins[0], outs[0].at[reach - 1], slots[0], there, at.q + 1 < at.Q)
        copies.local(ins[0], outs[0].at[reach])
        for j in range(1, reach + 1):
            yield "go"
            came = outs[0].at[reach - j]
            copies.arrived(came, slots[j - 1], (at.r, at.s), at.q >= j)
            if j < reach:
                passes = (at.q >= j) & (at.q + 1 < at.Q)
                copies.push(came, outs[0].at[reach - j - 1], slots[j], there, passes)

    shape = (reach + 1,) + value.shape
    outs = [like(shape, value.dtype)]
    return Job([value], outs, run, {"chain"}, vmem=(0,), relay=True)


def window_backward(place, value):
    reach = place.Q // 2

    def run(at, copies, ins, outs):
        slots = [copies.slot() for _ in range(reach)]
        for j in range(1, reach + 1):
            target = (at.q - j) * TP + at.p
            copies.push(
                ins[0].at[reach - j], outs[0].at[j - 1], slots[j - 1], (at.r, target), at.q >= j
            )
        yield "go"
        for j in range(1, reach + 1):
            copies.arrived(outs[0].at[j - 1], slots[j - 1], (at.r, at.s), at.q + j < at.Q)

    shape = (reach,) + value.shape[1:]
    return Job([value], [like(shape, value.dtype)], run, {"zall"})


def halo_tokens(value):
    rows = value.shape[0]

    def run(at, copies, ins, outs):
        ahead = [copies.slot() for _ in range(TP)]
        back = [copies.slot() for _ in range(TP)]
        first = (at.p == 0) & (at.q > 0)
        last = (at.p == TP - 1) & (at.q < at.Q - 1)
        for j in range(TP):
            tail = ins[0].at[pl.ds(rows - HALO, HALO)]
            there = (at.r, (at.q + 1) * TP + j)
            copies.push(tail, outs[0], ahead[j], there, last, ahead[0])
            head = ins[0].at[pl.ds(0, HALO)]
            there = (at.r, (at.q - 1) * TP + j)
            copies.push(head, outs[1], back[j], there, first, back[0])
        yield "go"
        copies.arrived(outs[0], ahead[0], (at.r, at.s), at.q > 0)
        copies.arrived(outs[1], back[0], (at.r, at.s), at.q < at.Q - 1)

    shape = (HALO,) + value.shape[1:]
    outs = [like(shape, value.dtype), like(shape, value.dtype)]
    return Job([value], outs, run, {"halo"}, vmem=(0,))


def spread_run(at, copies, source, held, first):
    slots = [copies.slot() for _ in range(TP - 1)]
    for j in range(1, TP):
        other = lax.rem(at.p + j, TP)
        copies.push(
            source.at[other], held.at[first + at.p], slots[j - 1], (at.r, at.q * TP + other)
        )
    copy = pltpu.make_async_copy(
        source.at[at.p], held.at[first + at.p], copies.recv.at[copies.slot()]
    )
    copy.start()
    yield "go"
    copy.wait()
    for j in range(1, TP):
        origin = lax.rem(at.p + TP - j, TP)
        copies.arrived(held.at[first + origin], slots[j - 1], (at.r, at.s))


def chain_run(at, copies, held, unit=TP):
    def block(r, q):
        return held.at[pl.ds(pl.multiple_of((r * at.Q + q) * unit, unit), unit)]

    right = [copies.slot() for _ in range(at.Q - 1)]
    left = [copies.slot() for _ in range(at.Q - 1)]
    across = [[copies.slot() for _ in range(at.Q)] for _ in range(at.R - 1)]

    def cross(q, index, cond):
        for j in range(1, at.R):
            other = lax.rem(at.r + j, at.R)
            copies.push(block(at.r, q), block(at.r, q), across[j - 1][index], (other, at.s), cond)

    copies.push(
        block(at.r, at.q), block(at.r, at.q), right[0], (at.r, at.s + TP), at.q < at.Q - 1
    )
    copies.push(block(at.r, at.q), block(at.r, at.q), left[0], (at.r, at.s - TP), at.q > 0)
    cross(at.q, 0, None)
    index = 0
    spots = {}
    for hop in range(1, at.Q):
        yield "go"
        from_left, from_right = at.q >= hop, at.q + hop < at.Q
        copies.arrived(block(at.r, at.q - hop), right[hop - 1], (at.r, at.s), from_left)
        if hop < at.Q - 1:
            copies.push(
                block(at.r, at.q - hop),
                block(at.r, at.q - hop),
                right[hop],
                (at.r, at.s + TP),
                from_left & (at.q < at.Q - 1),
            )
        copies.arrived(block(at.r, at.q + hop), left[hop - 1], (at.r, at.s), from_right)
        if hop < at.Q - 1:
            copies.push(
                block(at.r, at.q + hop),
                block(at.r, at.q + hop),
                left[hop],
                (at.r, at.s - TP),
                from_right & (at.q > 0),
            )
        for side, sign in ((from_left, -1), (from_right, 1)):
            spots[(hop, sign)] = [copies.slot() for _ in range(at.R - 1)]
            for j in range(1, at.R):
                other = lax.rem(at.r + j, at.R)
                piece = block(at.r, at.q + sign * hop)
                copies.push(piece, piece, spots[(hop, sign)][j - 1], (other, at.s), side)
    yield "go"
    for j in range(1, at.R):
        source = lax.rem(at.r + at.R - j, at.R)
        copies.arrived(block(source, at.q), across[j - 1][0], (at.r, at.s))
        for hop in range(1, at.Q):
            for sign in (-1, 1):
                there = at.q + sign * hop
                copies.arrived(
                    block(source, there),
                    spots[(hop, sign)][j - 1],
                    (at.r, at.s),
                    at.q >= hop if sign < 0 else there < at.Q,
                )


def spread(source):
    def run(at, copies, ins, outs):
        yield from spread_run(at, copies, ins[0], outs[0], 0)

    outs = [like(source.shape, source.dtype)]
    return Job([source], outs, run, {"plane"}, vmem=(0,), late=True)


def spread_all(place, source):
    def run(at, copies, ins, outs):
        yield from spread_run(at, copies, ins[0], outs[0], (at.r * at.Q + at.q) * TP)
        yield from chain_run(at, copies, outs[0])

    outs = [like((place.R * place.S,) + source.shape[1:], source.dtype)]
    return Job([source], outs, run, {"plane", "chain", "core"}, vmem=(0,), relay=True)


def home_all(place, source):
    def run(at, copies, ins, outs):
        r, s, slot, here = home_of(at)
        _, _, own = visitor_of(at)
        index = copies.slot()
        copies.push(ins[0], outs[0].at[slot], index, (r, s), here == 0)
        copy = pltpu.make_async_copy(ins[0], outs[0].at[slot], copies.recv.at[copies.slot()])
        when(here == 1, copy.start)
        yield "go"
        when(here == 1, copy.wait)
        copies.arrived(outs[0].at[at.r * at.Q + at.q], index, (at.r, at.s), own == 0)
        yield from chain_run(at, copies, outs[0], 1)

    outs = [like((place.R * place.Q,) + source.shape, source.dtype)]
    return Job([source], outs, run, {"home", "chain", "core"}, vmem=(0,), relay=True)


FACTOR = 1.0 / math.sqrt(HD)


def masked_keys(kv_ref, first, kv_s):
    index = lax.broadcasted_iota(jnp.int32, kv_ref.shape, 0)
    kv_s[...] = jnp.where(index >= first, kv_ref[...].astype(F32), 0.0).astype(BF)


def attend_forward(q, kv, q_seg, key_seg, first, block):
    N, QS = q.shape
    M, KS = kv.shape[0], kv.shape[1] // 2
    ahead = M - N
    span = ahead + block
    kv_heads = KS // HD
    groups = QS // KS

    def body(first_ref, q_ref, kv_ref, qs_ref, ks_ref, o_ref, kv_s):
        masked_keys(kv_ref, first_ref[0], kv_s)

        @pl.loop(0, N // block)
        def _(i):
            start = pl.multiple_of(i * block, block)
            here, keys = pl.ds(start, block), pl.ds(start, span)
            row = lax.broadcasted_iota(jnp.int32, (block, span), 0) + ahead
            col = lax.broadcasted_iota(jnp.int32, (block, span), 1)
            open_ = (qs_ref[here, :1] == ks_ref[:1, keys]) & (col <= row)
            open_ = open_ & (col + start >= first_ref[0])
            open_ = jnp.concatenate([open_] * groups, axis=0)
            queries = q_ref[here, :]
            done = []
            for k in range(kv_heads):
                mine = [
                    queries[:, (k * groups + g) * HD : (k * groups + g + 1) * HD]
                    for g in range(groups)
                ]
                key = kv_s[keys, k * HD : (k + 1) * HD]
                value = kv_s[keys, KS + k * HD : KS + (k + 1) * HD]
                score = jnp.where(open_, dot_nt(jnp.concatenate(mine, axis=0), key) * FACTOR, MASKED)
                weight = jnp.exp(score - jnp.max(score, axis=-1, keepdims=True))
                weight = weight / jnp.sum(weight, axis=-1, keepdims=True)
                out = dot(weight.astype(BF), value).astype(BF)
                done.extend(out[g * block : (g + 1) * block] for g in range(groups))
            o_ref[here, :] = jnp.concatenate(done, axis=1)

    return attend_call(
        body, like((N, QS)), [pltpu.VMEM(kv.shape, BF)], 4 * N * span * QS, first, q, kv, q_seg, key_seg
    )


def attend_call(body, outs, scratch, flops, first, *arrays):
    return pl.pallas_call(
        body,
        out_shape=outs,
        in_specs=[pl.BlockSpec(memory_space=pltpu.SMEM)]
        + [pl.BlockSpec(memory_space=pltpu.VMEM) for _ in arrays],
        out_specs=jax.tree.map(lambda _: pl.BlockSpec(memory_space=pltpu.VMEM), outs),
        scratch_shapes=scratch,
        cost_estimate=pl.CostEstimate(flops=flops, bytes_accessed=COST, transcendentals=0),
    )(first, *arrays)


def attend_backward(q, kv, d_o, q_seg, key_seg, first, block):
    N, QS = q.shape
    M, KS = kv.shape[0], kv.shape[1] // 2
    ahead = M - N
    span = ahead + block
    kv_heads = KS // HD
    groups = QS // KS

    def body(first_ref, q_ref, kv_ref, do_ref, qs_ref, ks_ref, dq_ref, dkv_ref, kv_s, *sums):
        masked_keys(kv_ref, first_ref[0], kv_s)
        for total in sums:
            total[...] = jnp.zeros_like(total)

        @pl.loop(0, N // block)
        def _(i):
            start = pl.multiple_of(i * block, block)
            here, keys = pl.ds(start, block), pl.ds(start, span)
            row = lax.broadcasted_iota(jnp.int32, (span, block), 0)
            col = lax.broadcasted_iota(jnp.int32, (span, block), 1) + ahead
            open_ = (ks_ref[keys, :1] == qs_ref[:1, here]) & (row <= col)
            open_ = open_ & (row + start >= first_ref[0])
            open_ = jnp.concatenate([open_] * groups, axis=1)
            queries, pulls = q_ref[here, :], do_ref[here, :]

            def heads_of(values, k):
                return jnp.concatenate(
                    [
                        values[:, (k * groups + g) * HD : (k * groups + g + 1) * HD]
                        for g in range(groups)
                    ],
                    axis=0,
                )

            done = []
            for k in range(kv_heads):
                mine, pull = heads_of(queries, k), heads_of(pulls, k)
                key = kv_s[keys, k * HD : (k + 1) * HD]
                value = kv_s[keys, KS + k * HD : KS + (k + 1) * HD]
                score = jnp.where(open_, dot_nt(key, mine) * FACTOR, MASKED)
                weight = jnp.exp(score - jnp.max(score, axis=0, keepdims=True))
                weight = weight / jnp.sum(weight, axis=0, keepdims=True)
                d_weight = dot_nt(value, pull)
                delta = jnp.sum(weight * d_weight, axis=0, keepdims=True)
                d_score = (weight * (d_weight - delta)).astype(BF)
                sums[k][keys, :] += dot(d_score, mine) * FACTOR
                sums[kv_heads + k][keys, :] += dot(weight.astype(BF), pull)
                dq = dot_tn(d_score, key) * FACTOR
                done.extend(dq[g * block : (g + 1) * block] for g in range(groups))
            dq_ref[here, :] = jnp.concatenate(done, axis=1)

        dkv_ref[...] = jnp.concatenate([total[...] for total in sums], axis=1)

    return attend_call(
        body,
        (like((N, QS), F32), like((M, 2 * KS), F32)),
        [pltpu.VMEM(kv.shape, BF)] + [pltpu.VMEM((M, HD), F32) for _ in range(2 * kv_heads)],
        10 * N * span * QS,
        first,
        q,
        kv,
        d_o,
        q_seg,
        key_seg,
    )


def turned(values, cosine, sine):
    lane = lax.broadcasted_iota(jnp.int32, values.shape, 1)
    ahead = pltpu.roll(values, 2 * HD - HD // 2, 1)
    behind = pltpu.roll(values, HD // 2, 1)
    other = jnp.where(lax.rem(lane, HD) < HD // 2, ahead, behind)
    return values * cosine + other * sine


def head_means(values):
    lane = lax.broadcasted_iota(jnp.int32, values.shape, 1)
    front = lane < HD
    first = jnp.sum(jnp.where(front, values, 0.0), axis=-1, keepdims=True)
    second = jnp.sum(jnp.where(front, 0.0, values), axis=-1, keepdims=True)
    return jnp.where(front, first, second) * (1.0 / HD)


def pairs_of(width):
    return [slice(c, c + 2 * HD) for c in range(0, width, 2 * HD)]


def heads_forward(n3, w, gains, cosine, sine, QS, KS):
    N = n3.shape[0]

    def body(n3_ref, w_ref, gains_ref, cos_ref, sin_ref, pre_ref, q_ref, kv_ref):
        pre_ref[...] = dot(n3_ref[...], w_ref[:, : QS + 2 * KS])

        def normed(cols, row):
            values = pre_ref[:, cols]
            inverse = lax.rsqrt(head_means(values * values) + EPSILON)
            values = values * inverse * gains_ref[row : row + 1, :]
            return turned(values, cos_ref[...], sin_ref[...]).astype(BF)

        for cols in pairs_of(QS):
            q_ref[:, cols] = normed(cols, 0)
        for cols in pairs_of(KS):
            kv_ref[:, cols] = normed(slice(QS + cols.start, QS + cols.stop), 1)
        kv_ref[:, KS:] = pre_ref[:, QS + KS :].astype(BF)

    outs = (like((N, QS + 2 * KS), F32), like((N, QS)), like((N, 2 * KS)))
    return plain_call(body, outs, (), n3, w, gains, cosine, sine)


def heads_backward(d_q, d_kv, got, count, pre, gains, cosine, sine, n3, g3, o, w):
    N, QS = d_q.shape
    KS = d_kv.shape[1] // 2
    D = n3.shape[1]
    W = QS + 2 * KS
    step = 256

    def body(
        count_ref, dq_ref, dkv_ref, got_ref, pre_ref, gains_ref, cos_ref, sin_ref, n3_ref, g3_ref,
        o_ref, w_ref, part_ref, rows_ref, heads_ref, all_ref,
    ):
        d_kv_sum = dkv_ref[...]
        for j in range(got_ref.shape[0]):
            d_kv_sum = d_kv_sum + jnp.where(j < count_ref[0], got_ref[j].astype(F32), 0.0)
        all_ref[:, QS + KS :] = d_kv_sum[:, KS:].astype(BF)

        def back(pull, cols, row):
            values = pre_ref[:, cols]
            inverse = lax.rsqrt(head_means(values * values) + EPSILON)
            pull = turned(pull, cos_ref[...], -sin_ref[...])
            scaled = pull * gains_ref[row : row + 1, :]
            mean = head_means(scaled * values)
            d_values = inverse * scaled - values * (inverse * inverse * inverse) * mean
            all_ref[:, cols] = d_values.astype(BF)
            return jnp.sum(pull * values * inverse, axis=0, keepdims=True)

        of_queries = [back(dq_ref[:, cols], cols, 0) for cols in pairs_of(QS)]
        of_keys = [
            back(d_kv_sum[:, cols], slice(QS + cols.start, QS + cols.stop), 1)
            for cols in pairs_of(KS)
        ]
        heads_ref[0:1, :] = sum(of_queries[1:], of_queries[0])
        heads_ref[1:2, :] = sum(of_keys[1:], of_keys[0])
        values, outputs = all_ref[...], o_ref[...]

        @pl.loop(0, D // step)
        def _(c):
            cols = pl.ds(pl.multiple_of(c * step, step), step)
            part_ref[:, cols] = dot_nt(values, w_ref[cols, :W])
            left = n3_ref[:, cols].astype(F32).T.astype(BF)
            rows_ref[cols, :W] = dot(left, values).astype(BF)
            right = g3_ref[:, cols].astype(F32).T.astype(BF)
            rows_ref[cols, W:] = dot(right, outputs).astype(BF)

    outs = (like((N, D), F32), like((D, W + QS)), like((2, 2 * HD), F32))
    return plain_call(
        body, outs, [pltpu.VMEM((N, W), BF)],
        count, d_q, d_kv, got, pre, gains, cosine, sine, n3, g3, o, w, smem=1,
    )


def plain_call(body, outs, scratch, *arrays, smem=0):
    return pl.pallas_call(
        body,
        out_shape=outs,
        in_specs=[
            pl.BlockSpec(memory_space=pltpu.SMEM if k < smem else pltpu.VMEM)
            for k in range(len(arrays))
        ],
        out_specs=tuple(pl.BlockSpec(memory_space=pltpu.VMEM) for _ in outs),
        scratch_shapes=scratch,
        cost_estimate=pl.CostEstimate(flops=0, bytes_accessed=COST, transcendentals=0),
    )(*arrays)


class Plane:
    def __init__(self, at, copies):
        self.at, self.copies = at, copies

    def swap(self, send, recv):
        at, slots = self.at, [self.copies.slot() for _ in range(TP - 1)]
        for j in range(1, TP):
            other = lax.rem(at.p + j, TP)
            there = (at.r, at.q * TP + other)
            self.copies.push(send.at[other], recv.at[at.p], slots[j - 1], there)
        return functools.partial(self.arrive, recv, slots)

    def gather(self, held):
        at, slots = self.at, [self.copies.slot() for _ in range(TP - 1)]
        for j in range(1, TP):
            there = (at.r, at.q * TP + lax.rem(at.p + j, TP))
            self.copies.push(held.at[at.p], held.at[at.p], slots[j - 1], there)
        return functools.partial(self.arrive, held, slots)

    def mate(self, k):
        p = self.at.p
        if k == 1:
            return p + 1 - 2 * lax.rem(p, 2)
        if k == 2:
            return p + 2 - 4 * (p // 2)
        return TP - 1 - p if k == TP - 1 else p

    def to_mate(self, source, held, k):
        at, slot = self.at, self.copies.slot()
        there = (at.r, at.q * TP + self.mate(k))
        self.copies.push(source, held.at[k], slot, there)
        return functools.partial(self.copies.arrived, held.at[k], slot, (at.r, at.s))

    def spread_mates(self, held):
        return [self.to_mate(held.at[0], held, k) for k in range(1, TP)]

    def sum_mates(self, own, recv):
        for k in range(1, TP):
            own = own + recv[k].astype(F32)
        return own

    def arrive(self, held, slots):
        at = self.at
        for j in range(1, TP):
            origin = lax.rem(at.p + TP - j, TP)
            self.copies.arrived(held.at[origin], slots[j - 1], (at.r, at.s))

    def settle(self, own, recv, n):
        total = own[pl.ds(pl.multiple_of(self.at.p * n, n), n), :]
        for j in range(1, TP):
            total = total + recv[lax.rem(self.at.p + j, TP)].astype(F32)
        return total


def columns_of(count, width, action):
    @pl.loop(0, count)
    def _(c):
        action(pl.ds(pl.multiple_of(c * width, width), width))


def rows_of(span, action):
    first, count = span

    @pl.loop(0, count // 64)
    def _(i):
        action(pl.ds(pl.multiple_of(first + i * 64, 64), 64))


def activate(gu, act, span, FS):
    def go(rows):
        gate, up = gu[rows, :FS], gu[rows, FS:]
        act[rows, :] = (jax.nn.silu(gate) * up).astype(BF)

    rows_of(span, go)


def deactivate(gu, d_act, dgu, span, FS):
    def go(rows):
        gate, up, pull = gu[rows, :FS], gu[rows, FS:], d_act[rows, :]
        sigma = jax.nn.sigmoid(gate)
        dgu[rows, :FS] = (pull * up * sigma * (1.0 + gate * (1.0 - sigma))).astype(BF)
        dgu[rows, FS:] = (pull * (gate * sigma)).astype(BF)

    rows_of(span, go)


def multiply(held, weights, out, span, parts):
    first, count = span
    n, D = held.shape[1:]
    values = held[first // n : (first + count) // n].reshape(count, D)
    rows = pl.ds(first, count)

    def go(cols):
        out[rows, cols] = dot(values, weights[:, cols])

    columns_of(parts, weights.shape[1] // parts, go)


def project(left, weights, part, span, send=None, order=None):
    first, count = span
    step = 256
    rows = pl.ds(first, count)
    n = send.shape[1] if send is not None else count

    def go(cols):
        out = dot_nt(left[rows, :], weights[cols, :])
        part[rows, cols] = out
        if send is not None:
            for k in range(first // n, (first + count) // n):
                block = out[k * n - first : (k + 1) * n - first].astype(BF)
                send[k if order is None else order[k], :, cols] = block

    columns_of(weights.shape[0] // step, step, go)


def feed_kernel(place, ident, mode, arrays, D, FS, n, side=0):
    N = n * TP
    R = place.R
    half = D // R
    W = 2 * FS if mode == "both" else 3 * FS
    forward, backward = mode in ("fwd", "both"), mode in ("both", "bwd")
    VM, HB = pltpu.VMEM, pl.ANY
    ins, scratch, outs = {}, {}, {}
    ins["weights"] = HB
    if mode == "fwd":
        ins.update(a_g=VM, h_in=VM, gain_next=VM)
        outs.update(
            h_out=((n, D), F32, VM), next_g=((TP, n, D), BF, VM), gu_out=((N, 2 * FS), F32, HB)
        )
    else:
        ins.update(first_part=VM, h_in=VM, gain=VM)
        outs.update(
            g_out=((n, D), F32, VM),
            next_g=((TP, n, D), BF, VM),
            d_gain=((1, D), F32, VM),
            half_out=((half, W), BF, VM),
        )
        scratch.update(
            first_send=((TP, n, D), BF),
            first_got=((TP, n, D), BF),
            a_v=((TP, n, D), BF),
            e_v=((TP, n, D), BF),
            d_act=((N, FS), F32),
            dgu=((N, 2 * FS), BF),
            grad_send=((R - 1, half, W), BF),
            grad_got=((R - 1, half, W), BF),
        )
    if mode == "both":
        ins.update(e_g=HB, e_own=VM, down=HB)
        down_piece = (half // place.Q, FS)
        outs.update(
            mid_out=((n, D), F32, VM),
            o_send=((TP, n, D), BF, VM),
            o_base=((n, D), F32, VM),
            down_out=((place.Q,) + down_piece, BF, VM),
        )
        scratch.update(
            down_send=((R - 1, half, FS), BF),
            down_got=((R - 1, half, FS), BF),
            down_half=((place.Q,) + down_piece, BF),
        )
    if mode == "bwd":
        ins.update(a_g=HB, gu_in=HB, g_in=VM, h_before=VM, gain_before=VM)
        piece = (half // place.Q, side)
        ins.update(side_in=VM)
        outs.update(
            d_gain_before=((1, D), F32, VM),
            halo=((HALO, D), BF, VM),
            side_out=((place.Q,) + piece, BF, VM),
        )
        scratch.update(side_got=((R - 1, half, side), BF), side_half=((place.Q,) + piece, BF))
    scratch.update(
        w=((D, 2 * FS), BF),
        wd=((D, FS), BF),
        gu=((N, 2 * FS), F32),
        act=((N, FS), BF),
        part=((N, D), F32),
        send=((TP, n, D), BF),
        got=((TP, n, D), BF),
    )
    in_names, out_names, scratch_names = list(ins), list(outs), list(scratch)
    kinds = {"plane"}
    if backward:
        kinds.add("core")
    if mode == "bwd":
        kinds.update({"back", "zall"})
    if mode == "both":
        kinds.add("zall")
    unit = D // (R * place.Q)
    sems = 32 + 3 * R + 4 * place.Q + 3 * R * place.Q

    def body(*refs):
        names = in_names + out_names + scratch_names
        v = dict(zip(names, refs))
        at = place.here()
        copies = Copies(refs[len(names)], refs[len(names) + 1])
        plane = Plane(at, copies)
        loads = refs[len(names) + 2]
        pending = {}

        def load(name, src, dst):
            pending[name] = pltpu.make_async_copy(src, dst, loads.at[len(pending)])
            pending[name].start()

        def load_blocks(name, source, target):
            for k in range(TP):
                load(name + str(k), source.at[plane.mate(k)], target.at[k])

        def loaded(*names):
            for name in names:
                pending[name].wait()

        def loaded_blocks(name):
            loaded(*[name + str(k) for k in range(TP)])

        if mode == "both":
            load("w", v["weights"], v["w"])
            load_blocks("e", v["e_g"], v["e_v"])
            own_rows = pl.ds(pl.multiple_of((at.r * at.Q + at.q) * unit, unit), unit)
            load("wd", v["down"], v["wd"].at[own_rows])
        else:
            load("w", v["weights"].at[:, : 2 * FS], v["w"])
            load("wd", v["weights"].at[:, 2 * FS :], v["wd"])
        if mode == "bwd":
            for k in range(TP):
                rows = pl.ds(pl.multiple_of(plane.mate(k) * n, n), n)
                load("gu%d" % k, v["gu_in"].at[rows], v["gu"].at[pl.ds(k * n, n)])
            load_blocks("a", v["a_g"], v["a_v"])
        meet(at, kinds)
        w, wd, gu, act = (v[k] for k in ("w", "wd", "gu", "act"))
        part, send, got = (v[k] for k in ("part", "send", "got"))

        def along_line(source, target):
            slots = [copies.slot() for _ in range(at.Q - 1)]
            for j in range(1, at.Q):
                other = lax.rem(at.q + j, at.Q)
                there = (at.r, other * TP + at.p)
                copies.push(source.at[other], target.at[at.q], slots[j - 1], there)
            target[at.q] = source[at.q]
            return slots

        def line_done(target, slots):
            for j in range(1, at.Q):
                origin = lax.rem(at.q + at.Q - j, at.Q)
                copies.arrived(target.at[origin], slots[j - 1], (at.r, at.s))

        def turned_rows(held, j):
            first_col = lax.rem(at.r + j, R) * half
            cols = pl.ds(pl.multiple_of(first_col, 128), half)
            return held[:, :, cols].reshape(N, half).astype(F32).T.astype(BF)

        if mode != "fwd":
            first = v["first_part"]
            mine = [pl.ds(pl.multiple_of(plane.mate(k) * n, n), n) for k in range(TP)]
            waits = []
            for k in range(1, TP):
                v["first_send"][k] = first[mine[k], :].astype(BF)
                waits.append(plane.to_mate(v["first_send"].at[k], v["first_got"], k))
        if mode == "fwd":
            pending["w"].wait()
            multiply(v["a_g"], w, gu, (0, N), 3)
            save = pltpu.make_async_copy(gu, v["gu_out"], loads.at[len(pending)])
            save.start()
            activate(gu, act, (0, N), FS)
            pending["wd"].wait()
            project(act, wd, part, (0, N), send)
            wait = plane.swap(send, got)
            wait()
            h_out = v["h_in"][...] + plane.settle(part, got, n)
            v["h_out"][...] = h_out
            v["next_g"][at.p] = (h_out * inverse_rms(h_out) * v["gain_next"][...]).astype(BF)
            wait = plane.gather(v["next_g"])
            wait()
            save.wait()
            copies.drain()
            return
        everything, own, near, far = (0, N), (0, n), (n, 2 * n), (3 * n, n)
        d_act, dgu = v["d_act"], v["dgu"]
        if mode == "both":
            loaded("wd")
            steps = chain_run(at, copies, wd, unit)
            next(steps)
            next(steps)
            for wait in waits:
                wait()
            h = v["h_in"][...] + plane.sum_mates(first[mine[0], :], v["first_got"])
            v["mid_out"][...] = h
            v["a_v"][0] = (h * inverse_rms(h) * v["gain"][...]).astype(BF)
            waits = plane.spread_mates(v["a_v"])
            for _ in range(at.Q - 3):
                next(steps)
            loaded("w")
            loaded_blocks("e")
            for span, awaited in ((own, ()), (near, waits[:2]), (far, waits[2:])):
                for wait in awaited:
                    wait()
                multiply(v["a_v"], w, gu, span, 3)
                activate(gu, act, span, FS)
            for _ in steps:
                pass
            down_slots = [copies.slot() for _ in range(R - 1)]
            for j in range(1, R):
                v["down_send"][j - 1] = dot(turned_rows(v["e_v"], j), act[...]).astype(BF)
                there = (lax.rem(at.r + j, R), at.s)
                copies.push(v["down_send"].at[j - 1], v["down_got"].at[j - 1], down_slots[j - 1], there)
            total = dot(turned_rows(v["e_v"], 0), act[...])
            for j in range(1, R):
                copies.arrived(v["down_got"].at[j - 1], down_slots[j - 1], (at.r, at.s))
                total = total + v["down_got"][j - 1].astype(F32)
            v["down_half"][...] = total.astype(BF).reshape(v["down_half"].shape)
            line_slots = along_line(v["down_half"], v["down_out"])
            multiply(v["e_v"], wd, d_act, everything, 3)
            waits = []
            for span, slots in ((near, (1, 2)), (far, (3,))):
                deactivate(gu, d_act, dgu, span, FS)
                project(dgu, w, part, span, send)
                waits.extend(plane.to_mate(send.at[k], got, k) for k in slots)
            deactivate(gu, d_act, dgu, own, FS)
            project(dgu, w, part, own)
        else:
            side_slots = [copies.slot() for _ in range(R - 1)]
            for j in range(1, R):
                other = lax.rem(at.r + j, R)
                copies.push(
                    v["side_in"].at[other], v["side_got"].at[j - 1], side_slots[j - 1], (other, at.s)
                )
            loaded_blocks("gu")
            activate(gu, act, everything, FS)
            for wait in waits:
                wait()
            h = v["h_in"][...]
            before = v["h_before"][...]
            r_before = inverse_rms(before)
            d_normed = plane.sum_mates(first[mine[0], :], v["first_got"])
            v["d_gain_before"][...] = jnp.sum(d_normed * before * r_before, axis=0, keepdims=True)
            g_mid = v["g_in"][...] + rms_pull(d_normed, before, r_before, v["gain_before"][...])
            v["g_out"][...] = g_mid
            v["e_v"][0] = g_mid.astype(BF)
            waits = plane.spread_mates(v["e_v"])
            loaded("w", "wd")
            loaded_blocks("a")
            total = v["side_in"][at.r].astype(F32)
            for j in range(1, R):
                copies.arrived(v["side_got"].at[j - 1], side_slots[j - 1], (at.r, at.s))
                total = total + v["side_got"][j - 1].astype(F32)
            v["side_half"][...] = total.astype(BF).reshape(v["side_half"].shape)
            line_slots = along_line(v["side_half"], v["side_out"])
            returns = []
            for span, awaited, slots in (
                (own, (), ()),
                (near, waits[:2], (1, 2)),
                (far, waits[2:], (3,)),
            ):
                for wait in awaited:
                    wait()
                multiply(v["e_v"], wd, d_act, span, 3)
                deactivate(gu, d_act, dgu, span, FS)
                project(dgu, w, part, span, send if slots else None)
                returns.extend(plane.to_mate(send.at[k], got, k) for k in slots)
            waits = returns
        values, pulls = v["a_v"], v["e_v"]

        slots = [copies.slot() for _ in range(R - 1)]
        for j in range(1, R):
            left = turned_rows(values, j)

            def put(cols, left=left, j=j):
                v["grad_send"][j - 1, :, cols] = dot(left, v["dgu"][:, cols]).astype(BF)

            columns_of(3, 2 * FS // 3, put)
            if mode == "bwd":
                v["grad_send"][j - 1, :, 2 * FS :] = dot(turned_rows(pulls, j), act[...]).astype(BF)
            other = lax.rem(at.r + j, R)
            copies.push(
                v["grad_send"].at[j - 1], v["grad_got"].at[j - 1], slots[j - 1], (other, at.s)
            )
        for wait in waits:
            wait()
        d_normed = plane.sum_mates(part[:n, :], got)
        r = inverse_rms(h)
        base = v["e_own"][...].astype(F32) if mode == "both" else v["g_out"][...]
        v["d_gain"][...] = jnp.sum(d_normed * h * r, axis=0, keepdims=True)
        g_new = base + rms_pull(d_normed, h, r, v["gain"][...])
        v["g_out"][...] = g_new
        v["next_g"][at.p] = g_new.astype(BF)
        wait = plane.gather(v["next_g"])
        if mode == "bwd":
            back = [copies.slot() for _ in range(TP)]
            for j in range(TP):
                copies.push(
                    v["next_g"].at[at.p, pl.ds(0, HALO)],
                    v["halo"],
                    back[j],
                    (at.r, (at.q - 1) * TP + j),
                    (at.p == 0) & (at.q > 0),
                    back[0],
                )
        if mode == "both":
            project(act, wd, part, everything, v["o_send"], [plane.mate(k) for k in range(TP)])
            v["o_base"][...] = h + part[:n, :]
        left = turned_rows(values, 0)
        for j in range(1, R):
            copies.arrived(v["grad_got"].at[j - 1], slots[j - 1], (at.r, at.s))

        def finish(cols):
            total = dot(left, v["dgu"][:, cols])
            for j in range(1, R):
                total = total + v["grad_got"][j - 1, :, cols].astype(F32)
            v["half_out"][:, cols] = total.astype(BF)

        columns_of(3, 2 * FS // 3, finish)
        if mode == "bwd":
            total = dot(turned_rows(pulls, 0), act[...])
            for j in range(1, R):
                total = total + v["grad_got"][j - 1, :, 2 * FS :].astype(F32)
            v["half_out"][:, 2 * FS :] = total.astype(BF)
        wait()
        if mode == "bwd":
            copies.arrived(v["halo"], back[0], (at.r, at.s), at.q < at.Q - 1)
            line_done(v["side_out"], line_slots)
        if mode == "both":
            line_done(v["down_out"], line_slots)
        copies.drain()

    results = pl.pallas_call(
        body,
        out_shape=tuple(like(outs[k][0], outs[k][1]) for k in out_names),
        in_specs=[pl.BlockSpec(memory_space=ins[k]) for k in in_names],
        out_specs=tuple(pl.BlockSpec(memory_space=outs[k][2]) for k in out_names),
        scratch_shapes=[pltpu.VMEM(*scratch[k]) for k in scratch_names]
        + [pltpu.SemaphoreType.DMA((sems,)), pltpu.SemaphoreType.DMA((sems,))]
        + [pltpu.SemaphoreType.DMA((12,))],
        compiler_params=pltpu.CompilerParams(collective_id=ident, has_side_effects=True),
        cost_estimate=pl.CostEstimate(flops=0, bytes_accessed=COST, transcendentals=0),
        name="feed_%s" % mode,
    )(*[arrays[k] for k in in_names])
    return dict(zip(out_names, results))


def doc_info(positions, lengths):
    doc_ends = jnp.cumsum(lengths, dtype=jnp.int32)
    passed = positions[:, None] >= doc_ends[None, :]
    segment = jnp.sum(passed.astype(jnp.int32), axis=1, dtype=jnp.int32)
    opening = jnp.sum(jnp.where(passed, lengths[None, :], 0), axis=1, dtype=jnp.int32)
    return (segment, positions - opening)


def inverse_rms(values):
    return lax.rsqrt(jnp.mean(values * values, axis=-1, keepdims=True) + EPSILON)


def rms_pull(upstream, values, inverse, norm_gain):
    scaled = upstream * norm_gain
    product_mean = jnp.mean(scaled * values, axis=-1, keepdims=True)
    return inverse * scaled - values * (inverse * inverse * inverse) * product_mean


def settle(own, arrived, p):
    index = jnp.arange(TP, dtype=jnp.int32)[:, None, None]
    others = jnp.where(index == p, 0.0, arrived.astype(F32))
    mine = lax.dynamic_index_in_dim(own, p, 0, keepdims=False)
    return mine + jnp.sum(others, axis=0)


def per_device(
    place,
    tokens,
    doc_lengths,
    cotangent,
    gain_conv,
    w_in,
    kernel,
    w_mix,
    gain_ffa,
    gate_a,
    up_a,
    down_a,
    gain_att,
    w_query,
    w_key,
    w_value,
    head_gains,
    w_attout,
    gain_ffb,
    gate_b,
    up_b,
    down_b,
):
    R, S, Q = place.R, place.S, place.Q
    n, D = tokens.shape[1], tokens.shape[2]
    shard = w_in.shape[0]
    FS = gate_a.shape[1] // TP
    CS = D // TP
    QS, KS = H * HD // TP, KVH * HD // TP
    taps = kernel.shape[0]
    N = n * TP
    r, s = lax.axis_index("rows"), lax.axis_index("seq")
    q, p = s // TP, lax.rem(s, TP)
    lengths = doc_lengths[0]

    def slices(weight):
        return weight.reshape(shard, TP, -1).transpose(1, 0, 2)

    def joined(*weights):
        return jnp.concatenate([slices(weight) for weight in weights], axis=2)

    columns = [[a * S + b * TP + c for a in range(R) for b in range(Q)] for c in range(TP)]
    lines = [[b * TP + c for b in range(Q)] for c in range(TP)]

    def gather_rest(plane):
        flat = plane.reshape(TP * shard, -1)
        return lax.all_gather(
            flat, ("rows", "seq"), axis=0, tiled=True, axis_index_groups=columns
        )

    def by_row(grads):
        return grads.astype(BF).reshape(R, S * shard, -1)

    def own_rows(rows, came, *later):
        return lax.optimization_barrier((collect(rows, came, r).astype(BF),) + later)

    def reduce_line(half):
        part = lax.psum_scatter(
            half, "seq", scatter_dimension=0, tiled=True, axis_index_groups=lines
        )
        return part.reshape(TP, shard, part.shape[1])

    in_cut = w_in.reshape(shard, 3, TP, CS).transpose(2, 0, 1, 3).reshape(TP, shard, 3 * CS)
    small = jnp.stack([gain_conv, gain_ffa, gain_att, gain_ffb] + [kernel[i] for i in range(taps)])
    small = jnp.pad(small, ((0, 16 - 4 - taps), (0, 128 - shard)))
    small = jnp.broadcast_to(small[None], (TP, 16, 128))

    mine = tokens[0]
    (tok_g,), (halo_a, halo_b), (in_g,), (mix_g,), (small_g,), (ffa_p,) = exchange(
        place,
        0,
        [
            gather_plane(mine),
            halo_tokens(mine),
            spread_all(place, in_cut),
            home_all(place, w_mix),
            spread_all(place, small),
            spread(joined(gate_a, up_a, down_a.T)),
        ],
    )
    wa = gather_rest(ffa_p)
    w_mix_s = mix_g.reshape(CS, D)
    vectors = small_g[:, : 4 + taps, :shard].transpose(1, 0, 2).reshape(4 + taps, D).astype(F32)
    g_conv, g_ffa, g_att, g_ffb = (vectors[i] for i in range(4))
    kernel_f = lax.dynamic_slice_in_dim(vectors[4:], p * CS, CS, 1)
    w_in_s = in_g.reshape(D, 3 * CS)

    def own(parts, index):
        return lax.dynamic_index_in_dim(parts, index, 0, keepdims=False).astype(F32)

    def collect(parts, came, index):
        slot = jnp.arange(came.shape[0], dtype=jnp.int32).reshape((-1,) + (1,) * (came.ndim - 1))
        mine_part = lax.dynamic_index_in_dim(parts, index, 0, keepdims=True).astype(F32)
        return jnp.sum(jnp.where(slot == index, mine_part, came.astype(F32)), axis=0)

    def after_core(parts, came):
        summed = collect(parts, came, r)
        return summed.reshape((Q, TP) + summed.shape[1:])

    total = S * n
    pos_ext = q * N - HALO + jnp.arange(N + 2 * HALO, dtype=jnp.int32)
    seg_ext, rel_ext = doc_info(pos_ext, lengths)
    valid = ((pos_ext >= 0) & (pos_ext < total))[:, None]
    x_ext = jnp.concatenate([halo_a, tok_g.reshape(N, D), halo_b], axis=0)
    x_ext = jnp.where(valid, x_ext, jnp.zeros_like(x_ext)).astype(F32)
    r0_ext = inverse_rms(x_ext)
    n1_ext = (x_ext * r0_ext * g_conv).astype(BF)
    z_ext = dot(n1_ext, w_in_s)
    b_ext, c_ext, v_ext = z_ext[:, :CS], z_ext[:, CS : 2 * CS], z_ext[:, 2 * CS :]
    u_ext = lax.optimization_barrier((b_ext * v_ext).astype(BF)).astype(F32)
    span = slice(HALO, HALO + N)
    same = [
        (seg_ext[HALO - 2 + k : HALO - 2 + k + N] == seg_ext[span]).astype(F32)[:, None]
        for k in range(taps)
    ]
    near = [u_ext[HALO - 2 + k : HALO - 2 + k + N] for k in range(taps)]
    conv = kernel_f[0] * near[0] * same[0]
    for k in range(1, taps):
        conv = conv + kernel_f[k] * near[k] * same[k]
    m_bf = (c_ext[span] * conv).astype(BF)
    part = dot(m_bf, w_mix_s).reshape(TP, n, D)
    (got,), (att_p,), (ffb_p,), (down_p,) = exchange(
        place,
        1,
        [
            swap_plane(part.astype(BF)),
            spread(joined(w_query, w_key, w_value, w_attout.T)),
            spread(joined(gate_b, up_b)),
            spread(joined(down_b.T)),
        ],
    )
    w_att = gather_rest(att_p)
    wb = gather_rest(ffb_p)
    x0 = mine.astype(F32)
    h1 = x0 + settle(part, got, p)

    r1 = inverse_rms(h1)
    a1 = (h1 * r1 * g_ffa).astype(BF)
    ((a1_g,),) = exchange(place, 2, [gather_plane(a1)])
    a1_g = a1_g.reshape(N, D)

    g_row = {name: value[None] for name, value in
             (("ffa", g_ffa), ("att", g_att), ("ffb", g_ffb))}
    fed = feed_kernel(
        place,
        3,
        "fwd",
        {"weights": wa, "a_g": a1_g.reshape(TP, n, D), "h_in": h1, "gain_next": g_row["att"]},
        D,
        FS,
        n,
    )
    h2, n3_g, gu1 = fed["h_out"], fed["next_g"], fed["gu_out"]

    n3_g = n3_g.reshape(N, D)
    w_out = w_att[:, QS + 2 * KS :]
    lane = jnp.arange(2 * HD, dtype=jnp.int32)
    frequency = jnp.exp(jnp.arange(HD // 2, dtype=F32) * (-2.0 * math.log(THETA) / HD))
    angles = rel_ext[span].astype(F32)[:, None] * jnp.tile(frequency, 4)[None, :]
    cosine = jnp.cos(angles)
    sine = jnp.sin(angles) * jnp.where(lane % HD < HD // 2, -1.0, 1.0)
    head_rows = jnp.tile(head_gains.astype(F32), (1, 2))
    pre, q_bf, kv_bf = heads_forward(n3_g, w_att, head_rows, cosine, sine, QS, KS)
    e_bf = cotangent[0]
    (kv_w,), (e_g,) = exchange(
        place,
        5,
        [window_forward(place, kv_bf), gather_plane(e_bf)],
    )
    reach = Q // 2 + 1
    kv_all = kv_w.reshape(reach * N, 2 * KS)
    q_seg = seg_ext[span]
    key_seg, _ = doc_info((q - reach + 1) * N + jnp.arange(reach * N, dtype=jnp.int32), lengths)
    first = jnp.maximum((reach - 1 - q) * N, 0).astype(jnp.int32).reshape(1)
    seg_col, seg_row = (jnp.broadcast_to(q_seg[:, None], (N, 128)), jnp.broadcast_to(q_seg, (8, N)))
    key_col = jnp.broadcast_to(key_seg[:, None], (reach * N, 128))
    key_row = jnp.broadcast_to(key_seg, (8, reach * N))
    o_bf = attend_forward(q_bf, kv_all, seg_col, key_row, first, 128)
    fed = feed_kernel(
        place,
        8,
        "both",
        {
            "weights": wb,
            "down": down_p.reshape(TP * shard, FS),
            "first_part": dot_nt(o_bf, w_out),
            "h_in": h2,
            "gain": g_row["ffb"],
            "e_g": e_g.reshape(TP, n, D),
            "e_own": e_bf,
        },
        D,
        FS,
        n,
    )
    full_down = jnp.sum(fed["down_out"].astype(F32), axis=0).astype(BF).reshape(TP, shard, FS)
    h3, g3, g3_g, half_b = fed["mid_out"], fed["g_out"], fed["next_g"], fed["half_out"]
    d_gain = {}
    d_gain["ffb"] = fed["d_gain"][0]

    g3_g = g3_g.reshape(N, D)
    d_o = dot(g3_g, w_out).astype(BF)
    d_q, d_kv = attend_backward(q_bf, kv_all, d_o, seg_row, key_col, first, 128)
    d_kv = d_kv.reshape(reach, N, 2 * KS)
    (got_kv,), (got_o,) = exchange(
        place, 10, [window_backward(place, d_kv.astype(BF)), swap_plane(fed["o_send"])]
    )
    index = jnp.arange(TP, dtype=jnp.int32)[:, None, None]
    h4 = fed["o_base"] + jnp.sum(jnp.where(index == p, 0.0, got_o.astype(F32)), axis=0)
    mixed = h4.astype(BF)[None]
    count = jnp.clip(Q - 1 - q, 0, reach - 1).astype(jnp.int32).reshape(1)
    half_b, got_kv = lax.optimization_barrier((half_b, got_kv))
    full_b = reduce_line(half_b)
    part, rows_att, d_heads = heads_backward(
        d_q, d_kv[-1], got_kv, count, pre, head_rows, cosine, sine, n3_g, g3_g, o_bf, w_att
    )
    d_heads = jnp.sum(d_heads.reshape(2, 2, HD), axis=1)
    rows_att = by_row(rows_att)
    fed = feed_kernel(
        place,
        13,
        "bwd",
        {
            "weights": wa,
            "first_part": part,
            "h_in": h1,
            "gain": g_row["ffa"],
            "a_g": a1_g.reshape(TP, n, D),
            "gu_in": gu1,
            "g_in": g3,
            "h_before": h2,
            "gain_before": g_row["att"],
            "side_in": rows_att,
        },
        D,
        FS,
        n,
        rows_att.shape[2],
    )
    full_att = jnp.sum(fed["side_out"].astype(F32), axis=0).astype(BF).reshape(TP, shard, -1)
    g1, g1_g, g1_halo = fed["g_out"], fed["next_g"], fed["halo"]
    d_gain["att"], d_gain["ffa"] = fed["d_gain_before"][0], fed["d_gain"][0]
    full_a = reduce_line(fed["half_out"])

    g1_halo = jnp.where(q < Q - 1, g1_halo, jnp.zeros_like(g1_halo))
    g1_ext = jnp.concatenate([g1_g.reshape(N, D), g1_halo], axis=0)
    d_m = dot_nt(g1_ext, w_mix_s)
    d_mix_s = dot_tn(m_bf, g1_ext[:N])
    d_c = d_m[:N] * conv
    d_conv = lax.optimization_barrier((d_m * c_ext[HALO:]).astype(BF)).astype(F32)
    d_kernel = jnp.stack(
        [jnp.sum(d_conv[:N] * near[k] * same[k], axis=0) for k in range(taps)]
    )
    d_u = jnp.zeros((N, CS), F32)
    for k in range(taps):
        ahead = taps - 1 - k
        match = (seg_ext[HALO + ahead : HALO + ahead + N] == seg_ext[span]).astype(F32)[:, None]
        d_u = d_u + kernel_f[k] * d_conv[ahead : ahead + N] * match
    d_z = jnp.concatenate([d_u * v_ext[span], d_c, d_u * b_ext[span]], axis=1).astype(BF)
    rows_in = dot_tn(n1_ext[span], d_z).astype(BF).reshape(R, S, shard, 3 * CS)
    rows_mix = d_mix_s.astype(BF).reshape(R, Q, shard, D)
    d_n1 = dot_nt(d_z, w_in_s)
    d_gain["conv"] = jnp.sum(d_n1 * x_ext[span] * r0_ext[span], axis=0)
    part = d_n1.reshape(TP, n, D)
    d_taps = lax.dynamic_update_slice(jnp.zeros((taps, D), F32), d_kernel, (0, p * CS))
    lanes = jnp.concatenate(
        [jnp.stack([d_gain["conv"], d_gain["ffa"], d_gain["att"], d_gain["ffb"]]), d_taps]
    )
    lanes = lanes.reshape(4 + taps, R * S, shard).transpose(1, 0, 2)
    lanes = jnp.pad(lanes, ((0, 0), (0, 0), (0, 128 - shard)))
    heads_row = jnp.broadcast_to(d_heads.reshape(1, 1, 2 * HD), (R * S, 1, 2 * HD))
    tiny = jnp.concatenate([lanes, heads_row], axis=1)
    tiny_rows = tiny.reshape(R, S, 4 + taps + 1, 128)
    (got,), (core_in,), (core_mix,), (core_t,), (plane_b,), (plane_down,), (plane_att,) = exchange(
        place,
        15,
        [
            swap_plane(part.astype(BF)),
            swap_core(rows_in),
            swap_core(rows_mix),
            swap_core(tiny_rows),
            swap_plane(full_b),
            swap_plane(full_down),
            swap_plane(full_att),
        ],
    )
    d_normed = settle(part, got, p)
    g0 = g1 + rms_pull(d_normed, x0, inverse_rms(x0), g_conv)
    d_tokens = g0.astype(BF)[None]

    tiny_line = after_core(tiny_rows, core_t)
    line_in = after_core(rows_in, core_in).astype(BF)
    line_mix = collect(rows_mix, core_mix, r).astype(BF)
    (plane_a,), (plane_in,), (plane_t,), (mix_back,) = exchange(
        place,
        16,
        [
            swap_plane(full_a),
            line_plane(line_in),
            line_plane(tiny_line),
            line_home(line_mix),
        ],
    )
    FF = TP * FS
    by_weight = [(k * FS, FS, k, 0) for k in range(3)]
    by_gate = [(k * CS, CS, 0, k * D) for k in range(3)]
    by_head = [(0, QS, 0, 0), (QS, KS, 1, 0), (QS + KS, KS, 2, 0), (QS + 2 * KS, QS, 3, 0)]
    ready = finish(
        place,
        place.here(),
        [
            (full_b, plane_b, by_weight[:2], [(shard, FF)] * 2),
            (full_down, plane_down, by_weight[:1], [(shard, FF)]),
            (full_att, plane_att, by_head, [(shard, TP * k) for k in (QS, KS, KS, QS)]),
            (full_a, plane_a, by_weight, [(shard, FF)] * 3),
            (None, plane_in, by_gate, [(shard, 3 * D)]),
        ],
        plane_t,
        mix_back,
        taps,
    )
    out_b, out_att, out_a, (out_in,) = ready[:3], ready[3:7], ready[7:10], ready[10:11]
    of_conv, of_ffa, of_att, of_ffb, of_taps, d_heads, out_mix = ready[11:]
    return (
        mixed,
        d_tokens,
        of_conv[0],
        out_in,
        of_taps,
        out_mix,
        of_ffa[0],
        out_a[0],
        out_a[1],
        out_a[2].T,
        of_att[0],
        out_att[0],
        out_att[1],
        out_att[2],
        d_heads,
        out_att[3].T,
        of_ffb[0],
        out_b[0],
        out_b[1],
        out_b[2].T,
    )


def solution(mesh):
    place = Place(mesh.shape["rows"], mesh.shape["seq"])
    whole = ("rows", "seq")
    wide, first, second = P("rows", "seq", None), P(whole, None), P(None, whole)
    in_specs = (
        (wide, P("rows", None), wide, P(whole), first, second, first)
        + (P(whole), first, first, second)
        + (P(whole), first, first, first, P(), second)
        + (P(whole), first, first, second)
    )
    out_specs = (
        (wide, wide, P(whole), first, second, first)
        + (P(whole), first, first, second)
        + (P(whole), first, first, first, P(), second)
        + (P(whole), first, first, second)
    )
    return jax.shard_map(
        functools.partial(per_device, place),
        mesh=mesh,
        in_specs=in_specs,
        out_specs=out_specs,
        check_vma=False,
    )
```

```python
import functools
import math

import jax
import jax.numpy as jnp
from jax import lax
from jax.experimental import pallas as pl
from jax.experimental.pallas import tpu as pltpu
from jax.sharding import PartitionSpec as P

H = 16
KVH = 8
HD = 64
TP = 4
HALO = 16
COST = 1_000_000

EPSILON = 1e-05
THETA = 1000000.0
MASKED = -1e30
MESH_ID = pl.DeviceIdType.MESH
BF = jnp.bfloat16
F32 = jnp.float32


def dot(left, right):
    return jnp.dot(left, right, preferred_element_type=F32)


def dot_tn(left, right):
    return lax.dot_general(left, right, (((0,), (0,)), ((), ())), preferred_element_type=F32)


def dot_nt(left, right):
    return lax.dot_general(left, right, (((1,), (1,)), ((), ())), preferred_element_type=F32)


class Place:
    def __init__(self, rows, seq):
        self.R, self.S = rows, seq
        self.Q = seq // TP

    def here(self):
        here = Place(self.R, self.S)
        here.r = lax.axis_index("rows")
        here.s = lax.axis_index("seq")
        here.q = here.s // TP
        here.p = lax.rem(here.s, TP)
        return here


class Copies:
    def __init__(self, send, recv):
        self.send, self.recv, self.count, self.sent = send, recv, 0, []

    def slot(self):
        self.count += 1
        return self.count - 1

    def remote(self, src, dst, slot, where, recv_slot=None):
        return pltpu.make_async_remote_copy(
            src_ref=src,
            dst_ref=dst,
            send_sem=self.send.at[slot],
            recv_sem=self.recv.at[slot if recv_slot is None else recv_slot],
            device_id=where,
            device_id_type=MESH_ID,
        )

    def push(self, src, dst, slot, where, cond=None, recv_slot=None):
        copy = self.remote(src, dst, slot, where, recv_slot)
        when(cond, copy.start)
        self.sent.append((copy.wait_send, cond))

    def arrived(self, dst, slot, where, cond=None):
        copy = self.remote(dst, dst, slot, where)
        when(cond, copy.wait_recv)

    def local(self, src, dst):
        slot = self.slot()
        copy = pltpu.make_async_copy(src, dst, self.recv.at[slot])
        copy.start()
        self.sent.append((copy.wait, None))

    def drain(self):
        for wait, cond in self.sent:
            when(cond, wait)


def when(cond, action):
    if cond is None:
        action()
    else:
        pl.when(cond)(lambda: action())


class Job:
    def __init__(
        self, ins, outs, run, kinds, aliases=(), vmem=(), relay=False, late=False, scratch=()
    ):
        self.ins, self.outs, self.run, self.kinds = ins, outs, run, kinds
        self.aliases, self.vmem, self.relay, self.late = aliases, vmem, relay, late
        self.scratch = scratch


def together(runs):
    while runs:
        runs = [steps for steps in runs if next(steps, "done") != "done"]
        yield "go"


def partners(at, kinds):
    found = []
    if "plane" in kinds:
        for j in range(1, TP):
            found.append((None, at.r, at.q * TP + lax.rem(at.p + j, TP)))
    if "core" in kinds:
        for j in range(1, at.R):
            found.append((None, lax.rem(at.r + j, at.R), at.s))
    if "zall" in kinds:
        for j in range(1, at.Q):
            found.append((None, at.r, lax.rem(at.q + j, at.Q) * TP + at.p))
    elif "chain" in kinds:
        found.append((at.q > 0, at.r, at.s - TP))
        found.append((at.q < at.Q - 1, at.r, at.s + TP))
    if "home" in kinds:
        r, s, _, same = home_of(at)
        found.append((same == 0, r, s))
        r, s, same = visitor_of(at)
        found.append((same == 0, r, s))
    if "back" in kinds:
        found.append((at.q < at.Q - 1, at.r, (at.q + 1) * TP))
        for j in range(TP):
            found.append(((at.p == 0) & (at.q > 0), at.r, (at.q - 1) * TP + j))
    if "halo" in kinds:
        found.append((at.q > 0, at.r, (at.q - 1) * TP + TP - 1))
        found.append((at.q < at.Q - 1, at.r, (at.q + 1) * TP))
        for j in range(TP):
            found.append(((at.p == TP - 1) & (at.q < at.Q - 1), at.r, (at.q + 1) * TP + j))
            found.append(((at.p == 0) & (at.q > 0), at.r, (at.q - 1) * TP + j))
    return found


def home_of(at):
    k = lax.rem(at.r * at.S + at.s, at.R * at.Q)
    r, s = k // at.Q, lax.rem(k, at.Q) * TP + (at.r * at.S + at.s) // (at.R * at.Q)
    return r, s, k, ((r == at.r) & (s == at.s)).astype(jnp.int32)


def visitor_of(at):
    d = at.p * (at.R * at.Q) + at.r * at.Q + at.q
    r, s = d // at.S, lax.rem(d, at.S)
    return r, s, ((r == at.r) & (s == at.s)).astype(jnp.int32)


def meet(at, kinds):
    barrier = pltpu.get_barrier_semaphore()
    peers = partners(at, kinds)
    for cond, r, s in peers:
        when(
            cond,
            functools.partial(
                pl.semaphore_signal, barrier, inc=1, device_id=(r, s), device_id_type=MESH_ID
            ),
        )
    awaited = sum(1 for cond, r, s in peers if cond is None)
    for cond, r, s in peers:
        if cond is not None:
            awaited = awaited + cond.astype(jnp.int32)
    pl.semaphore_wait(barrier, awaited)


def exchange(place, ident, jobs):
    kinds = set().union(*[job.kinds for job in jobs])
    n_in = sum(len(job.ins) for job in jobs)
    n_out = sum(len(job.outs) for job in jobs)
    sems = 24 + sum(
        12 + 4 * len(job.ins) + 2 * place.Q + place.R * place.Q * 2 for job in jobs
    )
    arrays, in_specs, outs, aliases = [], [], [], {}
    for job in jobs:
        for k, o in job.aliases:
            aliases[len(arrays) + k] = len(outs) + o
        for k, value in enumerate(job.ins):
            arrays.append(value)
            in_specs.append(pl.BlockSpec(memory_space=pltpu.VMEM if k in job.vmem else pl.ANY))
        outs.extend(job.outs)

    def body(*refs):
        at = place.here()
        ins, results = refs[:n_in], refs[n_in : n_in + n_out]
        copies = Copies(refs[n_in + n_out], refs[n_in + n_out + 1])
        held = refs[n_in + n_out + 2 :]
        meet(at, kinds)
        runs, i, o, h = [], 0, 0, 0
        for job in jobs:
            mine = list(results[o : o + len(job.outs)]) + list(held[h : h + len(job.scratch)])
            runs.append(job.run(at, copies, ins[i : i + len(job.ins)], mine))
            i, o, h = i + len(job.ins), o + len(job.outs), h + len(job.scratch)
        pairs = list(zip(jobs, runs))
        relays = together([steps for job, steps in pairs if job.relay])
        next(relays, "done")
        for steps in [steps for job, steps in pairs if not job.relay and not job.late]:
            next(steps)
        next(relays, "done")
        for steps in [steps for job, steps in pairs if job.late]:
            next(steps)
        for _ in relays:
            pass
        for steps in [steps for job, steps in pairs if not job.relay]:
            for _ in steps:
                pass
        copies.drain()

    results = pl.pallas_call(
        body,
        out_shape=tuple(outs),
        in_specs=in_specs,
        out_specs=tuple(
            pl.BlockSpec(memory_space=pltpu.VMEM if job.scratch else pl.ANY)
            for job in jobs
            for _ in job.outs
        ),
        scratch_shapes=[pltpu.SemaphoreType.DMA((sems,)), pltpu.SemaphoreType.DMA((sems,))]
        + [pltpu.VMEM(*shape) for job in jobs for shape in job.scratch],
        input_output_aliases=aliases,
        compiler_params=pltpu.CompilerParams(collective_id=ident, has_side_effects=True),
        cost_estimate=pl.CostEstimate(flops=0, bytes_accessed=COST, transcendentals=0),
        name="exchange_%d" % ident,
    )(*arrays)
    given, o = [], 0
    for job in jobs:
        given.append(results[o : o + len(job.outs)])
        o += len(job.outs)
    return given


def like(shape, dtype=BF):
    return jax.ShapeDtypeStruct(shape, dtype)


def gather_plane(value):
    def run(at, copies, ins, outs):
        slots = [copies.slot() for _ in range(TP - 1)]
        for j in range(1, TP):
            peer = at.q * TP + lax.rem(at.p + j, TP)
            copies.push(ins[0], outs[0].at[at.p], slots[j - 1], (at.r, peer))
        copies.local(ins[0], outs[0].at[at.p])
        yield "go"
        for j in range(1, TP):
            origin = lax.rem(at.p + TP - j, TP)
            copies.arrived(outs[0].at[origin], slots[j - 1], (at.r, at.s))

    return Job([value], [like((TP,) + value.shape, value.dtype)], run, {"plane"}, vmem=(0,))


def swap_plane(value):
    def run(at, copies, ins, outs):
        slots = [copies.slot() for _ in range(TP - 1)]
        for j in range(1, TP):
            other = lax.rem(at.p + j, TP)
            copies.push(
                ins[0].at[other], outs[0].at[at.p], slots[j - 1], (at.r, at.q * TP + other)
            )
        yield "go"
        for j in range(1, TP):
            origin = lax.rem(at.p + TP - j, TP)
            copies.arrived(outs[0].at[origin], slots[j - 1], (at.r, at.s))

    return Job([value], [like(value.shape, value.dtype)], run, {"plane"})


def line_sum(at, copies, source, held):
    slots = [copies.slot() for _ in range(at.Q - 1)]
    for j in range(1, at.Q):
        other = lax.rem(at.q + j, at.Q)
        there = (at.r, other * TP + at.p)
        copies.push(source.at[other], held.at[at.q], slots[j - 1], there)
    held[at.q] = source[at.q]
    yield "go"
    yield "go"
    for j in range(1, at.Q):
        origin = lax.rem(at.q + at.Q - j, at.Q)
        copies.arrived(held.at[origin], slots[j - 1], (at.r, at.s))
    total = held[0].astype(F32)
    for k in range(1, at.Q):
        total = total + held[k].astype(F32)
    return total


def line_plane(value):
    def run(at, copies, ins, outs):
        held, summed = outs[1:]
        total = yield from line_sum(at, copies, ins[0], held)
        summed[...] = total.astype(summed.dtype)
        slots = [copies.slot() for _ in range(TP - 1)]
        for j in range(1, TP):
            other = lax.rem(at.p + j, TP)
            there = (at.r, at.q * TP + other)
            copies.push(summed.at[other], outs[0].at[at.p], slots[j - 1], there)
        outs[0][at.p] = summed[at.p]
        yield "go"
        for j in range(1, TP):
            origin = lax.rem(at.p + TP - j, TP)
            copies.arrived(outs[0].at[origin], slots[j - 1], (at.r, at.s))

    scratch = ((value.shape, value.dtype), (value.shape[1:], value.dtype))
    outs = [like(value.shape[1:], value.dtype)]
    kinds = {"zall", "plane"}
    return Job([value], outs, run, kinds, vmem=(0,), relay=True, scratch=scratch)


def line_home(value):
    def run(at, copies, ins, outs):
        held, summed, got = outs[1:]
        total = yield from line_sum(at, copies, ins[0], held)
        summed[...] = total.astype(summed.dtype)
        r, s, own = visitor_of(at)
        _, _, _, here = home_of(at)
        slot = copies.slot()
        copies.push(summed, got, slot, (r, s), own == 0)
        yield "go"
        copies.arrived(got, slot, (at.r, at.s), here == 0)

        @pl.when(here == 0)
        def _():
            outs[0][...] = got[...]

        @pl.when(here == 1)
        def _():
            outs[0][...] = summed[...]

    one = (value.shape[1:], value.dtype)
    outs = [like(*one)]
    kinds = {"zall", "home"}
    return Job([value], outs, run, kinds, vmem=(0,), relay=True, scratch=((value.shape, value.dtype), one, one))


def finish(place, at, sliced, tiny, mix, taps):
    shard, D = mix.shape
    shapes = [shape for _, _, _, outs in sliced for shape in outs]
    tiny_shapes = [(1, shard)] * 4 + [(taps, shard), (2, HD)]
    arrays = [x for own, came, _, _ in sliced for x in (own, came) if x is not None] + [tiny, mix]
    where = at.p.astype(jnp.int32).reshape(1)

    def body(where_ref, *refs):
        ins, outs = refs[: len(arrays)], refs[len(arrays) :]

        ins = list(ins)
        first = 0
        for own, _, parts, made in sliced:
            mine = None if own is None else ins.pop(0)
            came = ins.pop(0)
            for k in range(TP):
                piece = came[k]
                if mine is not None:
                    piece = jnp.where(where_ref[0] == k, mine[k], piece)
                piece = piece.astype(F32)
                for start, width, out, base in parts:
                    there = slice(base + k * width, base + (k + 1) * width)
                    outs[first + out][:, there] = piece[:, start : start + width]
            first += len(made)
        total = ins[0][0]
        for k in range(1, TP):
            total = total + ins[0][k]
        for k in range(4):
            outs[first + k][...] = total[k : k + 1, :shard]
        outs[first + 4][...] = total[4 : 4 + taps, :shard]
        row = total[4 + taps : 5 + taps, :]
        outs[first + 5][0:1, :] = row[:, :HD]
        outs[first + 5][1:2, :] = row[:, HD:]
        outs[first + 6][...] = ins[1][...].astype(F32)

    outs = [like(shape, F32) for shape in shapes + tiny_shapes + [(shard, D)]]
    return plain_call(body, tuple(outs), (), where, *arrays, smem=1)


def swap_core(value):
    def run(at, copies, ins, outs):
        slots = [copies.slot() for _ in range(at.R - 1)]
        for j in range(1, at.R):
            other = lax.rem(at.r + j, at.R)
            copies.push(ins[0].at[other], outs[0].at[at.r], slots[j - 1], (other, at.s))
        yield "go"
        for j in range(1, at.R):
            origin = lax.rem(at.r + at.R - j, at.R)
            copies.arrived(outs[0].at[origin], slots[j - 1], (at.r, at.s))

    return Job([value], [like(value.shape, value.dtype)], run, {"core"})


def window_forward(place, value):
    reach = place.Q // 2

    def run(at, copies, ins, outs):
        slots = [copies.slot() for _ in range(reach)]
        there = (at.r, at.s + TP)
        copies.push(ins[0], outs[0].at[reach - 1], slots[0], there, at.q + 1 < at.Q)
        copies.local(ins[0], outs[0].at[reach])
        for j in range(1, reach + 1):
            yield "go"
            came = outs[0].at[reach - j]
            copies.arrived(came, slots[j - 1], (at.r, at.s), at.q >= j)
            if j < reach:
                passes = (at.q >= j) & (at.q + 1 < at.Q)
                copies.push(came, outs[0].at[reach - j - 1], slots[j], there, passes)

    shape = (reach + 1,) + value.shape
    outs = [like(shape, value.dtype)]
    return Job([value], outs, run, {"chain"}, vmem=(0,), relay=True)


def window_backward(place, value):
    reach = place.Q // 2

    def run(at, copies, ins, outs):
        got, summed = outs[1:]
        slots = [copies.slot() for _ in range(reach)]
        there = (at.r, at.s - TP)
        for j in range(reach, 0, -1):
            step = reach - j
            source = ins[0].at[step]
            if step > 0:
                came = (at.q + 1 < at.Q) & (at.q >= j)
                copies.arrived(got.at[step - 1], slots[step - 1], (at.r, at.s), came)
                total = jnp.where(came, got[step - 1].astype(F32), 0.0)
                summed[step - 1] = (total + ins[0][step].astype(F32)).astype(value.dtype)
                source = summed.at[step - 1]
            target = got.at[step] if j > 1 else outs[0]
            copies.push(source, target, slots[step], there, at.q >= j)
            yield "go"
        copies.arrived(outs[0], slots[reach - 1], (at.r, at.s), at.q + 1 < at.Q)

    piece = value.shape[1:]
    held = ((max(reach - 1, 1),) + piece, value.dtype)
    outs = [like(piece, value.dtype)]
    return Job([value], outs, run, {"chain"}, vmem=(0,), relay=True, scratch=(held, held))


def halo_tokens(value):
    rows = value.shape[0]

    def run(at, copies, ins, outs):
        ahead = [copies.slot() for _ in range(TP)]
        back = [copies.slot() for _ in range(TP)]
        first = (at.p == 0) & (at.q > 0)
        last = (at.p == TP - 1) & (at.q < at.Q - 1)
        for j in range(TP):
            tail = ins[0].at[pl.ds(rows - HALO, HALO)]
            there = (at.r, (at.q + 1) * TP + j)
            copies.push(tail, outs[0], ahead[j], there, last, ahead[0])
            head = ins[0].at[pl.ds(0, HALO)]
            there = (at.r, (at.q - 1) * TP + j)
            copies.push(head, outs[1], back[j], there, first, back[0])
        yield "go"
        copies.arrived(outs[0], ahead[0], (at.r, at.s), at.q > 0)
        copies.arrived(outs[1], back[0], (at.r, at.s), at.q < at.Q - 1)

    shape = (HALO,) + value.shape[1:]
    outs = [like(shape, value.dtype), like(shape, value.dtype)]
    return Job([value], outs, run, {"halo"}, vmem=(0,))


def side_by_side(*weights):
    layout, there = [], 0
    for index, weight in enumerate(weights):
        width = weight.shape[1] // TP
        layout.append((index, 0, width, width, there))
        there += width
    return layout


def spread_run(at, copies, sources, held, first, layout):
    def cut(index, start, stride, width, member):
        if stride == 0:
            return sources[index]
        return sources[index].at[:, pl.ds(pl.multiple_of(start + member * stride, 128), width)]

    def place_of(member, width, there):
        return held.at[first + member, :, pl.ds(there, width)]

    slots = [[copies.slot() for _ in layout] for _ in range(TP - 1)]
    for j in range(1, TP):
        other = lax.rem(at.p + j, TP)
        for k, (index, start, stride, width, there) in enumerate(layout):
            copies.push(
                cut(index, start, stride, width, other),
                place_of(at.p, width, there),
                slots[j - 1][k],
                (at.r, at.q * TP + other),
            )
    own = []
    for index, start, stride, width, there in layout:
        piece = cut(index, start, stride, width, at.p)
        sem = copies.recv.at[copies.slot()]
        own.append(pltpu.make_async_copy(piece, place_of(at.p, width, there), sem))
        own[-1].start()
    yield "go"
    for copy in own:
        copy.wait()
    for j in range(1, TP):
        origin = lax.rem(at.p + TP - j, TP)
        for k, (_, _, _, width, there) in enumerate(layout):
            copies.arrived(place_of(origin, width, there), slots[j - 1][k], (at.r, at.s))


def chain_run(at, copies, held, unit=TP):
    def block(r, q):
        return held.at[pl.ds(pl.multiple_of((r * at.Q + q) * unit, unit), unit)]

    right = [copies.slot() for _ in range(at.Q - 1)]
    left = [copies.slot() for _ in range(at.Q - 1)]
    across = [[copies.slot() for _ in range(at.Q)] for _ in range(at.R - 1)]

    def cross(q, index, cond):
        for j in range(1, at.R):
            other = lax.rem(at.r + j, at.R)
            copies.push(block(at.r, q), block(at.r, q), across[j - 1][index], (other, at.s), cond)

    copies.push(
        block(at.r, at.q), block(at.r, at.q), right[0], (at.r, at.s + TP), at.q < at.Q - 1
    )
    copies.push(block(at.r, at.q), block(at.r, at.q), left[0], (at.r, at.s - TP), at.q > 0)
    cross(at.q, 0, None)
    index = 0
    spots = {}
    for hop in range(1, at.Q):
        yield "go"
        from_left, from_right = at.q >= hop, at.q + hop < at.Q
        copies.arrived(block(at.r, at.q - hop), right[hop - 1], (at.r, at.s), from_left)
        if hop < at.Q - 1:
            copies.push(
                block(at.r, at.q - hop),
                block(at.r, at.q - hop),
                right[hop],
                (at.r, at.s + TP),
                from_left & (at.q < at.Q - 1),
            )
        copies.arrived(block(at.r, at.q + hop), left[hop - 1], (at.r, at.s), from_right)
        if hop < at.Q - 1:
            copies.push(
                block(at.r, at.q + hop),
                block(at.r, at.q + hop),
                left[hop],
                (at.r, at.s - TP),
                from_right & (at.q > 0),
            )
        for side, sign in ((from_left, -1), (from_right, 1)):
            spots[(hop, sign)] = [copies.slot() for _ in range(at.R - 1)]
            for j in range(1, at.R):
                other = lax.rem(at.r + j, at.R)
                piece = block(at.r, at.q + sign * hop)
                copies.push(piece, piece, spots[(hop, sign)][j - 1], (other, at.s), side)
    yield "go"
    for j in range(1, at.R):
        source = lax.rem(at.r + at.R - j, at.R)
        copies.arrived(block(source, at.q), across[j - 1][0], (at.r, at.s))
        for hop in range(1, at.Q):
            for sign in (-1, 1):
                there = at.q + sign * hop
                copies.arrived(
                    block(source, there),
                    spots[(hop, sign)][j - 1],
                    (at.r, at.s),
                    at.q >= hop if sign < 0 else there < at.Q,
                )


def spread(*sources):
    layout = side_by_side(*sources)

    def run(at, copies, ins, outs):
        yield from spread_run(at, copies, ins, outs[0], 0, layout)

    shape = (TP, sources[0].shape[0], sum(part[3] for part in layout))
    outs = [like(shape, sources[0].dtype)]
    return Job(sources, outs, run, {"plane"}, vmem=tuple(range(len(sources))), late=True)


def spread_all(place, source, layout):
    def run(at, copies, ins, outs):
        yield from spread_run(at, copies, ins, outs[0], (at.r * at.Q + at.q) * TP, layout)
        yield from chain_run(at, copies, outs[0])

    shape = (place.R * place.S, source.shape[0], sum(part[3] for part in layout))
    outs = [like(shape, source.dtype)]
    return Job([source], outs, run, {"plane", "chain", "core"}, vmem=(0,), relay=True)


def home_all(place, source):
    def run(at, copies, ins, outs):
        r, s, slot, here = home_of(at)
        _, _, own = visitor_of(at)
        index = copies.slot()
        copies.push(ins[0], outs[0].at[slot], index, (r, s), here == 0)
        copy = pltpu.make_async_copy(ins[0], outs[0].at[slot], copies.recv.at[copies.slot()])
        when(here == 1, copy.start)
        yield "go"
        when(here == 1, copy.wait)
        copies.arrived(outs[0].at[at.r * at.Q + at.q], index, (at.r, at.s), own == 0)
        yield from chain_run(at, copies, outs[0], 1)

    outs = [like((place.R * place.Q,) + source.shape, source.dtype)]
    return Job([source], outs, run, {"home", "chain", "core"}, vmem=(0,), relay=True)


FACTOR = 1.0 / math.sqrt(HD)


def masked_keys(kv_ref, first, kv_s):
    index = lax.broadcasted_iota(jnp.int32, kv_ref.shape, 0)
    kv_s[...] = jnp.where(index >= first, kv_ref[...].astype(F32), 0.0).astype(BF)


def attend_forward(q, kv, q_seg, key_seg, first, block):
    N, QS = q.shape
    M, KS = kv.shape[0], kv.shape[1] // 2
    ahead = M - N
    span = ahead + block
    kv_heads = KS // HD
    groups = QS // KS

    def body(first_ref, q_ref, kv_ref, qs_ref, ks_ref, o_ref, kv_s):
        masked_keys(kv_ref, first_ref[0], kv_s)

        @pl.loop(0, N // block)
        def _(i):
            start = pl.multiple_of(i * block, block)
            here, keys = pl.ds(start, block), pl.ds(start, span)
            row = lax.broadcasted_iota(jnp.int32, (block, span), 0) + ahead
            col = lax.broadcasted_iota(jnp.int32, (block, span), 1)
            open_ = (qs_ref[here, :1] == ks_ref[:1, keys]) & (col <= row)
            open_ = open_ & (col + start >= first_ref[0])
            open_ = jnp.concatenate([open_] * groups, axis=0)
            queries = q_ref[here, :]
            done = []
            for k in range(kv_heads):
                mine = [
                    queries[:, (k * groups + g) * HD : (k * groups + g + 1) * HD]
                    for g in range(groups)
                ]
                key = kv_s[keys, k * HD : (k + 1) * HD]
                value = kv_s[keys, KS + k * HD : KS + (k + 1) * HD]
                score = jnp.where(open_, dot_nt(jnp.concatenate(mine, axis=0), key) * FACTOR, MASKED)
                weight = jnp.exp(score - jnp.max(score, axis=-1, keepdims=True))
                weight = weight / jnp.sum(weight, axis=-1, keepdims=True)
                out = dot(weight.astype(BF), value).astype(BF)
                done.extend(out[g * block : (g + 1) * block] for g in range(groups))
            o_ref[here, :] = jnp.concatenate(done, axis=1)

    return attend_call(
        body, like((N, QS)), [pltpu.VMEM(kv.shape, BF)], 4 * N * span * QS, first, q, kv, q_seg, key_seg
    )


def attend_call(body, outs, scratch, flops, first, *arrays):
    return pl.pallas_call(
        body,
        out_shape=outs,
        in_specs=[pl.BlockSpec(memory_space=pltpu.SMEM)]
        + [pl.BlockSpec(memory_space=pltpu.VMEM) for _ in arrays],
        out_specs=jax.tree.map(lambda _: pl.BlockSpec(memory_space=pltpu.VMEM), outs),
        scratch_shapes=scratch,
        cost_estimate=pl.CostEstimate(flops=flops, bytes_accessed=COST, transcendentals=0),
    )(first, *arrays)


def attend_backward(q, kv, d_o, q_seg, key_seg, first, block):
    N, QS = q.shape
    M, KS = kv.shape[0], kv.shape[1] // 2
    ahead = M - N
    span = ahead + block
    kv_heads = KS // HD
    groups = QS // KS

    def body(first_ref, q_ref, kv_ref, do_ref, qs_ref, ks_ref, dq_ref, dkv_ref, kv_s, *sums):
        masked_keys(kv_ref, first_ref[0], kv_s)
        for total in sums:
            total[...] = jnp.zeros_like(total)

        @pl.loop(0, N // block)
        def _(i):
            start = pl.multiple_of(i * block, block)
            here, keys = pl.ds(start, block), pl.ds(start, span)
            row = lax.broadcasted_iota(jnp.int32, (span, block), 0)
            col = lax.broadcasted_iota(jnp.int32, (span, block), 1) + ahead
            open_ = (ks_ref[keys, :1] == qs_ref[:1, here]) & (row <= col)
            open_ = open_ & (row + start >= first_ref[0])
            open_ = jnp.concatenate([open_] * groups, axis=1)
            queries, pulls = q_ref[here, :], do_ref[here, :]

            def heads_of(values, k):
                return jnp.concatenate(
                    [
                        values[:, (k * groups + g) * HD : (k * groups + g + 1) * HD]
                        for g in range(groups)
                    ],
                    axis=0,
                )

            done = []
            for k in range(kv_heads):
                mine, pull = heads_of(queries, k), heads_of(pulls, k)
                key = kv_s[keys, k * HD : (k + 1) * HD]
                value = kv_s[keys, KS + k * HD : KS + (k + 1) * HD]
                score = jnp.where(open_, dot_nt(key, mine) * FACTOR, MASKED)
                weight = jnp.exp(score - jnp.max(score, axis=0, keepdims=True))
                weight = weight / jnp.sum(weight, axis=0, keepdims=True)
                d_weight = dot_nt(value, pull)
                delta = jnp.sum(weight * d_weight, axis=0, keepdims=True)
                d_score = (weight * (d_weight - delta)).astype(BF)
                sums[k][keys, :] += dot(d_score, mine) * FACTOR
                sums[kv_heads + k][keys, :] += dot(weight.astype(BF), pull)
                dq = dot_tn(d_score, key) * FACTOR
                done.extend(dq[g * block : (g + 1) * block] for g in range(groups))
            dq_ref[here, :] = jnp.concatenate(done, axis=1)

        dkv_ref[...] = jnp.concatenate([total[...] for total in sums], axis=1)

    return attend_call(
        body,
        (like((N, QS), F32), like((M, 2 * KS), F32)),
        [pltpu.VMEM(kv.shape, BF)] + [pltpu.VMEM((M, HD), F32) for _ in range(2 * kv_heads)],
        10 * N * span * QS,
        first,
        q,
        kv,
        d_o,
        q_seg,
        key_seg,
    )


def turned(values, cosine, sine):
    lane = lax.broadcasted_iota(jnp.int32, values.shape, 1)
    ahead = pltpu.roll(values, 2 * HD - HD // 2, 1)
    behind = pltpu.roll(values, HD // 2, 1)
    other = jnp.where(lax.rem(lane, HD) < HD // 2, ahead, behind)
    return values * cosine + other * sine


def head_means(values):
    lane = lax.broadcasted_iota(jnp.int32, values.shape, 1)
    front = lane < HD
    first = jnp.sum(jnp.where(front, values, 0.0), axis=-1, keepdims=True)
    second = jnp.sum(jnp.where(front, 0.0, values), axis=-1, keepdims=True)
    return jnp.where(front, first, second) * (1.0 / HD)


def pairs_of(width):
    return [slice(c, c + 2 * HD) for c in range(0, width, 2 * HD)]


def heads_forward(n3, w, gains, cosine, sine, QS, KS):
    N = n3.shape[0]

    def body(n3_ref, w_ref, gains_ref, cos_ref, sin_ref, pre_ref, q_ref, kv_ref):
        pre_ref[...] = dot(n3_ref[...], w_ref[:, : QS + 2 * KS])

        def normed(cols, row):
            values = pre_ref[:, cols]
            inverse = lax.rsqrt(head_means(values * values) + EPSILON)
            values = values * inverse * gains_ref[row : row + 1, :]
            return turned(values, cos_ref[...], sin_ref[...]).astype(BF)

        for cols in pairs_of(QS):
            q_ref[:, cols] = normed(cols, 0)
        for cols in pairs_of(KS):
            kv_ref[:, cols] = normed(slice(QS + cols.start, QS + cols.stop), 1)
        kv_ref[:, KS:] = pre_ref[:, QS + KS :].astype(BF)

    outs = (like((N, QS + 2 * KS), F32), like((N, QS)), like((N, 2 * KS)))
    return plain_call(body, outs, (), n3, w, gains, cosine, sine)


def heads_backward(d_q, d_kv, got, count, pre, gains, cosine, sine, n3, g3, o, w):
    N, QS = d_q.shape
    KS = d_kv.shape[1] // 2
    D = n3.shape[1]
    W = QS + 2 * KS
    step = 256

    def body(
        count_ref, dq_ref, dkv_ref, got_ref, pre_ref, gains_ref, cos_ref, sin_ref, n3_ref, g3_ref,
        o_ref, w_ref, part_ref, rows_ref, heads_ref, all_ref,
    ):
        later = jnp.where(count_ref[0] > 0, got_ref[...].astype(F32), 0.0)
        d_kv_sum = dkv_ref[...] + later
        all_ref[:, QS + KS :] = d_kv_sum[:, KS:].astype(BF)

        def back(pull, cols, row):
            values = pre_ref[:, cols]
            inverse = lax.rsqrt(head_means(values * values) + EPSILON)
            pull = turned(pull, cos_ref[...], -sin_ref[...])
            scaled = pull * gains_ref[row : row + 1, :]
            mean = head_means(scaled * values)
            d_values = inverse * scaled - values * (inverse * inverse * inverse) * mean
            all_ref[:, cols] = d_values.astype(BF)
            return jnp.sum(pull * values * inverse, axis=0, keepdims=True)

        of_queries = [back(dq_ref[:, cols], cols, 0) for cols in pairs_of(QS)]
        of_keys = [
            back(d_kv_sum[:, cols], slice(QS + cols.start, QS + cols.stop), 1)
            for cols in pairs_of(KS)
        ]
        heads_ref[0:1, :] = sum(of_queries[1:], of_queries[0])
        heads_ref[1:2, :] = sum(of_keys[1:], of_keys[0])
        values, outputs = all_ref[...], o_ref[...]

        @pl.loop(0, D // step)
        def _(c):
            cols = pl.ds(pl.multiple_of(c * step, step), step)
            part_ref[:, cols] = dot_nt(values, w_ref[cols, :W])
            left = n3_ref[:, cols].astype(F32).T.astype(BF)
            rows_ref[cols, :W] = dot(left, values).astype(BF)
            right = g3_ref[:, cols].astype(F32).T.astype(BF)
            rows_ref[cols, W:] = dot(right, outputs).astype(BF)

    outs = (like((N, D), F32), like((D, W + QS)), like((2, 2 * HD), F32))
    return plain_call(
        body, outs, [pltpu.VMEM((N, W), BF)],
        count, d_q, d_kv, got, pre, gains, cosine, sine, n3, g3, o, w, smem=1,
    )


def plain_call(body, outs, scratch, *arrays, smem=0):
    return pl.pallas_call(
        body,
        out_shape=outs,
        in_specs=[
            pl.BlockSpec(memory_space=pltpu.SMEM if k < smem else pltpu.VMEM)
            for k in range(len(arrays))
        ],
        out_specs=tuple(pl.BlockSpec(memory_space=pltpu.VMEM) for _ in outs),
        scratch_shapes=scratch,
        cost_estimate=pl.CostEstimate(flops=0, bytes_accessed=COST, transcendentals=0),
    )(*arrays)


class Plane:
    def __init__(self, at, copies):
        self.at, self.copies = at, copies

    def swap(self, send, recv):
        at, slots = self.at, [self.copies.slot() for _ in range(TP - 1)]
        for j in range(1, TP):
            other = lax.rem(at.p + j, TP)
            there = (at.r, at.q * TP + other)
            self.copies.push(send.at[other], recv.at[at.p], slots[j - 1], there)
        return functools.partial(self.arrive, recv, slots)

    def gather(self, held):
        at, slots = self.at, [self.copies.slot() for _ in range(TP - 1)]
        for j in range(1, TP):
            there = (at.r, at.q * TP + lax.rem(at.p + j, TP))
            self.copies.push(held.at[at.p], held.at[at.p], slots[j - 1], there)
        return functools.partial(self.arrive, held, slots)

    def mate(self, k):
        p = self.at.p
        if k == 1:
            return p + 1 - 2 * lax.rem(p, 2)
        if k == 2:
            return p + 2 - 4 * (p // 2)
        return TP - 1 - p if k == TP - 1 else p

    def to_mate(self, source, held, k):
        at, slot = self.at, self.copies.slot()
        there = (at.r, at.q * TP + self.mate(k))
        self.copies.push(source, held.at[k], slot, there)
        return functools.partial(self.copies.arrived, held.at[k], slot, (at.r, at.s))

    def spread_mates(self, held):
        return [self.to_mate(held.at[0], held, k) for k in range(1, TP)]

    def sum_mates(self, own, recv):
        for k in range(1, TP):
            own = own + recv[k].astype(F32)
        return own

    def arrive(self, held, slots):
        at = self.at
        for j in range(1, TP):
            origin = lax.rem(at.p + TP - j, TP)
            self.copies.arrived(held.at[origin], slots[j - 1], (at.r, at.s))

    def settle(self, own, recv, n):
        total = own[pl.ds(pl.multiple_of(self.at.p * n, n), n), :]
        for j in range(1, TP):
            total = total + recv[lax.rem(self.at.p + j, TP)].astype(F32)
        return total


def columns_of(count, width, action):
    @pl.loop(0, count)
    def _(c):
        action(pl.ds(pl.multiple_of(c * width, width), width))


def rows_of(span, action):
    first, count = span

    @pl.loop(0, count // 64)
    def _(i):
        action(pl.ds(pl.multiple_of(first + i * 64, 64), 64))


def activate(gu, act, span, FS):
    def go(rows):
        gate, up = gu[rows, :FS], gu[rows, FS:]
        act[rows, :] = (jax.nn.silu(gate) * up).astype(BF)

    rows_of(span, go)


def deactivate(gu, d_act, dgu, span, FS):
    def go(rows):
        gate, up, pull = gu[rows, :FS], gu[rows, FS:], d_act[rows, :]
        sigma = jax.nn.sigmoid(gate)
        dgu[rows, :FS] = (pull * up * sigma * (1.0 + gate * (1.0 - sigma))).astype(BF)
        dgu[rows, FS:] = (pull * (gate * sigma)).astype(BF)

    rows_of(span, go)


def multiply(held, weights, out, span, parts):
    first, count = span
    n, D = held.shape[1:]
    values = held[first // n : (first + count) // n].reshape(count, D)
    rows = pl.ds(first, count)

    def go(cols):
        out[rows, cols] = dot(values, weights[:, cols])

    columns_of(parts, weights.shape[1] // parts, go)


def project(left, weights, part, span, send=None, order=None):
    first, count = span
    step = 256
    rows = pl.ds(first, count)
    n = send.shape[1] if send is not None else count

    def go(cols):
        out = dot_nt(left[rows, :], weights[cols, :])
        part[rows, cols] = out
        if send is not None:
            for k in range(first // n, (first + count) // n):
                block = out[k * n - first : (k + 1) * n - first].astype(BF)
                send[k if order is None else order[k], :, cols] = block

    columns_of(weights.shape[0] // step, step, go)


def feed_kernel(place, ident, mode, arrays, D, FS, n, side=0):
    N = n * TP
    R = place.R
    half = D // R
    W = 2 * FS if mode == "both" else 3 * FS
    forward, backward = mode in ("fwd", "both"), mode in ("both", "bwd")
    VM, HB = pltpu.VMEM, pl.ANY
    ins, scratch, outs = {}, {}, {}
    ins["weights"] = HB
    if mode == "fwd":
        ins.update(a_g=VM, h_in=VM, gain_next=VM)
        outs.update(
            h_out=((n, D), F32, VM), next_g=((TP, n, D), BF, VM), gu_out=((N, 2 * FS), F32, HB)
        )
    else:
        ins.update(first_part=VM, h_in=VM, gain=VM)
        outs.update(
            g_out=((n, D), F32, VM),
            next_g=((TP, n, D), BF, VM),
            d_gain=((1, D), F32, VM),
            half_out=((half, FS if mode == "both" else W), BF, VM),
        )
        scratch.update(
            first_send=((TP, n, D), BF),
            first_got=((TP, n, D), BF),
            a_v=((TP, n, D), BF),
            e_v=((TP, n, D), BF),
            d_act=((N, FS), F32),
            dgu=((N, 2 * FS), BF),
            grad_send=((R - 1, half, W), BF),
            grad_got=((R - 1, half, W), BF),
        )
    if mode == "both":
        ins.update(e_g=HB, e_own=VM, down=HB)
        down_piece = (half // place.Q, FS)
        outs.update(
            mid_out=((n, D), F32, VM),
            o_send=((TP, n, D), BF, VM),
            o_base=((n, D), F32, VM),
            down_out=((place.Q,) + down_piece, BF, VM),
            half_up=((half, FS), BF, VM),
        )
        scratch.update(
            down_send=((R - 1, half, FS), BF),
            down_got=((R - 1, half, FS), BF),
            down_half=((place.Q,) + down_piece, BF),
        )
    if mode == "bwd":
        ins.update(a_g=HB, gu_in=HB, g_in=VM, h_before=VM, gain_before=VM)
        piece = (half // place.Q, side)
        ins.update(side_in=VM)
        outs.update(
            d_gain_before=((1, D), F32, VM),
            halo=((HALO, D), BF, VM),
            side_out=((place.Q,) + piece, BF, VM),
        )
        scratch.update(side_got=((R - 1, half, side), BF), side_half=((place.Q,) + piece, BF))
    scratch.update(
        w=((D, 2 * FS), BF),
        wd=((D, FS), BF),
        gu=((N, 2 * FS), F32),
        act=((N, FS), BF),
        part=((N, D), F32),
        send=((TP, n, D), BF),
        got=((TP, n, D), BF),
    )
    in_names, out_names, scratch_names = list(ins), list(outs), list(scratch)
    kinds = {"plane"}
    if backward:
        kinds.add("core")
    if mode == "bwd":
        kinds.update({"back", "zall"})
    if mode == "both":
        kinds.add("zall")
    unit = D // (R * place.Q)
    sems = 32 + 3 * R + 4 * place.Q + 3 * R * place.Q

    def body(*refs):
        names = in_names + out_names + scratch_names
        v = dict(zip(names, refs))
        at = place.here()
        copies = Copies(refs[len(names)], refs[len(names) + 1])
        plane = Plane(at, copies)
        loads = refs[len(names) + 2]
        pending = {}

        def load(name, src, dst):
            pending[name] = pltpu.make_async_copy(src, dst, loads.at[len(pending)])
            pending[name].start()

        def load_blocks(name, source, target):
            for k in range(TP):
                load(name + str(k), source.at[plane.mate(k)], target.at[k])

        def loaded(*names):
            for name in names:
                pending[name].wait()

        def loaded_blocks(name):
            loaded(*[name + str(k) for k in range(TP)])

        if mode == "both":
            load("w", v["weights"], v["w"])
            load_blocks("e", v["e_g"], v["e_v"])
            own_rows = pl.ds(pl.multiple_of((at.r * at.Q + at.q) * unit, unit), unit)
            load("wd", v["down"], v["wd"].at[own_rows])
        else:
            load("w", v["weights"].at[:, : 2 * FS], v["w"])
            load("wd", v["weights"].at[:, 2 * FS : 3 * FS], v["wd"])
        if mode == "bwd":
            for k in range(TP):
                rows = pl.ds(pl.multiple_of(plane.mate(k) * n, n), n)
                load("gu%d" % k, v["gu_in"].at[rows], v["gu"].at[pl.ds(k * n, n)])
            load_blocks("a", v["a_g"], v["a_v"])
        meet(at, kinds)
        w, wd, gu, act = (v[k] for k in ("w", "wd", "gu", "act"))
        part, send, got = (v[k] for k in ("part", "send", "got"))

        def along_line(source, target):
            slots = [copies.slot() for _ in range(at.Q - 1)]
            for j in range(1, at.Q):
                other = lax.rem(at.q + j, at.Q)
                there = (at.r, other * TP + at.p)
                copies.push(source.at[other], target.at[at.q], slots[j - 1], there)
            target[at.q] = source[at.q]
            return slots

        def line_done(target, slots):
            for j in range(1, at.Q):
                origin = lax.rem(at.q + at.Q - j, at.Q)
                copies.arrived(target.at[origin], slots[j - 1], (at.r, at.s))

        def turned_rows(held, j):
            first_col = lax.rem(at.r + j, R) * half
            cols = pl.ds(pl.multiple_of(first_col, 128), half)
            return held[:, :, cols].reshape(N, half).astype(F32).T.astype(BF)

        if mode != "fwd":
            first = v["first_part"]
            mine = [pl.ds(pl.multiple_of(plane.mate(k) * n, n), n) for k in range(TP)]
            waits = []
            for k in range(1, TP):
                v["first_send"][k] = first[mine[k], :].astype(BF)
                waits.append(plane.to_mate(v["first_send"].at[k], v["first_got"], k))
        if mode == "fwd":
            pending["w"].wait()
            multiply(v["a_g"], w, gu, (0, N), 3)
            save = pltpu.make_async_copy(gu, v["gu_out"], loads.at[len(pending)])
            save.start()
            activate(gu, act, (0, N), FS)
            pending["wd"].wait()
            project(act, wd, part, (0, N), send)
            wait = plane.swap(send, got)
            wait()
            h_out = v["h_in"][...] + plane.settle(part, got, n)
            v["h_out"][...] = h_out
            v["next_g"][at.p] = (h_out * inverse_rms(h_out) * v["gain_next"][...]).astype(BF)
            wait = plane.gather(v["next_g"])
            wait()
            save.wait()
            copies.drain()
            return
        everything, own, near, far = (0, N), (0, n), (n, 2 * n), (3 * n, n)
        d_act, dgu = v["d_act"], v["dgu"]
        if mode == "both":
            loaded("wd")
            steps = chain_run(at, copies, wd, unit)
            next(steps)
            next(steps)
            for wait in waits:
                wait()
            h = v["h_in"][...] + plane.sum_mates(first[mine[0], :], v["first_got"])
            v["mid_out"][...] = h
            v["a_v"][0] = (h * inverse_rms(h) * v["gain"][...]).astype(BF)
            waits = plane.spread_mates(v["a_v"])
            for _ in range(at.Q - 3):
                next(steps)
            loaded("w")
            loaded_blocks("e")
            for span, awaited in ((own, ()), (near, waits[:2]), (far, waits[2:])):
                for wait in awaited:
                    wait()
                multiply(v["a_v"], w, gu, span, 3)
                activate(gu, act, span, FS)
            for _ in steps:
                pass
            down_slots = [copies.slot() for _ in range(R - 1)]
            for j in range(1, R):
                v["down_send"][j - 1] = dot(turned_rows(v["e_v"], j), act[...]).astype(BF)
                there = (lax.rem(at.r + j, R), at.s)
                copies.push(v["down_send"].at[j - 1], v["down_got"].at[j - 1], down_slots[j - 1], there)
            total = dot(turned_rows(v["e_v"], 0), act[...])
            for j in range(1, R):
                copies.arrived(v["down_got"].at[j - 1], down_slots[j - 1], (at.r, at.s))
                total = total + v["down_got"][j - 1].astype(F32)
            v["down_half"][...] = total.astype(BF).reshape(v["down_half"].shape)
            line_slots = along_line(v["down_half"], v["down_out"])
            multiply(v["e_v"], wd, d_act, everything, 3)
            waits = []
            for span, slots in ((near, (1, 2)), (far, (3,))):
                deactivate(gu, d_act, dgu, span, FS)
                project(dgu, w, part, span, send)
                waits.extend(plane.to_mate(send.at[k], got, k) for k in slots)
            deactivate(gu, d_act, dgu, own, FS)
            project(dgu, w, part, own)
        else:
            side_slots = [copies.slot() for _ in range(R - 1)]
            for j in range(1, R):
                other = lax.rem(at.r + j, R)
                copies.push(
                    v["side_in"].at[other], v["side_got"].at[j - 1], side_slots[j - 1], (other, at.s)
                )
            loaded_blocks("gu")
            activate(gu, act, everything, FS)
            for wait in waits:
                wait()
            h = v["h_in"][...]
            before = v["h_before"][...]
            r_before = inverse_rms(before)
            d_normed = plane.sum_mates(first[mine[0], :], v["first_got"])
            v["d_gain_before"][...] = jnp.sum(d_normed * before * r_before, axis=0, keepdims=True)
            g_mid = v["g_in"][...] + rms_pull(d_normed, before, r_before, v["gain_before"][...])
            v["g_out"][...] = g_mid
            v["e_v"][0] = g_mid.astype(BF)
            waits = plane.spread_mates(v["e_v"])
            loaded("w", "wd")
            loaded_blocks("a")
            total = v["side_in"][at.r].astype(F32)
            for j in range(1, R):
                copies.arrived(v["side_got"].at[j - 1], side_slots[j - 1], (at.r, at.s))
                total = total + v["side_got"][j - 1].astype(F32)
            v["side_half"][...] = total.astype(BF).reshape(v["side_half"].shape)
            line_slots = along_line(v["side_half"], v["side_out"])
            returns = []
            for span, awaited, slots in (
                (own, (), ()),
                (near, waits[:2], (1, 2)),
                (far, waits[2:], (3,)),
            ):
                for wait in awaited:
                    wait()
                multiply(v["e_v"], wd, d_act, span, 3)
                deactivate(gu, d_act, dgu, span, FS)
                project(dgu, w, part, span, send if slots else None)
                returns.extend(plane.to_mate(send.at[k], got, k) for k in slots)
            waits = returns
        values, pulls = v["a_v"], v["e_v"]

        slots = [copies.slot() for _ in range(R - 1)]
        for j in range(1, R):
            left = turned_rows(values, j)

            def put(cols, left=left, j=j):
                v["grad_send"][j - 1, :, cols] = dot(left, v["dgu"][:, cols]).astype(BF)

            columns_of(3, 2 * FS // 3, put)
            if mode == "bwd":
                v["grad_send"][j - 1, :, 2 * FS :] = dot(turned_rows(pulls, j), act[...]).astype(BF)
            other = lax.rem(at.r + j, R)
            copies.push(
                v["grad_send"].at[j - 1], v["grad_got"].at[j - 1], slots[j - 1], (other, at.s)
            )
        for wait in waits:
            wait()
        d_normed = plane.sum_mates(part[:n, :], got)
        r = inverse_rms(h)
        base = v["e_own"][...].astype(F32) if mode == "both" else v["g_out"][...]
        v["d_gain"][...] = jnp.sum(d_normed * h * r, axis=0, keepdims=True)
        g_new = base + rms_pull(d_normed, h, r, v["gain"][...])
        v["g_out"][...] = g_new
        v["next_g"][at.p] = g_new.astype(BF)
        wait = plane.gather(v["next_g"])
        if mode == "bwd":
            back = [copies.slot() for _ in range(TP)]
            for j in range(TP):
                copies.push(
                    v["next_g"].at[at.p, pl.ds(0, HALO)],
                    v["halo"],
                    back[j],
                    (at.r, (at.q - 1) * TP + j),
                    (at.p == 0) & (at.q > 0),
                    back[0],
                )
        if mode == "both":
            project(act, wd, part, everything, v["o_send"], [plane.mate(k) for k in range(TP)])
            v["o_base"][...] = h + part[:n, :]
        left = turned_rows(values, 0)
        for j in range(1, R):
            copies.arrived(v["grad_got"].at[j - 1], slots[j - 1], (at.r, at.s))

        def finish(target, base, shift):
            step = FS // 3

            @pl.loop(0, 3)
            def _(c):
                cols = pl.ds(pl.multiple_of(base + c * step, 128), step)
                total = dot(left, v["dgu"][:, cols])
                for j in range(1, R):
                    total = total + v["grad_got"][j - 1, :, cols].astype(F32)
                there = pl.ds(pl.multiple_of(base - shift + c * step, 128), step)
                target[:, there] = total.astype(BF)

        finish(v["half_out"], 0, 0)
        if mode == "both":
            finish(v["half_up"], FS, FS)
        else:
            finish(v["half_out"], FS, 0)
        if mode == "bwd":
            total = dot(turned_rows(pulls, 0), act[...])
            for j in range(1, R):
                total = total + v["grad_got"][j - 1, :, 2 * FS :].astype(F32)
            v["half_out"][:, 2 * FS :] = total.astype(BF)
        wait()
        if mode == "bwd":
            copies.arrived(v["halo"], back[0], (at.r, at.s), at.q < at.Q - 1)
            line_done(v["side_out"], line_slots)
        if mode == "both":
            line_done(v["down_out"], line_slots)
        copies.drain()

    results = pl.pallas_call(
        body,
        out_shape=tuple(like(outs[k][0], outs[k][1]) for k in out_names),
        in_specs=[pl.BlockSpec(memory_space=ins[k]) for k in in_names],
        out_specs=tuple(pl.BlockSpec(memory_space=outs[k][2]) for k in out_names),
        scratch_shapes=[pltpu.VMEM(*scratch[k]) for k in scratch_names]
        + [pltpu.SemaphoreType.DMA((sems,)), pltpu.SemaphoreType.DMA((sems,))]
        + [pltpu.SemaphoreType.DMA((12,))],
        compiler_params=pltpu.CompilerParams(collective_id=ident, has_side_effects=True),
        cost_estimate=pl.CostEstimate(flops=0, bytes_accessed=COST, transcendentals=0),
        name="feed_%s" % mode,
    )(*[arrays[k] for k in in_names])
    return dict(zip(out_names, results))


def doc_info(positions, lengths):
    doc_ends = jnp.cumsum(lengths, dtype=jnp.int32)
    passed = positions[:, None] >= doc_ends[None, :]
    segment = jnp.sum(passed.astype(jnp.int32), axis=1, dtype=jnp.int32)
    opening = jnp.sum(jnp.where(passed, lengths[None, :], 0), axis=1, dtype=jnp.int32)
    return (segment, positions - opening)


def inverse_rms(values):
    return lax.rsqrt(jnp.mean(values * values, axis=-1, keepdims=True) + EPSILON)


def rms_pull(upstream, values, inverse, norm_gain):
    scaled = upstream * norm_gain
    product_mean = jnp.mean(scaled * values, axis=-1, keepdims=True)
    return inverse * scaled - values * (inverse * inverse * inverse) * product_mean


def settle(own, arrived, p):
    index = jnp.arange(TP, dtype=jnp.int32)[:, None, None]
    others = jnp.where(index == p, 0.0, arrived.astype(F32))
    mine = lax.dynamic_index_in_dim(own, p, 0, keepdims=False)
    return mine + jnp.sum(others, axis=0)


def per_device(
    place,
    tokens,
    doc_lengths,
    cotangent,
    gain_conv,
    w_in,
    kernel,
    w_mix,
    gain_ffa,
    gate_a,
    up_a,
    down_a,
    gain_att,
    w_query,
    w_key,
    w_value,
    head_gains,
    w_attout,
    gain_ffb,
    gate_b,
    up_b,
    down_b,
):
    R, S, Q = place.R, place.S, place.Q
    n, D = tokens.shape[1], tokens.shape[2]
    shard = w_in.shape[0]
    FS = gate_a.shape[1] // TP
    CS = D // TP
    QS, KS = H * HD // TP, KVH * HD // TP
    taps = kernel.shape[0]
    N = n * TP
    r, s = lax.axis_index("rows"), lax.axis_index("seq")
    q, p = s // TP, lax.rem(s, TP)
    lengths = doc_lengths[0]

    columns = [[a * S + b * TP + c for a in range(R) for b in range(Q)] for c in range(TP)]
    lines = [[b * TP + c for b in range(Q)] for c in range(TP)]

    def gather_rest(plane):
        flat = plane.reshape(TP * shard, -1)
        return lax.all_gather(
            flat, ("rows", "seq"), axis=0, tiled=True, axis_index_groups=columns
        )

    def by_row(grads):
        return grads.astype(BF).reshape(R, S * shard, -1)

    def own_rows(rows, came, *later):
        return lax.optimization_barrier((collect(rows, came, r).astype(BF),) + later)

    def reduce_line(half):
        part = lax.psum_scatter(
            half, "seq", scatter_dimension=0, tiled=True, axis_index_groups=lines
        )
        return part.reshape(TP, shard, part.shape[1])

    in_layout = [(0, k * D, CS, CS, k * CS) for k in range(3)]
    small = jnp.stack([gain_conv, gain_ffa, gain_att, gain_ffb] + [kernel[i] for i in range(taps)])
    small = jnp.pad(small, ((0, 16 - 4 - taps), (0, 128 - shard)))

    mine = tokens[0]
    (tok_g,), (halo_a, halo_b), (in_g,), (mix_g,), (small_g,), (ffa_p,) = exchange(
        place,
        0,
        [
            gather_plane(mine),
            halo_tokens(mine),
            spread_all(place, w_in, in_layout),
            home_all(place, w_mix),
            spread_all(place, small, [(0, 0, 0, 128, 0)]),
            spread(gate_a, up_a, down_a.T, w_query, w_key, w_value, w_attout.T),
        ],
    )
    wide = gather_rest(ffa_p)
    w_att = wide[:, 3 * FS :]
    w_mix_s = mix_g.reshape(CS, D)
    vectors = small_g[:, : 4 + taps, :shard].transpose(1, 0, 2).reshape(4 + taps, D).astype(F32)
    g_conv, g_ffa, g_att, g_ffb = (vectors[i] for i in range(4))
    kernel_f = lax.dynamic_slice_in_dim(vectors[4:], p * CS, CS, 1)
    w_in_s = in_g.reshape(D, 3 * CS)

    def own(parts, index):
        return lax.dynamic_index_in_dim(parts, index, 0, keepdims=False).astype(F32)

    def collect(parts, came, index):
        slot = jnp.arange(came.shape[0], dtype=jnp.int32).reshape((-1,) + (1,) * (came.ndim - 1))
        mine_part = lax.dynamic_index_in_dim(parts, index, 0, keepdims=True).astype(F32)
        return jnp.sum(jnp.where(slot == index, mine_part, came.astype(F32)), axis=0)

    def after_core(parts, came):
        summed = collect(parts, came, r)
        return summed.reshape((Q, TP) + summed.shape[1:])

    total = S * n
    pos_ext = q * N - HALO + jnp.arange(N + 2 * HALO, dtype=jnp.int32)
    seg_ext, rel_ext = doc_info(pos_ext, lengths)
    valid = ((pos_ext >= 0) & (pos_ext < total))[:, None]
    x_ext = jnp.concatenate([halo_a, tok_g.reshape(N, D), halo_b], axis=0)
    x_ext = jnp.where(valid, x_ext, jnp.zeros_like(x_ext)).astype(F32)
    r0_ext = inverse_rms(x_ext)
    n1_ext = (x_ext * r0_ext * g_conv).astype(BF)
    z_ext = dot(n1_ext, w_in_s)
    b_ext, c_ext, v_ext = z_ext[:, :CS], z_ext[:, CS : 2 * CS], z_ext[:, 2 * CS :]
    u_ext = lax.optimization_barrier((b_ext * v_ext).astype(BF)).astype(F32)
    span = slice(HALO, HALO + N)
    same = [
        (seg_ext[HALO - 2 + k : HALO - 2 + k + N] == seg_ext[span]).astype(F32)[:, None]
        for k in range(taps)
    ]
    near = [u_ext[HALO - 2 + k : HALO - 2 + k + N] for k in range(taps)]
    conv = kernel_f[0] * near[0] * same[0]
    for k in range(1, taps):
        conv = conv + kernel_f[k] * near[k] * same[k]
    m_bf = (c_ext[span] * conv).astype(BF)
    part = dot(m_bf, w_mix_s).reshape(TP, n, D)
    (got,), (ffb_p,), (down_p,) = exchange(
        place,
        1,
        [
            swap_plane(part.astype(BF)),
            spread(gate_b, up_b),
            spread(down_b.T),
        ],
    )
    wb = gather_rest(ffb_p)
    x0 = mine.astype(F32)
    h1 = x0 + settle(part, got, p)

    r1 = inverse_rms(h1)
    a1 = (h1 * r1 * g_ffa).astype(BF)
    ((a1_g,),) = exchange(place, 2, [gather_plane(a1)])
    a1_g = a1_g.reshape(N, D)

    g_row = {name: value[None] for name, value in
             (("ffa", g_ffa), ("att", g_att), ("ffb", g_ffb))}
    fed = feed_kernel(
        place,
        3,
        "fwd",
        {"weights": wide, "a_g": a1_g.reshape(TP, n, D), "h_in": h1, "gain_next": g_row["att"]},
        D,
        FS,
        n,
    )
    h2, n3_g, gu1 = fed["h_out"], fed["next_g"], fed["gu_out"]

    n3_g = n3_g.reshape(N, D)
    w_out = w_att[:, QS + 2 * KS :]
    lane = jnp.arange(2 * HD, dtype=jnp.int32)
    frequency = jnp.exp(jnp.arange(HD // 2, dtype=F32) * (-2.0 * math.log(THETA) / HD))
    angles = rel_ext[span].astype(F32)[:, None] * jnp.tile(frequency, 4)[None, :]
    cosine = jnp.cos(angles)
    sine = jnp.sin(angles) * jnp.where(lane % HD < HD // 2, -1.0, 1.0)
    head_rows = jnp.tile(head_gains.astype(F32), (1, 2))
    pre, q_bf, kv_bf = heads_forward(n3_g, w_att, head_rows, cosine, sine, QS, KS)
    e_bf = cotangent[0]
    (kv_w,), (e_g,) = exchange(
        place,
        5,
        [window_forward(place, kv_bf), gather_plane(e_bf)],
    )
    reach = Q // 2 + 1
    kv_all = kv_w.reshape(reach * N, 2 * KS)
    q_seg = seg_ext[span]
    key_seg, _ = doc_info((q - reach + 1) * N + jnp.arange(reach * N, dtype=jnp.int32), lengths)
    first = jnp.maximum((reach - 1 - q) * N, 0).astype(jnp.int32).reshape(1)
    seg_col, seg_row = (jnp.broadcast_to(q_seg[:, None], (N, 128)), jnp.broadcast_to(q_seg, (8, N)))
    key_col = jnp.broadcast_to(key_seg[:, None], (reach * N, 128))
    key_row = jnp.broadcast_to(key_seg, (8, reach * N))
    o_bf = attend_forward(q_bf, kv_all, seg_col, key_row, first, 128)
    fed = feed_kernel(
        place,
        8,
        "both",
        {
            "weights": wb,
            "down": down_p.reshape(TP * shard, FS),
            "first_part": dot_nt(o_bf, w_out),
            "h_in": h2,
            "gain": g_row["ffb"],
            "e_g": e_g.reshape(TP, n, D),
            "e_own": e_bf,
        },
        D,
        FS,
        n,
    )
    full_down = jnp.sum(fed["down_out"].astype(F32), axis=0).astype(BF).reshape(TP, shard, FS)
    h3, g3, g3_g, half_b = fed["mid_out"], fed["g_out"], fed["next_g"], fed["half_out"]
    d_gain = {}
    d_gain["ffb"] = fed["d_gain"][0]

    g3_g = g3_g.reshape(N, D)
    d_o = dot(g3_g, w_out).astype(BF)
    d_q, d_kv = attend_backward(q_bf, kv_all, d_o, seg_row, key_col, first, 128)
    d_kv = d_kv.reshape(reach, N, 2 * KS)
    (got_kv,), (got_o,) = exchange(
        place, 10, [window_backward(place, d_kv.astype(BF)), swap_plane(fed["o_send"])]
    )
    index = jnp.arange(TP, dtype=jnp.int32)[:, None, None]
    h4 = fed["o_base"] + jnp.sum(jnp.where(index == p, 0.0, got_o.astype(F32)), axis=0)
    mixed = h4.astype(BF)[None]
    count = (q + 1 < Q).astype(jnp.int32).reshape(1)
    half_up, got_kv = lax.optimization_barrier((fed["half_up"], got_kv))
    full_gate, full_up = reduce_line(half_b), reduce_line(half_up)
    part, rows_att, d_heads = heads_backward(
        d_q, d_kv[-1], got_kv, count, pre, head_rows, cosine, sine, n3_g, g3_g, o_bf, w_att
    )
    d_heads = jnp.sum(d_heads.reshape(2, 2, HD), axis=1)
    rows_att = by_row(rows_att)
    part, full_gate = lax.optimization_barrier((part, full_gate))
    fed = feed_kernel(
        place,
        13,
        "bwd",
        {
            "weights": wide,
            "first_part": part,
            "h_in": h1,
            "gain": g_row["ffa"],
            "a_g": a1_g.reshape(TP, n, D),
            "gu_in": gu1,
            "g_in": g3,
            "h_before": h2,
            "gain_before": g_row["att"],
            "side_in": rows_att,
        },
        D,
        FS,
        n,
        rows_att.shape[2],
    )
    full_att = jnp.sum(fed["side_out"].astype(F32), axis=0).astype(BF).reshape(TP, shard, -1)
    g1, g1_g, g1_halo = fed["g_out"], fed["next_g"], fed["halo"]
    d_gain["att"], d_gain["ffa"] = fed["d_gain_before"][0], fed["d_gain"][0]
    full_a = reduce_line(fed["half_out"])

    g1_halo = jnp.where(q < Q - 1, g1_halo, jnp.zeros_like(g1_halo))
    g1_ext = jnp.concatenate([g1_g.reshape(N, D), g1_halo], axis=0)
    d_m = dot_nt(g1_ext, w_mix_s)
    d_mix_s = dot_tn(m_bf, g1_ext[:N])
    d_c = d_m[:N] * conv
    d_conv = lax.optimization_barrier((d_m * c_ext[HALO:]).astype(BF)).astype(F32)
    d_kernel = jnp.stack(
        [jnp.sum(d_conv[:N] * near[k] * same[k], axis=0) for k in range(taps)]
    )
    d_u = jnp.zeros((N, CS), F32)
    for k in range(taps):
        ahead = taps - 1 - k
        match = (seg_ext[HALO + ahead : HALO + ahead + N] == seg_ext[span]).astype(F32)[:, None]
        d_u = d_u + kernel_f[k] * d_conv[ahead : ahead + N] * match
    d_z = jnp.concatenate([d_u * v_ext[span], d_c, d_u * b_ext[span]], axis=1).astype(BF)
    rows_in = dot_tn(n1_ext[span], d_z).astype(BF).reshape(R, S, shard, 3 * CS)
    rows_mix = d_mix_s.astype(BF).reshape(R, Q, shard, D)
    d_n1 = dot_nt(d_z, w_in_s)
    d_gain["conv"] = jnp.sum(d_n1 * x_ext[span] * r0_ext[span], axis=0)
    part = d_n1.reshape(TP, n, D)
    d_taps = lax.dynamic_update_slice(jnp.zeros((taps, D), F32), d_kernel, (0, p * CS))
    lanes = jnp.concatenate(
        [jnp.stack([d_gain["conv"], d_gain["ffa"], d_gain["att"], d_gain["ffb"]]), d_taps]
    )
    lanes = lanes.reshape(4 + taps, R * S, shard).transpose(1, 0, 2)
    lanes = jnp.pad(lanes, ((0, 0), (0, 0), (0, 128 - shard)))
    heads_row = jnp.broadcast_to(d_heads.reshape(1, 1, 2 * HD), (R * S, 1, 2 * HD))
    tiny = jnp.concatenate([lanes, heads_row], axis=1)
    tiny_rows = tiny.reshape(R, S, 4 + taps + 1, 128)
    (got,), (core_in,), (core_mix,), (core_t,), *plane_b, (plane_att,) = exchange(
        place,
        15,
        [
            swap_plane(part.astype(BF)),
            swap_core(rows_in),
            swap_core(rows_mix),
            swap_core(tiny_rows),
            swap_plane(full_gate),
            swap_plane(full_up),
            swap_plane(full_down),
            swap_plane(full_att),
        ],
    )
    d_normed = settle(part, got, p)
    g0 = g1 + rms_pull(d_normed, x0, inverse_rms(x0), g_conv)
    d_tokens = g0.astype(BF)[None]

    tiny_line = after_core(tiny_rows, core_t)
    line_in = after_core(rows_in, core_in).astype(BF)
    line_mix = collect(rows_mix, core_mix, r).astype(BF)
    (plane_a,), (plane_in,), (plane_t,), (mix_back,) = exchange(
        place,
        16,
        [
            swap_plane(full_a),
            line_plane(line_in),
            line_plane(tiny_line),
            line_home(line_mix),
        ],
    )
    FF = TP * FS
    by_weight = [(k * FS, FS, k, 0) for k in range(3)]
    by_gate = [(k * CS, CS, 0, k * D) for k in range(3)]
    by_head = [(0, QS, 0, 0), (QS, KS, 1, 0), (QS + KS, KS, 2, 0), (QS + 2 * KS, QS, 3, 0)]
    ready = finish(
        place,
        place.here(),
        [
            *[
                (own, came[0], by_weight[:1], [(shard, FF)])
                for own, came in zip((full_gate, full_up, full_down), plane_b)
            ],
            (full_att, plane_att, by_head, [(shard, TP * k) for k in (QS, KS, KS, QS)]),
            (full_a, plane_a, by_weight, [(shard, FF)] * 3),
            (None, plane_in, by_gate, [(shard, 3 * D)]),
        ],
        plane_t,
        mix_back,
        taps,
    )
    out_b, out_att, out_a, (out_in,) = ready[:3], ready[3:7], ready[7:10], ready[10:11]
    of_conv, of_ffa, of_att, of_ffb, of_taps, d_heads, out_mix = ready[11:]
    return (
        mixed,
        d_tokens,
        of_conv[0],
        out_in,
        of_taps,
        out_mix,
        of_ffa[0],
        out_a[0],
        out_a[1],
        out_a[2].T,
        of_att[0],
        out_att[0],
        out_att[1],
        out_att[2],
        d_heads,
        out_att[3].T,
        of_ffb[0],
        out_b[0],
        out_b[1],
        out_b[2].T,
    )


def solution(mesh):
    place = Place(mesh.shape["rows"], mesh.shape["seq"])
    whole = ("rows", "seq")
    wide, first, second = P("rows", "seq", None), P(whole, None), P(None, whole)
    in_specs = (
        (wide, P("rows", None), wide, P(whole), first, second, first)
        + (P(whole), first, first, second)
        + (P(whole), first, first, first, P(), second)
        + (P(whole), first, first, second)
    )
    out_specs = (
        (wide, wide, P(whole), first, second, first)
        + (P(whole), first, first, second)
        + (P(whole), first, first, first, P(), second)
        + (P(whole), first, first, second)
    )
    return jax.shard_map(
        functools.partial(per_device, place),
        mesh=mesh,
        in_specs=in_specs,
        out_specs=out_specs,
        check_vma=False,
    )
```

```python
import functools
import math

import jax
import jax.numpy as jnp
from jax import lax
from jax.experimental import pallas as pl
from jax.experimental.pallas import tpu as pltpu
from jax.sharding import PartitionSpec as P

H = 16
KVH = 8
HD = 64
TP = 4
HALO = 16
COST = 1_000_000

EPSILON = 1e-05
THETA = 1000000.0
MASKED = -1e30
MESH_ID = pl.DeviceIdType.MESH
BF = jnp.bfloat16
F32 = jnp.float32


def dot(left, right):
    return jnp.dot(left, right, preferred_element_type=F32)


def dot_tn(left, right):
    return lax.dot_general(left, right, (((0,), (0,)), ((), ())), preferred_element_type=F32)


def dot_nt(left, right):
    return lax.dot_general(left, right, (((1,), (1,)), ((), ())), preferred_element_type=F32)


class Place:
    def __init__(self, rows, seq):
        self.R, self.S = rows, seq
        self.Q = seq // TP

    def here(self):
        here = Place(self.R, self.S)
        here.r = lax.axis_index("rows")
        here.s = lax.axis_index("seq")
        here.q = here.s // TP
        here.p = lax.rem(here.s, TP)
        return here


class Copies:
    def __init__(self, send, recv):
        self.send, self.recv, self.count, self.sent = send, recv, 0, []

    def slot(self):
        self.count += 1
        return self.count - 1

    def remote(self, src, dst, slot, where, recv_slot=None):
        return pltpu.make_async_remote_copy(
            src_ref=src,
            dst_ref=dst,
            send_sem=self.send.at[slot],
            recv_sem=self.recv.at[slot if recv_slot is None else recv_slot],
            device_id=where,
            device_id_type=MESH_ID,
        )

    def push(self, src, dst, slot, where, cond=None, recv_slot=None):
        copy = self.remote(src, dst, slot, where, recv_slot)
        when(cond, copy.start)
        self.sent.append((copy.wait_send, cond))

    def arrived(self, dst, slot, where, cond=None):
        copy = self.remote(dst, dst, slot, where)
        when(cond, copy.wait_recv)

    def local(self, src, dst):
        slot = self.slot()
        copy = pltpu.make_async_copy(src, dst, self.recv.at[slot])
        copy.start()
        self.sent.append((copy.wait, None))

    def drain(self):
        for wait, cond in self.sent:
            when(cond, wait)


def when(cond, action):
    if cond is None:
        action()
    else:
        pl.when(cond)(lambda: action())


class Job:
    def __init__(
        self, ins, outs, run, kinds, aliases=(), vmem=(), relay=False, late=False, scratch=()
    ):
        self.ins, self.outs, self.run, self.kinds = ins, outs, run, kinds
        self.aliases, self.vmem, self.relay, self.late = aliases, vmem, relay, late
        self.scratch = scratch


def together(runs):
    while runs:
        runs = [steps for steps in runs if next(steps, "done") != "done"]
        yield "go"


def partners(at, kinds):
    found = []
    if "plane" in kinds:
        for j in range(1, TP):
            found.append((None, at.r, at.q * TP + lax.rem(at.p + j, TP)))
    if "core" in kinds:
        for j in range(1, at.R):
            found.append((None, lax.rem(at.r + j, at.R), at.s))
    if "zall" in kinds:
        for j in range(1, at.Q):
            found.append((None, at.r, lax.rem(at.q + j, at.Q) * TP + at.p))
    elif "chain" in kinds:
        found.append((at.q > 0, at.r, at.s - TP))
        found.append((at.q < at.Q - 1, at.r, at.s + TP))
    if "home" in kinds:
        r, s, _, same = home_of(at)
        found.append((same == 0, r, s))
        r, s, same = visitor_of(at)
        found.append((same == 0, r, s))
    if "back" in kinds:
        found.append((at.q < at.Q - 1, at.r, (at.q + 1) * TP))
        for j in range(TP):
            found.append(((at.p == 0) & (at.q > 0), at.r, (at.q - 1) * TP + j))
    if "halo" in kinds:
        found.append((at.q > 0, at.r, (at.q - 1) * TP + TP - 1))
        found.append((at.q < at.Q - 1, at.r, (at.q + 1) * TP))
        for j in range(TP):
            found.append(((at.p == TP - 1) & (at.q < at.Q - 1), at.r, (at.q + 1) * TP + j))
            found.append(((at.p == 0) & (at.q > 0), at.r, (at.q - 1) * TP + j))
    return found


def home_of(at):
    k = lax.rem(at.r * at.S + at.s, at.R * at.Q)
    r, s = k // at.Q, lax.rem(k, at.Q) * TP + (at.r * at.S + at.s) // (at.R * at.Q)
    return r, s, k, ((r == at.r) & (s == at.s)).astype(jnp.int32)


def visitor_of(at):
    d = at.p * (at.R * at.Q) + at.r * at.Q + at.q
    r, s = d // at.S, lax.rem(d, at.S)
    return r, s, ((r == at.r) & (s == at.s)).astype(jnp.int32)


def meet(at, kinds):
    barrier = pltpu.get_barrier_semaphore()
    peers = partners(at, kinds)
    for cond, r, s in peers:
        when(
            cond,
            functools.partial(
                pl.semaphore_signal, barrier, inc=1, device_id=(r, s), device_id_type=MESH_ID
            ),
        )
    awaited = sum(1 for cond, r, s in peers if cond is None)
    for cond, r, s in peers:
        if cond is not None:
            awaited = awaited + cond.astype(jnp.int32)
    pl.semaphore_wait(barrier, awaited)


def exchange(place, ident, jobs):
    kinds = set().union(*[job.kinds for job in jobs])
    n_in = sum(len(job.ins) for job in jobs)
    n_out = sum(len(job.outs) for job in jobs)
    sems = 24 + sum(
        12 + 4 * len(job.ins) + 2 * place.Q + place.R * place.Q * 2 for job in jobs
    )
    arrays, in_specs, outs, aliases = [], [], [], {}
    for job in jobs:
        for k, o in job.aliases:
            aliases[len(arrays) + k] = len(outs) + o
        for k, value in enumerate(job.ins):
            arrays.append(value)
            in_specs.append(pl.BlockSpec(memory_space=pltpu.VMEM if k in job.vmem else pl.ANY))
        outs.extend(job.outs)

    def body(*refs):
        at = place.here()
        ins, results = refs[:n_in], refs[n_in : n_in + n_out]
        copies = Copies(refs[n_in + n_out], refs[n_in + n_out + 1])
        held = refs[n_in + n_out + 2 :]
        meet(at, kinds)
        runs, i, o, h = [], 0, 0, 0
        for job in jobs:
            mine = list(results[o : o + len(job.outs)]) + list(held[h : h + len(job.scratch)])
            runs.append(job.run(at, copies, ins[i : i + len(job.ins)], mine))
            i, o, h = i + len(job.ins), o + len(job.outs), h + len(job.scratch)
        pairs = list(zip(jobs, runs))
        relays = together([steps for job, steps in pairs if job.relay])
        next(relays, "done")
        for steps in [steps for job, steps in pairs if not job.relay and not job.late]:
            next(steps)
        next(relays, "done")
        for steps in [steps for job, steps in pairs if job.late]:
            next(steps)
        for _ in relays:
            pass
        for steps in [steps for job, steps in pairs if not job.relay]:
            for _ in steps:
                pass
        copies.drain()

    results = pl.pallas_call(
        body,
        out_shape=tuple(outs),
        in_specs=in_specs,
        out_specs=tuple(
            pl.BlockSpec(memory_space=pltpu.VMEM if job.scratch else pl.ANY)
            for job in jobs
            for _ in job.outs
        ),
        scratch_shapes=[pltpu.SemaphoreType.DMA((sems,)), pltpu.SemaphoreType.DMA((sems,))]
        + [pltpu.VMEM(*shape) for job in jobs for shape in job.scratch],
        input_output_aliases=aliases,
        compiler_params=pltpu.CompilerParams(collective_id=ident, has_side_effects=True),
        cost_estimate=pl.CostEstimate(flops=0, bytes_accessed=COST, transcendentals=0),
        name="exchange_%d" % ident,
    )(*arrays)
    given, o = [], 0
    for job in jobs:
        given.append(results[o : o + len(job.outs)])
        o += len(job.outs)
    return given


def like(shape, dtype=BF):
    return jax.ShapeDtypeStruct(shape, dtype)


def gather_plane(value):
    def run(at, copies, ins, outs):
        slots = [copies.slot() for _ in range(TP - 1)]
        for j in range(1, TP):
            peer = at.q * TP + lax.rem(at.p + j, TP)
            copies.push(ins[0], outs[0].at[at.p], slots[j - 1], (at.r, peer))
        copies.local(ins[0], outs[0].at[at.p])
        yield "go"
        for j in range(1, TP):
            origin = lax.rem(at.p + TP - j, TP)
            copies.arrived(outs[0].at[origin], slots[j - 1], (at.r, at.s))

    return Job([value], [like((TP,) + value.shape, value.dtype)], run, {"plane"}, vmem=(0,))


def swap_plane(value):
    def run(at, copies, ins, outs):
        slots = [copies.slot() for _ in range(TP - 1)]
        for j in range(1, TP):
            other = lax.rem(at.p + j, TP)
            copies.push(
                ins[0].at[other], outs[0].at[at.p], slots[j - 1], (at.r, at.q * TP + other)
            )
        yield "go"
        for j in range(1, TP):
            origin = lax.rem(at.p + TP - j, TP)
            copies.arrived(outs[0].at[origin], slots[j - 1], (at.r, at.s))

    return Job([value], [like(value.shape, value.dtype)], run, {"plane"})


def line_sum(at, copies, source, held):
    slots = [copies.slot() for _ in range(at.Q - 1)]
    for j in range(1, at.Q):
        other = lax.rem(at.q + j, at.Q)
        there = (at.r, other * TP + at.p)
        copies.push(source.at[other], held.at[at.q], slots[j - 1], there)
    held[at.q] = source[at.q]
    yield "go"
    yield "go"
    for j in range(1, at.Q):
        origin = lax.rem(at.q + at.Q - j, at.Q)
        copies.arrived(held.at[origin], slots[j - 1], (at.r, at.s))
    total = held[0].astype(F32)
    for k in range(1, at.Q):
        total = total + held[k].astype(F32)
    return total


def line_plane(value):
    def run(at, copies, ins, outs):
        held, summed = outs[1:]
        total = yield from line_sum(at, copies, ins[0], held)
        summed[...] = total.astype(summed.dtype)
        slots = [copies.slot() for _ in range(TP - 1)]
        for j in range(1, TP):
            other = lax.rem(at.p + j, TP)
            there = (at.r, at.q * TP + other)
            copies.push(summed.at[other], outs[0].at[at.p], slots[j - 1], there)
        outs[0][at.p] = summed[at.p]
        yield "go"
        for j in range(1, TP):
            origin = lax.rem(at.p + TP - j, TP)
            copies.arrived(outs[0].at[origin], slots[j - 1], (at.r, at.s))

    scratch = ((value.shape, value.dtype), (value.shape[1:], value.dtype))
    outs = [like(value.shape[1:], value.dtype)]
    kinds = {"zall", "plane"}
    return Job([value], outs, run, kinds, vmem=(0,), relay=True, scratch=scratch)


def line_home(value):
    def run(at, copies, ins, outs):
        held, summed, got = outs[1:]
        total = yield from line_sum(at, copies, ins[0], held)
        summed[...] = total.astype(summed.dtype)
        r, s, own = visitor_of(at)
        _, _, _, here = home_of(at)
        slot = copies.slot()
        copies.push(summed, got, slot, (r, s), own == 0)
        yield "go"
        copies.arrived(got, slot, (at.r, at.s), here == 0)

        @pl.when(here == 0)
        def _():
            outs[0][...] = got[...]

        @pl.when(here == 1)
        def _():
            outs[0][...] = summed[...]

    one = (value.shape[1:], value.dtype)
    outs = [like(*one)]
    kinds = {"zall", "home"}
    return Job([value], outs, run, kinds, vmem=(0,), relay=True, scratch=((value.shape, value.dtype), one, one))


def finish(place, at, sliced, tiny, mix, taps):
    shard, D = mix.shape
    shapes = [shape for _, _, _, outs in sliced for shape in outs]
    tiny_shapes = [(1, shard)] * 4 + [(taps, shard), (2, HD)]
    arrays = [x for own, came, _, _ in sliced for x in (own, came) if x is not None] + [tiny, mix]
    where = at.p.astype(jnp.int32).reshape(1)

    def body(where_ref, *refs):
        ins, outs = refs[: len(arrays)], refs[len(arrays) :]

        ins = list(ins)
        first = 0
        for own, _, parts, made in sliced:
            mine = None if own is None else ins.pop(0)
            came = ins.pop(0)
            for k in range(TP):
                piece = came[k]
                if mine is not None:
                    piece = jnp.where(where_ref[0] == k, mine[k], piece)
                piece = piece.astype(F32)
                for start, width, out, base in parts:
                    there = slice(base + k * width, base + (k + 1) * width)
                    outs[first + out][:, there] = piece[:, start : start + width]
            first += len(made)
        total = ins[0][0]
        for k in range(1, TP):
            total = total + ins[0][k]
        for k in range(4):
            outs[first + k][...] = total[k : k + 1, :shard]
        outs[first + 4][...] = total[4 : 4 + taps, :shard]
        row = total[4 + taps : 5 + taps, :]
        outs[first + 5][0:1, :] = row[:, :HD]
        outs[first + 5][1:2, :] = row[:, HD:]
        outs[first + 6][...] = ins[1][...].astype(F32)

    outs = [like(shape, F32) for shape in shapes + tiny_shapes + [(shard, D)]]
    return plain_call(body, tuple(outs), (), where, *arrays, smem=1)


def swap_core(value):
    def run(at, copies, ins, outs):
        slots = [copies.slot() for _ in range(at.R - 1)]
        for j in range(1, at.R):
            other = lax.rem(at.r + j, at.R)
            copies.push(ins[0].at[other], outs[0].at[at.r], slots[j - 1], (other, at.s))
        yield "go"
        for j in range(1, at.R):
            origin = lax.rem(at.r + at.R - j, at.R)
            copies.arrived(outs[0].at[origin], slots[j - 1], (at.r, at.s))

    return Job([value], [like(value.shape, value.dtype)], run, {"core"})


def window_forward(place, value):
    reach = place.Q // 2

    def run(at, copies, ins, outs):
        slots = [copies.slot() for _ in range(reach)]
        there = (at.r, at.s + TP)
        copies.push(ins[0], outs[0].at[reach - 1], slots[0], there, at.q + 1 < at.Q)
        copies.local(ins[0], outs[0].at[reach])
        for j in range(1, reach + 1):
            yield "go"
            came = outs[0].at[reach - j]
            copies.arrived(came, slots[j - 1], (at.r, at.s), at.q >= j)
            if j < reach:
                passes = (at.q >= j) & (at.q + 1 < at.Q)
                copies.push(came, outs[0].at[reach - j - 1], slots[j], there, passes)

    shape = (reach + 1,) + value.shape
    outs = [like(shape, value.dtype)]
    return Job([value], outs, run, {"chain"}, vmem=(0,), relay=True)


def window_backward(place, value):
    reach = place.Q // 2

    def run(at, copies, ins, outs):
        got, summed = outs[1:]
        slots = [copies.slot() for _ in range(reach)]
        there = (at.r, at.s - TP)
        for j in range(reach, 0, -1):
            step = reach - j
            source = ins[0].at[step]
            if step > 0:
                came = (at.q + 1 < at.Q) & (at.q >= j)
                copies.arrived(got.at[step - 1], slots[step - 1], (at.r, at.s), came)
                total = jnp.where(came, got[step - 1].astype(F32), 0.0)
                summed[step - 1] = (total + ins[0][step].astype(F32)).astype(value.dtype)
                source = summed.at[step - 1]
            target = got.at[step] if j > 1 else outs[0]
            copies.push(source, target, slots[step], there, at.q >= j)
            yield "go"
        copies.arrived(outs[0], slots[reach - 1], (at.r, at.s), at.q + 1 < at.Q)

    piece = value.shape[1:]
    held = ((max(reach - 1, 1),) + piece, value.dtype)
    outs = [like(piece, value.dtype)]
    return Job([value], outs, run, {"chain"}, vmem=(0,), relay=True, scratch=(held, held))


def halo_tokens(value):
    rows = value.shape[0]

    def run(at, copies, ins, outs):
        ahead = [copies.slot() for _ in range(TP)]
        back = [copies.slot() for _ in range(TP)]
        first = (at.p == 0) & (at.q > 0)
        last = (at.p == TP - 1) & (at.q < at.Q - 1)
        for j in range(TP):
            tail = ins[0].at[pl.ds(rows - HALO, HALO)]
            there = (at.r, (at.q + 1) * TP + j)
            copies.push(tail, outs[0], ahead[j], there, last, ahead[0])
            head = ins[0].at[pl.ds(0, HALO)]
            there = (at.r, (at.q - 1) * TP + j)
            copies.push(head, outs[1], back[j], there, first, back[0])
        yield "go"
        copies.arrived(outs[0], ahead[0], (at.r, at.s), at.q > 0)
        copies.arrived(outs[1], back[0], (at.r, at.s), at.q < at.Q - 1)

    shape = (HALO,) + value.shape[1:]
    outs = [like(shape, value.dtype), like(shape, value.dtype)]
    return Job([value], outs, run, {"halo"}, vmem=(0,))


def side_by_side(*weights):
    layout, there = [], 0
    for index, weight in enumerate(weights):
        width = weight.shape[1] // TP
        layout.append((index, 0, width, width, there))
        there += width
    return layout


def spread_run(at, copies, sources, held, first, layout):
    def cut(index, start, stride, width, member):
        if stride == 0:
            return sources[index]
        return sources[index].at[:, pl.ds(pl.multiple_of(start + member * stride, 128), width)]

    def place_of(member, width, there):
        return held.at[first + member, :, pl.ds(there, width)]

    slots = [[copies.slot() for _ in layout] for _ in range(TP - 1)]
    for j in range(1, TP):
        other = lax.rem(at.p + j, TP)
        for k, (index, start, stride, width, there) in enumerate(layout):
            copies.push(
                cut(index, start, stride, width, other),
                place_of(at.p, width, there),
                slots[j - 1][k],
                (at.r, at.q * TP + other),
            )
    own = []
    for index, start, stride, width, there in layout:
        piece = cut(index, start, stride, width, at.p)
        sem = copies.recv.at[copies.slot()]
        own.append(pltpu.make_async_copy(piece, place_of(at.p, width, there), sem))
        own[-1].start()
    yield "go"
    for copy in own:
        copy.wait()
    for j in range(1, TP):
        origin = lax.rem(at.p + TP - j, TP)
        for k, (_, _, _, width, there) in enumerate(layout):
            copies.arrived(place_of(origin, width, there), slots[j - 1][k], (at.r, at.s))


def chain_run(at, copies, held, unit=TP):
    def block(r, q):
        return held.at[pl.ds(pl.multiple_of((r * at.Q + q) * unit, unit), unit)]

    right = [copies.slot() for _ in range(at.Q - 1)]
    left = [copies.slot() for _ in range(at.Q - 1)]
    across = [[copies.slot() for _ in range(at.Q)] for _ in range(at.R - 1)]

    def cross(q, index, cond):
        for j in range(1, at.R):
            other = lax.rem(at.r + j, at.R)
            copies.push(block(at.r, q), block(at.r, q), across[j - 1][index], (other, at.s), cond)

    copies.push(
        block(at.r, at.q), block(at.r, at.q), right[0], (at.r, at.s + TP), at.q < at.Q - 1
    )
    copies.push(block(at.r, at.q), block(at.r, at.q), left[0], (at.r, at.s - TP), at.q > 0)
    cross(at.q, 0, None)
    index = 0
    spots = {}
    for hop in range(1, at.Q):
        yield "go"
        from_left, from_right = at.q >= hop, at.q + hop < at.Q
        copies.arrived(block(at.r, at.q - hop), right[hop - 1], (at.r, at.s), from_left)
        if hop < at.Q - 1:
            copies.push(
                block(at.r, at.q - hop),
                block(at.r, at.q - hop),
                right[hop],
                (at.r, at.s + TP),
                from_left & (at.q < at.Q - 1),
            )
        copies.arrived(block(at.r, at.q + hop), left[hop - 1], (at.r, at.s), from_right)
        if hop < at.Q - 1:
            copies.push(
                block(at.r, at.q + hop),
                block(at.r, at.q + hop),
                left[hop],
                (at.r, at.s - TP),
                from_right & (at.q > 0),
            )
        for side, sign in ((from_left, -1), (from_right, 1)):
            spots[(hop, sign)] = [copies.slot() for _ in range(at.R - 1)]
            for j in range(1, at.R):
                other = lax.rem(at.r + j, at.R)
                piece = block(at.r, at.q + sign * hop)
                copies.push(piece, piece, spots[(hop, sign)][j - 1], (other, at.s), side)
    yield "go"
    for j in range(1, at.R):
        source = lax.rem(at.r + at.R - j, at.R)
        copies.arrived(block(source, at.q), across[j - 1][0], (at.r, at.s))
        for hop in range(1, at.Q):
            for sign in (-1, 1):
                there = at.q + sign * hop
                copies.arrived(
                    block(source, there),
                    spots[(hop, sign)][j - 1],
                    (at.r, at.s),
                    at.q >= hop if sign < 0 else there < at.Q,
                )


def spread(*sources):
    layout = side_by_side(*sources)

    def run(at, copies, ins, outs):
        yield from spread_run(at, copies, ins, outs[0], 0, layout)

    shape = (TP, sources[0].shape[0], sum(part[3] for part in layout))
    outs = [like(shape, sources[0].dtype)]
    return Job(sources, outs, run, {"plane"}, vmem=tuple(range(len(sources))), late=True)


def spread_all(place, source, layout):
    def run(at, copies, ins, outs):
        yield from spread_run(at, copies, ins, outs[0], (at.r * at.Q + at.q) * TP, layout)
        yield from chain_run(at, copies, outs[0])

    shape = (place.R * place.S, source.shape[0], sum(part[3] for part in layout))
    outs = [like(shape, source.dtype)]
    return Job([source], outs, run, {"plane", "chain", "core"}, vmem=(0,), relay=True)


def home_all(place, source):
    def run(at, copies, ins, outs):
        r, s, slot, here = home_of(at)
        _, _, own = visitor_of(at)
        index = copies.slot()
        copies.push(ins[0], outs[0].at[slot], index, (r, s), here == 0)
        copy = pltpu.make_async_copy(ins[0], outs[0].at[slot], copies.recv.at[copies.slot()])
        when(here == 1, copy.start)
        yield "go"
        when(here == 1, copy.wait)
        copies.arrived(outs[0].at[at.r * at.Q + at.q], index, (at.r, at.s), own == 0)
        yield from chain_run(at, copies, outs[0], 1)

    outs = [like((place.R * place.Q,) + source.shape, source.dtype)]
    return Job([source], outs, run, {"home", "chain", "core"}, vmem=(0,), relay=True)


FACTOR = 1.0 / math.sqrt(HD)


def masked_keys(kv_ref, first, kv_s):
    index = lax.broadcasted_iota(jnp.int32, kv_ref.shape, 0)
    kv_s[...] = jnp.where(index >= first, kv_ref[...].astype(F32), 0.0).astype(BF)


def attend_forward(q, kv, q_seg, key_seg, first, block):
    N, QS = q.shape
    M, KS = kv.shape[0], kv.shape[1] // 2
    ahead = M - N
    span = ahead + block
    kv_heads = KS // HD
    groups = QS // KS

    def body(first_ref, q_ref, kv_ref, qs_ref, ks_ref, o_ref, kv_s):
        masked_keys(kv_ref, first_ref[0], kv_s)

        @pl.loop(0, N // block)
        def _(i):
            start = pl.multiple_of(i * block, block)
            here, keys = pl.ds(start, block), pl.ds(start, span)
            row = lax.broadcasted_iota(jnp.int32, (block, span), 0) + ahead
            col = lax.broadcasted_iota(jnp.int32, (block, span), 1)
            open_ = (qs_ref[here, :1] == ks_ref[:1, keys]) & (col <= row)
            open_ = open_ & (col + start >= first_ref[0])
            open_ = jnp.concatenate([open_] * groups, axis=0)
            queries = q_ref[here, :]
            done = []
            for k in range(kv_heads):
                mine = [
                    queries[:, (k * groups + g) * HD : (k * groups + g + 1) * HD]
                    for g in range(groups)
                ]
                key = kv_s[keys, k * HD : (k + 1) * HD]
                value = kv_s[keys, KS + k * HD : KS + (k + 1) * HD]
                score = jnp.where(open_, dot_nt(jnp.concatenate(mine, axis=0), key) * FACTOR, MASKED)
                weight = jnp.exp(score - jnp.max(score, axis=-1, keepdims=True))
                weight = weight / jnp.sum(weight, axis=-1, keepdims=True)
                out = dot(weight.astype(BF), value).astype(BF)
                done.extend(out[g * block : (g + 1) * block] for g in range(groups))
            o_ref[here, :] = jnp.concatenate(done, axis=1)

    return attend_call(
        body, like((N, QS)), [pltpu.VMEM(kv.shape, BF)], 4 * N * span * QS, first, q, kv, q_seg, key_seg
    )


def attend_call(body, outs, scratch, flops, first, *arrays):
    return pl.pallas_call(
        body,
        out_shape=outs,
        in_specs=[pl.BlockSpec(memory_space=pltpu.SMEM)]
        + [pl.BlockSpec(memory_space=pltpu.VMEM) for _ in arrays],
        out_specs=jax.tree.map(lambda _: pl.BlockSpec(memory_space=pltpu.VMEM), outs),
        scratch_shapes=scratch,
        cost_estimate=pl.CostEstimate(flops=flops, bytes_accessed=COST, transcendentals=0),
    )(first, *arrays)


def attend_backward(q, kv, d_o, q_seg, key_seg, first, block):
    N, QS = q.shape
    M, KS = kv.shape[0], kv.shape[1] // 2
    ahead = M - N
    span = ahead + block
    kv_heads = KS // HD
    groups = QS // KS

    def body(first_ref, q_ref, kv_ref, do_ref, qs_ref, ks_ref, dq_ref, dkv_ref, kv_s, *sums):
        masked_keys(kv_ref, first_ref[0], kv_s)
        for total in sums:
            total[...] = jnp.zeros_like(total)

        @pl.loop(0, N // block)
        def _(i):
            start = pl.multiple_of(i * block, block)
            here, keys = pl.ds(start, block), pl.ds(start, span)
            row = lax.broadcasted_iota(jnp.int32, (span, block), 0)
            col = lax.broadcasted_iota(jnp.int32, (span, block), 1) + ahead
            open_ = (ks_ref[keys, :1] == qs_ref[:1, here]) & (row <= col)
            open_ = open_ & (row + start >= first_ref[0])
            open_ = jnp.concatenate([open_] * groups, axis=1)
            queries, pulls = q_ref[here, :], do_ref[here, :]

            def heads_of(values, k):
                return jnp.concatenate(
                    [
                        values[:, (k * groups + g) * HD : (k * groups + g + 1) * HD]
                        for g in range(groups)
                    ],
                    axis=0,
                )

            done = []
            for k in range(kv_heads):
                mine, pull = heads_of(queries, k), heads_of(pulls, k)
                key = kv_s[keys, k * HD : (k + 1) * HD]
                value = kv_s[keys, KS + k * HD : KS + (k + 1) * HD]
                score = jnp.where(open_, dot_nt(key, mine) * FACTOR, MASKED)
                weight = jnp.exp(score - jnp.max(score, axis=0, keepdims=True))
                weight = weight / jnp.sum(weight, axis=0, keepdims=True)
                d_weight = dot_nt(value, pull)
                delta = jnp.sum(weight * d_weight, axis=0, keepdims=True)
                d_score = (weight * (d_weight - delta)).astype(BF)
                sums[k][keys, :] += dot(d_score, mine) * FACTOR
                sums[kv_heads + k][keys, :] += dot(weight.astype(BF), pull)
                dq = dot_tn(d_score, key) * FACTOR
                done.extend(dq[g * block : (g + 1) * block] for g in range(groups))
            dq_ref[here, :] = jnp.concatenate(done, axis=1)

        dkv_ref[...] = jnp.concatenate([total[...] for total in sums], axis=1)

    return attend_call(
        body,
        (like((N, QS), F32), like((M, 2 * KS), F32)),
        [pltpu.VMEM(kv.shape, BF)] + [pltpu.VMEM((M, HD), F32) for _ in range(2 * kv_heads)],
        10 * N * span * QS,
        first,
        q,
        kv,
        d_o,
        q_seg,
        key_seg,
    )


def turned(values, cosine, sine):
    lane = lax.broadcasted_iota(jnp.int32, values.shape, 1)
    ahead = pltpu.roll(values, 2 * HD - HD // 2, 1)
    behind = pltpu.roll(values, HD // 2, 1)
    other = jnp.where(lax.rem(lane, HD) < HD // 2, ahead, behind)
    return values * cosine + other * sine


def head_means(values):
    lane = lax.broadcasted_iota(jnp.int32, values.shape, 1)
    front = lane < HD
    first = jnp.sum(jnp.where(front, values, 0.0), axis=-1, keepdims=True)
    second = jnp.sum(jnp.where(front, 0.0, values), axis=-1, keepdims=True)
    return jnp.where(front, first, second) * (1.0 / HD)


def pairs_of(width):
    return [slice(c, c + 2 * HD) for c in range(0, width, 2 * HD)]


def heads_forward(n3, w, gains, cosine, sine, QS, KS):
    N = n3.shape[0]

    def body(n3_ref, w_ref, gains_ref, cos_ref, sin_ref, pre_ref, q_ref, kv_ref):
        pre_ref[...] = dot(n3_ref[...], w_ref[:, : QS + 2 * KS])

        def normed(cols, row):
            values = pre_ref[:, cols]
            inverse = lax.rsqrt(head_means(values * values) + EPSILON)
            values = values * inverse * gains_ref[row : row + 1, :]
            return turned(values, cos_ref[...], sin_ref[...]).astype(BF)

        for cols in pairs_of(QS):
            q_ref[:, cols] = normed(cols, 0)
        for cols in pairs_of(KS):
            kv_ref[:, cols] = normed(slice(QS + cols.start, QS + cols.stop), 1)
        kv_ref[:, KS:] = pre_ref[:, QS + KS :].astype(BF)

    outs = (like((N, QS + 2 * KS), F32), like((N, QS)), like((N, 2 * KS)))
    return plain_call(body, outs, (), n3, w, gains, cosine, sine)


def heads_backward(d_q, d_kv, got, count, pre, gains, cosine, sine, n3, g3, o, w):
    N, QS = d_q.shape
    KS = d_kv.shape[1] // 2
    D = n3.shape[1]
    W = QS + 2 * KS
    step = 256

    def body(
        count_ref, dq_ref, dkv_ref, got_ref, pre_ref, gains_ref, cos_ref, sin_ref, n3_ref, g3_ref,
        o_ref, w_ref, part_ref, rows_ref, heads_ref, all_ref,
    ):
        later = jnp.where(count_ref[0] > 0, got_ref[...].astype(F32), 0.0)
        d_kv_sum = dkv_ref[...] + later
        all_ref[:, QS + KS :] = d_kv_sum[:, KS:].astype(BF)

        def back(pull, cols, row):
            values = pre_ref[:, cols]
            inverse = lax.rsqrt(head_means(values * values) + EPSILON)
            pull = turned(pull, cos_ref[...], -sin_ref[...])
            scaled = pull * gains_ref[row : row + 1, :]
            mean = head_means(scaled * values)
            d_values = inverse * scaled - values * (inverse * inverse * inverse) * mean
            all_ref[:, cols] = d_values.astype(BF)
            return jnp.sum(pull * values * inverse, axis=0, keepdims=True)

        of_queries = [back(dq_ref[:, cols], cols, 0) for cols in pairs_of(QS)]
        of_keys = [
            back(d_kv_sum[:, cols], slice(QS + cols.start, QS + cols.stop), 1)
            for cols in pairs_of(KS)
        ]
        heads_ref[0:1, :] = sum(of_queries[1:], of_queries[0])
        heads_ref[1:2, :] = sum(of_keys[1:], of_keys[0])
        values, outputs = all_ref[...], o_ref[...]

        @pl.loop(0, D // step)
        def _(c):
            cols = pl.ds(pl.multiple_of(c * step, step), step)
            part_ref[:, cols] = dot_nt(values, w_ref[cols, :W])
            left = n3_ref[:, cols].astype(F32).T.astype(BF)
            rows_ref[cols, :W] = dot(left, values).astype(BF)
            right = g3_ref[:, cols].astype(F32).T.astype(BF)
            rows_ref[cols, W:] = dot(right, outputs).astype(BF)

    outs = (like((N, D), F32), like((D, W + QS)), like((2, 2 * HD), F32))
    return plain_call(
        body, outs, [pltpu.VMEM((N, W), BF)],
        count, d_q, d_kv, got, pre, gains, cosine, sine, n3, g3, o, w, smem=1,
    )


def plain_call(body, outs, scratch, *arrays, smem=0):
    return pl.pallas_call(
        body,
        out_shape=outs,
        in_specs=[
            pl.BlockSpec(memory_space=pltpu.SMEM if k < smem else pltpu.VMEM)
            for k in range(len(arrays))
        ],
        out_specs=tuple(pl.BlockSpec(memory_space=pltpu.VMEM) for _ in outs),
        scratch_shapes=scratch,
        cost_estimate=pl.CostEstimate(flops=0, bytes_accessed=COST, transcendentals=0),
    )(*arrays)


class Plane:
    def __init__(self, at, copies):
        self.at, self.copies = at, copies

    def swap(self, send, recv):
        at, slots = self.at, [self.copies.slot() for _ in range(TP - 1)]
        for j in range(1, TP):
            other = lax.rem(at.p + j, TP)
            there = (at.r, at.q * TP + other)
            self.copies.push(send.at[other], recv.at[at.p], slots[j - 1], there)
        return functools.partial(self.arrive, recv, slots)

    def gather(self, held):
        at, slots = self.at, [self.copies.slot() for _ in range(TP - 1)]
        for j in range(1, TP):
            there = (at.r, at.q * TP + lax.rem(at.p + j, TP))
            self.copies.push(held.at[at.p], held.at[at.p], slots[j - 1], there)
        return functools.partial(self.arrive, held, slots)

    def mate(self, k):
        p = self.at.p
        if k == 1:
            return p + 1 - 2 * lax.rem(p, 2)
        if k == 2:
            return p + 2 - 4 * (p // 2)
        return TP - 1 - p if k == TP - 1 else p

    def to_mate(self, source, held, k):
        at, slot = self.at, self.copies.slot()
        there = (at.r, at.q * TP + self.mate(k))
        self.copies.push(source, held.at[k], slot, there)
        return functools.partial(self.copies.arrived, held.at[k], slot, (at.r, at.s))

    def spread_mates(self, held):
        return [self.to_mate(held.at[0], held, k) for k in range(1, TP)]

    def sum_mates(self, own, recv):
        for k in range(1, TP):
            own = own + recv[k].astype(F32)
        return own

    def arrive(self, held, slots):
        at = self.at
        for j in range(1, TP):
            origin = lax.rem(at.p + TP - j, TP)
            self.copies.arrived(held.at[origin], slots[j - 1], (at.r, at.s))

    def settle(self, own, recv, n):
        total = own[pl.ds(pl.multiple_of(self.at.p * n, n), n), :]
        for j in range(1, TP):
            total = total + recv[lax.rem(self.at.p + j, TP)].astype(F32)
        return total


def columns_of(count, width, action):
    @pl.loop(0, count)
    def _(c):
        action(pl.ds(pl.multiple_of(c * width, width), width))


def rows_of(span, action):
    first, count = span

    @pl.loop(0, count // 64)
    def _(i):
        action(pl.ds(pl.multiple_of(first + i * 64, 64), 64))


def activate(gu, act, span, FS):
    def go(rows):
        gate, up = gu[rows, :FS], gu[rows, FS:]
        act[rows, :] = (jax.nn.silu(gate) * up).astype(BF)

    rows_of(span, go)


def deactivate(gu, d_act, dgu, span, FS):
    def go(rows):
        gate, up, pull = gu[rows, :FS], gu[rows, FS:], d_act[rows, :]
        sigma = jax.nn.sigmoid(gate)
        dgu[rows, :FS] = (pull * up * sigma * (1.0 + gate * (1.0 - sigma))).astype(BF)
        dgu[rows, FS:] = (pull * (gate * sigma)).astype(BF)

    rows_of(span, go)


def multiply(held, weights, out, span, parts):
    first, count = span
    n, D = held.shape[1:]
    values = held[first // n : (first + count) // n].reshape(count, D)
    rows = pl.ds(first, count)

    def go(cols):
        out[rows, cols] = dot(values, weights[:, cols])

    columns_of(parts, weights.shape[1] // parts, go)


def project(left, weights, part, span, send=None, order=None):
    first, count = span
    step = 256
    rows = pl.ds(first, count)
    n = send.shape[1] if send is not None else count

    def go(cols):
        out = dot_nt(left[rows, :], weights[cols, :])
        part[rows, cols] = out
        if send is not None:
            for k in range(first // n, (first + count) // n):
                block = out[k * n - first : (k + 1) * n - first].astype(BF)
                send[k if order is None else order[k], :, cols] = block

    columns_of(weights.shape[0] // step, step, go)


def feed_kernel(place, ident, mode, arrays, D, FS, n, side=0):
    N = n * TP
    R = place.R
    half = D // R
    W = 2 * FS if mode == "both" else 3 * FS
    forward, backward = mode in ("fwd", "both"), mode in ("both", "bwd")
    VM, HB = pltpu.VMEM, pl.ANY
    ins, scratch, outs = {}, {}, {}
    ins["weights"] = HB
    if mode == "fwd":
        ins.update(a_g=VM, h_in=VM, gain_next=VM)
        outs.update(
            h_out=((n, D), F32, VM), next_g=((TP, n, D), BF, VM), gu_out=((N, 2 * FS), F32, HB)
        )
    else:
        ins.update(first_part=VM, h_in=VM, gain=VM)
        outs.update(
            g_out=((n, D), F32, VM),
            next_g=((TP, n, D), BF, VM),
            d_gain=((1, D), F32, VM),
            half_out=((half, FS if mode == "both" else W), BF, VM),
        )
        scratch.update(
            first_send=((TP, n, D), BF),
            first_got=((TP, n, D), BF),
            a_v=((TP, n, D), BF),
            e_v=((TP, n, D), BF),
            d_act=((N, FS), F32),
            dgu=((N, 2 * FS), BF),
            grad_send=((R - 1, half, W), BF),
            grad_got=((R - 1, half, W), BF),
        )
    if mode == "both":
        ins.update(e_g=HB, e_own=VM, down=HB)
        down_piece = (half // place.Q, FS)
        outs.update(
            mid_out=((n, D), F32, VM),
            o_send=((TP, n, D), BF, VM),
            o_base=((n, D), F32, VM),
            down_out=((place.Q,) + down_piece, BF, VM),
            half_up=((half, FS), BF, VM),
        )
        scratch.update(
            down_send=((R - 1, half, FS), BF),
            down_got=((R - 1, half, FS), BF),
            down_half=((place.Q,) + down_piece, BF),
        )
    if mode == "bwd":
        ins.update(a_g=HB, gu_in=HB, g_in=VM, h_before=VM, gain_before=VM)
        piece = (half // place.Q, side)
        ins.update(side_in=VM)
        outs.update(
            d_gain_before=((1, D), F32, VM),
            halo=((HALO, D), BF, VM),
            side_out=((place.Q,) + piece, BF, VM),
        )
        scratch.update(side_got=((R - 1, half, side), BF), side_half=((place.Q,) + piece, BF))
    scratch.update(
        w=((D, 2 * FS), BF),
        wd=((D, FS), BF),
        gu=((N, 2 * FS), F32),
        act=((N, FS), BF),
        part=((N, D), F32),
        send=((TP, n, D), BF),
        got=((TP, n, D), BF),
    )
    in_names, out_names, scratch_names = list(ins), list(outs), list(scratch)
    kinds = {"plane"}
    if backward:
        kinds.add("core")
    if mode == "bwd":
        kinds.update({"back", "zall"})
    if mode == "both":
        kinds.add("zall")
    unit = D // (R * place.Q)
    sems = 32 + 3 * R + 4 * place.Q + 3 * R * place.Q

    def body(*refs):
        names = in_names + out_names + scratch_names
        v = dict(zip(names, refs))
        at = place.here()
        copies = Copies(refs[len(names)], refs[len(names) + 1])
        plane = Plane(at, copies)
        loads = refs[len(names) + 2]
        pending = {}

        def load(name, src, dst):
            pending[name] = pltpu.make_async_copy(src, dst, loads.at[len(pending)])
            pending[name].start()

        def load_blocks(name, source, target):
            for k in range(TP):
                load(name + str(k), source.at[plane.mate(k)], target.at[k])

        def loaded(*names):
            for name in names:
                pending[name].wait()

        def loaded_blocks(name):
            loaded(*[name + str(k) for k in range(TP)])

        if mode == "both":
            load("w", v["weights"], v["w"])
            load_blocks("e", v["e_g"], v["e_v"])
            own_rows = pl.ds(pl.multiple_of((at.r * at.Q + at.q) * unit, unit), unit)
            load("wd", v["down"], v["wd"].at[own_rows])
        else:
            load("w", v["weights"].at[:, : 2 * FS], v["w"])
            load("wd", v["weights"].at[:, 2 * FS : 3 * FS], v["wd"])
        if mode == "bwd":
            for k in range(TP):
                rows = pl.ds(pl.multiple_of(plane.mate(k) * n, n), n)
                load("gu%d" % k, v["gu_in"].at[rows], v["gu"].at[pl.ds(k * n, n)])
            load_blocks("a", v["a_g"], v["a_v"])
        meet(at, kinds)
        w, wd, gu, act = (v[k] for k in ("w", "wd", "gu", "act"))
        part, send, got = (v[k] for k in ("part", "send", "got"))

        def along_line(source, target):
            slots = [copies.slot() for _ in range(at.Q - 1)]
            for j in range(1, at.Q):
                other = lax.rem(at.q + j, at.Q)
                there = (at.r, other * TP + at.p)
                copies.push(source.at[other], target.at[at.q], slots[j - 1], there)
            target[at.q] = source[at.q]
            return slots

        def line_done(target, slots):
            for j in range(1, at.Q):
                origin = lax.rem(at.q + at.Q - j, at.Q)
                copies.arrived(target.at[origin], slots[j - 1], (at.r, at.s))

        def turned_rows(held, j):
            first_col = lax.rem(at.r + j, R) * half
            cols = pl.ds(pl.multiple_of(first_col, 128), half)
            return held[:, :, cols].reshape(N, half).astype(F32).T.astype(BF)

        def send_down():
            down_slots = [copies.slot() for _ in range(R - 1)]
            for j in range(1, R):
                v["down_send"][j - 1] = dot(turned_rows(v["e_v"], j), act[...]).astype(BF)
                there = (lax.rem(at.r + j, R), at.s)
                copies.push(v["down_send"].at[j - 1], v["down_got"].at[j - 1], down_slots[j - 1], there)
            total = dot(turned_rows(v["e_v"], 0), act[...])
            for j in range(1, R):
                copies.arrived(v["down_got"].at[j - 1], down_slots[j - 1], (at.r, at.s))
                total = total + v["down_got"][j - 1].astype(F32)
            v["down_half"][...] = total.astype(BF).reshape(v["down_half"].shape)
            return along_line(v["down_half"], v["down_out"])

        if mode != "fwd":
            first = v["first_part"]
            mine = [pl.ds(pl.multiple_of(plane.mate(k) * n, n), n) for k in range(TP)]
            waits = []
            for k in range(1, TP):
                v["first_send"][k] = first[mine[k], :].astype(BF)
                waits.append(plane.to_mate(v["first_send"].at[k], v["first_got"], k))
        if mode == "fwd":
            pending["w"].wait()
            multiply(v["a_g"], w, gu, (0, N), 3)
            save = pltpu.make_async_copy(gu, v["gu_out"], loads.at[len(pending)])
            save.start()
            activate(gu, act, (0, N), FS)
            pending["wd"].wait()
            project(act, wd, part, (0, N), send)
            wait = plane.swap(send, got)
            wait()
            h_out = v["h_in"][...] + plane.settle(part, got, n)
            v["h_out"][...] = h_out
            v["next_g"][at.p] = (h_out * inverse_rms(h_out) * v["gain_next"][...]).astype(BF)
            wait = plane.gather(v["next_g"])
            wait()
            save.wait()
            copies.drain()
            return
        everything, own, near, far = (0, N), (0, n), (n, 2 * n), (3 * n, n)
        d_act, dgu = v["d_act"], v["dgu"]
        if mode == "both":
            loaded("wd")
            steps = chain_run(at, copies, wd, unit)
            next(steps)
            next(steps)
            for wait in waits:
                wait()
            h = v["h_in"][...] + plane.sum_mates(first[mine[0], :], v["first_got"])
            v["mid_out"][...] = h
            v["a_v"][0] = (h * inverse_rms(h) * v["gain"][...]).astype(BF)
            waits = plane.spread_mates(v["a_v"])
            for _ in range(at.Q - 3):
                next(steps)
            loaded("w")
            loaded_blocks("e")
            for span, awaited in ((own, ()), (near, waits[:2]), (far, waits[2:])):
                for wait in awaited:
                    wait()
                multiply(v["a_v"], w, gu, span, 3)
                activate(gu, act, span, FS)
            for _ in steps:
                pass
            multiply(v["e_v"], wd, d_act, everything, 3)
            waits = []
            for span, slots in ((near, (1, 2)), (far, (3,))):
                deactivate(gu, d_act, dgu, span, FS)
                project(dgu, w, part, span, send)
                waits.extend(plane.to_mate(send.at[k], got, k) for k in slots)
                if span is near:
                    line_slots = send_down()
            deactivate(gu, d_act, dgu, own, FS)
            project(dgu, w, part, own)
        else:
            side_slots = [copies.slot() for _ in range(R - 1)]
            for j in range(1, R):
                other = lax.rem(at.r + j, R)
                copies.push(
                    v["side_in"].at[other], v["side_got"].at[j - 1], side_slots[j - 1], (other, at.s)
                )
            loaded_blocks("gu")
            activate(gu, act, everything, FS)
            for wait in waits:
                wait()
            h = v["h_in"][...]
            before = v["h_before"][...]
            r_before = inverse_rms(before)
            d_normed = plane.sum_mates(first[mine[0], :], v["first_got"])
            v["d_gain_before"][...] = jnp.sum(d_normed * before * r_before, axis=0, keepdims=True)
            g_mid = v["g_in"][...] + rms_pull(d_normed, before, r_before, v["gain_before"][...])
            v["g_out"][...] = g_mid
            v["e_v"][0] = g_mid.astype(BF)
            waits = plane.spread_mates(v["e_v"])
            loaded("w", "wd")
            loaded_blocks("a")
            total = v["side_in"][at.r].astype(F32)
            for j in range(1, R):
                copies.arrived(v["side_got"].at[j - 1], side_slots[j - 1], (at.r, at.s))
                total = total + v["side_got"][j - 1].astype(F32)
            v["side_half"][...] = total.astype(BF).reshape(v["side_half"].shape)
            line_slots = along_line(v["side_half"], v["side_out"])
            returns = []
            for span, awaited, slots in (
                (own, (), ()),
                (near, waits[:2], (1, 2)),
                (far, waits[2:], (3,)),
            ):
                for wait in awaited:
                    wait()
                multiply(v["e_v"], wd, d_act, span, 3)
                deactivate(gu, d_act, dgu, span, FS)
                project(dgu, w, part, span, send if slots else None)
                returns.extend(plane.to_mate(send.at[k], got, k) for k in slots)
            waits = returns
        values, pulls = v["a_v"], v["e_v"]

        slots = [copies.slot() for _ in range(R - 1)]
        for j in range(1, R):
            left = turned_rows(values, j)

            def put(cols, left=left, j=j):
                v["grad_send"][j - 1, :, cols] = dot(left, v["dgu"][:, cols]).astype(BF)

            columns_of(3, 2 * FS // 3, put)
            if mode == "bwd":
                v["grad_send"][j - 1, :, 2 * FS :] = dot(turned_rows(pulls, j), act[...]).astype(BF)
            other = lax.rem(at.r + j, R)
            copies.push(
                v["grad_send"].at[j - 1], v["grad_got"].at[j - 1], slots[j - 1], (other, at.s)
            )
        for wait in waits:
            wait()
        d_normed = plane.sum_mates(part[:n, :], got)
        r = inverse_rms(h)
        base = v["e_own"][...].astype(F32) if mode == "both" else v["g_out"][...]
        v["d_gain"][...] = jnp.sum(d_normed * h * r, axis=0, keepdims=True)
        g_new = base + rms_pull(d_normed, h, r, v["gain"][...])
        v["g_out"][...] = g_new
        v["next_g"][at.p] = g_new.astype(BF)
        wait = plane.gather(v["next_g"])
        if mode == "bwd":
            back = [copies.slot() for _ in range(TP)]
            for j in range(TP):
                copies.push(
                    v["next_g"].at[at.p, pl.ds(0, HALO)],
                    v["halo"],
                    back[j],
                    (at.r, (at.q - 1) * TP + j),
                    (at.p == 0) & (at.q > 0),
                    back[0],
                )
        if mode == "both":
            project(act, wd, part, everything, v["o_send"], [plane.mate(k) for k in range(TP)])
            v["o_base"][...] = h + part[:n, :]
        left = turned_rows(values, 0)
        for j in range(1, R):
            copies.arrived(v["grad_got"].at[j - 1], slots[j - 1], (at.r, at.s))

        def finish(target, base, shift):
            step = FS // 3

            @pl.loop(0, 3)
            def _(c):
                cols = pl.ds(pl.multiple_of(base + c * step, 128), step)
                total = dot(left, v["dgu"][:, cols])
                for j in range(1, R):
                    total = total + v["grad_got"][j - 1, :, cols].astype(F32)
                there = pl.ds(pl.multiple_of(base - shift + c * step, 128), step)
                target[:, there] = total.astype(BF)

        finish(v["half_out"], 0, 0)
        if mode == "both":
            finish(v["half_up"], FS, FS)
        else:
            finish(v["half_out"], FS, 0)
        if mode == "bwd":
            total = dot(turned_rows(pulls, 0), act[...])
            for j in range(1, R):
                total = total + v["grad_got"][j - 1, :, 2 * FS :].astype(F32)
            v["half_out"][:, 2 * FS :] = total.astype(BF)
        wait()
        if mode == "bwd":
            copies.arrived(v["halo"], back[0], (at.r, at.s), at.q < at.Q - 1)
            line_done(v["side_out"], line_slots)
        if mode == "both":
            line_done(v["down_out"], line_slots)
        copies.drain()

    results = pl.pallas_call(
        body,
        out_shape=tuple(like(outs[k][0], outs[k][1]) for k in out_names),
        in_specs=[pl.BlockSpec(memory_space=ins[k]) for k in in_names],
        out_specs=tuple(pl.BlockSpec(memory_space=outs[k][2]) for k in out_names),
        scratch_shapes=[pltpu.VMEM(*scratch[k]) for k in scratch_names]
        + [pltpu.SemaphoreType.DMA((sems,)), pltpu.SemaphoreType.DMA((sems,))]
        + [pltpu.SemaphoreType.DMA((12,))],
        compiler_params=pltpu.CompilerParams(collective_id=ident, has_side_effects=True),
        cost_estimate=pl.CostEstimate(flops=0, bytes_accessed=COST, transcendentals=0),
        name="feed_%s" % mode,
    )(*[arrays[k] for k in in_names])
    return dict(zip(out_names, results))


def doc_info(positions, lengths):
    doc_ends = jnp.cumsum(lengths, dtype=jnp.int32)
    passed = positions[:, None] >= doc_ends[None, :]
    segment = jnp.sum(passed.astype(jnp.int32), axis=1, dtype=jnp.int32)
    opening = jnp.sum(jnp.where(passed, lengths[None, :], 0), axis=1, dtype=jnp.int32)
    return (segment, positions - opening)


def inverse_rms(values):
    return lax.rsqrt(jnp.mean(values * values, axis=-1, keepdims=True) + EPSILON)


def rms_pull(upstream, values, inverse, norm_gain):
    scaled = upstream * norm_gain
    product_mean = jnp.mean(scaled * values, axis=-1, keepdims=True)
    return inverse * scaled - values * (inverse * inverse * inverse) * product_mean


def settle(own, arrived, p):
    index = jnp.arange(TP, dtype=jnp.int32)[:, None, None]
    others = jnp.where(index == p, 0.0, arrived.astype(F32))
    mine = lax.dynamic_index_in_dim(own, p, 0, keepdims=False)
    return mine + jnp.sum(others, axis=0)


def per_device(
    place,
    tokens,
    doc_lengths,
    cotangent,
    gain_conv,
    w_in,
    kernel,
    w_mix,
    gain_ffa,
    gate_a,
    up_a,
    down_a,
    gain_att,
    w_query,
    w_key,
    w_value,
    head_gains,
    w_attout,
    gain_ffb,
    gate_b,
    up_b,
    down_b,
):
    R, S, Q = place.R, place.S, place.Q
    n, D = tokens.shape[1], tokens.shape[2]
    shard = w_in.shape[0]
    FS = gate_a.shape[1] // TP
    CS = D // TP
    QS, KS = H * HD // TP, KVH * HD // TP
    taps = kernel.shape[0]
    N = n * TP
    r, s = lax.axis_index("rows"), lax.axis_index("seq")
    q, p = s // TP, lax.rem(s, TP)
    lengths = doc_lengths[0]

    columns = [[a * S + b * TP + c for a in range(R) for b in range(Q)] for c in range(TP)]
    lines = [[b * TP + c for b in range(Q)] for c in range(TP)]

    def gather_rest(plane):
        flat = plane.reshape(TP * shard, -1)
        return lax.all_gather(
            flat, ("rows", "seq"), axis=0, tiled=True, axis_index_groups=columns
        )

    def by_row(grads):
        return grads.astype(BF).reshape(R, S * shard, -1)

    def own_rows(rows, came, *later):
        return lax.optimization_barrier((collect(rows, came, r).astype(BF),) + later)

    def reduce_line(half):
        part = lax.psum_scatter(
            half, "seq", scatter_dimension=0, tiled=True, axis_index_groups=lines
        )
        return part.reshape(TP, shard, part.shape[1])

    in_layout = [(0, k * D, CS, CS, k * CS) for k in range(3)]
    small = jnp.stack([gain_conv, gain_ffa, gain_att, gain_ffb] + [kernel[i] for i in range(taps)])
    small = jnp.pad(small, ((0, 16 - 4 - taps), (0, 128 - shard)))

    mine = tokens[0]
    (tok_g,), (halo_a, halo_b), (in_g,), (mix_g,), (small_g,), (ffa_p,) = exchange(
        place,
        0,
        [
            gather_plane(mine),
            halo_tokens(mine),
            spread_all(place, w_in, in_layout),
            home_all(place, w_mix),
            spread_all(place, small, [(0, 0, 0, 128, 0)]),
            spread(gate_a, up_a, down_a.T, w_query, w_key, w_value, w_attout.T),
        ],
    )
    wide = gather_rest(ffa_p)
    w_att = wide[:, 3 * FS :]
    w_mix_s = mix_g.reshape(CS, D)
    vectors = small_g[:, : 4 + taps, :shard].transpose(1, 0, 2).reshape(4 + taps, D).astype(F32)
    g_conv, g_ffa, g_att, g_ffb = (vectors[i] for i in range(4))
    kernel_f = lax.dynamic_slice_in_dim(vectors[4:], p * CS, CS, 1)
    w_in_s = in_g.reshape(D, 3 * CS)

    def own(parts, index):
        return lax.dynamic_index_in_dim(parts, index, 0, keepdims=False).astype(F32)

    def collect(parts, came, index):
        slot = jnp.arange(came.shape[0], dtype=jnp.int32).reshape((-1,) + (1,) * (came.ndim - 1))
        mine_part = lax.dynamic_index_in_dim(parts, index, 0, keepdims=True).astype(F32)
        return jnp.sum(jnp.where(slot == index, mine_part, came.astype(F32)), axis=0)

    def after_core(parts, came):
        summed = collect(parts, came, r)
        return summed.reshape((Q, TP) + summed.shape[1:])

    total = S * n
    pos_ext = q * N - HALO + jnp.arange(N + 2 * HALO, dtype=jnp.int32)
    seg_ext, rel_ext = doc_info(pos_ext, lengths)
    valid = ((pos_ext >= 0) & (pos_ext < total))[:, None]
    x_ext = jnp.concatenate([halo_a, tok_g.reshape(N, D), halo_b], axis=0)
    x_ext = jnp.where(valid, x_ext, jnp.zeros_like(x_ext)).astype(F32)
    r0_ext = inverse_rms(x_ext)
    n1_ext = (x_ext * r0_ext * g_conv).astype(BF)
    z_ext = dot(n1_ext, w_in_s)
    b_ext, c_ext, v_ext = z_ext[:, :CS], z_ext[:, CS : 2 * CS], z_ext[:, 2 * CS :]
    u_ext = lax.optimization_barrier((b_ext * v_ext).astype(BF)).astype(F32)
    span = slice(HALO, HALO + N)
    same = [
        (seg_ext[HALO - 2 + k : HALO - 2 + k + N] == seg_ext[span]).astype(F32)[:, None]
        for k in range(taps)
    ]
    near = [u_ext[HALO - 2 + k : HALO - 2 + k + N] for k in range(taps)]
    conv = kernel_f[0] * near[0] * same[0]
    for k in range(1, taps):
        conv = conv + kernel_f[k] * near[k] * same[k]
    m_bf = (c_ext[span] * conv).astype(BF)
    part = dot(m_bf, w_mix_s).reshape(TP, n, D)
    (got,), (ffb_p,), (down_p,) = exchange(
        place,
        1,
        [
            swap_plane(part.astype(BF)),
            spread(gate_b, up_b),
            spread(down_b.T),
        ],
    )
    wb = gather_rest(ffb_p)
    x0 = mine.astype(F32)
    h1 = x0 + settle(part, got, p)

    r1 = inverse_rms(h1)
    a1 = (h1 * r1 * g_ffa).astype(BF)
    ((a1_g,),) = exchange(place, 2, [gather_plane(a1)])
    a1_g = a1_g.reshape(N, D)

    g_row = {name: value[None] for name, value in
             (("ffa", g_ffa), ("att", g_att), ("ffb", g_ffb))}
    fed = feed_kernel(
        place,
        3,
        "fwd",
        {"weights": wide, "a_g": a1_g.reshape(TP, n, D), "h_in": h1, "gain_next": g_row["att"]},
        D,
        FS,
        n,
    )
    h2, n3_g, gu1 = fed["h_out"], fed["next_g"], fed["gu_out"]

    n3_g = n3_g.reshape(N, D)
    w_out = w_att[:, QS + 2 * KS :]
    lane = jnp.arange(2 * HD, dtype=jnp.int32)
    frequency = jnp.exp(jnp.arange(HD // 2, dtype=F32) * (-2.0 * math.log(THETA) / HD))
    angles = rel_ext[span].astype(F32)[:, None] * jnp.tile(frequency, 4)[None, :]
    cosine = jnp.cos(angles)
    sine = jnp.sin(angles) * jnp.where(lane % HD < HD // 2, -1.0, 1.0)
    head_rows = jnp.tile(head_gains.astype(F32), (1, 2))
    pre, q_bf, kv_bf = heads_forward(n3_g, w_att, head_rows, cosine, sine, QS, KS)
    e_bf = cotangent[0]
    (kv_w,), (e_g,) = exchange(
        place,
        5,
        [window_forward(place, kv_bf), gather_plane(e_bf)],
    )
    reach = Q // 2 + 1
    kv_all = kv_w.reshape(reach * N, 2 * KS)
    q_seg = seg_ext[span]
    key_seg, _ = doc_info((q - reach + 1) * N + jnp.arange(reach * N, dtype=jnp.int32), lengths)
    first = jnp.maximum((reach - 1 - q) * N, 0).astype(jnp.int32).reshape(1)
    seg_col, seg_row = (jnp.broadcast_to(q_seg[:, None], (N, 128)), jnp.broadcast_to(q_seg, (8, N)))
    key_col = jnp.broadcast_to(key_seg[:, None], (reach * N, 128))
    key_row = jnp.broadcast_to(key_seg, (8, reach * N))
    o_bf = attend_forward(q_bf, kv_all, seg_col, key_row, first, 128)
    fed = feed_kernel(
        place,
        8,
        "both",
        {
            "weights": wb,
            "down": down_p.reshape(TP * shard, FS),
            "first_part": dot_nt(o_bf, w_out),
            "h_in": h2,
            "gain": g_row["ffb"],
            "e_g": e_g.reshape(TP, n, D),
            "e_own": e_bf,
        },
        D,
        FS,
        n,
    )
    full_down = jnp.sum(fed["down_out"].astype(F32), axis=0).astype(BF).reshape(TP, shard, FS)
    h3, g3, g3_g, half_b = fed["mid_out"], fed["g_out"], fed["next_g"], fed["half_out"]
    d_gain = {}
    d_gain["ffb"] = fed["d_gain"][0]

    g3_g = g3_g.reshape(N, D)
    d_o = dot(g3_g, w_out).astype(BF)
    d_q, d_kv = attend_backward(q_bf, kv_all, d_o, seg_row, key_col, first, 128)
    d_kv = d_kv.reshape(reach, N, 2 * KS)
    (got_kv,), (got_o,) = exchange(
        place, 10, [window_backward(place, d_kv.astype(BF)), swap_plane(fed["o_send"])]
    )
    index = jnp.arange(TP, dtype=jnp.int32)[:, None, None]
    h4 = fed["o_base"] + jnp.sum(jnp.where(index == p, 0.0, got_o.astype(F32)), axis=0)
    mixed = h4.astype(BF)[None]
    count = (q + 1 < Q).astype(jnp.int32).reshape(1)
    half_up, got_kv = lax.optimization_barrier((fed["half_up"], got_kv))
    full_gate, full_up = reduce_line(half_b), reduce_line(half_up)
    part, rows_att, d_heads = heads_backward(
        d_q, d_kv[-1], got_kv, count, pre, head_rows, cosine, sine, n3_g, g3_g, o_bf, w_att
    )
    d_heads = jnp.sum(d_heads.reshape(2, 2, HD), axis=1)
    rows_att = by_row(rows_att)
    part, full_gate = lax.optimization_barrier((part, full_gate))
    fed = feed_kernel(
        place,
        13,
        "bwd",
        {
            "weights": wide,
            "first_part": part,
            "h_in": h1,
            "gain": g_row["ffa"],
            "a_g": a1_g.reshape(TP, n, D),
            "gu_in": gu1,
            "g_in": g3,
            "h_before": h2,
            "gain_before": g_row["att"],
            "side_in": rows_att,
        },
        D,
        FS,
        n,
        rows_att.shape[2],
    )
    full_att = jnp.sum(fed["side_out"].astype(F32), axis=0).astype(BF).reshape(TP, shard, -1)
    g1, g1_g, g1_halo = fed["g_out"], fed["next_g"], fed["halo"]
    d_gain["att"], d_gain["ffa"] = fed["d_gain_before"][0], fed["d_gain"][0]
    full_a = reduce_line(fed["half_out"])

    g1_halo = jnp.where(q < Q - 1, g1_halo, jnp.zeros_like(g1_halo))
    g1_ext = jnp.concatenate([g1_g.reshape(N, D), g1_halo], axis=0)
    d_m = dot_nt(g1_ext, w_mix_s)
    d_mix_s = dot_tn(m_bf, g1_ext[:N])
    d_c = d_m[:N] * conv
    d_conv = lax.optimization_barrier((d_m * c_ext[HALO:]).astype(BF)).astype(F32)
    d_kernel = jnp.stack(
        [jnp.sum(d_conv[:N] * near[k] * same[k], axis=0) for k in range(taps)]
    )
    d_u = jnp.zeros((N, CS), F32)
    for k in range(taps):
        ahead = taps - 1 - k
        match = (seg_ext[HALO + ahead : HALO + ahead + N] == seg_ext[span]).astype(F32)[:, None]
        d_u = d_u + kernel_f[k] * d_conv[ahead : ahead + N] * match
    d_z = jnp.concatenate([d_u * v_ext[span], d_c, d_u * b_ext[span]], axis=1).astype(BF)
    rows_in = dot_tn(n1_ext[span], d_z).astype(BF).reshape(R, S, shard, 3 * CS)
    rows_mix = d_mix_s.astype(BF).reshape(R, Q, shard, D)
    d_n1 = dot_nt(d_z, w_in_s)
    d_gain["conv"] = jnp.sum(d_n1 * x_ext[span] * r0_ext[span], axis=0)
    part = d_n1.reshape(TP, n, D)
    d_taps = lax.dynamic_update_slice(jnp.zeros((taps, D), F32), d_kernel, (0, p * CS))
    lanes = jnp.concatenate(
        [jnp.stack([d_gain["conv"], d_gain["ffa"], d_gain["att"], d_gain["ffb"]]), d_taps]
    )
    lanes = lanes.reshape(4 + taps, R * S, shard).transpose(1, 0, 2)
    lanes = jnp.pad(lanes, ((0, 0), (0, 0), (0, 128 - shard)))
    heads_row = jnp.broadcast_to(d_heads.reshape(1, 1, 2 * HD), (R * S, 1, 2 * HD))
    tiny = jnp.concatenate([lanes, heads_row], axis=1)
    tiny_rows = tiny.reshape(R, S, 4 + taps + 1, 128)
    (got,), (core_in,), (core_mix,), (core_t,), *plane_b, (plane_att,) = exchange(
        place,
        15,
        [
            swap_plane(part.astype(BF)),
            swap_core(rows_in),
            swap_core(rows_mix),
            swap_core(tiny_rows),
            swap_plane(full_gate),
            swap_plane(full_up),
            swap_plane(full_down),
            swap_plane(full_att),
        ],
    )
    d_normed = settle(part, got, p)
    g0 = g1 + rms_pull(d_normed, x0, inverse_rms(x0), g_conv)
    d_tokens = g0.astype(BF)[None]

    tiny_line = after_core(tiny_rows, core_t)
    line_in = after_core(rows_in, core_in).astype(BF)
    line_mix = collect(rows_mix, core_mix, r).astype(BF)
    (plane_a,), (plane_in,), (plane_t,), (mix_back,) = exchange(
        place,
        16,
        [
            swap_plane(full_a),
            line_plane(line_in),
            line_plane(tiny_line),
            line_home(line_mix),
        ],
    )
    FF = TP * FS
    by_weight = [(k * FS, FS, k, 0) for k in range(3)]
    by_gate = [(k * CS, CS, 0, k * D) for k in range(3)]
    by_head = [(0, QS, 0, 0), (QS, KS, 1, 0), (QS + KS, KS, 2, 0), (QS + 2 * KS, QS, 3, 0)]
    ready = finish(
        place,
        place.here(),
        [
            *[
                (own, came[0], by_weight[:1], [(shard, FF)])
                for own, came in zip((full_gate, full_up, full_down), plane_b)
            ],
            (full_att, plane_att, by_head, [(shard, TP * k) for k in (QS, KS, KS, QS)]),
            (full_a, plane_a, by_weight, [(shard, FF)] * 3),
            (None, plane_in, by_gate, [(shard, 3 * D)]),
        ],
        plane_t,
        mix_back,
        taps,
    )
    out_b, out_att, out_a, (out_in,) = ready[:3], ready[3:7], ready[7:10], ready[10:11]
    of_conv, of_ffa, of_att, of_ffb, of_taps, d_heads, out_mix = ready[11:]
    return (
        mixed,
        d_tokens,
        of_conv[0],
        out_in,
        of_taps,
        out_mix,
        of_ffa[0],
        out_a[0],
        out_a[1],
        out_a[2].T,
        of_att[0],
        out_att[0],
        out_att[1],
        out_att[2],
        d_heads,
        out_att[3].T,
        of_ffb[0],
        out_b[0],
        out_b[1],
        out_b[2].T,
    )


def solution(mesh):
    place = Place(mesh.shape["rows"], mesh.shape["seq"])
    whole = ("rows", "seq")
    wide, first, second = P("rows", "seq", None), P(whole, None), P(None, whole)
    in_specs = (
        (wide, P("rows", None), wide, P(whole), first, second, first)
        + (P(whole), first, first, second)
        + (P(whole), first, first, first, P(), second)
        + (P(whole), first, first, second)
    )
    out_specs = (
        (wide, wide, P(whole), first, second, first)
        + (P(whole), first, first, second)
        + (P(whole), first, first, first, P(), second)
        + (P(whole), first, first, second)
    )
    return jax.shard_map(
        functools.partial(per_device, place),
        mesh=mesh,
        in_specs=in_specs,
        out_specs=out_specs,
        check_vma=False,
    )
```

```python
import functools
import math

import jax
import jax.numpy as jnp
from jax import lax
from jax.experimental import pallas as pl
from jax.experimental.pallas import tpu as pltpu
from jax.sharding import PartitionSpec as P

H = 16
KVH = 8
HD = 64
TP = 4
HALO = 16
COST = 1_000_000

EPSILON = 1e-05
THETA = 1000000.0
MASKED = -1e30
MESH_ID = pl.DeviceIdType.MESH
BF = jnp.bfloat16
F32 = jnp.float32


def dot(left, right):
    return jnp.dot(left, right, preferred_element_type=F32)


def dot_tn(left, right):
    return lax.dot_general(left, right, (((0,), (0,)), ((), ())), preferred_element_type=F32)


def dot_nt(left, right):
    return lax.dot_general(left, right, (((1,), (1,)), ((), ())), preferred_element_type=F32)


class Place:
    def __init__(self, rows, seq):
        self.R, self.S = rows, seq
        self.Q = seq // TP

    def here(self):
        here = Place(self.R, self.S)
        here.r = lax.axis_index("rows")
        here.s = lax.axis_index("seq")
        here.q = here.s // TP
        here.p = lax.rem(here.s, TP)
        return here


class Copies:
    def __init__(self, send, recv):
        self.send, self.recv, self.count, self.sent = send, recv, 0, []

    def slot(self):
        self.count += 1
        return self.count - 1

    def remote(self, src, dst, slot, where, recv_slot=None):
        return pltpu.make_async_remote_copy(
            src_ref=src,
            dst_ref=dst,
            send_sem=self.send.at[slot],
            recv_sem=self.recv.at[slot if recv_slot is None else recv_slot],
            device_id=where,
            device_id_type=MESH_ID,
        )

    def push(self, src, dst, slot, where, cond=None, recv_slot=None):
        copy = self.remote(src, dst, slot, where, recv_slot)
        when(cond, copy.start)
        self.sent.append((copy.wait_send, cond))

    def arrived(self, dst, slot, where, cond=None):
        copy = self.remote(dst, dst, slot, where)
        when(cond, copy.wait_recv)

    def local(self, src, dst):
        slot = self.slot()
        copy = pltpu.make_async_copy(src, dst, self.recv.at[slot])
        copy.start()
        self.sent.append((copy.wait, None))

    def drain(self):
        for wait, cond in self.sent:
            when(cond, wait)


def when(cond, action):
    if cond is None:
        action()
    else:
        pl.when(cond)(lambda: action())


class Job:
    def __init__(
        self, ins, outs, run, kinds, aliases=(), vmem=(), relay=False, late=False, scratch=()
    ):
        self.ins, self.outs, self.run, self.kinds = ins, outs, run, kinds
        self.aliases, self.vmem, self.relay, self.late = aliases, vmem, relay, late
        self.scratch = scratch


def together(runs):
    while runs:
        runs = [steps for steps in runs if next(steps, "done") != "done"]
        yield "go"


def partners(at, kinds):
    found = []
    if "plane" in kinds:
        for j in range(1, TP):
            found.append((None, at.r, at.q * TP + lax.rem(at.p + j, TP)))
    if "core" in kinds:
        for j in range(1, at.R):
            found.append((None, lax.rem(at.r + j, at.R), at.s))
    if "zall" in kinds:
        for j in range(1, at.Q):
            found.append((None, at.r, lax.rem(at.q + j, at.Q) * TP + at.p))
    elif "chain" in kinds:
        found.append((at.q > 0, at.r, at.s - TP))
        found.append((at.q < at.Q - 1, at.r, at.s + TP))
    if "home" in kinds:
        r, s, _, same = home_of(at)
        found.append((same == 0, r, s))
        r, s, same = visitor_of(at)
        found.append((same == 0, r, s))
    if "back" in kinds:
        found.append((at.q < at.Q - 1, at.r, (at.q + 1) * TP))
        for j in range(TP):
            found.append(((at.p == 0) & (at.q > 0), at.r, (at.q - 1) * TP + j))
    if "halo" in kinds:
        found.append((at.q > 0, at.r, (at.q - 1) * TP + TP - 1))
        found.append((at.q < at.Q - 1, at.r, (at.q + 1) * TP))
        for j in range(TP):
            found.append(((at.p == TP - 1) & (at.q < at.Q - 1), at.r, (at.q + 1) * TP + j))
            found.append(((at.p == 0) & (at.q > 0), at.r, (at.q - 1) * TP + j))
    return found


def home_of(at):
    k = lax.rem(at.r * at.S + at.s, at.R * at.Q)
    r, s = k // at.Q, lax.rem(k, at.Q) * TP + (at.r * at.S + at.s) // (at.R * at.Q)
    return r, s, k, ((r == at.r) & (s == at.s)).astype(jnp.int32)


def visitor_of(at):
    d = at.p * (at.R * at.Q) + at.r * at.Q + at.q
    r, s = d // at.S, lax.rem(d, at.S)
    return r, s, ((r == at.r) & (s == at.s)).astype(jnp.int32)


def meet(at, kinds):
    barrier = pltpu.get_barrier_semaphore()
    peers = partners(at, kinds)
    for cond, r, s in peers:
        when(
            cond,
            functools.partial(
                pl.semaphore_signal, barrier, inc=1, device_id=(r, s), device_id_type=MESH_ID
            ),
        )
    awaited = sum(1 for cond, r, s in peers if cond is None)
    for cond, r, s in peers:
        if cond is not None:
            awaited = awaited + cond.astype(jnp.int32)
    pl.semaphore_wait(barrier, awaited)


def exchange(place, ident, jobs):
    kinds = set().union(*[job.kinds for job in jobs])
    n_in = sum(len(job.ins) for job in jobs)
    n_out = sum(len(job.outs) for job in jobs)
    sems = 24 + sum(
        12 + 4 * len(job.ins) + 2 * place.Q + place.R * place.Q * 2 for job in jobs
    )
    arrays, in_specs, outs, aliases = [], [], [], {}
    for job in jobs:
        for k, o in job.aliases:
            aliases[len(arrays) + k] = len(outs) + o
        for k, value in enumerate(job.ins):
            arrays.append(value)
            in_specs.append(pl.BlockSpec(memory_space=pltpu.VMEM if k in job.vmem else pl.ANY))
        outs.extend(job.outs)

    def body(*refs):
        at = place.here()
        ins, results = refs[:n_in], refs[n_in : n_in + n_out]
        copies = Copies(refs[n_in + n_out], refs[n_in + n_out + 1])
        held = refs[n_in + n_out + 2 :]
        meet(at, kinds)
        runs, i, o, h = [], 0, 0, 0
        for job in jobs:
            mine = list(results[o : o + len(job.outs)]) + list(held[h : h + len(job.scratch)])
            runs.append(job.run(at, copies, ins[i : i + len(job.ins)], mine))
            i, o, h = i + len(job.ins), o + len(job.outs), h + len(job.scratch)
        pairs = list(zip(jobs, runs))
        relays = together([steps for job, steps in pairs if job.relay])
        next(relays, "done")
        for steps in [steps for job, steps in pairs if not job.relay and not job.late]:
            next(steps)
        next(relays, "done")
        for steps in [steps for job, steps in pairs if job.late]:
            next(steps)
        for _ in relays:
            pass
        for steps in [steps for job, steps in pairs if not job.relay]:
            for _ in steps:
                pass
        copies.drain()

    results = pl.pallas_call(
        body,
        out_shape=tuple(outs),
        in_specs=in_specs,
        out_specs=tuple(
            pl.BlockSpec(memory_space=pltpu.VMEM if job.scratch else pl.ANY)
            for job in jobs
            for _ in job.outs
        ),
        scratch_shapes=[pltpu.SemaphoreType.DMA((sems,)), pltpu.SemaphoreType.DMA((sems,))]
        + [pltpu.VMEM(*shape) for job in jobs for shape in job.scratch],
        input_output_aliases=aliases,
        compiler_params=pltpu.CompilerParams(collective_id=ident, has_side_effects=True),
        cost_estimate=pl.CostEstimate(flops=0, bytes_accessed=COST, transcendentals=0),
        name="exchange_%d" % ident,
    )(*arrays)
    given, o = [], 0
    for job in jobs:
        given.append(results[o : o + len(job.outs)])
        o += len(job.outs)
    return given


def like(shape, dtype=BF):
    return jax.ShapeDtypeStruct(shape, dtype)


def gather_plane(value):
    def run(at, copies, ins, outs):
        slots = [copies.slot() for _ in range(TP - 1)]
        for j in range(1, TP):
            peer = at.q * TP + lax.rem(at.p + j, TP)
            copies.push(ins[0], outs[0].at[at.p], slots[j - 1], (at.r, peer))
        copies.local(ins[0], outs[0].at[at.p])
        yield "go"
        for j in range(1, TP):
            origin = lax.rem(at.p + TP - j, TP)
            copies.arrived(outs[0].at[origin], slots[j - 1], (at.r, at.s))

    return Job([value], [like((TP,) + value.shape, value.dtype)], run, {"plane"}, vmem=(0,))


def swap_plane(value):
    def run(at, copies, ins, outs):
        slots = [copies.slot() for _ in range(TP - 1)]
        for j in range(1, TP):
            other = lax.rem(at.p + j, TP)
            copies.push(
                ins[0].at[other], outs[0].at[at.p], slots[j - 1], (at.r, at.q * TP + other)
            )
        yield "go"
        for j in range(1, TP):
            origin = lax.rem(at.p + TP - j, TP)
            copies.arrived(outs[0].at[origin], slots[j - 1], (at.r, at.s))

    return Job([value], [like(value.shape, value.dtype)], run, {"plane"})


def line_sum(at, copies, source, held):
    slots = [copies.slot() for _ in range(at.Q - 1)]
    for j in range(1, at.Q):
        other = lax.rem(at.q + j, at.Q)
        there = (at.r, other * TP + at.p)
        copies.push(source.at[other], held.at[at.q], slots[j - 1], there)
    held[at.q] = source[at.q]
    yield "go"
    yield "go"
    for j in range(1, at.Q):
        origin = lax.rem(at.q + at.Q - j, at.Q)
        copies.arrived(held.at[origin], slots[j - 1], (at.r, at.s))
    total = held[0].astype(F32)
    for k in range(1, at.Q):
        total = total + held[k].astype(F32)
    return total


def line_plane(value):
    def run(at, copies, ins, outs):
        held, summed = outs[1:]
        total = yield from line_sum(at, copies, ins[0], held)
        summed[...] = total.astype(summed.dtype)
        slots = [copies.slot() for _ in range(TP - 1)]
        for j in range(1, TP):
            other = lax.rem(at.p + j, TP)
            there = (at.r, at.q * TP + other)
            copies.push(summed.at[other], outs[0].at[at.p], slots[j - 1], there)
        outs[0][at.p] = summed[at.p]
        yield "go"
        for j in range(1, TP):
            origin = lax.rem(at.p + TP - j, TP)
            copies.arrived(outs[0].at[origin], slots[j - 1], (at.r, at.s))

    scratch = ((value.shape, value.dtype), (value.shape[1:], value.dtype))
    outs = [like(value.shape[1:], value.dtype)]
    kinds = {"zall", "plane"}
    return Job([value], outs, run, kinds, vmem=(0,), relay=True, scratch=scratch)


def line_home(value):
    def run(at, copies, ins, outs):
        held, summed, got = outs[1:]
        total = yield from line_sum(at, copies, ins[0], held)
        summed[...] = total.astype(summed.dtype)
        r, s, own = visitor_of(at)
        _, _, _, here = home_of(at)
        slot = copies.slot()
        copies.push(summed, got, slot, (r, s), own == 0)
        yield "go"
        copies.arrived(got, slot, (at.r, at.s), here == 0)

        @pl.when(here == 0)
        def _():
            outs[0][...] = got[...]

        @pl.when(here == 1)
        def _():
            outs[0][...] = summed[...]

    one = (value.shape[1:], value.dtype)
    outs = [like(*one)]
    kinds = {"zall", "home"}
    return Job([value], outs, run, kinds, vmem=(0,), relay=True, scratch=((value.shape, value.dtype), one, one))


def finish(place, at, sliced, tiny, mix, taps):
    shard, D = mix.shape
    shapes = [shape for _, _, _, outs in sliced for shape in outs]
    tiny_shapes = [(1, shard)] * 4 + [(taps, shard), (2, HD)]
    arrays = [x for own, came, _, _ in sliced for x in (own, came) if x is not None] + [tiny, mix]
    where = at.p.astype(jnp.int32).reshape(1)

    def body(where_ref, *refs):
        ins, outs = refs[: len(arrays)], refs[len(arrays) :]

        ins = list(ins)
        first = 0
        for own, _, parts, made in sliced:
            mine = None if own is None else ins.pop(0)
            came = ins.pop(0)
            for k in range(TP):
                piece = came[k]
                if mine is not None:
                    piece = jnp.where(where_ref[0] == k, mine[k], piece)
                piece = piece.astype(F32)
                for start, width, out, base in parts:
                    there = slice(base + k * width, base + (k + 1) * width)
                    outs[first + out][:, there] = piece[:, start : start + width]
            first += len(made)
        total = ins[0][0]
        for k in range(1, TP):
            total = total + ins[0][k]
        for k in range(4):
            outs[first + k][...] = total[k : k + 1, :shard]
        outs[first + 4][...] = total[4 : 4 + taps, :shard]
        row = total[4 + taps : 5 + taps, :]
        outs[first + 5][0:1, :] = row[:, :HD]
        outs[first + 5][1:2, :] = row[:, HD:]
        outs[first + 6][...] = ins[1][...].astype(F32)

    outs = [like(shape, F32) for shape in shapes + tiny_shapes + [(shard, D)]]
    return plain_call(body, tuple(outs), (), where, *arrays, smem=1)


def swap_core(value):
    def run(at, copies, ins, outs):
        slots = [copies.slot() for _ in range(at.R - 1)]
        for j in range(1, at.R):
            other = lax.rem(at.r + j, at.R)
            copies.push(ins[0].at[other], outs[0].at[at.r], slots[j - 1], (other, at.s))
        yield "go"
        for j in range(1, at.R):
            origin = lax.rem(at.r + at.R - j, at.R)
            copies.arrived(outs[0].at[origin], slots[j - 1], (at.r, at.s))

    return Job([value], [like(value.shape, value.dtype)], run, {"core"})


def window_forward(place, value):
    reach = place.Q // 2

    def run(at, copies, ins, outs):
        slots = [copies.slot() for _ in range(reach)]
        there = (at.r, at.s + TP)
        copies.push(ins[0], outs[0].at[reach - 1], slots[0], there, at.q + 1 < at.Q)
        copies.local(ins[0], outs[0].at[reach])
        for j in range(1, reach + 1):
            yield "go"
            came = outs[0].at[reach - j]
            copies.arrived(came, slots[j - 1], (at.r, at.s), at.q >= j)
            if j < reach:
                passes = (at.q >= j) & (at.q + 1 < at.Q)
                copies.push(came, outs[0].at[reach - j - 1], slots[j], there, passes)

    shape = (reach + 1,) + value.shape
    outs = [like(shape, value.dtype)]
    return Job([value], outs, run, {"chain"}, vmem=(0,), relay=True)


def window_backward(place, value):
    reach = place.Q // 2

    def run(at, copies, ins, outs):
        got, summed = outs[1:]
        slots = [copies.slot() for _ in range(reach)]
        there = (at.r, at.s - TP)
        for j in range(reach, 0, -1):
            step = reach - j
            source = ins[0].at[step]
            if step > 0:
                came = (at.q + 1 < at.Q) & (at.q >= j)
                copies.arrived(got.at[step - 1], slots[step - 1], (at.r, at.s), came)
                total = jnp.where(came, got[step - 1].astype(F32), 0.0)
                summed[step - 1] = (total + ins[0][step].astype(F32)).astype(value.dtype)
                source = summed.at[step - 1]
            target = got.at[step] if j > 1 else outs[0]
            copies.push(source, target, slots[step], there, at.q >= j)
            yield "go"
        copies.arrived(outs[0], slots[reach - 1], (at.r, at.s), at.q + 1 < at.Q)

    piece = value.shape[1:]
    held = ((max(reach - 1, 1),) + piece, value.dtype)
    outs = [like(piece, value.dtype)]
    return Job([value], outs, run, {"chain"}, vmem=(0,), relay=True, scratch=(held, held))


def halo_tokens(value):
    rows = value.shape[0]

    def run(at, copies, ins, outs):
        ahead = [copies.slot() for _ in range(TP)]
        back = [copies.slot() for _ in range(TP)]
        first = (at.p == 0) & (at.q > 0)
        last = (at.p == TP - 1) & (at.q < at.Q - 1)
        for j in range(TP):
            tail = ins[0].at[pl.ds(rows - HALO, HALO)]
            there = (at.r, (at.q + 1) * TP + j)
            copies.push(tail, outs[0], ahead[j], there, last, ahead[0])
            head = ins[0].at[pl.ds(0, HALO)]
            there = (at.r, (at.q - 1) * TP + j)
            copies.push(head, outs[1], back[j], there, first, back[0])
        yield "go"
        copies.arrived(outs[0], ahead[0], (at.r, at.s), at.q > 0)
        copies.arrived(outs[1], back[0], (at.r, at.s), at.q < at.Q - 1)

    shape = (HALO,) + value.shape[1:]
    outs = [like(shape, value.dtype), like(shape, value.dtype)]
    return Job([value], outs, run, {"halo"}, vmem=(0,))


def side_by_side(*weights):
    layout, there = [], 0
    for index, weight in enumerate(weights):
        width = weight.shape[1] // TP
        layout.append((index, 0, width, width, there))
        there += width
    return layout


def spread_run(at, copies, sources, held, first, layout):
    def cut(index, start, stride, width, member):
        if stride == 0:
            return sources[index]
        return sources[index].at[:, pl.ds(pl.multiple_of(start + member * stride, 128), width)]

    def place_of(member, width, there):
        return held.at[first + member, :, pl.ds(there, width)]

    slots = [[copies.slot() for _ in layout] for _ in range(TP - 1)]
    for j in range(1, TP):
        other = lax.rem(at.p + j, TP)
        for k, (index, start, stride, width, there) in enumerate(layout):
            copies.push(
                cut(index, start, stride, width, other),
                place_of(at.p, width, there),
                slots[j - 1][k],
                (at.r, at.q * TP + other),
            )
    own = []
    for index, start, stride, width, there in layout:
        piece = cut(index, start, stride, width, at.p)
        sem = copies.recv.at[copies.slot()]
        own.append(pltpu.make_async_copy(piece, place_of(at.p, width, there), sem))
        own[-1].start()
    yield "go"
    for copy in own:
        copy.wait()
    for j in range(1, TP):
        origin = lax.rem(at.p + TP - j, TP)
        for k, (_, _, _, width, there) in enumerate(layout):
            copies.arrived(place_of(origin, width, there), slots[j - 1][k], (at.r, at.s))


def chain_run(at, copies, held, unit=TP):
    def block(r, q):
        return held.at[pl.ds(pl.multiple_of((r * at.Q + q) * unit, unit), unit)]

    right = [copies.slot() for _ in range(at.Q - 1)]
    left = [copies.slot() for _ in range(at.Q - 1)]
    across = [[copies.slot() for _ in range(at.Q)] for _ in range(at.R - 1)]

    def cross(q, index, cond):
        for j in range(1, at.R):
            other = lax.rem(at.r + j, at.R)
            copies.push(block(at.r, q), block(at.r, q), across[j - 1][index], (other, at.s), cond)

    copies.push(
        block(at.r, at.q), block(at.r, at.q), right[0], (at.r, at.s + TP), at.q < at.Q - 1
    )
    copies.push(block(at.r, at.q), block(at.r, at.q), left[0], (at.r, at.s - TP), at.q > 0)
    cross(at.q, 0, None)
    index = 0
    spots = {}
    for hop in range(1, at.Q):
        yield "go"
        from_left, from_right = at.q >= hop, at.q + hop < at.Q
        copies.arrived(block(at.r, at.q - hop), right[hop - 1], (at.r, at.s), from_left)
        if hop < at.Q - 1:
            copies.push(
                block(at.r, at.q - hop),
                block(at.r, at.q - hop),
                right[hop],
                (at.r, at.s + TP),
                from_left & (at.q < at.Q - 1),
            )
        copies.arrived(block(at.r, at.q + hop), left[hop - 1], (at.r, at.s), from_right)
        if hop < at.Q - 1:
            copies.push(
                block(at.r, at.q + hop),
                block(at.r, at.q + hop),
                left[hop],
                (at.r, at.s - TP),
                from_right & (at.q > 0),
            )
        for side, sign in ((from_left, -1), (from_right, 1)):
            spots[(hop, sign)] = [copies.slot() for _ in range(at.R - 1)]
            for j in range(1, at.R):
                other = lax.rem(at.r + j, at.R)
                piece = block(at.r, at.q + sign * hop)
                copies.push(piece, piece, spots[(hop, sign)][j - 1], (other, at.s), side)
    yield "go"
    for j in range(1, at.R):
        source = lax.rem(at.r + at.R - j, at.R)
        copies.arrived(block(source, at.q), across[j - 1][0], (at.r, at.s))
        for hop in range(1, at.Q):
            for sign in (-1, 1):
                there = at.q + sign * hop
                copies.arrived(
                    block(source, there),
                    spots[(hop, sign)][j - 1],
                    (at.r, at.s),
                    at.q >= hop if sign < 0 else there < at.Q,
                )


def spread(*sources):
    layout = side_by_side(*sources)

    def run(at, copies, ins, outs):
        yield from spread_run(at, copies, ins, outs[0], 0, layout)

    shape = (TP, sources[0].shape[0], sum(part[3] for part in layout))
    outs = [like(shape, sources[0].dtype)]
    return Job(sources, outs, run, {"plane"}, vmem=tuple(range(len(sources))), late=True)


def spread_all(place, source, layout):
    def run(at, copies, ins, outs):
        yield from spread_run(at, copies, ins, outs[0], (at.r * at.Q + at.q) * TP, layout)
        yield from chain_run(at, copies, outs[0])

    shape = (place.R * place.S, source.shape[0], sum(part[3] for part in layout))
    outs = [like(shape, source.dtype)]
    return Job([source], outs, run, {"plane", "chain", "core"}, vmem=(0,), relay=True)


def home_all(place, source):
    def run(at, copies, ins, outs):
        r, s, slot, here = home_of(at)
        _, _, own = visitor_of(at)
        index = copies.slot()
        copies.push(ins[0], outs[0].at[slot], index, (r, s), here == 0)
        copy = pltpu.make_async_copy(ins[0], outs[0].at[slot], copies.recv.at[copies.slot()])
        when(here == 1, copy.start)
        yield "go"
        when(here == 1, copy.wait)
        copies.arrived(outs[0].at[at.r * at.Q + at.q], index, (at.r, at.s), own == 0)
        yield from chain_run(at, copies, outs[0], 1)

    outs = [like((place.R * place.Q,) + source.shape, source.dtype)]
    return Job([source], outs, run, {"home", "chain", "core"}, vmem=(0,), relay=True)


FACTOR = 1.0 / math.sqrt(HD)


def masked_keys(kv_ref, first, kv_s):
    index = lax.broadcasted_iota(jnp.int32, kv_ref.shape, 0)
    kv_s[...] = jnp.where(index >= first, kv_ref[...].astype(F32), 0.0).astype(BF)


def attend_forward(q, kv, q_seg, key_seg, first, block):
    N, QS = q.shape
    M, KS = kv.shape[0], kv.shape[1] // 2
    ahead = M - N
    span = ahead + block
    kv_heads = KS // HD
    groups = QS // KS

    def body(first_ref, q_ref, kv_ref, qs_ref, ks_ref, o_ref, kv_s):
        masked_keys(kv_ref, first_ref[0], kv_s)

        @pl.loop(0, N // block)
        def _(i):
            start = pl.multiple_of(i * block, block)
            here, keys = pl.ds(start, block), pl.ds(start, span)
            row = lax.broadcasted_iota(jnp.int32, (block, span), 0) + ahead
            col = lax.broadcasted_iota(jnp.int32, (block, span), 1)
            open_ = (qs_ref[here, :1] == ks_ref[:1, keys]) & (col <= row)
            open_ = open_ & (col + start >= first_ref[0])
            open_ = jnp.concatenate([open_] * groups, axis=0)
            queries = q_ref[here, :]
            done = []
            for k in range(kv_heads):
                mine = [
                    queries[:, (k * groups + g) * HD : (k * groups + g + 1) * HD]
                    for g in range(groups)
                ]
                key = kv_s[keys, k * HD : (k + 1) * HD]
                value = kv_s[keys, KS + k * HD : KS + (k + 1) * HD]
                score = jnp.where(open_, dot_nt(jnp.concatenate(mine, axis=0), key) * FACTOR, MASKED)
                weight = jnp.exp(score - jnp.max(score, axis=-1, keepdims=True))
                weight = weight / jnp.sum(weight, axis=-1, keepdims=True)
                out = dot(weight.astype(BF), value).astype(BF)
                done.extend(out[g * block : (g + 1) * block] for g in range(groups))
            o_ref[here, :] = jnp.concatenate(done, axis=1)

    return attend_call(
        body, like((N, QS)), [pltpu.VMEM(kv.shape, BF)], 4 * N * span * QS, first, q, kv, q_seg, key_seg
    )


def attend_call(body, outs, scratch, flops, first, *arrays):
    return pl.pallas_call(
        body,
        out_shape=outs,
        in_specs=[pl.BlockSpec(memory_space=pltpu.SMEM)]
        + [pl.BlockSpec(memory_space=pltpu.VMEM) for _ in arrays],
        out_specs=jax.tree.map(lambda _: pl.BlockSpec(memory_space=pltpu.VMEM), outs),
        scratch_shapes=scratch,
        cost_estimate=pl.CostEstimate(flops=flops, bytes_accessed=COST, transcendentals=0),
    )(first, *arrays)


def attend_backward(q, kv, d_o, q_seg, key_seg, first, block):
    N, QS = q.shape
    M, KS = kv.shape[0], kv.shape[1] // 2
    ahead = M - N
    span = ahead + block
    kv_heads = KS // HD
    groups = QS // KS

    def body(first_ref, q_ref, kv_ref, do_ref, qs_ref, ks_ref, dq_ref, dkv_ref, kv_s, *sums):
        masked_keys(kv_ref, first_ref[0], kv_s)
        for total in sums:
            total[...] = jnp.zeros_like(total)

        @pl.loop(0, N // block)
        def _(i):
            start = pl.multiple_of(i * block, block)
            here, keys = pl.ds(start, block), pl.ds(start, span)
            row = lax.broadcasted_iota(jnp.int32, (span, block), 0)
            col = lax.broadcasted_iota(jnp.int32, (span, block), 1) + ahead
            open_ = (ks_ref[keys, :1] == qs_ref[:1, here]) & (row <= col)
            open_ = open_ & (row + start >= first_ref[0])
            open_ = jnp.concatenate([open_] * groups, axis=1)
            queries, pulls = q_ref[here, :], do_ref[here, :]

            def heads_of(values, k):
                return jnp.concatenate(
                    [
                        values[:, (k * groups + g) * HD : (k * groups + g + 1) * HD]
                        for g in range(groups)
                    ],
                    axis=0,
                )

            done = []
            for k in range(kv_heads):
                mine, pull = heads_of(queries, k), heads_of(pulls, k)
                key = kv_s[keys, k * HD : (k + 1) * HD]
                value = kv_s[keys, KS + k * HD : KS + (k + 1) * HD]
                score = jnp.where(open_, dot_nt(key, mine) * FACTOR, MASKED)
                weight = jnp.exp(score - jnp.max(score, axis=0, keepdims=True))
                weight = weight / jnp.sum(weight, axis=0, keepdims=True)
                d_weight = dot_nt(value, pull)
                delta = jnp.sum(weight * d_weight, axis=0, keepdims=True)
                d_score = (weight * (d_weight - delta)).astype(BF)
                sums[k][keys, :] += dot(d_score, mine) * FACTOR
                sums[kv_heads + k][keys, :] += dot(weight.astype(BF), pull)
                dq = dot_tn(d_score, key) * FACTOR
                done.extend(dq[g * block : (g + 1) * block] for g in range(groups))
            dq_ref[here, :] = jnp.concatenate(done, axis=1)

        dkv_ref[...] = jnp.concatenate([total[...] for total in sums], axis=1)

    return attend_call(
        body,
        (like((N, QS), F32), like((M, 2 * KS), F32)),
        [pltpu.VMEM(kv.shape, BF)] + [pltpu.VMEM((M, HD), F32) for _ in range(2 * kv_heads)],
        10 * N * span * QS,
        first,
        q,
        kv,
        d_o,
        q_seg,
        key_seg,
    )


def turned(values, cosine, sine):
    lane = lax.broadcasted_iota(jnp.int32, values.shape, 1)
    ahead = pltpu.roll(values, 2 * HD - HD // 2, 1)
    behind = pltpu.roll(values, HD // 2, 1)
    other = jnp.where(lax.rem(lane, HD) < HD // 2, ahead, behind)
    return values * cosine + other * sine


def head_means(values):
    lane = lax.broadcasted_iota(jnp.int32, values.shape, 1)
    front = lane < HD
    first = jnp.sum(jnp.where(front, values, 0.0), axis=-1, keepdims=True)
    second = jnp.sum(jnp.where(front, 0.0, values), axis=-1, keepdims=True)
    return jnp.where(front, first, second) * (1.0 / HD)


def pairs_of(width):
    return [slice(c, c + 2 * HD) for c in range(0, width, 2 * HD)]


def heads_forward(n3, w, gains, cosine, sine, QS, KS):
    N = n3.shape[0]

    def body(n3_ref, w_ref, gains_ref, cos_ref, sin_ref, pre_ref, q_ref, kv_ref):
        pre_ref[...] = dot(n3_ref[...], w_ref[:, : QS + 2 * KS])

        def normed(cols, row):
            values = pre_ref[:, cols]
            inverse = lax.rsqrt(head_means(values * values) + EPSILON)
            values = values * inverse * gains_ref[row : row + 1, :]
            return turned(values, cos_ref[...], sin_ref[...]).astype(BF)

        for cols in pairs_of(QS):
            q_ref[:, cols] = normed(cols, 0)
        for cols in pairs_of(KS):
            kv_ref[:, cols] = normed(slice(QS + cols.start, QS + cols.stop), 1)
        kv_ref[:, KS:] = pre_ref[:, QS + KS :].astype(BF)

    outs = (like((N, QS + 2 * KS), F32), like((N, QS)), like((N, 2 * KS)))
    return plain_call(body, outs, (), n3, w, gains, cosine, sine)


def heads_backward(d_q, d_kv, got, count, pre, gains, cosine, sine, n3, g3, o, w):
    N, QS = d_q.shape
    KS = d_kv.shape[1] // 2
    D = n3.shape[1]
    W = QS + 2 * KS
    step = 256

    def body(
        count_ref, dq_ref, dkv_ref, got_ref, pre_ref, gains_ref, cos_ref, sin_ref, n3_ref, g3_ref,
        o_ref, w_ref, part_ref, rows_ref, heads_ref, all_ref,
    ):
        later = jnp.where(count_ref[0] > 0, got_ref[...].astype(F32), 0.0)
        d_kv_sum = dkv_ref[...] + later
        all_ref[:, QS + KS :] = d_kv_sum[:, KS:].astype(BF)

        def back(pull, cols, row):
            values = pre_ref[:, cols]
            inverse = lax.rsqrt(head_means(values * values) + EPSILON)
            pull = turned(pull, cos_ref[...], -sin_ref[...])
            scaled = pull * gains_ref[row : row + 1, :]
            mean = head_means(scaled * values)
            d_values = inverse * scaled - values * (inverse * inverse * inverse) * mean
            all_ref[:, cols] = d_values.astype(BF)
            return jnp.sum(pull * values * inverse, axis=0, keepdims=True)

        of_queries = [back(dq_ref[:, cols], cols, 0) for cols in pairs_of(QS)]
        of_keys = [
            back(d_kv_sum[:, cols], slice(QS + cols.start, QS + cols.stop), 1)
            for cols in pairs_of(KS)
        ]
        heads_ref[0:1, :] = sum(of_queries[1:], of_queries[0])
        heads_ref[1:2, :] = sum(of_keys[1:], of_keys[0])
        values, outputs = all_ref[...], o_ref[...]

        @pl.loop(0, D // step)
        def _(c):
            cols = pl.ds(pl.multiple_of(c * step, step), step)
            part_ref[:, cols] = dot_nt(values, w_ref[cols, :W])
            left = n3_ref[:, cols].astype(F32).T.astype(BF)
            rows_ref[cols, :W] = dot(left, values).astype(BF)
            right = g3_ref[:, cols].astype(F32).T.astype(BF)
            rows_ref[cols, W:] = dot(right, outputs).astype(BF)

    outs = (like((N, D), F32), like((D, W + QS)), like((2, 2 * HD), F32))
    return plain_call(
        body, outs, [pltpu.VMEM((N, W), BF)],
        count, d_q, d_kv, got, pre, gains, cosine, sine, n3, g3, o, w, smem=1,
    )


def plain_call(body, outs, scratch, *arrays, smem=0):
    return pl.pallas_call(
        body,
        out_shape=outs,
        in_specs=[
            pl.BlockSpec(memory_space=pltpu.SMEM if k < smem else pltpu.VMEM)
            for k in range(len(arrays))
        ],
        out_specs=tuple(pl.BlockSpec(memory_space=pltpu.VMEM) for _ in outs),
        scratch_shapes=scratch,
        cost_estimate=pl.CostEstimate(flops=0, bytes_accessed=COST, transcendentals=0),
    )(*arrays)


class Plane:
    def __init__(self, at, copies):
        self.at, self.copies = at, copies

    def gather(self, held):
        at, slots = self.at, [self.copies.slot() for _ in range(TP - 1)]
        for j in range(1, TP):
            there = (at.r, at.q * TP + lax.rem(at.p + j, TP))
            self.copies.push(held.at[at.p], held.at[at.p], slots[j - 1], there)
        return functools.partial(self.arrive, held, slots)

    def mate(self, k):
        p = self.at.p
        if k == 1:
            return p + 1 - 2 * lax.rem(p, 2)
        if k == 2:
            return p + 2 - 4 * (p // 2)
        return TP - 1 - p if k == TP - 1 else p

    def to_mate(self, source, held, k):
        at, slot = self.at, self.copies.slot()
        there = (at.r, at.q * TP + self.mate(k))
        self.copies.push(source, held.at[k], slot, there)
        return functools.partial(self.copies.arrived, held.at[k], slot, (at.r, at.s))

    def spread_mates(self, held):
        return [self.to_mate(held.at[0], held, k) for k in range(1, TP)]

    def sum_mates(self, own, recv):
        for k in range(1, TP):
            own = own + recv[k].astype(F32)
        return own

    def arrive(self, held, slots):
        at = self.at
        for j in range(1, TP):
            origin = lax.rem(at.p + TP - j, TP)
            self.copies.arrived(held.at[origin], slots[j - 1], (at.r, at.s))


def columns_of(count, width, action):
    @pl.loop(0, count)
    def _(c):
        action(pl.ds(pl.multiple_of(c * width, width), width))


def rows_of(span, action):
    first, count = span

    @pl.loop(0, count // 64)
    def _(i):
        action(pl.ds(pl.multiple_of(first + i * 64, 64), 64))


def activate(gu, act, span, FS):
    def go(rows):
        gate, up = gu[rows, :FS], gu[rows, FS:]
        act[rows, :] = (jax.nn.silu(gate) * up).astype(BF)

    rows_of(span, go)


def deactivate(gu, d_act, dgu, span, FS):
    def go(rows):
        gate, up, pull = gu[rows, :FS], gu[rows, FS:], d_act[rows, :]
        sigma = jax.nn.sigmoid(gate)
        dgu[rows, :FS] = (pull * up * sigma * (1.0 + gate * (1.0 - sigma))).astype(BF)
        dgu[rows, FS:] = (pull * (gate * sigma)).astype(BF)

    rows_of(span, go)


def multiply(held, weights, out, span, parts):
    first, count = span
    n, D = held.shape[1:]
    values = held[first // n : (first + count) // n].reshape(count, D)
    rows = pl.ds(first, count)

    def go(cols):
        out[rows, cols] = dot(values, weights[:, cols])

    columns_of(parts, weights.shape[1] // parts, go)


def project(left, weights, part, span, send=None, order=None):
    first, count = span
    step = 256
    rows = pl.ds(first, count)
    n = send.shape[1] if send is not None else count

    def go(cols):
        out = dot_nt(left[rows, :], weights[cols, :])
        part[rows, cols] = out
        if send is not None:
            for k in range(first // n, (first + count) // n):
                block = out[k * n - first : (k + 1) * n - first].astype(BF)
                send[k if order is None else order[k], :, cols] = block

    columns_of(weights.shape[0] // step, step, go)


def feed_kernel(place, ident, mode, arrays, D, FS, n, side=0):
    N = n * TP
    R = place.R
    half = D // R
    W = 2 * FS if mode == "both" else 3 * FS
    forward, backward = mode in ("fwd", "both"), mode in ("both", "bwd")
    VM, HB = pltpu.VMEM, pl.ANY
    ins, scratch, outs = {}, {}, {}
    ins["weights"] = HB
    if mode == "fwd":
        ins.update(a_g=HB, h_in=VM, gain_next=VM)
        scratch.update(a_v=((TP, n, D), BF))
        outs.update(
            h_out=((n, D), F32, VM), next_g=((TP, n, D), BF, VM), gu_out=((N, 2 * FS), F32, HB)
        )
    else:
        ins.update(first_part=VM, h_in=VM, gain=VM)
        outs.update(
            g_out=((n, D), F32, VM),
            next_g=((TP, n, D), BF, VM),
            d_gain=((1, D), F32, VM),
            half_out=((half, FS if mode == "both" else W), BF, VM),
        )
        scratch.update(
            first_send=((TP, n, D), BF),
            first_got=((TP, n, D), BF),
            a_v=((TP, n, D), BF),
            e_v=((TP, n, D), BF),
            d_act=((N, FS), F32),
            dgu=((N, 2 * FS), BF),
            grad_send=((R - 1, half, W), BF),
            grad_got=((R - 1, half, W), BF),
        )
    if mode == "both":
        ins.update(e_g=HB, e_own=VM, down=HB)
        down_piece = (half // place.Q, FS)
        outs.update(
            mid_out=((n, D), F32, VM),
            o_send=((TP, n, D), BF, VM),
            o_base=((n, D), F32, VM),
            down_out=((place.Q,) + down_piece, BF, VM),
            half_up=((half, FS), BF, VM),
        )
        scratch.update(
            down_send=((R - 1, half, FS), BF),
            down_got=((R - 1, half, FS), BF),
            down_half=((place.Q,) + down_piece, BF),
        )
    if mode == "bwd":
        ins.update(a_g=HB, gu_in=HB, g_in=VM, h_before=VM, gain_before=VM)
        piece = (half // place.Q, side)
        ins.update(side_in=VM)
        outs.update(
            d_gain_before=((1, D), F32, VM),
            halo=((HALO, D), BF, VM),
            side_out=((place.Q,) + piece, BF, VM),
        )
        scratch.update(side_got=((R - 1, half, side), BF), side_half=((place.Q,) + piece, BF))
    scratch.update(
        w=((D, 2 * FS), BF),
        wd=((D, FS), BF),
        gu=((N, 2 * FS), F32),
        act=((N, FS), BF),
        part=((N, D), F32),
        send=((TP, n, D), BF),
        got=((TP, n, D), BF),
    )
    in_names, out_names, scratch_names = list(ins), list(outs), list(scratch)
    kinds = {"plane"}
    if backward:
        kinds.add("core")
    if mode == "bwd":
        kinds.update({"back", "zall"})
    if mode == "both":
        kinds.add("zall")
    unit = D // (R * place.Q)
    sems = 32 + 3 * R + 4 * place.Q + 3 * R * place.Q

    def body(*refs):
        names = in_names + out_names + scratch_names
        v = dict(zip(names, refs))
        at = place.here()
        copies = Copies(refs[len(names)], refs[len(names) + 1])
        plane = Plane(at, copies)
        loads = refs[len(names) + 2]
        pending = {}

        def load(name, src, dst):
            pending[name] = pltpu.make_async_copy(src, dst, loads.at[len(pending)])
            pending[name].start()

        def load_blocks(name, source, target):
            for k in range(TP):
                load(name + str(k), source.at[plane.mate(k)], target.at[k])

        def loaded(*names):
            for name in names:
                pending[name].wait()

        def loaded_blocks(name):
            loaded(*[name + str(k) for k in range(TP)])

        if mode == "both":
            load("w", v["weights"], v["w"])
            load_blocks("e", v["e_g"], v["e_v"])
            own_rows = pl.ds(pl.multiple_of((at.r * at.Q + at.q) * unit, unit), unit)
            load("wd", v["down"], v["wd"].at[own_rows])
        else:
            load("w", v["weights"].at[:, : 2 * FS], v["w"])
            load("wd", v["weights"].at[:, 2 * FS : 3 * FS], v["wd"])
        if mode == "bwd":
            for k in range(TP):
                rows = pl.ds(pl.multiple_of(plane.mate(k) * n, n), n)
                load("gu%d" % k, v["gu_in"].at[rows], v["gu"].at[pl.ds(k * n, n)])
        if mode != "both":
            load_blocks("a", v["a_g"], v["a_v"])
        meet(at, kinds)
        w, wd, gu, act = (v[k] for k in ("w", "wd", "gu", "act"))
        part, send, got = (v[k] for k in ("part", "send", "got"))

        def along_line(source, target):
            slots = [copies.slot() for _ in range(at.Q - 1)]
            for j in range(1, at.Q):
                other = lax.rem(at.q + j, at.Q)
                there = (at.r, other * TP + at.p)
                copies.push(source.at[other], target.at[at.q], slots[j - 1], there)
            target[at.q] = source[at.q]
            return slots

        def line_done(target, slots):
            for j in range(1, at.Q):
                origin = lax.rem(at.q + at.Q - j, at.Q)
                copies.arrived(target.at[origin], slots[j - 1], (at.r, at.s))

        def turned_rows(held, j):
            first_col = lax.rem(at.r + j, R) * half
            cols = pl.ds(pl.multiple_of(first_col, 128), half)
            return held[:, :, cols].reshape(N, half).astype(F32).T.astype(BF)

        def send_down():
            down_slots = [copies.slot() for _ in range(R - 1)]
            for j in range(1, R):
                v["down_send"][j - 1] = dot(turned_rows(v["e_v"], j), act[...]).astype(BF)
                there = (lax.rem(at.r + j, R), at.s)
                copies.push(v["down_send"].at[j - 1], v["down_got"].at[j - 1], down_slots[j - 1], there)
            total = dot(turned_rows(v["e_v"], 0), act[...])
            for j in range(1, R):
                copies.arrived(v["down_got"].at[j - 1], down_slots[j - 1], (at.r, at.s))
                total = total + v["down_got"][j - 1].astype(F32)
            v["down_half"][...] = total.astype(BF).reshape(v["down_half"].shape)
            return along_line(v["down_half"], v["down_out"])

        if mode != "fwd":
            first = v["first_part"]
            mine = [pl.ds(pl.multiple_of(plane.mate(k) * n, n), n) for k in range(TP)]
            waits = []
            for k in range(1, TP):
                v["first_send"][k] = first[mine[k], :].astype(BF)
                waits.append(plane.to_mate(v["first_send"].at[k], v["first_got"], k))
        everything, own, near, far = (0, N), (0, n), (n, 2 * n), (3 * n, n)
        if mode == "fwd":
            loaded("w", "wd")
            loaded_blocks("a")
            waits = []
            for span, slots in ((near, (1, 2)), (far, (3,)), (own, ())):
                multiply(v["a_v"], w, gu, span, 3)
                activate(gu, act, span, FS)
                project(act, wd, part, span, send if slots else None)
                waits.extend(plane.to_mate(send.at[k], got, k) for k in slots)
            for k in range(TP):
                rows = pl.ds(pl.multiple_of(plane.mate(k) * n, n), n)
                load("save%d" % k, gu.at[pl.ds(k * n, n)], v["gu_out"].at[rows])
            for wait in waits:
                wait()
            h_out = v["h_in"][...] + plane.sum_mates(part[:n, :], got)
            v["h_out"][...] = h_out
            v["next_g"][at.p] = (h_out * inverse_rms(h_out) * v["gain_next"][...]).astype(BF)
            wait = plane.gather(v["next_g"])
            wait()
            loaded_blocks("save")
            copies.drain()
            return
        d_act, dgu = v["d_act"], v["dgu"]
        if mode == "both":
            loaded("wd")
            steps = chain_run(at, copies, wd, unit)
            next(steps)
            next(steps)
            for wait in waits:
                wait()
            h = v["h_in"][...] + plane.sum_mates(first[mine[0], :], v["first_got"])
            v["mid_out"][...] = h
            v["a_v"][0] = (h * inverse_rms(h) * v["gain"][...]).astype(BF)
            waits = plane.spread_mates(v["a_v"])
            for _ in range(at.Q - 3):
                next(steps)
            loaded("w")
            loaded_blocks("e")
            for span, awaited in ((own, ()), (near, waits[:2]), (far, waits[2:])):
                for wait in awaited:
                    wait()
                multiply(v["a_v"], w, gu, span, 3)
                activate(gu, act, span, FS)
            for _ in steps:
                pass
            multiply(v["e_v"], wd, d_act, everything, 3)
            waits = []
            for span, slots in ((near, (1, 2)), (far, (3,))):
                deactivate(gu, d_act, dgu, span, FS)
                project(dgu, w, part, span, send)
                waits.extend(plane.to_mate(send.at[k], got, k) for k in slots)
                if span is near:
                    line_slots = send_down()
            deactivate(gu, d_act, dgu, own, FS)
            project(dgu, w, part, own)
        else:
            side_slots = [copies.slot() for _ in range(R - 1)]
            for j in range(1, R):
                other = lax.rem(at.r + j, R)
                copies.push(
                    v["side_in"].at[other], v["side_got"].at[j - 1], side_slots[j - 1], (other, at.s)
                )
            loaded_blocks("gu")
            activate(gu, act, everything, FS)
            for wait in waits:
                wait()
            h = v["h_in"][...]
            before = v["h_before"][...]
            r_before = inverse_rms(before)
            d_normed = plane.sum_mates(first[mine[0], :], v["first_got"])
            v["d_gain_before"][...] = jnp.sum(d_normed * before * r_before, axis=0, keepdims=True)
            g_mid = v["g_in"][...] + rms_pull(d_normed, before, r_before, v["gain_before"][...])
            v["g_out"][...] = g_mid
            v["e_v"][0] = g_mid.astype(BF)
            waits = plane.spread_mates(v["e_v"])
            loaded("w", "wd")
            loaded_blocks("a")
            total = v["side_in"][at.r].astype(F32)
            for j in range(1, R):
                copies.arrived(v["side_got"].at[j - 1], side_slots[j - 1], (at.r, at.s))
                total = total + v["side_got"][j - 1].astype(F32)
            v["side_half"][...] = total.astype(BF).reshape(v["side_half"].shape)
            line_slots = along_line(v["side_half"], v["side_out"])
            returns = []
            for span, awaited, slots in (
                (own, (), ()),
                (near, waits[:2], (1, 2)),
                (far, waits[2:], (3,)),
            ):
                for wait in awaited:
                    wait()
                multiply(v["e_v"], wd, d_act, span, 3)
                deactivate(gu, d_act, dgu, span, FS)
                project(dgu, w, part, span, send if slots else None)
                returns.extend(plane.to_mate(send.at[k], got, k) for k in slots)
            waits = returns
        values, pulls = v["a_v"], v["e_v"]

        slots = [copies.slot() for _ in range(R - 1)]
        for j in range(1, R):
            left = turned_rows(values, j)

            def put(cols, left=left, j=j):
                v["grad_send"][j - 1, :, cols] = dot(left, v["dgu"][:, cols]).astype(BF)

            columns_of(3, 2 * FS // 3, put)
            if mode == "bwd":
                v["grad_send"][j - 1, :, 2 * FS :] = dot(turned_rows(pulls, j), act[...]).astype(BF)
            other = lax.rem(at.r + j, R)
            copies.push(
                v["grad_send"].at[j - 1], v["grad_got"].at[j - 1], slots[j - 1], (other, at.s)
            )
        for wait in waits:
            wait()
        d_normed = plane.sum_mates(part[:n, :], got)
        r = inverse_rms(h)
        base = v["e_own"][...].astype(F32) if mode == "both" else v["g_out"][...]
        v["d_gain"][...] = jnp.sum(d_normed * h * r, axis=0, keepdims=True)
        g_new = base + rms_pull(d_normed, h, r, v["gain"][...])
        v["g_out"][...] = g_new
        v["next_g"][at.p] = g_new.astype(BF)
        wait = plane.gather(v["next_g"])
        if mode == "bwd":
            back = [copies.slot() for _ in range(TP)]
            for j in range(TP):
                copies.push(
                    v["next_g"].at[at.p, pl.ds(0, HALO)],
                    v["halo"],
                    back[j],
                    (at.r, (at.q - 1) * TP + j),
                    (at.p == 0) & (at.q > 0),
                    back[0],
                )
        if mode == "both":
            project(act, wd, part, everything, v["o_send"], [plane.mate(k) for k in range(TP)])
            v["o_base"][...] = h + part[:n, :]
        left = turned_rows(values, 0)
        for j in range(1, R):
            copies.arrived(v["grad_got"].at[j - 1], slots[j - 1], (at.r, at.s))

        def finish(target, base, shift):
            step = FS // 3

            @pl.loop(0, 3)
            def _(c):
                cols = pl.ds(pl.multiple_of(base + c * step, 128), step)
                total = dot(left, v["dgu"][:, cols])
                for j in range(1, R):
                    total = total + v["grad_got"][j - 1, :, cols].astype(F32)
                there = pl.ds(pl.multiple_of(base - shift + c * step, 128), step)
                target[:, there] = total.astype(BF)

        finish(v["half_out"], 0, 0)
        if mode == "both":
            finish(v["half_up"], FS, FS)
        else:
            finish(v["half_out"], FS, 0)
        if mode == "bwd":
            total = dot(turned_rows(pulls, 0), act[...])
            for j in range(1, R):
                total = total + v["grad_got"][j - 1, :, 2 * FS :].astype(F32)
            v["half_out"][:, 2 * FS :] = total.astype(BF)
        wait()
        if mode == "bwd":
            copies.arrived(v["halo"], back[0], (at.r, at.s), at.q < at.Q - 1)
            line_done(v["side_out"], line_slots)
        if mode == "both":
            line_done(v["down_out"], line_slots)
        copies.drain()

    results = pl.pallas_call(
        body,
        out_shape=tuple(like(outs[k][0], outs[k][1]) for k in out_names),
        in_specs=[pl.BlockSpec(memory_space=ins[k]) for k in in_names],
        out_specs=tuple(pl.BlockSpec(memory_space=outs[k][2]) for k in out_names),
        scratch_shapes=[pltpu.VMEM(*scratch[k]) for k in scratch_names]
        + [pltpu.SemaphoreType.DMA((sems,)), pltpu.SemaphoreType.DMA((sems,))]
        + [pltpu.SemaphoreType.DMA((12,))],
        compiler_params=pltpu.CompilerParams(collective_id=ident, has_side_effects=True),
        cost_estimate=pl.CostEstimate(flops=0, bytes_accessed=COST, transcendentals=0),
        name="feed_%s" % mode,
    )(*[arrays[k] for k in in_names])
    return dict(zip(out_names, results))


def doc_info(positions, lengths):
    doc_ends = jnp.cumsum(lengths, dtype=jnp.int32)
    passed = positions[:, None] >= doc_ends[None, :]
    segment = jnp.sum(passed.astype(jnp.int32), axis=1, dtype=jnp.int32)
    opening = jnp.sum(jnp.where(passed, lengths[None, :], 0), axis=1, dtype=jnp.int32)
    return (segment, positions - opening)


def inverse_rms(values):
    return lax.rsqrt(jnp.mean(values * values, axis=-1, keepdims=True) + EPSILON)


def rms_pull(upstream, values, inverse, norm_gain):
    scaled = upstream * norm_gain
    product_mean = jnp.mean(scaled * values, axis=-1, keepdims=True)
    return inverse * scaled - values * (inverse * inverse * inverse) * product_mean


def settle(own, arrived, p):
    index = jnp.arange(TP, dtype=jnp.int32)[:, None, None]
    others = jnp.where(index == p, 0.0, arrived.astype(F32))
    mine = lax.dynamic_index_in_dim(own, p, 0, keepdims=False)
    return mine + jnp.sum(others, axis=0)


def per_device(
    place,
    tokens,
    doc_lengths,
    cotangent,
    gain_conv,
    w_in,
    kernel,
    w_mix,
    gain_ffa,
    gate_a,
    up_a,
    down_a,
    gain_att,
    w_query,
    w_key,
    w_value,
    head_gains,
    w_attout,
    gain_ffb,
    gate_b,
    up_b,
    down_b,
):
    R, S, Q = place.R, place.S, place.Q
    n, D = tokens.shape[1], tokens.shape[2]
    shard = w_in.shape[0]
    FS = gate_a.shape[1] // TP
    CS = D // TP
    QS, KS = H * HD // TP, KVH * HD // TP
    taps = kernel.shape[0]
    N = n * TP
    r, s = lax.axis_index("rows"), lax.axis_index("seq")
    q, p = s // TP, lax.rem(s, TP)
    lengths = doc_lengths[0]

    columns = [[a * S + b * TP + c for a in range(R) for b in range(Q)] for c in range(TP)]
    lines = [[b * TP + c for b in range(Q)] for c in range(TP)]

    def gather_rest(plane):
        flat = plane.reshape(TP * shard, -1)
        return lax.all_gather(
            flat, ("rows", "seq"), axis=0, tiled=True, axis_index_groups=columns
        )

    def by_row(grads):
        return grads.astype(BF).reshape(R, S * shard, -1)

    def own_rows(rows, came, *later):
        return lax.optimization_barrier((collect(rows, came, r).astype(BF),) + later)

    def reduce_line(half):
        part = lax.psum_scatter(
            half, "seq", scatter_dimension=0, tiled=True, axis_index_groups=lines
        )
        return part.reshape(TP, shard, part.shape[1])

    in_layout = [(0, k * D, CS, CS, k * CS) for k in range(3)]
    small = jnp.stack([gain_conv, gain_ffa, gain_att, gain_ffb] + [kernel[i] for i in range(taps)])
    small = jnp.pad(small, ((0, 16 - 4 - taps), (0, 128 - shard)))

    mine = tokens[0]
    (tok_g,), (halo_a, halo_b), (in_g,), (mix_g,), (small_g,), (ffa_p,) = exchange(
        place,
        0,
        [
            gather_plane(mine),
            halo_tokens(mine),
            spread_all(place, w_in, in_layout),
            home_all(place, w_mix),
            spread_all(place, small, [(0, 0, 0, 128, 0)]),
            spread(gate_a, up_a, down_a.T, w_query, w_key, w_value, w_attout.T),
        ],
    )
    wide = gather_rest(ffa_p)
    w_att = wide[:, 3 * FS :]
    w_mix_s = mix_g.reshape(CS, D)
    vectors = small_g[:, : 4 + taps, :shard].transpose(1, 0, 2).reshape(4 + taps, D).astype(F32)
    g_conv, g_ffa, g_att, g_ffb = (vectors[i] for i in range(4))
    kernel_f = lax.dynamic_slice_in_dim(vectors[4:], p * CS, CS, 1)
    w_in_s = in_g.reshape(D, 3 * CS)

    def own(parts, index):
        return lax.dynamic_index_in_dim(parts, index, 0, keepdims=False).astype(F32)

    def collect(parts, came, index):
        slot = jnp.arange(came.shape[0], dtype=jnp.int32).reshape((-1,) + (1,) * (came.ndim - 1))
        mine_part = lax.dynamic_index_in_dim(parts, index, 0, keepdims=True).astype(F32)
        return jnp.sum(jnp.where(slot == index, mine_part, came.astype(F32)), axis=0)

    def after_core(parts, came):
        summed = collect(parts, came, r)
        return summed.reshape((Q, TP) + summed.shape[1:])

    total = S * n
    pos_ext = q * N - HALO + jnp.arange(N + 2 * HALO, dtype=jnp.int32)
    seg_ext, rel_ext = doc_info(pos_ext, lengths)
    valid = ((pos_ext >= 0) & (pos_ext < total))[:, None]
    x_ext = jnp.concatenate([halo_a, tok_g.reshape(N, D), halo_b], axis=0)
    x_ext = jnp.where(valid, x_ext, jnp.zeros_like(x_ext)).astype(F32)
    r0_ext = inverse_rms(x_ext)
    n1_ext = (x_ext * r0_ext * g_conv).astype(BF)
    z_ext = dot(n1_ext, w_in_s)
    b_ext, c_ext, v_ext = z_ext[:, :CS], z_ext[:, CS : 2 * CS], z_ext[:, 2 * CS :]
    u_ext = lax.optimization_barrier((b_ext * v_ext).astype(BF)).astype(F32)
    span = slice(HALO, HALO + N)
    same = [
        (seg_ext[HALO - 2 + k : HALO - 2 + k + N] == seg_ext[span]).astype(F32)[:, None]
        for k in range(taps)
    ]
    near = [u_ext[HALO - 2 + k : HALO - 2 + k + N] for k in range(taps)]
    conv = kernel_f[0] * near[0] * same[0]
    for k in range(1, taps):
        conv = conv + kernel_f[k] * near[k] * same[k]
    m_bf = (c_ext[span] * conv).astype(BF)
    part = dot(m_bf, w_mix_s).reshape(TP, n, D)
    (got,), (ffb_p,), (down_p,) = exchange(
        place,
        1,
        [
            swap_plane(part.astype(BF)),
            spread(gate_b, up_b),
            spread(down_b.T),
        ],
    )
    wb = gather_rest(ffb_p)
    x0 = mine.astype(F32)
    h1 = x0 + settle(part, got, p)

    r1 = inverse_rms(h1)
    a1 = (h1 * r1 * g_ffa).astype(BF)
    ((a1_g,),) = exchange(place, 2, [gather_plane(a1)])
    a1_g = a1_g.reshape(N, D)

    g_row = {name: value[None] for name, value in
             (("ffa", g_ffa), ("att", g_att), ("ffb", g_ffb))}
    fed = feed_kernel(
        place,
        3,
        "fwd",
        {"weights": wide, "a_g": a1_g.reshape(TP, n, D), "h_in": h1, "gain_next": g_row["att"]},
        D,
        FS,
        n,
    )
    h2, n3_g, gu1 = fed["h_out"], fed["next_g"], fed["gu_out"]

    n3_g = n3_g.reshape(N, D)
    w_out = w_att[:, QS + 2 * KS :]
    lane = jnp.arange(2 * HD, dtype=jnp.int32)
    frequency = jnp.exp(jnp.arange(HD // 2, dtype=F32) * (-2.0 * math.log(THETA) / HD))
    angles = rel_ext[span].astype(F32)[:, None] * jnp.tile(frequency, 4)[None, :]
    cosine = jnp.cos(angles)
    sine = jnp.sin(angles) * jnp.where(lane % HD < HD // 2, -1.0, 1.0)
    head_rows = jnp.tile(head_gains.astype(F32), (1, 2))
    pre, q_bf, kv_bf = heads_forward(n3_g, w_att, head_rows, cosine, sine, QS, KS)
    e_bf = cotangent[0]
    (kv_w,), (e_g,) = exchange(
        place,
        5,
        [window_forward(place, kv_bf), gather_plane(e_bf)],
    )
    reach = Q // 2 + 1
    kv_all = kv_w.reshape(reach * N, 2 * KS)
    q_seg = seg_ext[span]
    key_seg, _ = doc_info((q - reach + 1) * N + jnp.arange(reach * N, dtype=jnp.int32), lengths)
    first = jnp.maximum((reach - 1 - q) * N, 0).astype(jnp.int32).reshape(1)
    seg_col, seg_row = (jnp.broadcast_to(q_seg[:, None], (N, 128)), jnp.broadcast_to(q_seg, (8, N)))
    key_col = jnp.broadcast_to(key_seg[:, None], (reach * N, 128))
    key_row = jnp.broadcast_to(key_seg, (8, reach * N))
    o_bf = attend_forward(q_bf, kv_all, seg_col, key_row, first, 128)
    fed = feed_kernel(
        place,
        8,
        "both",
        {
            "weights": wb,
            "down": down_p.reshape(TP * shard, FS),
            "first_part": dot_nt(o_bf, w_out),
            "h_in": h2,
            "gain": g_row["ffb"],
            "e_g": e_g.reshape(TP, n, D),
            "e_own": e_bf,
        },
        D,
        FS,
        n,
    )
    full_down = jnp.sum(fed["down_out"].astype(F32), axis=0).astype(BF).reshape(TP, shard, FS)
    h3, g3, g3_g, half_b = fed["mid_out"], fed["g_out"], fed["next_g"], fed["half_out"]
    d_gain = {}
    d_gain["ffb"] = fed["d_gain"][0]

    g3_g = g3_g.reshape(N, D)
    d_o = dot(g3_g, w_out).astype(BF)
    d_q, d_kv = attend_backward(q_bf, kv_all, d_o, seg_row, key_col, first, 128)
    d_kv = d_kv.reshape(reach, N, 2 * KS)
    (got_kv,), (got_o,) = exchange(
        place, 10, [window_backward(place, d_kv.astype(BF)), swap_plane(fed["o_send"])]
    )
    index = jnp.arange(TP, dtype=jnp.int32)[:, None, None]
    h4 = fed["o_base"] + jnp.sum(jnp.where(index == p, 0.0, got_o.astype(F32)), axis=0)
    mixed = h4.astype(BF)[None]
    count = (q + 1 < Q).astype(jnp.int32).reshape(1)
    half_up, got_kv = lax.optimization_barrier((fed["half_up"], got_kv))
    full_gate, full_up = reduce_line(half_b), reduce_line(half_up)
    part, rows_att, d_heads = heads_backward(
        d_q, d_kv[-1], got_kv, count, pre, head_rows, cosine, sine, n3_g, g3_g, o_bf, w_att
    )
    d_heads = jnp.sum(d_heads.reshape(2, 2, HD), axis=1)
    rows_att = by_row(rows_att)
    part, full_gate = lax.optimization_barrier((part, full_gate))
    fed = feed_kernel(
        place,
        13,
        "bwd",
        {
            "weights": wide,
            "first_part": part,
            "h_in": h1,
            "gain": g_row["ffa"],
            "a_g": a1_g.reshape(TP, n, D),
            "gu_in": gu1,
            "g_in": g3,
            "h_before": h2,
            "gain_before": g_row["att"],
            "side_in": rows_att,
        },
        D,
        FS,
        n,
        rows_att.shape[2],
    )
    full_att = jnp.sum(fed["side_out"].astype(F32), axis=0).astype(BF).reshape(TP, shard, -1)
    g1, g1_g, g1_halo = fed["g_out"], fed["next_g"], fed["halo"]
    d_gain["att"], d_gain["ffa"] = fed["d_gain_before"][0], fed["d_gain"][0]
    full_a = reduce_line(fed["half_out"])

    g1_halo = jnp.where(q < Q - 1, g1_halo, jnp.zeros_like(g1_halo))
    g1_ext = jnp.concatenate([g1_g.reshape(N, D), g1_halo], axis=0)
    d_m = dot_nt(g1_ext, w_mix_s)
    d_mix_s = dot_tn(m_bf, g1_ext[:N])
    d_c = d_m[:N] * conv
    d_conv = lax.optimization_barrier((d_m * c_ext[HALO:]).astype(BF)).astype(F32)
    d_kernel = jnp.stack(
        [jnp.sum(d_conv[:N] * near[k] * same[k], axis=0) for k in range(taps)]
    )
    d_u = jnp.zeros((N, CS), F32)
    for k in range(taps):
        ahead = taps - 1 - k
        match = (seg_ext[HALO + ahead : HALO + ahead + N] == seg_ext[span]).astype(F32)[:, None]
        d_u = d_u + kernel_f[k] * d_conv[ahead : ahead + N] * match
    d_z = jnp.concatenate([d_u * v_ext[span], d_c, d_u * b_ext[span]], axis=1).astype(BF)
    rows_in = dot_tn(n1_ext[span], d_z).astype(BF).reshape(R, S, shard, 3 * CS)
    rows_mix = d_mix_s.astype(BF).reshape(R, Q, shard, D)
    d_n1 = dot_nt(d_z, w_in_s)
    d_gain["conv"] = jnp.sum(d_n1 * x_ext[span] * r0_ext[span], axis=0)
    part = d_n1.reshape(TP, n, D)
    d_taps = lax.dynamic_update_slice(jnp.zeros((taps, D), F32), d_kernel, (0, p * CS))
    lanes = jnp.concatenate(
        [jnp.stack([d_gain["conv"], d_gain["ffa"], d_gain["att"], d_gain["ffb"]]), d_taps]
    )
    lanes = lanes.reshape(4 + taps, R * S, shard).transpose(1, 0, 2)
    lanes = jnp.pad(lanes, ((0, 0), (0, 0), (0, 128 - shard)))
    heads_row = jnp.broadcast_to(d_heads.reshape(1, 1, 2 * HD), (R * S, 1, 2 * HD))
    tiny = jnp.concatenate([lanes, heads_row], axis=1)
    tiny_rows = tiny.reshape(R, S, 4 + taps + 1, 128)
    (got,), (core_in,), (core_mix,), (core_t,), *plane_b, (plane_att,) = exchange(
        place,
        15,
        [
            swap_plane(part.astype(BF)),
            swap_core(rows_in),
            swap_core(rows_mix),
            swap_core(tiny_rows),
            swap_plane(full_gate),
            swap_plane(full_up),
            swap_plane(full_down),
            swap_plane(full_att),
        ],
    )
    d_normed = settle(part, got, p)
    g0 = g1 + rms_pull(d_normed, x0, inverse_rms(x0), g_conv)
    d_tokens = g0.astype(BF)[None]

    tiny_line = after_core(tiny_rows, core_t)
    line_in = after_core(rows_in, core_in).astype(BF)
    line_mix = collect(rows_mix, core_mix, r).astype(BF)
    (plane_a,), (plane_in,), (plane_t,), (mix_back,) = exchange(
        place,
        16,
        [
            swap_plane(full_a),
            line_plane(line_in),
            line_plane(tiny_line),
            line_home(line_mix),
        ],
    )
    FF = TP * FS
    by_weight = [(k * FS, FS, k, 0) for k in range(3)]
    by_gate = [(k * CS, CS, 0, k * D) for k in range(3)]
    by_head = [(0, QS, 0, 0), (QS, KS, 1, 0), (QS + KS, KS, 2, 0), (QS + 2 * KS, QS, 3, 0)]
    ready = finish(
        place,
        place.here(),
        [
            *[
                (own, came[0], by_weight[:1], [(shard, FF)])
                for own, came in zip((full_gate, full_up, full_down), plane_b)
            ],
            (full_att, plane_att, by_head, [(shard, TP * k) for k in (QS, KS, KS, QS)]),
            (full_a, plane_a, by_weight, [(shard, FF)] * 3),
            (None, plane_in, by_gate, [(shard, 3 * D)]),
        ],
        plane_t,
        mix_back,
        taps,
    )
    out_b, out_att, out_a, (out_in,) = ready[:3], ready[3:7], ready[7:10], ready[10:11]
    of_conv, of_ffa, of_att, of_ffb, of_taps, d_heads, out_mix = ready[11:]
    return (
        mixed,
        d_tokens,
        of_conv[0],
        out_in,
        of_taps,
        out_mix,
        of_ffa[0],
        out_a[0],
        out_a[1],
        out_a[2].T,
        of_att[0],
        out_att[0],
        out_att[1],
        out_att[2],
        d_heads,
        out_att[3].T,
        of_ffb[0],
        out_b[0],
        out_b[1],
        out_b[2].T,
    )


def solution(mesh):
    place = Place(mesh.shape["rows"], mesh.shape["seq"])
    whole = ("rows", "seq")
    wide, first, second = P("rows", "seq", None), P(whole, None), P(None, whole)
    in_specs = (
        (wide, P("rows", None), wide, P(whole), first, second, first)
        + (P(whole), first, first, second)
        + (P(whole), first, first, first, P(), second)
        + (P(whole), first, first, second)
    )
    out_specs = (
        (wide, wide, P(whole), first, second, first)
        + (P(whole), first, first, second)
        + (P(whole), first, first, first, P(), second)
        + (P(whole), first, first, second)
    )
    return jax.shard_map(
        functools.partial(per_device, place),
        mesh=mesh,
        in_specs=in_specs,
        out_specs=out_specs,
        check_vma=False,
    )
```
